32 devices in a mesh: shard: 4 (over y, x), ctx: 2 (over core), tp: 4 (over z).
Axes of the slice: x: 2, y: 2, z: 4, core: 2. Of those that a mesh axis runs over, the one named last changes fastest.
Arguments:
- hidden_in: bfloat16 [2048, 2048], P(('shard', 'ctx')), may hold values from -6 to 6
- cotangent: bfloat16 [2048, 2048], P(('shard', 'ctx')), may hold values from -6 to 6
- teacher_out: bfloat16 [2048, 2048], P(('shard', 'ctx')), may hold values from -6 to 6
- teacher_mix: bfloat16 [2048, 2048], P(('shard', 'ctx')), may hold values from -6 to 6
- valid_mask: int32 [2048], P(('shard', 'ctx')), may hold values from 0 to 1, as said below
- doc_start: int32 [2048], P(('shard', 'ctx')), may hold values 0 or 1
- attn_gain: bfloat16 [2048], P(('shard', 'ctx')), may hold values from 0.5 to 1.5
- w_query: bfloat16 [2048, 2048], P(('shard', 'ctx'), 'tp'), may hold values from -0.125 to 0.125
- w_key: bfloat16 [2048, 2048], P(('shard', 'ctx'), 'tp'), may hold values from -0.125 to 0.125
- w_value: bfloat16 [2048, 2048], P(('shard', 'ctx'), 'tp'), may hold values from -0.125 to 0.125
- w_forget: bfloat16 [2048, 256], P(('shard', 'ctx'), 'tp'), may hold values from -0.125 to 0.125
- forget_bias: bfloat16 [4, 64], P('tp', ('shard', 'ctx')), may hold values from 1 to 8
- head_gain: bfloat16 [4, 512], P('tp', ('shard', 'ctx')), may hold values from 0.5 to 1.5
- w_outgate: bfloat16 [2048, 2048], P(('shard', 'ctx'), 'tp'), may hold values from -0.125 to 0.125
- w_out: bfloat16 [2048, 2048], P(('shard', 'ctx'), 'tp'), may hold values from -0.25 to 0.25
- mlp_gain: bfloat16 [2048], P(('shard', 'ctx')), may hold values from 0.5 to 1.5
- w_gate: bfloat16 [2048, 5632], P(('shard', 'ctx'), 'tp'), may hold values from -0.125 to 0.125
- w_up: bfloat16 [2048, 5632], P(('shard', 'ctx'), 'tp'), may hold values from -0.125 to 0.125
- w_down: bfloat16 [2048, 5632], P(('shard', 'ctx'), 'tp'), may hold values from -0.15625 to 0.15625
Outputs:
- output: bfloat16 [2048, 2048], P(('shard', 'ctx'))
- loss_out: float32 [], replicated
- loss_mix: float32 [], replicated
- input_grad: float32 [2048, 2048], P(('shard', 'ctx'))
- grad_attn_gain: float32 [2048], P(('shard', 'ctx'))
- grad_query: float32 [2048, 2048], P(('shard', 'ctx'), 'tp')
- grad_key: float32 [2048, 2048], P(('shard', 'ctx'), 'tp')
- grad_value: float32 [2048, 2048], P(('shard', 'ctx'), 'tp')
- grad_forget: float32 [2048, 256], P(('shard', 'ctx'), 'tp')
- grad_forget_bias: float32 [4, 64], P('tp', ('shard', 'ctx'))
- grad_head_gain: float32 [4, 512], P('tp', ('shard', 'ctx'))
- grad_outgate: float32 [2048, 2048], P(('shard', 'ctx'), 'tp')
- grad_out_proj: float32 [2048, 2048], P(('shard', 'ctx'), 'tp')
- grad_mlp_gain: float32 [2048], P(('shard', 'ctx'))
- grad_gate: float32 [2048, 5632], P(('shard', 'ctx'), 'tp')
- grad_up: float32 [2048, 5632], P(('shard', 'ctx'), 'tp')
- grad_down: float32 [2048, 5632], P(('shard', 'ctx'), 'tp')
The draws below stay inside these ranges and needn't reach their ends.
Inputs may be any that keep to these rules, and one draw needn't show every extreme that they name: `valid_mask`: the first token is always counted.
All inputs are finite; a program needn't handle non-finite values. No bound on the sum of `doc_start` on one device may be relied on, other than what follows from the above.
Results may differ from the reference program's by a relative error of at most 0.015.
Values may be sent and summed in bfloat16 or wider, within the bound.
A program may use at most 192 MiB of HBM per device.

```python
import jax
import jax.numpy as jnp
from jax import lax

D = 2048
H = 4
DH = 512
M = 64
FF = 5632
TOK_DEV = 256
GROUP = 64
SEQ = 512
SEQS = 4
TOKENS = 2048


def draw_valid_mask(key, part):
    positions = jnp.arange(TOKENS, dtype=jnp.int32)
    limits = 250 + 500 * positions // TOKENS
    rolls = jax.random.randint(key, (TOKENS,), 0, 1000, dtype=jnp.int32)
    chosen = (rolls < limits).astype(jnp.int32)
    return jnp.where(positions == 0, 1, chosen).astype(jnp.int32)


def place_ends(values, stream_key, smallest, largest):
    shape = values.shape
    index_at = [jax.random.randint(jax.random.fold_in(stream_key, axis), (), 0, shape[axis]) for axis in range(len(shape))]
    values = values.at[tuple(index_at)].set(smallest)
    longest = shape.index(max(shape))
    index_at[longest] = (index_at[longest] + 1) % shape[longest]
    return values.at[tuple(index_at)].set(largest)


def steps_of(key, dims, cuts, least, top_value):
    factor_of = 1.0
    for axis_at, shards_of in cuts:
        steps = jax.random.uniform(jax.random.fold_in(jax.random.fold_in(key, 6), axis_at), (shards_of,), jnp.float32, least / len(cuts), top_value / len(cuts))
        factor_of = factor_of * jnp.repeat(jnp.exp(steps), dims[axis_at] // shards_of).reshape((-1,) + (1,) * (len(dims) - 1 - axis_at))
    return factor_of


def gaussian(key, dims, deviation, most, shards=(), held_as=jnp.bfloat16):
    entries = jax.random.normal(key, dims, jnp.float32) * deviation
    if len(shards) > 0:
        entries = steps_of(key, dims, shards, -0.22, 0.18) * entries
    return jnp.clip(entries, min=-most, max=most).astype(held_as)


def setup_inputs(seed: int = 0) -> dict:
    streams_of = jax.random.split(jax.random.key(seed), 20)
    hidden_in = gaussian(streams_of[0], (TOKENS, D), 1.0, 6.0, ((0, 8),))
    cotangent = gaussian(streams_of[1], (TOKENS, D), 1.0, 6.0, ((0, 8),))
    teacher_out = gaussian(streams_of[2], (TOKENS, D), 1.0, 6.0, ((0, 8),))
    teacher_mix = gaussian(streams_of[3], (TOKENS, D), 1.0, 6.0, ((0, 8),))
    valid_mask = draw_valid_mask(jax.random.fold_in(streams_of[19], 71), 0)
    doc_start = place_ends((jax.random.randint(streams_of[5], (TOKENS,), 0, 4 * TOK_DEV) < 1).astype(jnp.int32), jax.random.fold_in(streams_of[5], 1), 0, 1)
    attn_gain = jnp.clip(1.0 + 0.1 * jax.random.normal(streams_of[6], (D,), jnp.float32), 0.5, 1.5).astype(jnp.bfloat16)
    w_query = gaussian(streams_of[7], (D, H * DH), D ** -0.5, 0.125, ((0, 8), (1, 4)))
    w_key = gaussian(streams_of[8], (D, H * DH), D ** -0.5, 0.125, ((0, 8), (1, 4)))
    w_value = gaussian(streams_of[9], (D, H * DH), D ** -0.5, 0.125, ((0, 8), (1, 4)))
    w_forget = gaussian(streams_of[10], (D, H * M), D ** -0.5, 0.125, ((0, 8), (1, 4)))
    forget_bias = jnp.clip(1.0 + 7.0 * jax.random.uniform(streams_of[11], (H, M), jnp.float32) ** steps_of(streams_of[11], (H, M), ((0, 4), (1, 8)), -0.2, 0.2), 1.0, 8.0).astype(jnp.bfloat16)
    head_gain = jnp.clip(1.0 + 0.1 * jax.random.normal(streams_of[12], (H, DH), jnp.float32), 0.5, 1.5).astype(jnp.bfloat16)
    w_outgate = gaussian(streams_of[13], (D, H * DH), D ** -0.5, 0.125, ((0, 8), (1, 4)))
    w_out = gaussian(streams_of[14], (D, H * DH), (D // 4) ** -0.5, 0.25, ((0, 8), (1, 4)))
    mlp_gain = jnp.clip(1.0 + 0.1 * jax.random.normal(streams_of[15], (D,), jnp.float32), 0.5, 1.5).astype(jnp.bfloat16)
    w_gate = gaussian(streams_of[16], (D, FF), D ** -0.5, 0.125, ((0, 8), (1, 4)))
    w_up = gaussian(streams_of[17], (D, FF), D ** -0.5, 0.125, ((0, 8), (1, 4)))
    w_down = gaussian(streams_of[18], (D, FF), (FF // 4) ** -0.5, 0.15625, ((0, 8), (1, 4)))
    return {"hidden_in": hidden_in, "cotangent": cotangent, "teacher_out": teacher_out, "teacher_mix": teacher_mix, "valid_mask": valid_mask, "doc_start": doc_start, "attn_gain": attn_gain, "w_query": w_query, "w_key": w_key, "w_value": w_value, "w_forget": w_forget, "forget_bias": forget_bias, "head_gain": head_gain, "w_outgate": w_outgate, "w_out": w_out, "mlp_gain": mlp_gain, "w_gate": w_gate, "w_up": w_up, "w_down": w_down}


EPSILON = 1e-06
GATE_NORM = 8.0
HIGH = lax.Precision.HIGHEST

@jax.custom_vjp
def low(v):
    return lax.optimization_barrier(v.astype(jnp.bfloat16)).astype(jnp.float32)

@jax.custom_vjp
def low_back(v):
    return v

def low_keep(v):
    return (low(v), None)

def low_pass(kept, grad):
    return (grad,)

def back_keep(v):
    return (v, None)

def back_low(kept, grad):
    return (low(grad),)
low.defvjp(low_keep, low_pass)
low_back.defvjp(back_keep, back_low)

def norm_rows(tensor, gain_row):
    return tensor * lax.rsqrt(lax.optimization_barrier(jnp.mean(tensor * tensor, axis=-1, keepdims=True)) + EPSILON) * gain_row

def matmul(factor_a, factor_b):
    return jnp.dot(factor_a, factor_b, precision=HIGH, preferred_element_type=jnp.float32)

def group_tail(log_decay, resets):
    cum_log = jnp.cumsum(log_decay, axis=1)
    counts = jnp.cumsum(resets, axis=1)
    same_end = (counts == counts[:, -1:]).astype(jnp.float32)
    lag_log = jnp.where(same_end[..., None] > 0, cum_log[:, -1:, :] - cum_log, 0.0)
    tail_decay = jnp.exp(lag_log) * same_end[..., None]
    carry_keep = (counts[:, -1] == 0).astype(jnp.float32)
    last_decay = jnp.exp(cum_log[:, -1, :]) * carry_keep[:, None]
    return (cum_log, counts, tail_decay, last_decay)

def group_decay(log_decay, resets):
    cum_log, counts, tail_decay, last_decay = group_tail(log_decay, resets)
    position = jnp.arange(log_decay.shape[1])
    causal = position[:, None] >= position[None, :]
    same_doc = (counts[:, :, None] == counts[:, None, :]) & causal[None]
    log_gap = cum_log[:, :, None, :] - cum_log[:, None, :, :]
    within = jnp.where(same_doc[..., None], jnp.exp(jnp.where(same_doc[..., None], log_gap, 0.0)), 0.0)
    live_mask = (counts == 0).astype(jnp.float32)
    head_decay = jnp.exp(cum_log) * live_mask[..., None]
    return (within, head_decay, tail_decay, last_decay)

def score_block(carried, pieces):
    query_feats, key_feats, log_decay, resets = pieces
    within, head_decay, tail_decay, last_decay = group_decay(log_decay, resets)
    write_rate = 1.0 - jnp.exp(log_decay)
    scaling = query_feats.shape[-1] ** (-0.5)
    pair_dots = jnp.einsum('btd,bsd->bts', query_feats, key_feats, precision=HIGH)
    inner_term = jnp.einsum('bts,btsm->btm', pair_dots, within * write_rate[:, None], precision=HIGH)
    outer_term = head_decay * jnp.einsum('btd,bmd->btm', query_feats, carried, precision=HIGH)
    new_state = last_decay[..., None] * carried + jnp.einsum('bsm,bsd->bmd', tail_decay * write_rate, key_feats, precision=HIGH)
    return (new_state, scaling * (inner_term + outer_term))

def value_block(carried, pieces):
    slot_probs, values, log_decay, resets = pieces
    within, head_decay, tail_decay, last_decay = group_decay(log_decay, resets)
    write_rate = 1.0 - jnp.exp(log_decay)
    mixing = jnp.einsum('btm,btsm->bts', slot_probs, within * write_rate[:, None], precision=HIGH)
    result = jnp.einsum('bts,bsd->btd', mixing, values, precision=HIGH)
    result = result + jnp.einsum('btm,bmd->btd', slot_probs * head_decay, carried, precision=HIGH)
    new_state = last_decay[..., None] * carried + jnp.einsum('bsm,bsd->bmd', tail_decay * write_rate, values, precision=HIGH)
    return (new_state, result)

def to_blocks(tensor, length):
    shaped = tensor.reshape((tensor.shape[0], tensor.shape[1] // length, length) + tensor.shape[2:])
    return jnp.moveaxis(shaped, 1, 0)

def from_blocks(tensor):
    joined = jnp.moveaxis(tensor, 0, 1)
    return joined.reshape((joined.shape[0], joined.shape[1] * joined.shape[2]) + joined.shape[3:])

def run_scores(query_feats, key_feats, log_decay, resets, start_state):
    pieces = (to_blocks(query_feats, GROUP), to_blocks(key_feats, GROUP), to_blocks(log_decay, GROUP), to_blocks(resets, GROUP))
    _, scores = lax.scan(jax.checkpoint(score_block), start_state, pieces)
    return from_blocks(scores)

def run_values(slot_probs, values, log_decay, resets, start_state):
    pieces = (to_blocks(slot_probs, GROUP), to_blocks(values, GROUP), to_blocks(log_decay, GROUP), to_blocks(resets, GROUP))
    _, mixed_out = lax.scan(jax.checkpoint(value_block), start_state, pieces)
    return from_blocks(mixed_out)

def post_norm(mix_tokens, gate_pre, gain_rows):
    normed = norm_rows(mix_tokens, gain_rows)
    return (normed * jax.nn.silu(gate_pre.reshape(mix_tokens.shape))).reshape(gate_pre.shape)

def split_heads(tensor):
    columns = tensor.shape[-1] // H
    shaped = tensor.reshape(SEQS, SEQ, H, columns).transpose(0, 2, 1, 3)
    return shaped.reshape(SEQS * H, SEQ, columns)

def join_heads(tensor):
    columns = tensor.shape[-1]
    shaped = tensor.reshape(SEQS, H, SEQ, columns).transpose(0, 2, 1, 3)
    return shaped.reshape(SEQS * SEQ, H * columns)

def forward(resets, hidden_in, attn_gain, w_query, w_key, w_value, w_forget, forget_bias, head_gain, w_outgate, w_out, mlp_gain, w_gate, w_up, w_down):
    normed_in = low(norm_rows(hidden_in, attn_gain))
    query_pre = low_back(matmul(normed_in, w_query))
    keys_pre = low_back(matmul(normed_in, w_key))
    query_feats = low(jax.nn.silu(query_pre))
    key_feats = low(jax.nn.silu(keys_pre))
    values = low(low_back(matmul(normed_in, w_value)))
    forget_pre = low_back(matmul(normed_in, w_forget) + forget_bias.reshape(-1))
    log_decay = jax.nn.log_sigmoid(forget_pre) / GATE_NORM
    gate_pre = low_back(matmul(normed_in, w_outgate))
    zero_state = jnp.zeros((SEQS * H, M, DH), jnp.float32)
    decay_heads = split_heads(log_decay)
    scores = run_scores(split_heads(query_feats), split_heads(key_feats), decay_heads, resets, zero_state)
    slot_probs = low(jax.nn.softmax(scores, axis=-1))
    slot_mix = run_values(slot_probs, split_heads(values), decay_heads, resets, zero_state)
    gated_out = low(post_norm(join_heads(slot_mix).reshape(TOKENS, H, DH), gate_pre, head_gain))
    branch = low_back(matmul(gated_out, w_out.T))
    middle = hidden_in + branch
    normed_mid = low(norm_rows(middle, mlp_gain))
    gate_val = low_back(matmul(normed_mid, w_gate))
    up_val = low_back(matmul(normed_mid, w_up))
    hidden_units = low(jax.nn.silu(gate_val) * up_val)
    result = middle + low_back(matmul(hidden_units, w_down.T))
    return (result, branch)

def reference(hidden_in, cotangent, teacher_out, teacher_mix, valid_mask, doc_start, attn_gain, w_query, w_key, w_value, w_forget, forget_bias, head_gain, w_outgate, w_out, mlp_gain, w_gate, w_up, w_down):
    resets = jnp.repeat(doc_start.reshape(SEQS, SEQ).astype(jnp.float32), H, axis=0)
    primals = tuple((tensor.astype(jnp.float32) for tensor in (hidden_in, attn_gain, w_query, w_key, w_value, w_forget, forget_bias, head_gain, w_outgate, w_out, mlp_gain, w_gate, w_up, w_down)))

    def bound_forward(*arguments):
        return forward(resets, *arguments)
    (result, branch), pullback = jax.vjp(bound_forward, *primals)
    mask_flat = valid_mask.astype(jnp.float32)
    mask_rows = mask_flat[:, None]
    count = jnp.sum(mask_flat)
    loss_scale = TOKENS / count
    diff_out = result - teacher_out.astype(jnp.float32)
    diff_mix = branch - teacher_mix.astype(jnp.float32)
    loss_out = jnp.sum(mask_rows * diff_out * diff_out) / (2.0 * D * count)
    loss_mix = jnp.sum(mask_rows * diff_mix * diff_mix) / (2.0 * D * count)
    grads = pullback((cotangent.astype(jnp.float32) + loss_scale * mask_rows * diff_out, loss_scale * mask_rows * diff_mix))
    return (result.astype(jnp.bfloat16), loss_out, loss_mix, grads[0], grads[1], grads[2], grads[3], grads[4], grads[5], grads[6], grads[7], grads[8], grads[9], grads[10], grads[11], grads[12], grads[13])
```

```python
import functools

import jax
import jax.numpy as jnp
from jax import lax
from jax.experimental import pallas as pl
from jax.experimental.pallas import tpu as pltpu
from jax.sharding import PartitionSpec as P

F32 = jnp.float32
BF = jnp.bfloat16
EPSILON = 1e-06
GATE_NORM = 8.0


def dot_nn(a, b):
    return lax.dot_general(a, b, (((1,), (0,)), ((), ())), preferred_element_type=F32)


def dot_nt(a, b):
    return lax.dot_general(a, b, (((1,), (1,)), ((), ())), preferred_element_type=F32)


def dot_tn(a, b):
    return lax.dot_general(a, b, (((0,), (0,)), ((), ())), preferred_element_type=F32)


def halves(x):
    hi = x.astype(BF)
    return hi, (x - hi.astype(F32)).astype(BF)


def sigmoid(u):
    return 1.0 / (1.0 + jnp.exp(-u))


def n_levels(tokens):
    return tokens.bit_length() - 1


def span_matrix(level, tokens):
    t = lax.broadcasted_iota(jnp.int32, (tokens, tokens), 0)
    u = lax.broadcasted_iota(jnp.int32, (tokens, tokens), 1)
    depth = n_levels(tokens)
    if level == depth:
        keep = u <= t
    elif level == depth + 1:
        keep = u > t
    else:
        half = 1 << level
        edge = (t & ~(2 * half - 1)) + half
        odd = (t & half) > 0
        keep = (odd & (u >= edge) & (u <= t)) | (~odd & (u > t) & (u < edge))
    return keep.astype(F32).astype(BF)


def odd_rows(level, tokens, columns):
    t = lax.broadcasted_iota(jnp.int32, (tokens, columns), 0)
    return (t & (1 << level)) > 0


def same_pair(level, tokens):
    t = lax.broadcasted_iota(jnp.int32, (tokens, tokens), 0)
    u = lax.broadcasted_iota(jnp.int32, (tokens, tokens), 1)
    return (t >> (level + 1)) == (u >> (level + 1))


def ends_kernel(pre_ref, resets_ref, keys_ref, values_ref, spans_ref, total_ref, ends_ref):
    tokens, slots = pre_ref.shape
    depth = n_levels(tokens)
    width = keys_ref.shape[1]
    pre = pre_ref[...]
    log_decay = (jnp.minimum(pre, 0.0) - jnp.log1p(jnp.exp(-jnp.abs(pre)))) / GATE_NORM
    write = 1.0 - jnp.exp(log_decay)
    hi, lo = halves(log_decay)
    resets = jnp.broadcast_to(resets_ref[...], (tokens, slots)).astype(BF)
    stacked = jnp.concatenate([hi, lo, resets], axis=1)
    for level in range(depth + 2):
        sums = dot_nn(span_matrix(level, tokens), stacked)
        gap = sums[:, :slots] + sums[:, slots : 2 * slots]
        live = sums[:, 2 * slots :] < 0.5
        span = jnp.where(live, jnp.exp(gap), 0.0)
        spans_ref[level] = span
        if level == depth:
            total_ref[...] = span[tokens - 1 :, :]
        if level == depth + 1:
            hi, lo = halves(span * write)
            ends_ref[:, :width] = dot_tn(hi, keys_ref[...]) + dot_tn(lo, keys_ref[...])
            ends_ref[:, width:] = dot_tn(hi, values_ref[...]) + dot_tn(lo, values_ref[...])


def run_ends(pre, resets, keys, values):
    tokens, slots = pre.shape
    depth = n_levels(tokens)
    return pl.pallas_call(
        ends_kernel,
        out_shape=(
            jax.ShapeDtypeStruct((depth + 2, tokens, slots), F32),
            jax.ShapeDtypeStruct((1, slots), F32),
            jax.ShapeDtypeStruct((slots, keys.shape[1] + values.shape[1]), F32),
        ),
        name="slot_ends",
    )(pre, resets, keys, values)


def decay_write(pre):
    log_decay = (jnp.minimum(pre, 0.0) - jnp.log1p(jnp.exp(-jnp.abs(pre)))) / GATE_NORM
    return jnp.exp(log_decay)


def forward_kernel(
    query_ref, keys_ref, values_ref, pre_ref, spans_ref, state_ref, gate_ref, gain_ref,
    probs_ref, pairs_ref, mixing_ref, mix_ref, gated_ref,
):
    tokens, slots = pre_ref.shape
    depth = n_levels(tokens)
    width = keys_ref.shape[1]
    scaling = width ** (-0.5)
    write = 1.0 - decay_write(pre_ref[...])
    query = query_ref[...]
    pairs = dot_nt(query, keys_ref[...])
    pairs_ref[...] = pairs
    t = lax.broadcasted_iota(jnp.int32, (tokens, tokens), 0)
    u = lax.broadcasted_iota(jnp.int32, (tokens, tokens), 1)
    diagonal = jnp.sum(jnp.where(t == u, pairs, 0.0), axis=1, keepdims=True)
    state_hi, state_lo = halves(state_ref[:, :width])
    head = spans_ref[depth]
    raw = head * (dot_nt(query, state_hi) + dot_nt(query, state_lo)) + diagonal * write
    for level in range(depth):
        span = spans_ref[level]
        odd = odd_rows(level, tokens, slots)
        left, left_lo = halves(jnp.where(same_pair(level, tokens), pairs, 0.0))
        right, right_lo = halves(jnp.where(odd, 0.0, span * write))
        pulled = dot_nn(left, right) + dot_nn(left_lo, right) + dot_nn(left, right_lo)
        raw = raw + jnp.where(odd, span, 0.0) * pulled
    scores = scaling * raw
    scores = scores - jnp.max(scores, axis=1, keepdims=True)
    raised = jnp.exp(scores)
    probs = raised / jnp.sum(raised, axis=1, keepdims=True)
    probs_ref[...] = probs
    probs = probs.astype(BF).astype(F32)
    mixing = jnp.zeros((tokens, tokens), F32)
    for level in reversed(range(depth)):
        span = spans_ref[level]
        odd = odd_rows(level, tokens, slots)
        left, left_lo = halves(jnp.where(odd, span * probs, 0.0))
        right, right_lo = halves(jnp.where(odd, 0.0, span * write))
        pushed = dot_nt(left, right) + dot_nt(left_lo, right) + dot_nt(left, right_lo)
        mixing = jnp.where(same_pair(level, tokens), pushed, mixing)
    mixing = jnp.where(t == u, jnp.sum(probs * write, axis=1, keepdims=True), mixing)
    mixing, mixing_lo = halves(mixing)
    mixing_ref[...] = mixing
    state_hi, state_lo = halves(state_ref[:, width:])
    carried, carried_lo = halves(probs * head)
    mix = dot_nn(mixing, values_ref[...]) + dot_nn(mixing_lo, values_ref[...])
    mix = mix + dot_nn(carried, state_hi) + dot_nn(carried, state_lo) + dot_nn(carried_lo, state_hi)
    mix_ref[...] = mix
    scale = lax.rsqrt(jnp.mean(mix * mix, axis=1, keepdims=True) + EPSILON)
    gate = gate_ref[...]
    gated_ref[...] = (mix * scale * gain_ref[...] * (gate * sigmoid(gate))).astype(BF)


def run_forward(query, keys, values, pre, spans, state, gate, gain):
    tokens, slots = pre.shape
    width = keys.shape[1]
    return pl.pallas_call(
        forward_kernel,
        out_shape=(
            jax.ShapeDtypeStruct((tokens, slots), F32),
            jax.ShapeDtypeStruct((tokens, tokens), F32),
            jax.ShapeDtypeStruct((tokens, tokens), BF),
            jax.ShapeDtypeStruct((tokens, width), F32),
            jax.ShapeDtypeStruct((tokens, width), BF),
        ),
        name="slot_forward",
    )(query, keys, values, pre, spans, state, gate, gain)


def backward_kernel(
    grad_ref, query_ref, keys_ref, values_ref, pre_ref, spans_ref, state_ref, gate_ref, gain_ref,
    probs_ref, pairs_ref, mixing_ref, mix_ref,
    gquery_ref, gkeys_ref, gvalues_ref, ggate_ref, ggain_ref, gwrite_ref, glog_ref, carry_ref,
):
    tokens, slots = pre_ref.shape
    depth = n_levels(tokens)
    width = keys_ref.shape[1]
    scaling = width ** (-0.5)
    gate = gate_ref[...]
    sig = sigmoid(gate)
    silu = gate * sig
    gain = gain_ref[...]
    mix = mix_ref[...]
    scale = lax.rsqrt(jnp.mean(mix * mix, axis=1, keepdims=True) + EPSILON)
    normed = mix * scale
    grad = grad_ref[...]
    ggate_ref[...] = (grad * gain * normed * (sig * (1.0 + gate * (1.0 - sig)))).astype(BF)
    ggain_ref[...] = jnp.sum(grad * normed * silu, axis=0, keepdims=True)
    inner = grad * gain * silu
    mix_grad = scale * (inner - normed * jnp.mean(normed * inner, axis=1, keepdims=True))
    mix_low = mix_grad.astype(BF)

    write = 1.0 - decay_write(pre_ref[...])
    query, keys, values = query_ref[...], keys_ref[...], values_ref[...]
    pairs = pairs_ref[...]
    pairs_t = dot_nt(keys, query)
    mix_rest = (mix_grad - mix_low.astype(F32)).astype(BF)
    weigh = dot_nt(mix_low, values) + dot_nt(mix_rest, values)
    weigh_t = dot_nt(values, mix_low) + dot_nt(values, mix_rest)
    t = lax.broadcasted_iota(jnp.int32, (tokens, tokens), 0)
    u = lax.broadcasted_iota(jnp.int32, (tokens, tokens), 1)
    pair_diag = jnp.sum(jnp.where(t == u, pairs, 0.0), axis=1, keepdims=True)
    weigh_diag = jnp.sum(jnp.where(t == u, weigh, 0.0), axis=1, keepdims=True)
    head = spans_ref[depth]
    probs = probs_ref[...]
    probs_low = probs.astype(BF).astype(F32)

    vstate_hi, vstate_lo = halves(state_ref[:, width:])
    head_probs = head * (
        dot_nt(mix_low, vstate_hi) + dot_nt(mix_low, vstate_lo) + dot_nt(mix_rest, vstate_hi)
    )
    probs_grad = head_probs + weigh_diag * write
    row_values, row_keys = [], []
    for level in range(depth):
        span = spans_ref[level]
        odd = odd_rows(level, tokens, slots)
        same = same_pair(level, tokens)
        right, right_lo = halves(jnp.where(odd, 0.0, span * write))
        reach = jnp.where(odd, span, 0.0)
        left, left_lo = halves(jnp.where(same, weigh, 0.0))
        term = reach * (dot_nn(left, right) + dot_nn(left_lo, right) + dot_nn(left, right_lo))
        row_values.append(term)
        left, left_lo = halves(jnp.where(same, pairs, 0.0))
        row_keys.append(reach * (dot_nn(left, right) + dot_nn(left_lo, right) + dot_nn(left, right_lo)))
        probs_grad = probs_grad + term
    scores_grad = probs * (probs_grad - jnp.sum(probs_grad * probs, axis=1, keepdims=True))
    scores_grad = scaling * scores_grad

    kstate_hi, kstate_lo = halves(state_ref[:, :width])
    head_keys = head * (dot_nt(query, kstate_hi) + dot_nt(query, kstate_lo))
    gwrite = pair_diag * scores_grad + weigh_diag * probs_low
    glog = dot_tn(span_matrix(depth, tokens), (head_keys * scores_grad + head_probs * probs_low).astype(BF))
    gpairs = jnp.zeros((tokens, tokens), F32)
    for level in reversed(range(depth)):
        span = spans_ref[level]
        odd = odd_rows(level, tokens, slots)
        same = same_pair(level, tokens)
        reach = jnp.where(odd, span, 0.0)
        source = jnp.where(odd, 0.0, span)
        key_side, key_rest = halves(reach * scores_grad)
        value_side, value_rest = halves(reach * probs_low)
        seen, seen_rest = halves(jnp.where(same, pairs_t, 0.0))
        felt, felt_rest = halves(jnp.where(same, weigh_t, 0.0))
        sent, sent_rest = halves(source * write)
        pushed = dot_nt(key_side, sent) + dot_nt(key_rest, sent) + dot_nt(key_side, sent_rest)
        gpairs = jnp.where(same, pushed, gpairs)
        column = source * (
            dot_nn(seen, key_side) + dot_nn(seen, key_rest) + dot_nn(seen_rest, key_side)
            + dot_nn(felt, value_side) + dot_nn(felt, value_rest) + dot_nn(felt_rest, value_side)
        )
        gwrite = gwrite + column
        moved = column * write + row_values[level] * probs_low + row_keys[level] * scores_grad
        spread = span_matrix(level, tokens)
        moved, moved_rest = halves(moved)
        glog = glog + dot_tn(spread, moved) + dot_tn(spread, moved_rest)
    gpairs = jnp.where(t == u, jnp.sum(scores_grad * write, axis=1, keepdims=True), gpairs)
    gpairs, gpairs_rest = halves(gpairs)
    gwrite_ref[...] = gwrite
    glog_ref[...] = glog
    key_head, key_head_rest = halves(scores_grad * head)
    gquery_ref[...] = (
        dot_nn(gpairs, keys)
        + dot_nn(gpairs_rest, keys)
        + dot_nn(key_head, kstate_hi)
        + dot_nn(key_head, kstate_lo)
        + dot_nn(key_head_rest, kstate_hi)
    )
    gkeys_ref[...] = dot_tn(gpairs, query) + dot_tn(gpairs_rest, query)
    gvalues_ref[...] = dot_tn(mixing_ref[...], mix_low)
    carry_ref[:, :width] = dot_tn(key_head, query) + dot_tn(key_head_rest, query)
    carry_ref[:, width:] = dot_tn((probs_low * head).astype(BF), mix_low)


def run_backward(grad, query, keys, values, pre, spans, state, gate, gain, probs, pairs, mixing, mix):
    tokens, slots = pre.shape
    width = keys.shape[1]
    wide = jax.ShapeDtypeStruct((tokens, width), F32)
    narrow = jax.ShapeDtypeStruct((tokens, slots), F32)
    return pl.pallas_call(
        backward_kernel,
        out_shape=(
            wide, wide, wide,
            jax.ShapeDtypeStruct((tokens, width), BF),
            jax.ShapeDtypeStruct((1, width), F32),
            narrow, narrow,
            jax.ShapeDtypeStruct((slots, 2 * width), F32),
        ),
        name="slot_backward",
    )(grad, query, keys, values, pre, spans, state, gate, gain, probs, pairs, mixing, mix)


def finish_kernel(
    gquery_ref, gkeys_ref, gvalues_ref, ggate_ref, gwrite_ref, glog_ref,
    keys_ref, values_ref, pre_ref, spans_ref, query_pre_ref, keys_pre_ref,
    state_ref, total_ref, ends_ref, out_ref,
):
    tokens, slots = pre_ref.shape
    depth = n_levels(tokens)
    width = keys_ref.shape[1]
    pre = pre_ref[...]
    decay = decay_write(pre)
    write = 1.0 - decay
    keys, values = keys_ref[...], values_ref[...]
    ends = ends_ref[...]
    ends_low = ends.astype(BF)
    tail = spans_ref[depth + 1]
    sent = (tail * write).astype(BF)
    column = tail * (dot_nt(keys, ends_low[:, :width]) + dot_nt(values, ends_low[:, width:]))
    glog = glog_ref[...] + dot_tn(span_matrix(depth + 1, tokens), (column * write).astype(BF))
    carried = lax.dot_general(
        jnp.ones((1, 2 * width), F32), ends * state_ref[...], (((1,), (1,)), ((), ())),
        precision=lax.Precision.HIGHEST, preferred_element_type=F32,
    )
    glog = glog + carried * total_ref[...]
    glog = glog - decay * (gwrite_ref[...] + column)
    u = query_pre_ref[...]
    s = sigmoid(u)
    out_ref[:, :width] = (gquery_ref[...] * (s * (1.0 + u * (1.0 - s)))).astype(BF)
    u = keys_pre_ref[...]
    s = sigmoid(u)
    gkeys = gkeys_ref[...] + dot_nn(sent, ends_low[:, :width])
    out_ref[:, width : 2 * width] = (gkeys * (s * (1.0 + u * (1.0 - s)))).astype(BF)
    out_ref[:, 2 * width : 3 * width] = (gvalues_ref[...] + dot_nn(sent, ends_low[:, width:])).astype(BF)
    out_ref[:, 3 * width : 4 * width] = ggate_ref[...]
    gforget = glog * sigmoid(-pre) / GATE_NORM
    room = out_ref.shape[1] - 4 * width - slots
    out_ref[:, 4 * width :] = jnp.concatenate(
        [gforget.astype(BF), jnp.zeros((tokens, room), BF)], axis=1
    )


def run_finish(gquery, gkeys, gvalues, ggate, gwrite, glog, keys, values, pre, spans, query_pre, keys_pre, state, total, ends):
    tokens, slots = pre.shape
    width = keys.shape[1]
    return pl.pallas_call(
        finish_kernel,
        out_shape=jax.ShapeDtypeStruct((tokens, 4 * width + 128), BF),
        name="slot_finish",
    )(gquery, gkeys, gvalues, ggate, gwrite, glog, keys, values, pre, spans, query_pre, keys_pre, state, total, ends)


MESH = pl.DeviceIdType.MESH


def greet(axes_of_peers):
    barrier = pltpu.get_barrier_semaphore()
    for peer in axes_of_peers:
        pl.semaphore_signal(barrier, inc=1, device_id=peer, device_id_type=MESH)
    pl.semaphore_wait(barrier, len(axes_of_peers))


def tp_peers():
    count = lax.axis_size("tp")
    me = lax.axis_index("tp")
    return me, [lax.rem(me + k, count) for k in range(1, count)]


def sum_over_tp(partial_ref, landed, send_sems, recv_sems):
    me, peers = tp_peers()
    copies = []
    for k, peer in enumerate(peers):
        copy = pltpu.make_async_remote_copy(
            src_ref=partial_ref.at[peer],
            dst_ref=landed.at[k],
            send_sem=send_sems.at[k],
            recv_sem=recv_sems.at[k],
            device_id={"tp": peer},
            device_id_type=MESH,
        )
        copy.start()
        copies.append(copy)
    total = partial_ref[me].astype(F32)
    for k, copy in enumerate(copies):
        copy.wait()
        total = total + landed[k].astype(F32)
    return total


def spread_over_tp(rows_ref, full_ref, send_sems, recv_sems):
    me, peers = tp_peers()
    copies = []
    for k, peer in enumerate(peers):
        copy = pltpu.make_async_remote_copy(
            src_ref=rows_ref,
            dst_ref=full_ref.at[me],
            send_sem=send_sems.at[k],
            recv_sem=recv_sems.at[k],
            device_id={"tp": peer},
            device_id_type=MESH,
        )
        copy.start()
        copies.append(copy)
    full_ref[me] = rows_ref[...]
    for copy in copies:
        copy.wait()


def exchange_kernel(epilogue, n_in, n_rows, partial_ref, *refs):
    me, peers = tp_peers()
    inputs = refs[:n_in]
    full_ref = refs[n_in]
    outputs = refs[n_in + 1 : n_in + 1 + n_rows]
    landed, rows_ref, send_a, recv_a, send_b, recv_b = refs[n_in + 1 + n_rows :]
    greet([{"tp": peer} for peer in peers])
    total = sum_over_tp(partial_ref, landed, send_a, recv_a)
    epilogue(total, me, inputs, outputs, rows_ref)
    spread_over_tp(rows_ref, full_ref, send_b, recv_b)


def run_exchange(epilogue, name, collective_id, partial, inputs, row_outputs):
    tp = lax.axis_size("tp")
    tokens, columns = partial.shape
    share = tokens // tp
    partial = partial.reshape(tp, share, columns)
    outs = pl.pallas_call(
        functools.partial(exchange_kernel, epilogue, len(inputs), len(row_outputs)),
        out_shape=(jax.ShapeDtypeStruct((tp, share, columns), BF), *row_outputs),
        in_specs=[pl.BlockSpec(memory_space=pltpu.VMEM)] * (1 + len(inputs)),
        out_specs=tuple([pl.BlockSpec(memory_space=pltpu.VMEM)] * (1 + len(row_outputs))),
        scratch_shapes=[
            pltpu.VMEM((tp - 1, share, columns), BF),
            pltpu.VMEM((share, columns), BF),
            pltpu.SemaphoreType.DMA((tp - 1,)),
            pltpu.SemaphoreType.DMA((tp - 1,)),
            pltpu.SemaphoreType.DMA((tp - 1,)),
            pltpu.SemaphoreType.DMA((tp - 1,)),
        ],
        compiler_params=pltpu.CompilerParams(collective_id=collective_id, has_side_effects=True),
        name=name,
    )(partial, *inputs)
    return (outs[0].reshape(tokens, columns), *outs[1:])


def middle_epilogue(total, me, inputs, outputs, rows_ref):
    hidden_ref, gain_ref = inputs
    (branch_ref,) = outputs
    branch_ref[...] = total
    middle = hidden_ref[me].astype(F32) + total
    scale = lax.rsqrt(jnp.mean(middle * middle, axis=1, keepdims=True) + EPSILON)
    rows_ref[...] = (middle * scale * gain_ref[...]).astype(BF)


def result_epilogue(total, me, inputs, outputs, rows_ref):
    hidden_ref, branch_ref, teacher_out_ref, teacher_mix_ref, cotangent_ref, mask_ref, scale_ref = inputs
    output_ref, grad_ref, losses_ref = outputs
    branch = branch_ref[...]
    result = hidden_ref[me].astype(F32) + branch + total
    output_ref[...] = result.astype(BF)
    mask = mask_ref[me]
    gap = result - teacher_out_ref[me].astype(F32)
    gap_mix = branch - teacher_mix_ref[me].astype(F32)
    loss_out = jnp.sum(mask * (gap * gap), keepdims=True)
    loss_mix = jnp.sum(mask * (gap_mix * gap_mix), keepdims=True)
    lane = lax.broadcasted_iota(jnp.int32, (1, 128), 1)
    losses_ref[...] = jnp.where(lane == 0, loss_out, 0.0) + jnp.where(lane == 1, loss_mix, 0.0)
    grad = cotangent_ref[me].astype(F32) + scale_ref[...] * mask * gap
    grad_ref[...] = grad
    rows_ref[...] = grad.astype(BF)


def norm_back(grad, rows, gain):
    scale = lax.rsqrt(jnp.mean(rows * rows, axis=1, keepdims=True) + EPSILON)
    unit = rows * scale
    gain_grad = jnp.sum(grad * unit, axis=0, keepdims=True)
    inner = grad * gain
    return scale * (inner - unit * jnp.mean(unit * inner, axis=1, keepdims=True)), gain_grad


def branch_epilogue(total, me, inputs, outputs, rows_ref):
    hidden_ref, branch_ref, teacher_mix_ref, grad_ref, mask_ref, scale_ref, gain_ref = inputs
    grad_middle_ref, gain_grad_ref = outputs
    branch = branch_ref[...]
    part, gain_grad = norm_back(total, hidden_ref[me].astype(F32) + branch, gain_ref[...])
    gain_grad_ref[...] = gain_grad
    grad_middle = part + grad_ref[...]
    grad_middle_ref[...] = grad_middle
    gap_mix = branch - teacher_mix_ref[me].astype(F32)
    rows_ref[...] = (grad_middle + scale_ref[...] * mask_ref[me] * gap_mix).astype(BF)


def input_epilogue(total, me, inputs, outputs, rows_ref):
    hidden_ref, grad_middle_ref, gain_ref = inputs
    (gain_grad_ref,) = outputs
    part, gain_grad = norm_back(total, hidden_ref[me].astype(F32), gain_ref[...])
    gain_grad_ref[...] = gain_grad
    rows_ref[...] = (part + grad_middle_ref[...]).astype(BF)


def scatter_kernel(count, inner, *refs):
    sources, rows_ref = refs[:count], refs[count]
    targets, full_ref = refs[count + 1 : 2 * count + 1], refs[2 * count + 1]
    send_sems, recv_sems, send_b, recv_b = refs[2 * count + 2 :]
    shards, ctxs = lax.axis_size("shard"), lax.axis_size("ctx")
    devices = shards * ctxs
    me = lax.axis_index("shard") * ctxs + lax.axis_index("ctx")
    _, across = tp_peers()
    peers = [lax.rem(me + k, devices) for k in range(1, devices)]
    places = [{"shard": lax.div(peer, ctxs), "ctx": lax.rem(peer, ctxs)} for peer in peers]
    greet(places + [{"tp": peer} for peer in across])
    copies = []
    for k, (peer, place) in enumerate(zip(peers, places)):
        for i in range(count):
            copy = pltpu.make_async_remote_copy(
                src_ref=sources[i].at[peer],
                dst_ref=targets[i].at[me],
                send_sem=send_sems.at[i, k],
                recv_sem=recv_sems.at[i, k],
                device_id=place,
                device_id_type=MESH,
            )
            copy.start()
            copies.append(copy)
    for i in range(count):
        targets[i][me] = sources[i][me]
    spread_over_tp(rows_ref, full_ref, send_b, recv_b)
    for copy in copies:
        copy.wait()


def run_scatter(arrays, rows, name, collective_id):
    shards, ctxs, tp = lax.axis_size("shard"), lax.axis_size("ctx"), lax.axis_size("tp")
    devices = shards * ctxs
    count = len(arrays)
    tokens, columns = arrays[0].shape
    step = columns // devices
    blocks = [a.reshape(tokens, devices, step).transpose(1, 0, 2) for a in arrays]
    outs = pl.pallas_call(
        functools.partial(scatter_kernel, count, None),
        out_shape=(
            *[jax.ShapeDtypeStruct((devices, tokens, step), BF)] * count,
            jax.ShapeDtypeStruct((tp, *rows.shape), BF),
        ),
        in_specs=[pl.BlockSpec(memory_space=pltpu.VMEM)] * (count + 1),
        out_specs=tuple([pl.BlockSpec(memory_space=pltpu.VMEM)] * (count + 1)),
        scratch_shapes=[
            pltpu.SemaphoreType.DMA((count, devices - 1)),
            pltpu.SemaphoreType.DMA((count, devices - 1)),
            pltpu.SemaphoreType.DMA((tp - 1,)),
            pltpu.SemaphoreType.DMA((tp - 1,)),
        ],
        compiler_params=pltpu.CompilerParams(collective_id=collective_id, has_side_effects=True),
        name=name,
    )(*blocks, rows)
    return [o.reshape(devices * tokens, step) for o in outs[:count]] + [outs[count].reshape(tp * rows.shape[0], -1)]


def passed_along(value, axis, steps):
    count = lax.axis_size(axis)
    leading, last = (max(0, -steps), min(count, count - steps))
    return lax.ppermute(value, axis, [(source, source + steps) for source in range(leading, last)])


def relay(value, decay, axis, steps):
    carried = passed_along(value, axis, steps)
    for _ in range(lax.axis_size(axis) - 2):
        carried = passed_along(value + decay * carried, axis, steps)
    return carried


GROUPED = ("shard", "ctx")


def gathered(value):
    return lax.all_gather(value, GROUPED, axis=0, tiled=True)


def per_device(
    hidden_in,
    cotangent,
    teacher_out,
    teacher_mix,
    valid_mask,
    doc_start,
    attn_gain,
    w_query,
    w_key,
    w_value,
    w_forget,
    forget_bias,
    head_gain,
    w_outgate,
    w_out,
    mlp_gain,
    w_gate,
    w_up,
    w_down,
):
    tokens, features = hidden_in.shape
    devices = lax.axis_size(GROUPED)
    tp = lax.axis_size("tp")
    share = tokens // tp
    rows = w_query.shape[0]
    width = w_query.shape[1]
    slots = w_forget.shape[1]
    units = w_gate.shape[1]
    tokens_all = tokens * devices
    mask_flat = valid_mask.astype(F32)

    def column(vector):
        flat = vector.reshape(-1, 1).astype(BF)
        return jnp.pad(flat, ((0, rows - flat.shape[0]), (0, 0)))

    count_own = jnp.sum(mask_flat).reshape(1)
    extras = jnp.concatenate(
        [column(attn_gain), column(mlp_gain), column(forget_bias), column(head_gain), column(count_own)], axis=1
    )
    extras = jnp.pad(extras, ((0, 0), (0, 128 - slots - extras.shape[1])))
    first = gathered(jnp.concatenate([w_query, w_key, w_value, w_outgate, w_forget, extras], axis=1))
    pack = jnp.concatenate([w_out, w_gate, w_up, w_down], axis=1)
    pack, first = lax.optimization_barrier((pack, first))
    second = gathered(pack)

    spare = first[:, 4 * width + slots :].astype(F32)
    attn_scale = spare[:, 0].reshape(1, -1)
    mlp_scale = spare[:, 1].reshape(1, -1)
    bias = spare[:, 2].reshape(devices, rows)[:, : slots // devices].reshape(1, slots)
    head_scale = spare[:, 3].reshape(devices, rows)[:, : width // devices].reshape(1, width)
    count_total = jnp.sum(spare[:, 4].reshape(devices, rows)[:, 0])
    loss_scale = (tokens_all / count_total).reshape(1, 1)

    hidden_f = hidden_in.astype(F32)
    scale = lax.rsqrt(jnp.mean(hidden_f * hidden_f, axis=-1, keepdims=True) + EPSILON)
    normed_in = (hidden_f * scale * attn_scale).astype(BF)
    pre_all = dot_nn(normed_in, first)
    query_pre = pre_all[:, :width]
    keys_pre = pre_all[:, width : 2 * width]
    query = jax.nn.silu(query_pre).astype(BF)
    keys = jax.nn.silu(keys_pre).astype(BF)
    values = pre_all[:, 2 * width : 3 * width].astype(BF)
    gate_pre = pre_all[:, 3 * width : 4 * width]
    forget_pre = pre_all[:, 4 * width : 4 * width + slots] + bias
    resets = doc_start.astype(F32)[:, None]

    spans, total, ends = run_ends(forget_pre, resets, keys, values)
    decay = total.reshape(slots, 1)
    state = relay(ends, decay, "ctx", 1)
    probs, pairs, mixing, mix, gated = run_forward(
        query, keys, values, forget_pre, spans, state, gate_pre, head_scale
    )
    out_w = second[:, :width]
    gate_w = second[:, width : width + units]
    up_w = second[:, width + units : width + 2 * units]
    down_w = second[:, width + 2 * units :]

    by_share = lambda tensor: tensor.reshape(tp, share, -1)
    hidden_s, teacher_out_s, teacher_mix_s, cotangent_s = map(by_share, (hidden_in, teacher_out, teacher_mix, cotangent))
    mask_s = by_share(mask_flat)
    narrow = lambda *shape: jax.ShapeDtypeStruct(shape, F32)

    normed_mid, branch = run_exchange(
        middle_epilogue, "sum_branch", 1, dot_nt(gated, out_w).astype(BF), (hidden_s, mlp_scale),
        (narrow(share, features),),
    )
    gate_val = dot_nn(normed_mid, gate_w)
    up_val = dot_nn(normed_mid, up_w)
    hidden_units = (jax.nn.silu(gate_val) * up_val).astype(BF)
    forward_all = gathered(jnp.concatenate([gated, hidden_units], axis=1))
    grad_mlp, output_rows, grad_result, losses = run_exchange(
        result_epilogue, "sum_result", 2, dot_nt(hidden_units, down_w).astype(BF),
        (hidden_s, branch, teacher_out_s, teacher_mix_s, cotangent_s, mask_s, loss_scale),
        (jax.ShapeDtypeStruct((share, features), BF), narrow(share, features), narrow(1, 128)),
    )
    grad_units = dot_nn(grad_mlp, down_w)
    gate_sig = jax.nn.sigmoid(gate_val)
    grad_gate_val = (grad_units * up_val * (gate_sig * (1.0 + gate_val * (1.0 - gate_sig)))).astype(BF)
    grad_up_val = (grad_units * (gate_val * gate_sig)).astype(BF)
    grad_both = jnp.concatenate([grad_gate_val, grad_up_val], axis=1)
    mlp_all = gathered(grad_both)
    grad_branch, grad_middle, mlp_gain_part = run_exchange(
        branch_epilogue, "sum_middle", 3, dot_nt(grad_both, second[:, width : width + 2 * units]).astype(BF),
        (hidden_s, branch, teacher_mix_s, grad_result, mask_s, loss_scale, mlp_scale),
        (narrow(share, features), narrow(1, features)),
    )
    grad_gated = dot_nn(grad_branch, out_w)
    gquery, gkeys, gvalues, ggate, head_gain_part, gwrite, glog, carry = run_backward(
        grad_gated, query, keys, values, forget_pre, spans, state, gate_pre, head_scale, probs, pairs, mixing, mix
    )
    later = relay(carry, decay, "ctx", -1)
    grad_pre = run_finish(
        gquery, gkeys, gvalues, ggate, gwrite, glog, keys, values, forget_pre, spans, query_pre, keys_pre,
        state, total, later,
    )
    attn_all = gathered(grad_pre)
    grad_in, attn_gain_part = run_exchange(
        input_epilogue, "sum_input", 4, dot_nt(grad_pre, first).astype(BF), (hidden_s, grad_middle, attn_scale),
        (narrow(1, features),),
    )
    normed_in_c, normed_mid_c, grad_mlp_c, grad_branch_c, output = run_scatter(
        (normed_in, normed_mid, grad_mlp, grad_branch), output_rows, "spread_rows", 5
    )
    gate_grad = dot_tn(normed_mid_c, mlp_all[:, :units])
    up_grad = dot_tn(normed_mid_c, mlp_all[:, units:])
    out_grad = dot_tn(grad_branch_c, forward_all[:, :width])
    down_grad = dot_tn(grad_mlp_c, forward_all[:, width:])
    query_grad = dot_tn(normed_in_c, attn_all[:, :width])
    keys_grad = dot_tn(normed_in_c, attn_all[:, width : 2 * width])
    values_grad = dot_tn(normed_in_c, attn_all[:, 2 * width : 3 * width])
    outgate_grad = dot_tn(normed_in_c, attn_all[:, 3 * width : 4 * width])
    forget_all = attn_all[:, 4 * width : 4 * width + slots]
    forget_grad = dot_tn(normed_in_c, forget_all)
    index = lax.axis_index(GROUPED)
    bias_grad = jnp.sum(forget_all.astype(F32), axis=0, keepdims=True)
    bias_grad = lax.dynamic_slice_in_dim(bias_grad, index * (slots // devices), slots // devices, axis=1)

    head_slots = jnp.where(jnp.arange(tp)[:, None] == lax.axis_index("tp"), head_gain_part, 0.0)
    packed = jnp.concatenate(
        [attn_gain_part.reshape(-1), mlp_gain_part.reshape(-1), head_slots.reshape(-1), losses.reshape(-1)]
    )
    packed = lax.psum(packed, ("shard", "ctx", "tp"))
    cut = lambda vector, size: lax.dynamic_slice_in_dim(vector, index * size, size)
    attn_gain_grad = cut(packed[:features], features // devices)
    mlp_gain_grad = cut(packed[features : 2 * features], features // devices)
    head_all = packed[2 * features : 2 * features + tp * width].reshape(tp, width)
    head_row = lax.dynamic_slice_in_dim(head_all, lax.axis_index("tp"), 1, axis=0)
    head_gain_grad = lax.dynamic_slice_in_dim(head_row, index * (width // devices), width // devices, axis=1)
    sums = packed[2 * features + tp * width :]
    loss_out = sums[0] / (2.0 * features * count_total)
    loss_mix = sums[1] / (2.0 * features * count_total)
    return (
        output,
        loss_out,
        loss_mix,
        grad_in.astype(F32),
        attn_gain_grad,
        query_grad,
        keys_grad,
        values_grad,
        forget_grad,
        bias_grad,
        head_gain_grad,
        outgate_grad,
        out_grad,
        mlp_gain_grad,
        gate_grad,
        up_grad,
        down_grad,
    )


def solution(mesh):
    return jax.shard_map(
        per_device,
        mesh=mesh,
        in_specs=(
            P(("shard", "ctx"), None),
            P(("shard", "ctx"), None),
            P(("shard", "ctx"), None),
            P(("shard", "ctx"), None),
            P(("shard", "ctx")),
            P(("shard", "ctx")),
            P(("shard", "ctx")),
            P(("shard", "ctx"), "tp"),
            P(("shard", "ctx"), "tp"),
            P(("shard", "ctx"), "tp"),
            P(("shard", "ctx"), "tp"),
            P("tp", ("shard", "ctx")),
            P("tp", ("shard", "ctx")),
            P(("shard", "ctx"), "tp"),
            P(("shard", "ctx"), "tp"),
            P(("shard", "ctx")),
            P(("shard", "ctx"), "tp"),
            P(("shard", "ctx"), "tp"),
            P(("shard", "ctx"), "tp"),
        ),
        out_specs=(
            P(("shard", "ctx"), None),
            P(),
            P(),
            P(("shard", "ctx"), None),
            P(("shard", "ctx")),
            P(("shard", "ctx"), "tp"),
            P(("shard", "ctx"), "tp"),
            P(("shard", "ctx"), "tp"),
            P(("shard", "ctx"), "tp"),
            P("tp", ("shard", "ctx")),
            P("tp", ("shard", "ctx")),
            P(("shard", "ctx"), "tp"),
            P(("shard", "ctx"), "tp"),
            P(("shard", "ctx")),
            P(("shard", "ctx"), "tp"),
            P(("shard", "ctx"), "tp"),
            P(("shard", "ctx"), "tp"),
        ),
        check_vma=False,
    )
```

```python
import functools

import jax
import jax.numpy as jnp
from jax import lax
from jax.experimental import pallas as pl
from jax.experimental.pallas import tpu as pltpu
from jax.sharding import PartitionSpec as P

F32 = jnp.float32
BF = jnp.bfloat16
EPSILON = 1e-06
GATE_NORM = 8.0


def dot_nn(a, b):
    return lax.dot_general(a, b, (((1,), (0,)), ((), ())), preferred_element_type=F32)


def dot_nt(a, b):
    return lax.dot_general(a, b, (((1,), (1,)), ((), ())), preferred_element_type=F32)


def dot_tn(a, b):
    return lax.dot_general(a, b, (((0,), (0,)), ((), ())), preferred_element_type=F32)


def halves(x):
    hi = x.astype(BF)
    return hi, (x - hi.astype(F32)).astype(BF)


def sigmoid(u):
    return 1.0 / (1.0 + jnp.exp(-u))


def n_levels(tokens):
    return tokens.bit_length() - 1


def span_matrix(level, tokens):
    t = lax.broadcasted_iota(jnp.int32, (tokens, tokens), 0)
    u = lax.broadcasted_iota(jnp.int32, (tokens, tokens), 1)
    depth = n_levels(tokens)
    if level == depth:
        keep = u <= t
    elif level == depth + 1:
        keep = u > t
    else:
        half = 1 << level
        edge = (t & ~(2 * half - 1)) + half
        odd = (t & half) > 0
        keep = (odd & (u >= edge) & (u <= t)) | (~odd & (u > t) & (u < edge))
    return keep.astype(F32).astype(BF)


def odd_rows(level, tokens, columns):
    t = lax.broadcasted_iota(jnp.int32, (tokens, columns), 0)
    return (t & (1 << level)) > 0


def same_pair(level, tokens):
    t = lax.broadcasted_iota(jnp.int32, (tokens, tokens), 0)
    u = lax.broadcasted_iota(jnp.int32, (tokens, tokens), 1)
    return (t >> (level + 1)) == (u >> (level + 1))


def ends_kernel(pre_ref, resets_ref, keys_ref, values_ref, spans_ref, total_ref, ends_ref):
    tokens, slots = pre_ref.shape
    depth = n_levels(tokens)
    width = keys_ref.shape[1]
    pre = pre_ref[...]
    log_decay = (jnp.minimum(pre, 0.0) - jnp.log1p(jnp.exp(-jnp.abs(pre)))) / GATE_NORM
    write = 1.0 - jnp.exp(log_decay)
    hi, lo = halves(log_decay)
    resets = jnp.broadcast_to(resets_ref[...], (tokens, slots)).astype(BF)
    stacked = jnp.concatenate([hi, lo, resets], axis=1)
    for level in range(depth + 2):
        sums = dot_nn(span_matrix(level, tokens), stacked)
        gap = sums[:, :slots] + sums[:, slots : 2 * slots]
        live = sums[:, 2 * slots :] < 0.5
        span = jnp.where(live, jnp.exp(gap), 0.0)
        spans_ref[level] = span
        if level == depth:
            total_ref[...] = span[tokens - 1 :, :]
        if level == depth + 1:
            hi, lo = halves(span * write)
            ends_ref[:, :width] = dot_tn(hi, keys_ref[...]) + dot_tn(lo, keys_ref[...])
            ends_ref[:, width:] = dot_tn(hi, values_ref[...]) + dot_tn(lo, values_ref[...])


def run_ends(pre, resets, keys, values):
    tokens, slots = pre.shape
    depth = n_levels(tokens)
    return pl.pallas_call(
        ends_kernel,
        out_shape=(
            jax.ShapeDtypeStruct((depth + 2, tokens, slots), F32),
            jax.ShapeDtypeStruct((1, slots), F32),
            jax.ShapeDtypeStruct((slots, keys.shape[1] + values.shape[1]), F32),
        ),
        name="slot_ends",
    )(pre, resets, keys, values)


def decay_write(pre):
    log_decay = (jnp.minimum(pre, 0.0) - jnp.log1p(jnp.exp(-jnp.abs(pre)))) / GATE_NORM
    return jnp.exp(log_decay)


def forward_kernel(
    query_ref, keys_ref, values_ref, pre_ref, spans_ref, state_ref, gate_ref, gain_ref,
    probs_ref, pairs_ref, mixing_ref, mix_ref, gated_ref,
):
    tokens, slots = pre_ref.shape
    depth = n_levels(tokens)
    width = keys_ref.shape[1]
    scaling = width ** (-0.5)
    write = 1.0 - decay_write(pre_ref[...])
    query = query_ref[...]
    pairs = dot_nt(query, keys_ref[...])
    pairs_ref[...] = pairs
    t = lax.broadcasted_iota(jnp.int32, (tokens, tokens), 0)
    u = lax.broadcasted_iota(jnp.int32, (tokens, tokens), 1)
    diagonal = jnp.sum(jnp.where(t == u, pairs, 0.0), axis=1, keepdims=True)
    state_hi, state_lo = halves(state_ref[:, :width])
    head = spans_ref[depth]
    raw = head * (dot_nt(query, state_hi) + dot_nt(query, state_lo)) + diagonal * write
    for level in range(depth):
        span = spans_ref[level]
        odd = odd_rows(level, tokens, slots)
        left, left_lo = halves(jnp.where(same_pair(level, tokens), pairs, 0.0))
        right, right_lo = halves(jnp.where(odd, 0.0, span * write))
        pulled = dot_nn(left, right) + dot_nn(left_lo, right) + dot_nn(left, right_lo)
        raw = raw + jnp.where(odd, span, 0.0) * pulled
    scores = scaling * raw
    scores = scores - jnp.max(scores, axis=1, keepdims=True)
    raised = jnp.exp(scores)
    probs = raised / jnp.sum(raised, axis=1, keepdims=True)
    probs_ref[...] = probs
    probs = probs.astype(BF).astype(F32)
    mixing = jnp.zeros((tokens, tokens), F32)
    for level in reversed(range(depth)):
        span = spans_ref[level]
        odd = odd_rows(level, tokens, slots)
        left, left_lo = halves(jnp.where(odd, span * probs, 0.0))
        right, right_lo = halves(jnp.where(odd, 0.0, span * write))
        pushed = dot_nt(left, right) + dot_nt(left_lo, right) + dot_nt(left, right_lo)
        mixing = jnp.where(same_pair(level, tokens), pushed, mixing)
    mixing = jnp.where(t == u, jnp.sum(probs * write, axis=1, keepdims=True), mixing)
    mixing, mixing_lo = halves(mixing)
    mixing_ref[...] = mixing
    state_hi, state_lo = halves(state_ref[:, width:])
    carried, carried_lo = halves(probs * head)
    mix = dot_nn(mixing, values_ref[...]) + dot_nn(mixing_lo, values_ref[...])
    mix = mix + dot_nn(carried, state_hi) + dot_nn(carried, state_lo) + dot_nn(carried_lo, state_hi)
    mix_ref[...] = mix
    scale = lax.rsqrt(jnp.mean(mix * mix, axis=1, keepdims=True) + EPSILON)
    gate = gate_ref[...]
    gated_ref[...] = (mix * scale * gain_ref[...] * (gate * sigmoid(gate))).astype(BF)


def run_forward(query, keys, values, pre, spans, state, gate, gain):
    tokens, slots = pre.shape
    width = keys.shape[1]
    return pl.pallas_call(
        forward_kernel,
        out_shape=(
            jax.ShapeDtypeStruct((tokens, slots), F32),
            jax.ShapeDtypeStruct((tokens, tokens), F32),
            jax.ShapeDtypeStruct((tokens, tokens), BF),
            jax.ShapeDtypeStruct((tokens, width), F32),
            jax.ShapeDtypeStruct((tokens, width), BF),
        ),
        name="slot_forward",
    )(query, keys, values, pre, spans, state, gate, gain)


def backward_kernel(
    grad_ref, query_ref, keys_ref, values_ref, pre_ref, spans_ref, state_ref, gate_ref, gain_ref,
    probs_ref, pairs_ref, mixing_ref, mix_ref,
    gquery_ref, gkeys_ref, gvalues_ref, ggate_ref, ggain_ref, gwrite_ref, glog_ref, carry_ref,
):
    tokens, slots = pre_ref.shape
    depth = n_levels(tokens)
    width = keys_ref.shape[1]
    scaling = width ** (-0.5)
    gate = gate_ref[...]
    sig = sigmoid(gate)
    silu = gate * sig
    gain = gain_ref[...]
    mix = mix_ref[...]
    scale = lax.rsqrt(jnp.mean(mix * mix, axis=1, keepdims=True) + EPSILON)
    normed = mix * scale
    grad = grad_ref[...]
    ggate_ref[...] = (grad * gain * normed * (sig * (1.0 + gate * (1.0 - sig)))).astype(BF)
    ggain_ref[...] = jnp.sum(grad * normed * silu, axis=0, keepdims=True)
    inner = grad * gain * silu
    mix_grad = scale * (inner - normed * jnp.mean(normed * inner, axis=1, keepdims=True))
    mix_low = mix_grad.astype(BF)

    write = 1.0 - decay_write(pre_ref[...])
    query, keys, values = query_ref[...], keys_ref[...], values_ref[...]
    pairs = pairs_ref[...]
    pairs_t = dot_nt(keys, query)
    mix_rest = (mix_grad - mix_low.astype(F32)).astype(BF)
    weigh = dot_nt(mix_low, values) + dot_nt(mix_rest, values)
    weigh_t = dot_nt(values, mix_low) + dot_nt(values, mix_rest)
    t = lax.broadcasted_iota(jnp.int32, (tokens, tokens), 0)
    u = lax.broadcasted_iota(jnp.int32, (tokens, tokens), 1)
    pair_diag = jnp.sum(jnp.where(t == u, pairs, 0.0), axis=1, keepdims=True)
    weigh_diag = jnp.sum(jnp.where(t == u, weigh, 0.0), axis=1, keepdims=True)
    head = spans_ref[depth]
    probs = probs_ref[...]
    probs_low = probs.astype(BF).astype(F32)

    vstate_hi, vstate_lo = halves(state_ref[:, width:])
    head_probs = head * (
        dot_nt(mix_low, vstate_hi) + dot_nt(mix_low, vstate_lo) + dot_nt(mix_rest, vstate_hi)
    )
    probs_grad = head_probs + weigh_diag * write
    row_values, row_keys = [], []
    for level in range(depth):
        span = spans_ref[level]
        odd = odd_rows(level, tokens, slots)
        same = same_pair(level, tokens)
        right, right_lo = halves(jnp.where(odd, 0.0, span * write))
        reach = jnp.where(odd, span, 0.0)
        left, left_lo = halves(jnp.where(same, weigh, 0.0))
        term = reach * (dot_nn(left, right) + dot_nn(left_lo, right) + dot_nn(left, right_lo))
        row_values.append(term)
        left, left_lo = halves(jnp.where(same, pairs, 0.0))
        row_keys.append(reach * (dot_nn(left, right) + dot_nn(left_lo, right) + dot_nn(left, right_lo)))
        probs_grad = probs_grad + term
    scores_grad = probs * (probs_grad - jnp.sum(probs_grad * probs, axis=1, keepdims=True))
    scores_grad = scaling * scores_grad

    kstate_hi, kstate_lo = halves(state_ref[:, :width])
    head_keys = head * (dot_nt(query, kstate_hi) + dot_nt(query, kstate_lo))
    gwrite = pair_diag * scores_grad + weigh_diag * probs_low
    glog = dot_tn(span_matrix(depth, tokens), (head_keys * scores_grad + head_probs * probs_low).astype(BF))
    gpairs = jnp.zeros((tokens, tokens), F32)
    for level in reversed(range(depth)):
        span = spans_ref[level]
        odd = odd_rows(level, tokens, slots)
        same = same_pair(level, tokens)
        reach = jnp.where(odd, span, 0.0)
        source = jnp.where(odd, 0.0, span)
        key_side, key_rest = halves(reach * scores_grad)
        value_side, value_rest = halves(reach * probs_low)
        seen, seen_rest = halves(jnp.where(same, pairs_t, 0.0))
        felt, felt_rest = halves(jnp.where(same, weigh_t, 0.0))
        sent, sent_rest = halves(source * write)
        pushed = dot_nt(key_side, sent) + dot_nt(key_rest, sent) + dot_nt(key_side, sent_rest)
        gpairs = jnp.where(same, pushed, gpairs)
        column = source * (
            dot_nn(seen, key_side) + dot_nn(seen, key_rest) + dot_nn(seen_rest, key_side)
            + dot_nn(felt, value_side) + dot_nn(felt, value_rest) + dot_nn(felt_rest, value_side)
        )
        gwrite = gwrite + column
        moved = column * write + row_values[level] * probs_low + row_keys[level] * scores_grad
        spread = span_matrix(level, tokens)
        moved, moved_rest = halves(moved)
        glog = glog + dot_tn(spread, moved) + dot_tn(spread, moved_rest)
    gpairs = jnp.where(t == u, jnp.sum(scores_grad * write, axis=1, keepdims=True), gpairs)
    gpairs, gpairs_rest = halves(gpairs)
    gwrite_ref[...] = gwrite
    glog_ref[...] = glog
    key_head, key_head_rest = halves(scores_grad * head)
    gquery_ref[...] = (
        dot_nn(gpairs, keys)
        + dot_nn(gpairs_rest, keys)
        + dot_nn(key_head, kstate_hi)
        + dot_nn(key_head, kstate_lo)
        + dot_nn(key_head_rest, kstate_hi)
    )
    gkeys_ref[...] = dot_tn(gpairs, query) + dot_tn(gpairs_rest, query)
    gvalues_ref[...] = dot_tn(mixing_ref[...], mix_low)
    carry_ref[:, :width] = dot_tn(key_head, query) + dot_tn(key_head_rest, query)
    carry_ref[:, width:] = dot_tn((probs_low * head).astype(BF), mix_low)


def run_backward(grad, query, keys, values, pre, spans, state, gate, gain, probs, pairs, mixing, mix):
    tokens, slots = pre.shape
    width = keys.shape[1]
    wide = jax.ShapeDtypeStruct((tokens, width), F32)
    narrow = jax.ShapeDtypeStruct((tokens, slots), F32)
    return pl.pallas_call(
        backward_kernel,
        out_shape=(
            wide, wide, wide,
            jax.ShapeDtypeStruct((tokens, width), BF),
            jax.ShapeDtypeStruct((1, width), F32),
            narrow, narrow,
            jax.ShapeDtypeStruct((slots, 2 * width), F32),
        ),
        name="slot_backward",
    )(grad, query, keys, values, pre, spans, state, gate, gain, probs, pairs, mixing, mix)


def finish_kernel(
    gquery_ref, gkeys_ref, gvalues_ref, ggate_ref, gwrite_ref, glog_ref,
    keys_ref, values_ref, pre_ref, spans_ref, query_pre_ref, keys_pre_ref,
    state_ref, total_ref, ends_ref, out_ref,
):
    tokens, slots = pre_ref.shape
    depth = n_levels(tokens)
    width = keys_ref.shape[1]
    pre = pre_ref[...]
    decay = decay_write(pre)
    write = 1.0 - decay
    keys, values = keys_ref[...], values_ref[...]
    ends = ends_ref[...]
    ends_low = ends.astype(BF)
    tail = spans_ref[depth + 1]
    sent = (tail * write).astype(BF)
    column = tail * (dot_nt(keys, ends_low[:, :width]) + dot_nt(values, ends_low[:, width:]))
    glog = glog_ref[...] + dot_tn(span_matrix(depth + 1, tokens), (column * write).astype(BF))
    carried = lax.dot_general(
        jnp.ones((1, 2 * width), F32), ends * state_ref[...], (((1,), (1,)), ((), ())),
        precision=lax.Precision.HIGHEST, preferred_element_type=F32,
    )
    glog = glog + carried * total_ref[...]
    glog = glog - decay * (gwrite_ref[...] + column)
    u = query_pre_ref[...]
    s = sigmoid(u)
    out_ref[:, :width] = (gquery_ref[...] * (s * (1.0 + u * (1.0 - s)))).astype(BF)
    u = keys_pre_ref[...]
    s = sigmoid(u)
    gkeys = gkeys_ref[...] + dot_nn(sent, ends_low[:, :width])
    out_ref[:, width : 2 * width] = (gkeys * (s * (1.0 + u * (1.0 - s)))).astype(BF)
    out_ref[:, 2 * width : 3 * width] = (gvalues_ref[...] + dot_nn(sent, ends_low[:, width:])).astype(BF)
    out_ref[:, 3 * width : 4 * width] = ggate_ref[...]
    gforget = glog * sigmoid(-pre) / GATE_NORM
    room = out_ref.shape[1] - 4 * width - slots
    out_ref[:, 4 * width :] = jnp.concatenate(
        [gforget.astype(BF), jnp.zeros((tokens, room), BF)], axis=1
    )


def run_finish(gquery, gkeys, gvalues, ggate, gwrite, glog, keys, values, pre, spans, query_pre, keys_pre, state, total, ends):
    tokens, slots = pre.shape
    width = keys.shape[1]
    return pl.pallas_call(
        finish_kernel,
        out_shape=jax.ShapeDtypeStruct((tokens, 4 * width + 128), BF),
        name="slot_finish",
    )(gquery, gkeys, gvalues, ggate, gwrite, glog, keys, values, pre, spans, query_pre, keys_pre, state, total, ends)


MESH = pl.DeviceIdType.MESH
GROUPED = ("shard", "ctx")


def greet(axes_of_peers):
    barrier = pltpu.get_barrier_semaphore()
    for peer in axes_of_peers:
        pl.semaphore_signal(barrier, inc=1, device_id=peer, device_id_type=MESH)
    pl.semaphore_wait(barrier, len(axes_of_peers))


def tp_peers():
    count = lax.axis_size("tp")
    me = lax.axis_index("tp")
    return me, [lax.rem(me + k, count) for k in range(1, count)]


def sum_over_tp(partial_ref, landed, send_sems, recv_sems):
    me, peers = tp_peers()
    copies = []
    for k, peer in enumerate(peers):
        copy = pltpu.make_async_remote_copy(
            src_ref=partial_ref.at[peer],
            dst_ref=landed.at[k],
            send_sem=send_sems.at[k],
            recv_sem=recv_sems.at[k],
            device_id={"tp": peer},
            device_id_type=MESH,
        )
        copy.start()
        copies.append(copy)
    total = partial_ref[me].astype(F32)
    for k, copy in enumerate(copies):
        copy.wait()
        total = total + landed[k].astype(F32)
    return total


def spread_over_tp(rows_ref, full_ref, send_sems, recv_sems):
    me, peers = tp_peers()
    copies = []
    for k, peer in enumerate(peers):
        copy = pltpu.make_async_remote_copy(
            src_ref=rows_ref,
            dst_ref=full_ref.at[me],
            send_sem=send_sems.at[k],
            recv_sem=recv_sems.at[k],
            device_id={"tp": peer},
            device_id_type=MESH,
        )
        copy.start()
        copies.append(copy)
    full_ref[me] = rows_ref[...]
    for copy in copies:
        copy.wait()


def plane_peers():
    shards, ctxs = lax.axis_size("shard"), lax.axis_size("ctx")
    devices = shards * ctxs
    me = lax.axis_index("shard") * ctxs + lax.axis_index("ctx")
    peers = [lax.rem(me + k, devices) for k in range(1, devices)]
    places = [{"shard": lax.div(peer, ctxs), "ctx": lax.rem(peer, ctxs)} for peer in peers]
    return me, peers, places


def start_scatter(sources, targets, send_sems, recv_sems):
    me, peers, places = plane_peers()
    copies = []
    for i, (source, target) in enumerate(zip(sources, targets)):
        step = target.shape[2]

        def block(at):
            if len(source.shape) == 3:
                return source.at[at]
            return source.at[:, pl.ds(pl.multiple_of(at * step, step), step)]

        for k, (peer, place) in enumerate(zip(peers, places)):
            copy = pltpu.make_async_remote_copy(
                src_ref=block(peer),
                dst_ref=target.at[me],
                send_sem=send_sems.at[i, k],
                recv_sem=recv_sems.at[i, k],
                device_id=place,
                device_id_type=MESH,
            )
            copy.start()
            copies.append(copy)
    for source, target in zip(sources, targets):
        target[me] = block_of(source, me, target.shape[2])
    return copies


def block_of(source, at, step):
    if len(source.shape) == 3:
        return source[at]
    return source[:, pl.ds(pl.multiple_of(at * step, step), step)]


def start_sums(row_ref, landed, send_sems, recv_sems, peers, places, me):
    copies = []
    landed[me] = row_ref[...]
    for k, place in enumerate(places):
        copy = pltpu.make_async_remote_copy(
            src_ref=row_ref,
            dst_ref=landed.at[me],
            send_sem=send_sems.at[k],
            recv_sem=recv_sems.at[k],
            device_id=place,
            device_id_type=MESH,
        )
        copy.start()
        copies.append(copy)
    return copies


def summed(landed):
    total = landed[0]
    for k in range(1, landed.shape[0]):
        total = total + landed[k]
    return total


def exchange_kernel(epilogue, n_in, n_rows, n_moved, n_sums, partial_ref, *refs):
    me, peers = tp_peers()
    inputs, refs = refs[:n_in], refs[n_in:]
    sources, refs = refs[:n_moved], refs[n_moved:]
    full_ref, refs = refs[0], refs[1:]
    outputs, refs = refs[:n_rows], refs[n_rows:]
    targets, refs = refs[:n_moved], refs[n_moved:]
    sums, refs = refs[: 2 * n_sums], refs[2 * n_sums :]
    landed, rows_ref, send_a, recv_a, send_b, recv_b, send_m, recv_m = refs[:8]
    own, plane, places = plane_peers()
    across = [{"tp": peer} for peer in peers]
    greet(across + (places if n_moved or n_sums else []))
    moves = start_scatter(sources, targets, send_m, recv_m)
    total = sum_over_tp(partial_ref, landed, send_a, recv_a)
    epilogue(total, me, inputs, outputs, rows_ref)
    if n_sums:
        row_ref, in_plane, plane_row, in_tp, send_p, recv_p, send_t, recv_t = refs[8:]
        width = outputs[0].shape[1]
        row_ref[:, :width] = outputs[0][...]
        row_ref[:, width:] = inputs[-1][...]
        started = start_sums(row_ref, in_plane, send_p, recv_p, plane, places, own)
    spread_over_tp(rows_ref, full_ref, send_b, recv_b)
    if n_sums:
        for copy in started:
            copy.wait()
        plane_row[...] = summed(in_plane)
        sums[0][...] = plane_row[...]
        started = start_sums(plane_row, in_tp, send_t, recv_t, peers, across, me)
        for copy in started:
            copy.wait()
        sums[1][...] = summed(in_tp)
    for copy in moves:
        copy.wait()


def run_exchange(epilogue, name, collective_id, partial, inputs, row_outputs, moved=(), summing=False):
    tp = lax.axis_size("tp")
    devices = lax.axis_size(GROUPED)
    tokens, columns = partial.shape
    share = tokens // tp
    partial = partial.reshape(tp, share, columns)
    step = columns // devices
    if step % 128:
        moved = [m.reshape(tokens, devices, step).transpose(1, 0, 2) for m in moved]
    count = len(moved)
    scratch = [
        pltpu.VMEM((tp - 1, share, columns), BF),
        pltpu.VMEM((share, columns), BF),
        *[pltpu.SemaphoreType.DMA((tp - 1,))] * 4,
        *[pltpu.SemaphoreType.DMA((max(count, 1), devices - 1))] * 2,
    ]
    extra = ()
    if summing:
        row = row_outputs[0].shape[1] + inputs[-1].shape[1]
        extra = (jax.ShapeDtypeStruct((1, row), F32),) * 2
        scratch += [
            pltpu.VMEM((1, row), F32),
            pltpu.VMEM((devices, 1, row), F32),
            pltpu.VMEM((1, row), F32),
            pltpu.VMEM((tp, 1, row), F32),
            *[pltpu.SemaphoreType.DMA((devices - 1,))] * 2,
            *[pltpu.SemaphoreType.DMA((tp - 1,))] * 2,
        ]
    out_shape = (
        jax.ShapeDtypeStruct((tp, share, columns), BF),
        *row_outputs,
        *[jax.ShapeDtypeStruct((devices, tokens, step), BF)] * count,
        *extra,
    )
    outs = pl.pallas_call(
        functools.partial(exchange_kernel, epilogue, len(inputs), len(row_outputs), count, int(summing)),
        out_shape=out_shape,
        in_specs=[pl.BlockSpec(memory_space=pltpu.VMEM)] * (1 + len(inputs) + count),
        out_specs=tuple([pl.BlockSpec(memory_space=pltpu.VMEM)] * len(out_shape)),
        scratch_shapes=scratch,
        compiler_params=pltpu.CompilerParams(collective_id=collective_id, has_side_effects=True),
        name=name,
    )(partial, *inputs, *moved)
    start = 1 + len(row_outputs)
    return (
        outs[0].reshape(tokens, columns),
        *outs[1:start],
        *[o.reshape(devices * tokens, step) for o in outs[start : start + count]],
        *outs[start + count :],
    )


def middle_epilogue(total, me, inputs, outputs, rows_ref):
    hidden_ref, gain_ref = inputs
    (branch_ref,) = outputs
    branch_ref[...] = total
    middle = hidden_ref[me].astype(F32) + total
    scale = lax.rsqrt(jnp.mean(middle * middle, axis=1, keepdims=True) + EPSILON)
    rows_ref[...] = (middle * scale * gain_ref[...]).astype(BF)


def result_epilogue(total, me, inputs, outputs, rows_ref):
    hidden_ref, branch_ref, teacher_out_ref, teacher_mix_ref, cotangent_ref, mask_ref, scale_ref = inputs
    output_ref, grad_ref, losses_ref = outputs
    branch = branch_ref[...]
    result = hidden_ref[me].astype(F32) + branch + total
    output_ref[...] = result.astype(BF)
    mask = mask_ref[me]
    gap = result - teacher_out_ref[me].astype(F32)
    gap_mix = branch - teacher_mix_ref[me].astype(F32)
    loss_out = jnp.sum(mask * (gap * gap), keepdims=True)
    loss_mix = jnp.sum(mask * (gap_mix * gap_mix), keepdims=True)
    lane = lax.broadcasted_iota(jnp.int32, (1, 128), 1)
    losses_ref[...] = jnp.where(lane == 0, loss_out, 0.0) + jnp.where(lane == 1, loss_mix, 0.0)
    grad = cotangent_ref[me].astype(F32) + scale_ref[...] * mask * gap
    grad_ref[...] = grad
    rows_ref[...] = grad.astype(BF)


def norm_back(grad, rows, gain):
    scale = lax.rsqrt(jnp.mean(rows * rows, axis=1, keepdims=True) + EPSILON)
    unit = rows * scale
    gain_grad = jnp.sum(grad * unit, axis=0, keepdims=True)
    inner = grad * gain
    return scale * (inner - unit * jnp.mean(unit * inner, axis=1, keepdims=True)), gain_grad


def branch_epilogue(total, me, inputs, outputs, rows_ref):
    hidden_ref, branch_ref, teacher_mix_ref, grad_ref, mask_ref, scale_ref, gain_ref = inputs
    grad_middle_ref, gain_grad_ref = outputs
    branch = branch_ref[...]
    part, gain_grad = norm_back(total, hidden_ref[me].astype(F32) + branch, gain_ref[...])
    gain_grad_ref[...] = gain_grad
    grad_middle = part + grad_ref[...]
    grad_middle_ref[...] = grad_middle
    gap_mix = branch - teacher_mix_ref[me].astype(F32)
    rows_ref[...] = (grad_middle + scale_ref[...] * mask_ref[me] * gap_mix).astype(BF)


def input_epilogue(total, me, inputs, outputs, rows_ref):
    hidden_ref, grad_middle_ref, gain_ref = inputs[:3]
    (gain_grad_ref,) = outputs
    part, gain_grad = norm_back(total, hidden_ref[me].astype(F32), gain_ref[...])
    gain_grad_ref[...] = gain_grad
    rows_ref[...] = (part + grad_middle_ref[...]).astype(BF)


def passed_along(value, axis, steps):
    count = lax.axis_size(axis)
    leading, last = (max(0, -steps), min(count, count - steps))
    return lax.ppermute(value, axis, [(source, source + steps) for source in range(leading, last)])


def relay(value, decay, axis, steps):
    carried = passed_along(value, axis, steps)
    for _ in range(lax.axis_size(axis) - 2):
        carried = passed_along(value + decay * carried, axis, steps)
    return carried


def gathered(value):
    return lax.all_gather(value, GROUPED, axis=0, tiled=True)


def per_device(
    hidden_in,
    cotangent,
    teacher_out,
    teacher_mix,
    valid_mask,
    doc_start,
    attn_gain,
    w_query,
    w_key,
    w_value,
    w_forget,
    forget_bias,
    head_gain,
    w_outgate,
    w_out,
    mlp_gain,
    w_gate,
    w_up,
    w_down,
):
    tokens, features = hidden_in.shape
    devices = lax.axis_size(GROUPED)
    tp = lax.axis_size("tp")
    share = tokens // tp
    rows = w_query.shape[0]
    width = w_query.shape[1]
    slots = w_forget.shape[1]
    units = w_gate.shape[1]
    tokens_all = tokens * devices
    mask_flat = valid_mask.astype(F32)

    def column(vector):
        flat = vector.reshape(-1, 1).astype(BF)
        return jnp.pad(flat, ((0, rows - flat.shape[0]), (0, 0)))

    count_own = jnp.sum(mask_flat).reshape(1)
    extras = jnp.concatenate(
        [column(attn_gain), column(mlp_gain), column(forget_bias), column(head_gain), column(count_own)], axis=1
    )
    extras = jnp.pad(extras, ((0, 0), (0, 128 - slots - extras.shape[1])))
    first = gathered(jnp.concatenate([w_query, w_key, w_value, w_outgate, w_forget, extras, w_out], axis=1))
    pack = jnp.concatenate([w_gate, w_up, w_down], axis=1)
    pack, first = lax.optimization_barrier((pack, first))
    second = gathered(pack)

    inner = 4 * width + 128
    out_w = first[:, inner:]
    first = first[:, :inner]
    spare = first[:, 4 * width + slots :].astype(F32)
    attn_scale = spare[:, 0].reshape(1, -1)
    mlp_scale = spare[:, 1].reshape(1, -1)
    bias = spare[:, 2].reshape(devices, rows)[:, : slots // devices].reshape(1, slots)
    head_scale = spare[:, 3].reshape(devices, rows)[:, : width // devices].reshape(1, width)
    count_total = jnp.sum(spare[:, 4].reshape(devices, rows)[:, 0])
    loss_scale = (tokens_all / count_total).reshape(1, 1)

    hidden_f = hidden_in.astype(F32)
    scale = lax.rsqrt(jnp.mean(hidden_f * hidden_f, axis=-1, keepdims=True) + EPSILON)
    normed_in = (hidden_f * scale * attn_scale).astype(BF)
    pre_all = dot_nn(normed_in, first)
    query_pre = pre_all[:, :width]
    keys_pre = pre_all[:, width : 2 * width]
    query = jax.nn.silu(query_pre).astype(BF)
    keys = jax.nn.silu(keys_pre).astype(BF)
    values = pre_all[:, 2 * width : 3 * width].astype(BF)
    gate_pre = pre_all[:, 3 * width : 4 * width]
    forget_pre = pre_all[:, 4 * width : 4 * width + slots] + bias
    resets = doc_start.astype(F32)[:, None]

    spans, total, ends = run_ends(forget_pre, resets, keys, values)
    decay = total.reshape(slots, 1)
    state = relay(ends, decay, "ctx", 1)
    probs, pairs, mixing, mix, gated = run_forward(
        query, keys, values, forget_pre, spans, state, gate_pre, head_scale
    )
    gate_w = second[:, :units]
    up_w = second[:, units : 2 * units]
    down_w = second[:, 2 * units :]

    by_share = lambda tensor: tensor.reshape(tp, share, -1)
    hidden_s, teacher_out_s, teacher_mix_s, cotangent_s = map(by_share, (hidden_in, teacher_out, teacher_mix, cotangent))
    mask_s = by_share(mask_flat)
    narrow = lambda *shape: jax.ShapeDtypeStruct(shape, F32)

    normed_mid, branch = run_exchange(
        middle_epilogue, "sum_branch", 1, dot_nt(gated, out_w).astype(BF), (hidden_s, mlp_scale),
        (narrow(share, features),),
    )
    gate_val = dot_nn(normed_mid, gate_w)
    up_val = dot_nn(normed_mid, up_w)
    hidden_units = (jax.nn.silu(gate_val) * up_val).astype(BF)
    forward_all = gathered(jnp.concatenate([gated, hidden_units], axis=1))
    grad_mlp, output_rows, grad_result, losses, normed_in_c, normed_mid_c = run_exchange(
        result_epilogue, "sum_result", 2, dot_nt(hidden_units, down_w).astype(BF),
        (hidden_s, branch, teacher_out_s, teacher_mix_s, cotangent_s, mask_s, loss_scale),
        (jax.ShapeDtypeStruct((share, features), BF), narrow(share, features), narrow(1, 128)),
        moved=(normed_in, normed_mid),
    )
    output = lax.all_gather(output_rows, "tp", axis=0, tiled=True)
    grad_units = dot_nn(grad_mlp, down_w)
    gate_sig = jax.nn.sigmoid(gate_val)
    grad_gate_val = (grad_units * up_val * (gate_sig * (1.0 + gate_val * (1.0 - gate_sig)))).astype(BF)
    grad_up_val = (grad_units * (gate_val * gate_sig)).astype(BF)
    grad_both = jnp.concatenate([grad_gate_val, grad_up_val], axis=1)
    mlp_all = gathered(grad_both)
    grad_branch, grad_middle, mlp_gain_part, grad_mlp_c = run_exchange(
        branch_epilogue, "sum_middle", 3, dot_nt(grad_both, second[:, : 2 * units]).astype(BF),
        (hidden_s, branch, teacher_mix_s, grad_result, mask_s, loss_scale, mlp_scale),
        (narrow(share, features), narrow(1, features)),
        moved=(grad_mlp,),
    )
    grad_gated = dot_nn(grad_branch, out_w)
    gquery, gkeys, gvalues, ggate, head_gain_part, gwrite, glog, carry = run_backward(
        grad_gated, query, keys, values, forget_pre, spans, state, gate_pre, head_scale, probs, pairs, mixing, mix
    )
    later = relay(carry, decay, "ctx", -1)
    grad_pre = run_finish(
        gquery, gkeys, gvalues, ggate, gwrite, glog, keys, values, forget_pre, spans, query_pre, keys_pre,
        state, total, later,
    )
    mlp_all, grad_pre = lax.optimization_barrier((mlp_all, grad_pre))
    attn_all = gathered(grad_pre)
    grad_in, _, grad_branch_c, plane_sums, all_sums = run_exchange(
        input_epilogue, "sum_input", 4, dot_nt(grad_pre, first).astype(BF),
        (hidden_s, grad_middle, attn_scale, jnp.concatenate([mlp_gain_part, head_gain_part, losses], axis=1)),
        (narrow(1, features),), moved=(grad_branch,), summing=True,
    )
    gate_grad = dot_tn(normed_mid_c, mlp_all[:, :units])
    up_grad = dot_tn(normed_mid_c, mlp_all[:, units:])
    out_grad = dot_tn(grad_branch_c, forward_all[:, :width])
    down_grad = dot_tn(grad_mlp_c, forward_all[:, width:])
    query_grad = dot_tn(normed_in_c, attn_all[:, :width])
    keys_grad = dot_tn(normed_in_c, attn_all[:, width : 2 * width])
    values_grad = dot_tn(normed_in_c, attn_all[:, 2 * width : 3 * width])
    outgate_grad = dot_tn(normed_in_c, attn_all[:, 3 * width : 4 * width])
    forget_all = attn_all[:, 4 * width : 4 * width + slots]
    forget_grad = dot_tn(normed_in_c, forget_all)
    index = lax.axis_index(GROUPED)
    bias_grad = jnp.sum(forget_all.astype(F32), axis=0, keepdims=True)
    bias_grad = lax.dynamic_slice_in_dim(bias_grad, index * (slots // devices), slots // devices, axis=1)

    cut = lambda row, size: lax.dynamic_slice_in_dim(row, index * size, size, axis=1)
    attn_gain_grad = cut(all_sums[:, :features], features // devices).reshape(-1)
    mlp_gain_grad = cut(all_sums[:, features : 2 * features], features // devices).reshape(-1)
    head_gain_grad = cut(plane_sums[:, 2 * features : 2 * features + width], width // devices)
    sums = all_sums[0, 2 * features + width :]
    loss_out = sums[0] / (2.0 * features * count_total)
    loss_mix = sums[1] / (2.0 * features * count_total)
    return (
        output,
        loss_out,
        loss_mix,
        grad_in.astype(F32),
        attn_gain_grad,
        query_grad,
        keys_grad,
        values_grad,
        forget_grad,
        bias_grad,
        head_gain_grad,
        outgate_grad,
        out_grad,
        mlp_gain_grad,
        gate_grad,
        up_grad,
        down_grad,
    )


def solution(mesh):
    return jax.shard_map(
        per_device,
        mesh=mesh,
        in_specs=(
            P(("shard", "ctx"), None),
            P(("shard", "ctx"), None),
            P(("shard", "ctx"), None),
            P(("shard", "ctx"), None),
            P(("shard", "ctx")),
            P(("shard", "ctx")),
            P(("shard", "ctx")),
            P(("shard", "ctx"), "tp"),
            P(("shard", "ctx"), "tp"),
            P(("shard", "ctx"), "tp"),
            P(("shard", "ctx"), "tp"),
            P("tp", ("shard", "ctx")),
            P("tp", ("shard", "ctx")),
            P(("shard", "ctx"), "tp"),
            P(("shard", "ctx"), "tp"),
            P(("shard", "ctx")),
            P(("shard", "ctx"), "tp"),
            P(("shard", "ctx"), "tp"),
            P(("shard", "ctx"), "tp"),
        ),
        out_specs=(
            P(("shard", "ctx"), None),
            P(),
            P(),
            P(("shard", "ctx"), None),
            P(("shard", "ctx")),
            P(("shard", "ctx"), "tp"),
            P(("shard", "ctx"), "tp"),
            P(("shard", "ctx"), "tp"),
            P(("shard", "ctx"), "tp"),
            P("tp", ("shard", "ctx")),
            P("tp", ("shard", "ctx")),
            P(("shard", "ctx"), "tp"),
            P(("shard", "ctx"), "tp"),
            P(("shard", "ctx")),
            P(("shard", "ctx"), "tp"),
            P(("shard", "ctx"), "tp"),
            P(("shard", "ctx"), "tp"),
        ),
        check_vma=False,
    )
```

```python
import functools

import jax
import jax.numpy as jnp
from jax import lax
from jax.experimental import pallas as pl
from jax.experimental.pallas import tpu as pltpu
from jax.sharding import PartitionSpec as P

F32 = jnp.float32
BF = jnp.bfloat16
EPSILON = 1e-06
GATE_NORM = 8.0


def dot_nn(a, b):
    return lax.dot_general(a, b, (((1,), (0,)), ((), ())), preferred_element_type=F32)


def dot_nt(a, b):
    return lax.dot_general(a, b, (((1,), (1,)), ((), ())), preferred_element_type=F32)


def dot_tn(a, b):
    return lax.dot_general(a, b, (((0,), (0,)), ((), ())), preferred_element_type=F32)


def halves(x):
    hi = x.astype(BF)
    return hi, (x - hi.astype(F32)).astype(BF)


def sigmoid(u):
    return 1.0 / (1.0 + jnp.exp(-u))


def n_levels(tokens):
    return tokens.bit_length() - 1


def span_matrix(level, tokens):
    t = lax.broadcasted_iota(jnp.int32, (tokens, tokens), 0)
    u = lax.broadcasted_iota(jnp.int32, (tokens, tokens), 1)
    depth = n_levels(tokens)
    if level == depth:
        keep = u <= t
    elif level == depth + 1:
        keep = u > t
    else:
        half = 1 << level
        edge = (t & ~(2 * half - 1)) + half
        odd = (t & half) > 0
        keep = (odd & (u >= edge) & (u <= t)) | (~odd & (u > t) & (u < edge))
    return keep.astype(F32).astype(BF)


def odd_rows(level, tokens, columns):
    t = lax.broadcasted_iota(jnp.int32, (tokens, columns), 0)
    return (t & (1 << level)) > 0


def same_pair(level, tokens):
    t = lax.broadcasted_iota(jnp.int32, (tokens, tokens), 0)
    u = lax.broadcasted_iota(jnp.int32, (tokens, tokens), 1)
    return (t >> (level + 1)) == (u >> (level + 1))


def ends_kernel(pre_ref, resets_ref, keys_ref, values_ref, spans_ref, total_ref, ends_ref):
    tokens, slots = pre_ref.shape
    depth = n_levels(tokens)
    width = keys_ref.shape[1]
    pre = pre_ref[...]
    log_decay = (jnp.minimum(pre, 0.0) - jnp.log1p(jnp.exp(-jnp.abs(pre)))) / GATE_NORM
    write = 1.0 - jnp.exp(log_decay)
    hi, lo = halves(log_decay)
    resets = jnp.broadcast_to(resets_ref[...], (tokens, slots)).astype(BF)
    stacked = jnp.concatenate([hi, lo, resets], axis=1)
    for level in range(depth + 2):
        sums = dot_nn(span_matrix(level, tokens), stacked)
        gap = sums[:, :slots] + sums[:, slots : 2 * slots]
        live = sums[:, 2 * slots :] < 0.5
        span = jnp.where(live, jnp.exp(gap), 0.0)
        spans_ref[level] = span
        if level == depth:
            total_ref[...] = span[tokens - 1 :, :]
        if level == depth + 1:
            hi, lo = halves(span * write)
            ends_ref[:, :width] = dot_tn(hi, keys_ref[...]) + dot_tn(lo, keys_ref[...])
            ends_ref[:, width:] = dot_tn(hi, values_ref[...]) + dot_tn(lo, values_ref[...])


def run_ends(pre, resets, keys, values):
    tokens, slots = pre.shape
    depth = n_levels(tokens)
    return pl.pallas_call(
        ends_kernel,
        out_shape=(
            jax.ShapeDtypeStruct((depth + 2, tokens, slots), F32),
            jax.ShapeDtypeStruct((1, slots), F32),
            jax.ShapeDtypeStruct((slots, keys.shape[1] + values.shape[1]), F32),
        ),
        name="slot_ends",
    )(pre, resets, keys, values)


def decay_write(pre):
    log_decay = (jnp.minimum(pre, 0.0) - jnp.log1p(jnp.exp(-jnp.abs(pre)))) / GATE_NORM
    return jnp.exp(log_decay)


def forward_kernel(
    query_ref, keys_ref, values_ref, pre_ref, spans_ref, state_ref, gate_ref, gain_ref,
    probs_ref, pairs_ref, mixing_ref, mix_ref, gated_ref,
):
    tokens, slots = pre_ref.shape
    depth = n_levels(tokens)
    width = keys_ref.shape[1]
    scaling = width ** (-0.5)
    write = 1.0 - decay_write(pre_ref[...])
    query = query_ref[...]
    pairs = dot_nt(query, keys_ref[...])
    pairs_ref[...] = pairs
    t = lax.broadcasted_iota(jnp.int32, (tokens, tokens), 0)
    u = lax.broadcasted_iota(jnp.int32, (tokens, tokens), 1)
    diagonal = jnp.sum(jnp.where(t == u, pairs, 0.0), axis=1, keepdims=True)
    state_hi, state_lo = halves(state_ref[:, :width])
    head = spans_ref[depth]
    raw = head * (dot_nt(query, state_hi) + dot_nt(query, state_lo)) + diagonal * write
    for level in range(depth):
        span = spans_ref[level]
        odd = odd_rows(level, tokens, slots)
        left, left_lo = halves(jnp.where(same_pair(level, tokens), pairs, 0.0))
        right, right_lo = halves(jnp.where(odd, 0.0, span * write))
        pulled = dot_nn(left, right) + dot_nn(left_lo, right) + dot_nn(left, right_lo)
        raw = raw + jnp.where(odd, span, 0.0) * pulled
    scores = scaling * raw
    scores = scores - jnp.max(scores, axis=1, keepdims=True)
    raised = jnp.exp(scores)
    probs = raised / jnp.sum(raised, axis=1, keepdims=True)
    probs_ref[...] = probs
    probs = probs.astype(BF).astype(F32)
    mixing = jnp.zeros((tokens, tokens), F32)
    for level in reversed(range(depth)):
        span = spans_ref[level]
        odd = odd_rows(level, tokens, slots)
        left, left_lo = halves(jnp.where(odd, span * probs, 0.0))
        right, right_lo = halves(jnp.where(odd, 0.0, span * write))
        pushed = dot_nt(left, right) + dot_nt(left_lo, right) + dot_nt(left, right_lo)
        mixing = jnp.where(same_pair(level, tokens), pushed, mixing)
    mixing = jnp.where(t == u, jnp.sum(probs * write, axis=1, keepdims=True), mixing)
    mixing, mixing_lo = halves(mixing)
    mixing_ref[...] = mixing
    state_hi, state_lo = halves(state_ref[:, width:])
    carried, carried_lo = halves(probs * head)
    mix = dot_nn(mixing, values_ref[...]) + dot_nn(mixing_lo, values_ref[...])
    mix = mix + dot_nn(carried, state_hi) + dot_nn(carried, state_lo) + dot_nn(carried_lo, state_hi)
    mix_ref[...] = mix
    scale = lax.rsqrt(jnp.mean(mix * mix, axis=1, keepdims=True) + EPSILON)
    gate = gate_ref[...]
    gated_ref[...] = (mix * scale * gain_ref[...] * (gate * sigmoid(gate))).astype(BF)


def run_forward(query, keys, values, pre, spans, state, gate, gain):
    tokens, slots = pre.shape
    width = keys.shape[1]
    return pl.pallas_call(
        forward_kernel,
        out_shape=(
            jax.ShapeDtypeStruct((tokens, slots), F32),
            jax.ShapeDtypeStruct((tokens, tokens), F32),
            jax.ShapeDtypeStruct((tokens, tokens), BF),
            jax.ShapeDtypeStruct((tokens, width), F32),
            jax.ShapeDtypeStruct((tokens, width), BF),
        ),
        name="slot_forward",
    )(query, keys, values, pre, spans, state, gate, gain)


def backward_kernel(
    grad_ref, query_ref, keys_ref, values_ref, pre_ref, spans_ref, state_ref, gate_ref, gain_ref,
    probs_ref, pairs_ref, mixing_ref, mix_ref,
    gquery_ref, gkeys_ref, gvalues_ref, ggate_ref, ggain_ref, gwrite_ref, glog_ref, carry_ref,
):
    tokens, slots = pre_ref.shape
    depth = n_levels(tokens)
    width = keys_ref.shape[1]
    scaling = width ** (-0.5)
    gate = gate_ref[...]
    sig = sigmoid(gate)
    silu = gate * sig
    gain = gain_ref[...]
    mix = mix_ref[...]
    scale = lax.rsqrt(jnp.mean(mix * mix, axis=1, keepdims=True) + EPSILON)
    normed = mix * scale
    grad = grad_ref[...]
    ggate_ref[...] = (grad * gain * normed * (sig * (1.0 + gate * (1.0 - sig)))).astype(BF)
    ggain_ref[...] = jnp.sum(grad * normed * silu, axis=0, keepdims=True)
    inner = grad * gain * silu
    mix_grad = scale * (inner - normed * jnp.mean(normed * inner, axis=1, keepdims=True))
    mix_low = mix_grad.astype(BF)

    write = 1.0 - decay_write(pre_ref[...])
    query, keys, values = query_ref[...], keys_ref[...], values_ref[...]
    pairs = pairs_ref[...]
    pairs_t = dot_nt(keys, query)
    mix_rest = (mix_grad - mix_low.astype(F32)).astype(BF)
    weigh = dot_nt(mix_low, values) + dot_nt(mix_rest, values)
    weigh_t = dot_nt(values, mix_low) + dot_nt(values, mix_rest)
    t = lax.broadcasted_iota(jnp.int32, (tokens, tokens), 0)
    u = lax.broadcasted_iota(jnp.int32, (tokens, tokens), 1)
    pair_diag = jnp.sum(jnp.where(t == u, pairs, 0.0), axis=1, keepdims=True)
    weigh_diag = jnp.sum(jnp.where(t == u, weigh, 0.0), axis=1, keepdims=True)
    head = spans_ref[depth]
    probs = probs_ref[...]
    probs_low = probs.astype(BF).astype(F32)

    vstate_hi, vstate_lo = halves(state_ref[:, width:])
    head_probs = head * (
        dot_nt(mix_low, vstate_hi) + dot_nt(mix_low, vstate_lo) + dot_nt(mix_rest, vstate_hi)
    )
    probs_grad = head_probs + weigh_diag * write
    row_values, row_keys = [], []
    for level in range(depth):
        span = spans_ref[level]
        odd = odd_rows(level, tokens, slots)
        same = same_pair(level, tokens)
        right, right_lo = halves(jnp.where(odd, 0.0, span * write))
        reach = jnp.where(odd, span, 0.0)
        left, left_lo = halves(jnp.where(same, weigh, 0.0))
        term = reach * (dot_nn(left, right) + dot_nn(left_lo, right) + dot_nn(left, right_lo))
        row_values.append(term)
        left, left_lo = halves(jnp.where(same, pairs, 0.0))
        row_keys.append(reach * (dot_nn(left, right) + dot_nn(left_lo, right) + dot_nn(left, right_lo)))
        probs_grad = probs_grad + term
    scores_grad = probs * (probs_grad - jnp.sum(probs_grad * probs, axis=1, keepdims=True))
    scores_grad = scaling * scores_grad

    kstate_hi, kstate_lo = halves(state_ref[:, :width])
    head_keys = head * (dot_nt(query, kstate_hi) + dot_nt(query, kstate_lo))
    gwrite = pair_diag * scores_grad + weigh_diag * probs_low
    glog = dot_tn(span_matrix(depth, tokens), (head_keys * scores_grad + head_probs * probs_low).astype(BF))
    gpairs = jnp.zeros((tokens, tokens), F32)
    for level in reversed(range(depth)):
        span = spans_ref[level]
        odd = odd_rows(level, tokens, slots)
        same = same_pair(level, tokens)
        reach = jnp.where(odd, span, 0.0)
        source = jnp.where(odd, 0.0, span)
        key_side, key_rest = halves(reach * scores_grad)
        value_side, value_rest = halves(reach * probs_low)
        seen, seen_rest = halves(jnp.where(same, pairs_t, 0.0))
        felt, felt_rest = halves(jnp.where(same, weigh_t, 0.0))
        sent, sent_rest = halves(source * write)
        pushed = dot_nt(key_side, sent) + dot_nt(key_rest, sent) + dot_nt(key_side, sent_rest)
        gpairs = jnp.where(same, pushed, gpairs)
        column = source * (
            dot_nn(seen, key_side) + dot_nn(seen, key_rest) + dot_nn(seen_rest, key_side)
            + dot_nn(felt, value_side) + dot_nn(felt, value_rest) + dot_nn(felt_rest, value_side)
        )
        gwrite = gwrite + column
        moved = column * write + row_values[level] * probs_low + row_keys[level] * scores_grad
        spread = span_matrix(level, tokens)
        moved, moved_rest = halves(moved)
        glog = glog + dot_tn(spread, moved) + dot_tn(spread, moved_rest)
    gpairs = jnp.where(t == u, jnp.sum(scores_grad * write, axis=1, keepdims=True), gpairs)
    gpairs, gpairs_rest = halves(gpairs)
    gwrite_ref[...] = gwrite
    glog_ref[...] = glog
    key_head, key_head_rest = halves(scores_grad * head)
    gquery_ref[...] = (
        dot_nn(gpairs, keys)
        + dot_nn(gpairs_rest, keys)
        + dot_nn(key_head, kstate_hi)
        + dot_nn(key_head, kstate_lo)
        + dot_nn(key_head_rest, kstate_hi)
    )
    gkeys_ref[...] = dot_tn(gpairs, query) + dot_tn(gpairs_rest, query)
    gvalues_ref[...] = dot_tn(mixing_ref[...], mix_low)
    carry_ref[:, :width] = dot_tn(key_head, query) + dot_tn(key_head_rest, query)
    carry_ref[:, width:] = dot_tn((probs_low * head).astype(BF), mix_low)


def run_backward(grad, query, keys, values, pre, spans, state, gate, gain, probs, pairs, mixing, mix):
    tokens, slots = pre.shape
    width = keys.shape[1]
    wide = jax.ShapeDtypeStruct((tokens, width), F32)
    narrow = jax.ShapeDtypeStruct((tokens, slots), F32)
    return pl.pallas_call(
        backward_kernel,
        out_shape=(
            wide, wide, wide,
            jax.ShapeDtypeStruct((tokens, width), BF),
            jax.ShapeDtypeStruct((1, width), F32),
            narrow, narrow,
            jax.ShapeDtypeStruct((slots, 2 * width), F32),
        ),
        name="slot_backward",
    )(grad, query, keys, values, pre, spans, state, gate, gain, probs, pairs, mixing, mix)


def finish_kernel(
    gquery_ref, gkeys_ref, gvalues_ref, ggate_ref, gwrite_ref, glog_ref,
    keys_ref, values_ref, pre_ref, spans_ref, query_pre_ref, keys_pre_ref,
    state_ref, total_ref, ends_ref, out_ref,
):
    tokens, slots = pre_ref.shape
    depth = n_levels(tokens)
    width = keys_ref.shape[1]
    pre = pre_ref[...]
    decay = decay_write(pre)
    write = 1.0 - decay
    keys, values = keys_ref[...], values_ref[...]
    ends = ends_ref[...]
    ends_low = ends.astype(BF)
    tail = spans_ref[depth + 1]
    sent = (tail * write).astype(BF)
    column = tail * (dot_nt(keys, ends_low[:, :width]) + dot_nt(values, ends_low[:, width:]))
    glog = glog_ref[...] + dot_tn(span_matrix(depth + 1, tokens), (column * write).astype(BF))
    carried = lax.dot_general(
        jnp.ones((1, 2 * width), F32), ends * state_ref[...], (((1,), (1,)), ((), ())),
        precision=lax.Precision.HIGHEST, preferred_element_type=F32,
    )
    glog = glog + carried * total_ref[...]
    glog = glog - decay * (gwrite_ref[...] + column)
    u = query_pre_ref[...]
    s = sigmoid(u)
    out_ref[:, :width] = (gquery_ref[...] * (s * (1.0 + u * (1.0 - s)))).astype(BF)
    u = keys_pre_ref[...]
    s = sigmoid(u)
    gkeys = gkeys_ref[...] + dot_nn(sent, ends_low[:, :width])
    out_ref[:, width : 2 * width] = (gkeys * (s * (1.0 + u * (1.0 - s)))).astype(BF)
    out_ref[:, 2 * width : 3 * width] = (gvalues_ref[...] + dot_nn(sent, ends_low[:, width:])).astype(BF)
    out_ref[:, 3 * width : 4 * width] = ggate_ref[...]
    gforget = glog * sigmoid(-pre) / GATE_NORM
    room = out_ref.shape[1] - 4 * width - slots
    out_ref[:, 4 * width :] = jnp.concatenate(
        [gforget.astype(BF), jnp.zeros((tokens, room), BF)], axis=1
    )


def run_finish(gquery, gkeys, gvalues, ggate, gwrite, glog, keys, values, pre, spans, query_pre, keys_pre, state, total, ends):
    tokens, slots = pre.shape
    width = keys.shape[1]
    return pl.pallas_call(
        finish_kernel,
        out_shape=jax.ShapeDtypeStruct((tokens, 4 * width + 128), BF),
        name="slot_finish",
    )(gquery, gkeys, gvalues, ggate, gwrite, glog, keys, values, pre, spans, query_pre, keys_pre, state, total, ends)


MESH = pl.DeviceIdType.MESH
GROUPED = ("shard", "ctx")


def greet(axes_of_peers):
    barrier = pltpu.get_barrier_semaphore()
    for peer in axes_of_peers:
        pl.semaphore_signal(barrier, inc=1, device_id=peer, device_id_type=MESH)
    pl.semaphore_wait(barrier, len(axes_of_peers))


def tp_peers():
    count = lax.axis_size("tp")
    me = lax.axis_index("tp")
    return me, [lax.rem(me + k, count) for k in range(1, count)]


CHUNKS = 2
LAG = 2


def tp_line(partial_ref, full_ref, riders, arrived, staged, sums_ref, finish, send_a, recv_a, send_b, recv_b):
    count = lax.axis_size("tp")
    me = lax.axis_index("tp")
    rows = partial_ref.shape[1] // CHUNKS
    places = [(me, lax.rem(me + 1, count)), (count - 1 - me, lax.rem(me + count - 1, count))]

    def block_at(side, place):
        return place if side == 0 else count - 1 - place

    def cut(chunk):
        return pl.ds(chunk * rows, rows)

    def sum_copy(side, hop, chunk, source):
        return pltpu.make_async_remote_copy(
            src_ref=source,
            dst_ref=arrived.at[side, hop, chunk],
            send_sem=send_a.at[side, hop, chunk],
            recv_sem=recv_a.at[side, hop, chunk],
            device_id={"tp": places[side][1]},
            device_id_type=MESH,
        )

    def add_hop(chunk, hop):
        for side, (place, _) in enumerate(places):
            block = block_at(side, count - 1 - hop)
            own = partial_ref.at[block, cut(chunk)]
            slot = staged.at[side, hop, chunk]

            @pl.when((place > 0) & (count - 1 - hop >= place))
            def _():
                sum_copy(side, hop, chunk, slot).wait_recv()

            @pl.when((place == 0) & (count - 1 - hop > place))
            def _():
                sum_copy(side, hop, chunk, own).start()

            @pl.when((place > 0) & (count - 1 - hop > place))
            def _():
                slot[...] = (own[...].astype(F32) + arrived[side, hop, chunk].astype(F32)).astype(BF)
                sum_copy(side, hop, chunk, slot).start()

    def close(chunk):
        sums_ref[...] = partial_ref[me, cut(chunk)].astype(F32)
        for side, (place, _) in enumerate(places):

            @pl.when(place > 0)
            def _():
                sums_ref[...] += arrived[side, count - 1 - place, chunk].astype(F32)

        finish(chunk, sums_ref[...])

    gathers = [(full_ref, cut(chunk)) for chunk in range(CHUNKS)]
    gathers += [(full, pl.ds(0, full.shape[1])) for _, full in riders]

    def row_copy(side, hop, which, block):
        full, part = gathers[which]
        return pltpu.make_async_remote_copy(
            src_ref=full.at[block, part],
            dst_ref=full.at[block, part],
            send_sem=send_b.at[side, hop, which],
            recv_sem=recv_b.at[side, hop, which],
            device_id={"tp": places[side][1]},
            device_id_type=MESH,
        )

    def offer(which):
        for side, (place, _) in enumerate(places):

            @pl.when(place < count - 1)
            def _():
                row_copy(side, 0, which, me).start()

    def forward(which, hop):
        for side, (place, _) in enumerate(places):
            block = block_at(side, jnp.maximum(place - hop, 0))

            @pl.when(place >= hop)
            def _():
                row_copy(side, hop - 1, which, block).wait_recv()

            if hop < count - 1:

                @pl.when((place >= hop) & (place < count - 1))
                def _():
                    row_copy(side, hop, which, block).start()

    for rows_ref, full in riders:
        full[me] = rows_ref[...]
    steps = []
    for chunk in range(CHUNKS):
        run = [functools.partial(add_hop, chunk, hop) for hop in range(count - 1)]
        run += [functools.partial(close, chunk), functools.partial(offer, chunk)]
        run += [functools.partial(forward, chunk, hop) for hop in range(1, count)]
        steps.append(run)
    for rider in range(CHUNKS, len(gathers)):
        steps.append([functools.partial(offer, rider), *[functools.partial(forward, rider, hop) for hop in range(1, count)]])
    length = max(LAG * at + len(run) for at, run in enumerate(steps))
    for tick in range(length):
        for at, run in enumerate(steps):
            if 0 <= tick - LAG * at < len(run):
                run[tick - LAG * at]()

    def drain():
        for side, (place, _) in enumerate(places):
            for hop in range(count - 1):

                @pl.when(count - 1 - hop > place)
                def _():
                    for chunk in range(CHUNKS):
                        sum_copy(side, hop, chunk, staged.at[side, hop, chunk]).wait_send()

                @pl.when((place >= hop) & (place < count - 1))
                def _():
                    block = block_at(side, jnp.maximum(place - hop, 0))
                    for which in range(len(gathers)):
                        row_copy(side, hop, which, block).wait_send()

    return drain


def plane_peers():
    shards, ctxs = lax.axis_size("shard"), lax.axis_size("ctx")
    devices = shards * ctxs
    me = lax.axis_index("shard") * ctxs + lax.axis_index("ctx")
    peers = [lax.rem(me + k, devices) for k in range(1, devices)]
    places = [{"shard": lax.div(peer, ctxs), "ctx": lax.rem(peer, ctxs)} for peer in peers]
    return me, peers, places


def start_scatter(sources, targets, send_sems, recv_sems):
    me, peers, places = plane_peers()
    copies = []
    for i, (source, target) in enumerate(zip(sources, targets)):
        step = target.shape[2]

        def block(at):
            if len(source.shape) == 3:
                return source.at[at]
            return source.at[:, pl.ds(pl.multiple_of(at * step, step), step)]

        for k, (peer, place) in enumerate(zip(peers, places)):
            copy = pltpu.make_async_remote_copy(
                src_ref=block(peer),
                dst_ref=target.at[me],
                send_sem=send_sems.at[i, k],
                recv_sem=recv_sems.at[i, k],
                device_id=place,
                device_id_type=MESH,
            )
            copy.start()
            copies.append(copy)
    for source, target in zip(sources, targets):
        target[me] = block_of(source, me, target.shape[2])
    return copies


def block_of(source, at, step):
    if len(source.shape) == 3:
        return source[at]
    return source[:, pl.ds(pl.multiple_of(at * step, step), step)]


def start_sums(row_ref, landed, send_sems, recv_sems, peers, places, me):
    copies = []
    landed[me] = row_ref[...]
    for k, place in enumerate(places):
        copy = pltpu.make_async_remote_copy(
            src_ref=row_ref,
            dst_ref=landed.at[me],
            send_sem=send_sems.at[k],
            recv_sem=recv_sems.at[k],
            device_id=place,
            device_id_type=MESH,
        )
        copy.start()
        copies.append(copy)
    return copies


def summed(landed):
    total = landed[0]
    for k in range(1, landed.shape[0]):
        total = total + landed[k]
    return total


def exchange_kernel(epilogue, n_in, n_rows, n_moved, n_riders, n_sums, partial_ref, *refs):
    me, peers = tp_peers()
    inputs, refs = refs[:n_in], refs[n_in:]
    sources, refs = refs[:n_moved], refs[n_moved:]
    riders, refs = refs[:n_riders], refs[n_riders:]
    full_ref, refs = refs[0], refs[1:]
    outputs, refs = refs[:n_rows], refs[n_rows:]
    targets, refs = refs[:n_moved], refs[n_moved:]
    fulls, refs = refs[:n_riders], refs[n_riders:]
    sums, refs = refs[: 2 * n_sums], refs[2 * n_sums :]
    arrived, staged, sums_ref, send_a, recv_a, send_b, recv_b, send_m, recv_m = refs[:9]
    own, plane, places = plane_peers()
    across = [{"tp": peer} for peer in peers]
    greet(across + (places if n_moved or n_sums else []))
    moves = start_scatter(sources, targets, send_m, recv_m)
    rows = full_ref.shape[1] // CHUNKS
    started = []

    def finish(chunk, total):
        part = pl.ds(chunk * rows, rows)
        full_ref[me, part] = epilogue(total, me, part, chunk == 0, inputs, outputs)
        if n_sums and chunk == CHUNKS - 1:
            row_ref, in_plane, _, _, send_p, recv_p = refs[9:15]
            width = outputs[0].shape[1]
            row_ref[:, :width] = outputs[0][...]
            row_ref[:, width:] = inputs[-1][...]
            started.extend(start_sums(row_ref, in_plane, send_p, recv_p, plane, places, own))

    drain = tp_line(
        partial_ref, full_ref, list(zip(riders, fulls)), arrived, staged, sums_ref, finish, send_a, recv_a, send_b, recv_b
    )
    if n_sums:
        row_ref, in_plane, plane_row, in_tp, send_p, recv_p, send_t, recv_t = refs[9:]
        for copy in started:
            copy.wait()
        plane_row[...] = summed(in_plane)
        sums[0][...] = plane_row[...]
        for copy in start_sums(plane_row, in_tp, send_t, recv_t, peers, across, me):
            copy.wait()
        sums[1][...] = summed(in_tp)
    drain()
    for copy in moves:
        copy.wait()


def run_exchange(epilogue, name, collective_id, partial, inputs, row_outputs, moved=(), riders=(), summing=False):
    tp = lax.axis_size("tp")
    devices = lax.axis_size(GROUPED)
    tokens, columns = partial.shape
    share = tokens // tp
    partial = partial.reshape(tp, share, columns)
    step = columns // devices
    if step % 128:
        moved = [m.reshape(tokens, devices, step).transpose(1, 0, 2) for m in moved]
    count = len(moved)
    scratch = [
        *[pltpu.VMEM((2, tp - 1, CHUNKS, share // CHUNKS, columns), BF)] * 2,
        pltpu.VMEM((share // CHUNKS, columns), F32),
        *[pltpu.SemaphoreType.DMA((2, tp - 1, CHUNKS))] * 2,
        *[pltpu.SemaphoreType.DMA((2, tp - 1, CHUNKS + len(riders)))] * 2,
        *[pltpu.SemaphoreType.DMA((max(count, 1), devices - 1))] * 2,
    ]
    extra = ()
    if summing:
        row = row_outputs[0].shape[1] + inputs[-1].shape[1]
        extra = (jax.ShapeDtypeStruct((1, row), F32),) * 2
        scratch += [
            pltpu.VMEM((1, row), F32),
            pltpu.VMEM((devices, 1, row), F32),
            pltpu.VMEM((1, row), F32),
            pltpu.VMEM((tp, 1, row), F32),
            *[pltpu.SemaphoreType.DMA((devices - 1,))] * 2,
            *[pltpu.SemaphoreType.DMA((tp - 1,))] * 2,
        ]
    out_shape = (
        jax.ShapeDtypeStruct((tp, share, columns), BF),
        *row_outputs,
        *[jax.ShapeDtypeStruct((devices, tokens, step), BF)] * count,
        *[jax.ShapeDtypeStruct((tp, *r.shape), BF) for r in riders],
        *extra,
    )
    outs = pl.pallas_call(
        functools.partial(
            exchange_kernel, epilogue, len(inputs), len(row_outputs), count, len(riders), int(summing)
        ),
        out_shape=out_shape,
        in_specs=[pl.BlockSpec(memory_space=pltpu.VMEM)] * (1 + len(inputs) + count + len(riders)),
        out_specs=tuple([pl.BlockSpec(memory_space=pltpu.VMEM)] * len(out_shape)),
        scratch_shapes=scratch,
        compiler_params=pltpu.CompilerParams(collective_id=collective_id, has_side_effects=True),
        name=name,
    )(partial, *inputs, *moved, *riders)
    start = 1 + len(row_outputs)
    return (
        outs[0].reshape(tokens, columns),
        *outs[1:start],
        *[o.reshape(devices * tokens, step) for o in outs[start : start + count]],
        *[o.reshape(tokens, -1) for o in outs[start + count : start + count + len(riders)]],
        *outs[start + count + len(riders) :],
    )


def middle_epilogue(total, me, part, first, inputs, outputs):
    hidden_ref, gain_ref = inputs
    (branch_ref,) = outputs
    branch_ref[part, :] = total
    middle = hidden_ref[me, part].astype(F32) + total
    scale = lax.rsqrt(jnp.mean(middle * middle, axis=1, keepdims=True) + EPSILON)
    return (middle * scale * gain_ref[...]).astype(BF)


def result_epilogue(total, me, part, first, inputs, outputs):
    hidden_ref, branch_ref, teacher_out_ref, teacher_mix_ref, cotangent_ref, mask_ref, scale_ref = inputs
    output_ref, grad_ref, losses_ref = outputs
    branch = branch_ref[part, :]
    result = hidden_ref[me, part].astype(F32) + branch + total
    output_ref[part, :] = result.astype(BF)
    mask = mask_ref[me, part]
    gap = result - teacher_out_ref[me, part].astype(F32)
    gap_mix = branch - teacher_mix_ref[me, part].astype(F32)
    loss_out = jnp.sum(mask * (gap * gap), keepdims=True)
    loss_mix = jnp.sum(mask * (gap_mix * gap_mix), keepdims=True)
    lane = lax.broadcasted_iota(jnp.int32, (1, 128), 1)
    losses = jnp.where(lane == 0, loss_out, 0.0) + jnp.where(lane == 1, loss_mix, 0.0)
    losses_ref[...] = losses if first else losses_ref[...] + losses
    grad = cotangent_ref[me, part].astype(F32) + scale_ref[...] * mask * gap
    grad_ref[part, :] = grad
    return grad.astype(BF)


def norm_back(grad, rows, gain):
    scale = lax.rsqrt(jnp.mean(rows * rows, axis=1, keepdims=True) + EPSILON)
    unit = rows * scale
    gain_grad = jnp.sum(grad * unit, axis=0, keepdims=True)
    inner = grad * gain
    return scale * (inner - unit * jnp.mean(unit * inner, axis=1, keepdims=True)), gain_grad


def branch_epilogue(total, me, part, first, inputs, outputs):
    hidden_ref, branch_ref, teacher_mix_ref, grad_ref, mask_ref, scale_ref, gain_ref = inputs
    grad_middle_ref, gain_grad_ref = outputs
    branch = branch_ref[part, :]
    back, gain_grad = norm_back(total, hidden_ref[me, part].astype(F32) + branch, gain_ref[...])
    gain_grad_ref[...] = gain_grad if first else gain_grad_ref[...] + gain_grad
    grad_middle = back + grad_ref[part, :]
    grad_middle_ref[part, :] = grad_middle
    gap_mix = branch - teacher_mix_ref[me, part].astype(F32)
    return (grad_middle + scale_ref[...] * mask_ref[me, part] * gap_mix).astype(BF)


def input_epilogue(total, me, part, first, inputs, outputs):
    hidden_ref, grad_middle_ref, gain_ref = inputs[:3]
    (gain_grad_ref,) = outputs
    back, gain_grad = norm_back(total, hidden_ref[me, part].astype(F32), gain_ref[...])
    gain_grad_ref[...] = gain_grad if first else gain_grad_ref[...] + gain_grad
    return (back + grad_middle_ref[part, :]).astype(BF)


def passed_along(value, axis, steps):
    count = lax.axis_size(axis)
    leading, last = (max(0, -steps), min(count, count - steps))
    return lax.ppermute(value, axis, [(source, source + steps) for source in range(leading, last)])


def relay(value, decay, axis, steps):
    carried = passed_along(value, axis, steps)
    for _ in range(lax.axis_size(axis) - 2):
        carried = passed_along(value + decay * carried, axis, steps)
    return carried


def gathered(value):
    return lax.all_gather(value, GROUPED, axis=0, tiled=True)


def per_device(
    hidden_in,
    cotangent,
    teacher_out,
    teacher_mix,
    valid_mask,
    doc_start,
    attn_gain,
    w_query,
    w_key,
    w_value,
    w_forget,
    forget_bias,
    head_gain,
    w_outgate,
    w_out,
    mlp_gain,
    w_gate,
    w_up,
    w_down,
):
    tokens, features = hidden_in.shape
    devices = lax.axis_size(GROUPED)
    tp = lax.axis_size("tp")
    share = tokens // tp
    rows = w_query.shape[0]
    width = w_query.shape[1]
    slots = w_forget.shape[1]
    units = w_gate.shape[1]
    tokens_all = tokens * devices
    mask_flat = valid_mask.astype(F32)

    def column(vector):
        flat = vector.reshape(-1, 1).astype(BF)
        return jnp.pad(flat, ((0, rows - flat.shape[0]), (0, 0)))

    count_own = jnp.sum(mask_flat).reshape(1)
    extras = jnp.concatenate(
        [column(attn_gain), column(mlp_gain), column(forget_bias), column(head_gain), column(count_own)], axis=1
    )
    extras = jnp.pad(extras, ((0, 0), (0, 128 - slots - extras.shape[1])))
    first = gathered(jnp.concatenate([w_query, w_key, w_value, w_outgate, w_forget, extras, w_out], axis=1))
    pack = jnp.concatenate([w_gate, w_up, w_down], axis=1)
    pack, first = lax.optimization_barrier((pack, first))
    second = gathered(pack)

    inner = 4 * width + 128
    out_w = first[:, inner:]
    first = first[:, :inner]
    spare = first[:, 4 * width + slots :].astype(F32)
    attn_scale = spare[:, 0].reshape(1, -1)
    mlp_scale = spare[:, 1].reshape(1, -1)
    bias = spare[:, 2].reshape(devices, rows)[:, : slots // devices].reshape(1, slots)
    head_scale = spare[:, 3].reshape(devices, rows)[:, : width // devices].reshape(1, width)
    count_total = jnp.sum(spare[:, 4].reshape(devices, rows)[:, 0])
    loss_scale = (tokens_all / count_total).reshape(1, 1)

    hidden_f = hidden_in.astype(F32)
    scale = lax.rsqrt(jnp.mean(hidden_f * hidden_f, axis=-1, keepdims=True) + EPSILON)
    normed_in = (hidden_f * scale * attn_scale).astype(BF)
    pre_all = dot_nn(normed_in, first)
    query_pre = pre_all[:, :width]
    keys_pre = pre_all[:, width : 2 * width]
    query = jax.nn.silu(query_pre).astype(BF)
    keys = jax.nn.silu(keys_pre).astype(BF)
    values = pre_all[:, 2 * width : 3 * width].astype(BF)
    gate_pre = pre_all[:, 3 * width : 4 * width]
    forget_pre = pre_all[:, 4 * width : 4 * width + slots] + bias
    resets = doc_start.astype(F32)[:, None]

    spans, total, ends = run_ends(forget_pre, resets, keys, values)
    decay = total.reshape(slots, 1)
    state = relay(ends, decay, "ctx", 1)
    probs, pairs, mixing, mix, gated = run_forward(
        query, keys, values, forget_pre, spans, state, gate_pre, head_scale
    )
    gate_w = second[:, :units]
    up_w = second[:, units : 2 * units]
    down_w = second[:, 2 * units :]

    by_share = lambda tensor: tensor.reshape(tp, share, -1)
    hidden_s, teacher_out_s, teacher_mix_s, cotangent_s = map(by_share, (hidden_in, teacher_out, teacher_mix, cotangent))
    mask_s = by_share(mask_flat)
    narrow = lambda *shape: jax.ShapeDtypeStruct(shape, F32)

    normed_mid, branch = run_exchange(
        middle_epilogue, "sum_branch", 1, dot_nt(gated, out_w).astype(BF), (hidden_s, mlp_scale),
        (narrow(share, features),),
    )
    gate_val = dot_nn(normed_mid, gate_w)
    up_val = dot_nn(normed_mid, up_w)
    hidden_units = (jax.nn.silu(gate_val) * up_val).astype(BF)
    forward_all = gathered(jnp.concatenate([gated, hidden_units], axis=1))
    grad_mlp, output_rows, grad_result, losses, normed_in_c, normed_mid_c = run_exchange(
        result_epilogue, "sum_result", 2, dot_nt(hidden_units, down_w).astype(BF),
        (hidden_s, branch, teacher_out_s, teacher_mix_s, cotangent_s, mask_s, loss_scale),
        (jax.ShapeDtypeStruct((share, features), BF), narrow(share, features), narrow(1, 128)),
        moved=(normed_in, normed_mid),
    )
    forward_all, grad_mlp = lax.optimization_barrier((forward_all, grad_mlp))
    grad_units = dot_nn(grad_mlp, down_w)
    gate_sig = jax.nn.sigmoid(gate_val)
    grad_gate_val = (grad_units * up_val * (gate_sig * (1.0 + gate_val * (1.0 - gate_sig)))).astype(BF)
    grad_up_val = (grad_units * (gate_val * gate_sig)).astype(BF)
    grad_both = jnp.concatenate([grad_gate_val, grad_up_val], axis=1)
    mlp_all = gathered(grad_both)
    grad_branch, grad_middle, mlp_gain_part, grad_mlp_c = run_exchange(
        branch_epilogue, "sum_middle", 3, dot_nt(grad_both, second[:, : 2 * units]).astype(BF),
        (hidden_s, branch, teacher_mix_s, grad_result, mask_s, loss_scale, mlp_scale),
        (narrow(share, features), narrow(1, features)),
        moved=(grad_mlp,),
    )
    grad_gated = dot_nn(grad_branch, out_w)
    gquery, gkeys, gvalues, ggate, head_gain_part, gwrite, glog, carry = run_backward(
        grad_gated, query, keys, values, forget_pre, spans, state, gate_pre, head_scale, probs, pairs, mixing, mix
    )
    later = relay(carry, decay, "ctx", -1)
    grad_pre = run_finish(
        gquery, gkeys, gvalues, ggate, gwrite, glog, keys, values, forget_pre, spans, query_pre, keys_pre,
        state, total, later,
    )
    mlp_all, grad_pre = lax.optimization_barrier((mlp_all, grad_pre))
    attn_all = gathered(grad_pre)
    grad_in, _, grad_branch_c, output, plane_sums, all_sums = run_exchange(
        input_epilogue, "sum_input", 4, dot_nt(grad_pre, first).astype(BF),
        (hidden_s, grad_middle, attn_scale, jnp.concatenate([mlp_gain_part, head_gain_part, losses], axis=1)),
        (narrow(1, features),), moved=(grad_branch,), riders=(output_rows,), summing=True,
    )
    gate_grad = dot_tn(normed_mid_c, mlp_all[:, :units])
    up_grad = dot_tn(normed_mid_c, mlp_all[:, units:])
    out_grad = dot_tn(grad_branch_c, forward_all[:, :width])
    down_grad = dot_tn(grad_mlp_c, forward_all[:, width:])
    query_grad = dot_tn(normed_in_c, attn_all[:, :width])
    keys_grad = dot_tn(normed_in_c, attn_all[:, width : 2 * width])
    values_grad = dot_tn(normed_in_c, attn_all[:, 2 * width : 3 * width])
    outgate_grad = dot_tn(normed_in_c, attn_all[:, 3 * width : 4 * width])
    forget_all = attn_all[:, 4 * width : 4 * width + slots]
    forget_grad = dot_tn(normed_in_c, forget_all)
    index = lax.axis_index(GROUPED)
    bias_grad = jnp.sum(forget_all.astype(F32), axis=0, keepdims=True)
    bias_grad = lax.dynamic_slice_in_dim(bias_grad, index * (slots // devices), slots // devices, axis=1)

    cut = lambda row, size: lax.dynamic_slice_in_dim(row, index * size, size, axis=1)
    attn_gain_grad = cut(all_sums[:, :features], features // devices).reshape(-1)
    mlp_gain_grad = cut(all_sums[:, features : 2 * features], features // devices).reshape(-1)
    head_gain_grad = cut(plane_sums[:, 2 * features : 2 * features + width], width // devices)
    sums = all_sums[0, 2 * features + width :]
    loss_out = sums[0] / (2.0 * features * count_total)
    loss_mix = sums[1] / (2.0 * features * count_total)
    return (
        output,
        loss_out,
        loss_mix,
        grad_in.astype(F32),
        attn_gain_grad,
        query_grad,
        keys_grad,
        values_grad,
        forget_grad,
        bias_grad,
        head_gain_grad,
        outgate_grad,
        out_grad,
        mlp_gain_grad,
        gate_grad,
        up_grad,
        down_grad,
    )


def solution(mesh):
    return jax.shard_map(
        per_device,
        mesh=mesh,
        in_specs=(
            P(("shard", "ctx"), None),
            P(("shard", "ctx"), None),
            P(("shard", "ctx"), None),
            P(("shard", "ctx"), None),
            P(("shard", "ctx")),
            P(("shard", "ctx")),
            P(("shard", "ctx")),
            P(("shard", "ctx"), "tp"),
            P(("shard", "ctx"), "tp"),
            P(("shard", "ctx"), "tp"),
            P(("shard", "ctx"), "tp"),
            P("tp", ("shard", "ctx")),
            P("tp", ("shard", "ctx")),
            P(("shard", "ctx"), "tp"),
            P(("shard", "ctx"), "tp"),
            P(("shard", "ctx")),
            P(("shard", "ctx"), "tp"),
            P(("shard", "ctx"), "tp"),
            P(("shard", "ctx"), "tp"),
        ),
        out_specs=(
            P(("shard", "ctx"), None),
            P(),
            P(),
            P(("shard", "ctx"), None),
            P(("shard", "ctx")),
            P(("shard", "ctx"), "tp"),
            P(("shard", "ctx"), "tp"),
            P(("shard", "ctx"), "tp"),
            P(("shard", "ctx"), "tp"),
            P("tp", ("shard", "ctx")),
            P("tp", ("shard", "ctx")),
            P(("shard", "ctx"), "tp"),
            P(("shard", "ctx"), "tp"),
            P(("shard", "ctx")),
            P(("shard", "ctx"), "tp"),
            P(("shard", "ctx"), "tp"),
            P(("shard", "ctx"), "tp"),
        ),
        check_vma=False,
    )
```

```python
import functools

import jax
import jax.numpy as jnp
from jax import lax
from jax.experimental import pallas as pl
from jax.experimental.pallas import tpu as pltpu
from jax.sharding import PartitionSpec as P

F32 = jnp.float32
BF = jnp.bfloat16
EPSILON = 1e-06
GATE_NORM = 8.0


def dot_nn(a, b):
    return lax.dot_general(a, b, (((1,), (0,)), ((), ())), preferred_element_type=F32)


def dot_nt(a, b):
    return lax.dot_general(a, b, (((1,), (1,)), ((), ())), preferred_element_type=F32)


def dot_tn(a, b):
    return lax.dot_general(a, b, (((0,), (0,)), ((), ())), preferred_element_type=F32)


def halves(x):
    hi = x.astype(BF)
    return hi, (x - hi.astype(F32)).astype(BF)


def sigmoid(u):
    return 1.0 / (1.0 + jnp.exp(-u))


def n_levels(tokens):
    return tokens.bit_length() - 1


def span_matrix(level, tokens):
    t = lax.broadcasted_iota(jnp.int32, (tokens, tokens), 0)
    u = lax.broadcasted_iota(jnp.int32, (tokens, tokens), 1)
    depth = n_levels(tokens)
    if level == depth:
        keep = u <= t
    elif level == depth + 1:
        keep = u > t
    else:
        half = 1 << level
        edge = (t & ~(2 * half - 1)) + half
        odd = (t & half) > 0
        keep = (odd & (u >= edge) & (u <= t)) | (~odd & (u > t) & (u < edge))
    return keep.astype(F32).astype(BF)


def odd_rows(level, tokens, columns):
    t = lax.broadcasted_iota(jnp.int32, (tokens, columns), 0)
    return (t & (1 << level)) > 0


def same_pair(level, tokens):
    t = lax.broadcasted_iota(jnp.int32, (tokens, tokens), 0)
    u = lax.broadcasted_iota(jnp.int32, (tokens, tokens), 1)
    return (t >> (level + 1)) == (u >> (level + 1))


def ends_kernel(pre_ref, resets_ref, keys_ref, values_ref, spans_ref, total_ref, ends_ref):
    tokens, slots = pre_ref.shape
    depth = n_levels(tokens)
    width = keys_ref.shape[1]
    pre = pre_ref[...]
    log_decay = (jnp.minimum(pre, 0.0) - jnp.log1p(jnp.exp(-jnp.abs(pre)))) / GATE_NORM
    write = 1.0 - jnp.exp(log_decay)
    hi, lo = halves(log_decay)
    resets = jnp.broadcast_to(resets_ref[...], (tokens, slots)).astype(BF)
    stacked = jnp.concatenate([hi, lo, resets], axis=1)
    for level in range(depth + 2):
        sums = dot_nn(span_matrix(level, tokens), stacked)
        gap = sums[:, :slots] + sums[:, slots : 2 * slots]
        live = sums[:, 2 * slots :] < 0.5
        span = jnp.where(live, jnp.exp(gap), 0.0)
        spans_ref[level] = span
        if level == depth:
            total_ref[...] = span[tokens - 1 :, :]
        if level == depth + 1:
            hi, lo = halves(span * write)
            ends_ref[:, :width] = dot_tn(hi, keys_ref[...]) + dot_tn(lo, keys_ref[...])
            ends_ref[:, width:] = dot_tn(hi, values_ref[...]) + dot_tn(lo, values_ref[...])


def run_ends(pre, resets, keys, values):
    tokens, slots = pre.shape
    depth = n_levels(tokens)
    return pl.pallas_call(
        ends_kernel,
        out_shape=(
            jax.ShapeDtypeStruct((depth + 2, tokens, slots), F32),
            jax.ShapeDtypeStruct((1, slots), F32),
            jax.ShapeDtypeStruct((slots, keys.shape[1] + values.shape[1]), F32),
        ),
        name="slot_ends",
    )(pre, resets, keys, values)


def decay_write(pre):
    log_decay = (jnp.minimum(pre, 0.0) - jnp.log1p(jnp.exp(-jnp.abs(pre)))) / GATE_NORM
    return jnp.exp(log_decay)


def forward_kernel(
    query_ref, keys_ref, values_ref, pre_ref, spans_ref, state_ref, gate_ref, gain_ref,
    probs_ref, pairs_ref, mixing_ref, mix_ref, gated_ref,
):
    tokens, slots = pre_ref.shape
    depth = n_levels(tokens)
    width = keys_ref.shape[1]
    scaling = width ** (-0.5)
    write = 1.0 - decay_write(pre_ref[...])
    query = query_ref[...]
    pairs = dot_nt(query, keys_ref[...])
    pairs_ref[...] = pairs
    t = lax.broadcasted_iota(jnp.int32, (tokens, tokens), 0)
    u = lax.broadcasted_iota(jnp.int32, (tokens, tokens), 1)
    diagonal = jnp.sum(jnp.where(t == u, pairs, 0.0), axis=1, keepdims=True)
    state_hi, state_lo = halves(state_ref[:, :width])
    head = spans_ref[depth]
    raw = head * (dot_nt(query, state_hi) + dot_nt(query, state_lo)) + diagonal * write
    for level in range(depth):
        span = spans_ref[level]
        odd = odd_rows(level, tokens, slots)
        left, left_lo = halves(jnp.where(same_pair(level, tokens), pairs, 0.0))
        right, right_lo = halves(jnp.where(odd, 0.0, span * write))
        pulled = dot_nn(left, right) + dot_nn(left_lo, right) + dot_nn(left, right_lo)
        raw = raw + jnp.where(odd, span, 0.0) * pulled
    scores = scaling * raw
    scores = scores - jnp.max(scores, axis=1, keepdims=True)
    raised = jnp.exp(scores)
    probs = raised / jnp.sum(raised, axis=1, keepdims=True)
    probs_ref[...] = probs
    probs = probs.astype(BF).astype(F32)
    mixing = jnp.zeros((tokens, tokens), F32)
    for level in reversed(range(depth)):
        span = spans_ref[level]
        odd = odd_rows(level, tokens, slots)
        left, left_lo = halves(jnp.where(odd, span * probs, 0.0))
        right, right_lo = halves(jnp.where(odd, 0.0, span * write))
        pushed = dot_nt(left, right) + dot_nt(left_lo, right) + dot_nt(left, right_lo)
        mixing = jnp.where(same_pair(level, tokens), pushed, mixing)
    mixing = jnp.where(t == u, jnp.sum(probs * write, axis=1, keepdims=True), mixing)
    mixing, mixing_lo = halves(mixing)
    mixing_ref[...] = mixing
    state_hi, state_lo = halves(state_ref[:, width:])
    carried, carried_lo = halves(probs * head)
    mix = dot_nn(mixing, values_ref[...]) + dot_nn(mixing_lo, values_ref[...])
    mix = mix + dot_nn(carried, state_hi) + dot_nn(carried, state_lo) + dot_nn(carried_lo, state_hi)
    mix_ref[...] = mix
    scale = lax.rsqrt(jnp.mean(mix * mix, axis=1, keepdims=True) + EPSILON)
    gate = gate_ref[...]
    gated_ref[...] = (mix * scale * gain_ref[...] * (gate * sigmoid(gate))).astype(BF)


def run_forward(query, keys, values, pre, spans, state, gate, gain):
    tokens, slots = pre.shape
    width = keys.shape[1]
    return pl.pallas_call(
        forward_kernel,
        out_shape=(
            jax.ShapeDtypeStruct((tokens, slots), F32),
            jax.ShapeDtypeStruct((tokens, tokens), F32),
            jax.ShapeDtypeStruct((tokens, tokens), BF),
            jax.ShapeDtypeStruct((tokens, width), F32),
            jax.ShapeDtypeStruct((tokens, width), BF),
        ),
        name="slot_forward",
    )(query, keys, values, pre, spans, state, gate, gain)


def backward_kernel(
    grad_ref, query_ref, keys_ref, values_ref, pre_ref, spans_ref, state_ref, gate_ref, gain_ref,
    probs_ref, pairs_ref, mixing_ref, mix_ref,
    gquery_ref, gkeys_ref, gvalues_ref, ggate_ref, ggain_ref, gwrite_ref, glog_ref, carry_ref,
):
    tokens, slots = pre_ref.shape
    depth = n_levels(tokens)
    width = keys_ref.shape[1]
    scaling = width ** (-0.5)
    gate = gate_ref[...]
    sig = sigmoid(gate)
    silu = gate * sig
    gain = gain_ref[...]
    mix = mix_ref[...]
    scale = lax.rsqrt(jnp.mean(mix * mix, axis=1, keepdims=True) + EPSILON)
    normed = mix * scale
    grad = grad_ref[...]
    ggate_ref[...] = (grad * gain * normed * (sig * (1.0 + gate * (1.0 - sig)))).astype(BF)
    ggain_ref[...] = jnp.sum(grad * normed * silu, axis=0, keepdims=True)
    inner = grad * gain * silu
    mix_grad = scale * (inner - normed * jnp.mean(normed * inner, axis=1, keepdims=True))
    mix_low = mix_grad.astype(BF)

    write = 1.0 - decay_write(pre_ref[...])
    query, keys, values = query_ref[...], keys_ref[...], values_ref[...]
    pairs = pairs_ref[...]
    pairs_t = dot_nt(keys, query)
    mix_rest = (mix_grad - mix_low.astype(F32)).astype(BF)
    weigh = dot_nt(mix_low, values) + dot_nt(mix_rest, values)
    weigh_t = dot_nt(values, mix_low) + dot_nt(values, mix_rest)
    t = lax.broadcasted_iota(jnp.int32, (tokens, tokens), 0)
    u = lax.broadcasted_iota(jnp.int32, (tokens, tokens), 1)
    pair_diag = jnp.sum(jnp.where(t == u, pairs, 0.0), axis=1, keepdims=True)
    weigh_diag = jnp.sum(jnp.where(t == u, weigh, 0.0), axis=1, keepdims=True)
    head = spans_ref[depth]
    probs = probs_ref[...]
    probs_low = probs.astype(BF).astype(F32)

    vstate_hi, vstate_lo = halves(state_ref[:, width:])
    head_probs = head * (
        dot_nt(mix_low, vstate_hi) + dot_nt(mix_low, vstate_lo) + dot_nt(mix_rest, vstate_hi)
    )
    probs_grad = head_probs + weigh_diag * write
    row_values, row_keys = [], []
    for level in range(depth):
        span = spans_ref[level]
        odd = odd_rows(level, tokens, slots)
        same = same_pair(level, tokens)
        right, right_lo = halves(jnp.where(odd, 0.0, span * write))
        reach = jnp.where(odd, span, 0.0)
        left, left_lo = halves(jnp.where(same, weigh, 0.0))
        term = reach * (dot_nn(left, right) + dot_nn(left_lo, right) + dot_nn(left, right_lo))
        row_values.append(term)
        left, left_lo = halves(jnp.where(same, pairs, 0.0))
        row_keys.append(reach * (dot_nn(left, right) + dot_nn(left_lo, right) + dot_nn(left, right_lo)))
        probs_grad = probs_grad + term
    scores_grad = probs * (probs_grad - jnp.sum(probs_grad * probs, axis=1, keepdims=True))
    scores_grad = scaling * scores_grad

    kstate_hi, kstate_lo = halves(state_ref[:, :width])
    head_keys = head * (dot_nt(query, kstate_hi) + dot_nt(query, kstate_lo))
    gwrite = pair_diag * scores_grad + weigh_diag * probs_low
    glog = dot_tn(span_matrix(depth, tokens), (head_keys * scores_grad + head_probs * probs_low).astype(BF))
    gpairs = jnp.zeros((tokens, tokens), F32)
    for level in reversed(range(depth)):
        span = spans_ref[level]
        odd = odd_rows(level, tokens, slots)
        same = same_pair(level, tokens)
        reach = jnp.where(odd, span, 0.0)
        source = jnp.where(odd, 0.0, span)
        key_side, key_rest = halves(reach * scores_grad)
        value_side, value_rest = halves(reach * probs_low)
        seen, seen_rest = halves(jnp.where(same, pairs_t, 0.0))
        felt, felt_rest = halves(jnp.where(same, weigh_t, 0.0))
        sent, sent_rest = halves(source * write)
        pushed = dot_nt(key_side, sent) + dot_nt(key_rest, sent) + dot_nt(key_side, sent_rest)
        gpairs = jnp.where(same, pushed, gpairs)
        column = source * (
            dot_nn(seen, key_side) + dot_nn(seen, key_rest) + dot_nn(seen_rest, key_side)
            + dot_nn(felt, value_side) + dot_nn(felt, value_rest) + dot_nn(felt_rest, value_side)
        )
        gwrite = gwrite + column
        moved = column * write + row_values[level] * probs_low + row_keys[level] * scores_grad
        spread = span_matrix(level, tokens)
        moved, moved_rest = halves(moved)
        glog = glog + dot_tn(spread, moved) + dot_tn(spread, moved_rest)
    gpairs = jnp.where(t == u, jnp.sum(scores_grad * write, axis=1, keepdims=True), gpairs)
    gpairs, gpairs_rest = halves(gpairs)
    gwrite_ref[...] = gwrite
    glog_ref[...] = glog
    key_head, key_head_rest = halves(scores_grad * head)
    gquery_ref[...] = (
        dot_nn(gpairs, keys)
        + dot_nn(gpairs_rest, keys)
        + dot_nn(key_head, kstate_hi)
        + dot_nn(key_head, kstate_lo)
        + dot_nn(key_head_rest, kstate_hi)
    )
    gkeys_ref[...] = dot_tn(gpairs, query) + dot_tn(gpairs_rest, query)
    gvalues_ref[...] = dot_tn(mixing_ref[...], mix_low)
    carry_ref[:, :width] = dot_tn(key_head, query) + dot_tn(key_head_rest, query)
    carry_ref[:, width:] = dot_tn((probs_low * head).astype(BF), mix_low)


def run_backward(grad, query, keys, values, pre, spans, state, gate, gain, probs, pairs, mixing, mix):
    tokens, slots = pre.shape
    width = keys.shape[1]
    wide = jax.ShapeDtypeStruct((tokens, width), F32)
    narrow = jax.ShapeDtypeStruct((tokens, slots), F32)
    return pl.pallas_call(
        backward_kernel,
        out_shape=(
            wide, wide, wide,
            jax.ShapeDtypeStruct((tokens, width), BF),
            jax.ShapeDtypeStruct((1, width), F32),
            narrow, narrow,
            jax.ShapeDtypeStruct((slots, 2 * width), F32),
        ),
        name="slot_backward",
    )(grad, query, keys, values, pre, spans, state, gate, gain, probs, pairs, mixing, mix)


def finish_kernel(
    gquery_ref, gkeys_ref, gvalues_ref, ggate_ref, gwrite_ref, glog_ref,
    keys_ref, values_ref, pre_ref, spans_ref, query_pre_ref, keys_pre_ref,
    state_ref, total_ref, ends_ref, out_ref,
):
    tokens, slots = pre_ref.shape
    depth = n_levels(tokens)
    width = keys_ref.shape[1]
    pre = pre_ref[...]
    decay = decay_write(pre)
    write = 1.0 - decay
    keys, values = keys_ref[...], values_ref[...]
    ends = ends_ref[...]
    ends_low = ends.astype(BF)
    tail = spans_ref[depth + 1]
    sent = (tail * write).astype(BF)
    column = tail * (dot_nt(keys, ends_low[:, :width]) + dot_nt(values, ends_low[:, width:]))
    glog = glog_ref[...] + dot_tn(span_matrix(depth + 1, tokens), (column * write).astype(BF))
    carried = lax.dot_general(
        jnp.ones((1, 2 * width), F32), ends * state_ref[...], (((1,), (1,)), ((), ())),
        precision=lax.Precision.HIGHEST, preferred_element_type=F32,
    )
    glog = glog + carried * total_ref[...]
    glog = glog - decay * (gwrite_ref[...] + column)
    u = query_pre_ref[...]
    s = sigmoid(u)
    out_ref[:, :width] = (gquery_ref[...] * (s * (1.0 + u * (1.0 - s)))).astype(BF)
    u = keys_pre_ref[...]
    s = sigmoid(u)
    gkeys = gkeys_ref[...] + dot_nn(sent, ends_low[:, :width])
    out_ref[:, width : 2 * width] = (gkeys * (s * (1.0 + u * (1.0 - s)))).astype(BF)
    out_ref[:, 2 * width : 3 * width] = (gvalues_ref[...] + dot_nn(sent, ends_low[:, width:])).astype(BF)
    out_ref[:, 3 * width : 4 * width] = ggate_ref[...]
    gforget = glog * sigmoid(-pre) / GATE_NORM
    room = out_ref.shape[1] - 4 * width - slots
    out_ref[:, 4 * width :] = jnp.concatenate(
        [gforget.astype(BF), jnp.zeros((tokens, room), BF)], axis=1
    )


def run_finish(gquery, gkeys, gvalues, ggate, gwrite, glog, keys, values, pre, spans, query_pre, keys_pre, state, total, ends):
    tokens, slots = pre.shape
    width = keys.shape[1]
    return pl.pallas_call(
        finish_kernel,
        out_shape=jax.ShapeDtypeStruct((tokens, 4 * width + 128), BF),
        name="slot_finish",
    )(gquery, gkeys, gvalues, ggate, gwrite, glog, keys, values, pre, spans, query_pre, keys_pre, state, total, ends)


MESH = pl.DeviceIdType.MESH
GROUPED = ("shard", "ctx")


def greet(axes_of_peers):
    barrier = pltpu.get_barrier_semaphore()
    for peer in axes_of_peers:
        pl.semaphore_signal(barrier, inc=1, device_id=peer, device_id_type=MESH)
    pl.semaphore_wait(barrier, len(axes_of_peers))


def tp_peers():
    count = lax.axis_size("tp")
    me = lax.axis_index("tp")
    return me, [lax.rem(me + k, count) for k in range(1, count)]


CHUNKS = 2
LAG = 2


def tp_line(partial_ref, full_ref, riders, arrived, staged, sums_ref, finish, send_a, recv_a, send_b, recv_b):
    count = lax.axis_size("tp")
    me = lax.axis_index("tp")
    rows = partial_ref.shape[1] // CHUNKS
    places = [(me, lax.rem(me + 1, count)), (count - 1 - me, lax.rem(me + count - 1, count))]

    def block_at(side, place):
        return place if side == 0 else count - 1 - place

    def cut(chunk):
        return pl.ds(chunk * rows, rows)

    def sum_copy(side, hop, chunk, source):
        return pltpu.make_async_remote_copy(
            src_ref=source,
            dst_ref=arrived.at[side, hop, chunk],
            send_sem=send_a.at[side, hop, chunk],
            recv_sem=recv_a.at[side, hop, chunk],
            device_id={"tp": places[side][1]},
            device_id_type=MESH,
        )

    def add_hop(chunk, tick):
        for side, (place, _) in enumerate(places):
            hop = jnp.clip(tick - place, 0, count - 2)
            block = block_at(side, count - 1 - hop)
            own = partial_ref.at[block, cut(chunk)]
            slot = staged.at[side, hop, chunk]
            if tick < count - 1:

                @pl.when(place == 0)
                def _():
                    sum_copy(side, hop, chunk, own).start()

            @pl.when((place > 0) & (place <= tick))
            def _():
                sum_copy(side, hop, chunk, slot).wait_recv()
                slot[...] = (own[...].astype(F32) + arrived[side, hop, chunk].astype(F32)).astype(BF)
                sum_copy(side, hop, chunk, slot).start()

    def close(chunk):
        sums_ref[...] = partial_ref[me, cut(chunk)].astype(F32)
        for side, (place, _) in enumerate(places):
            hop = jnp.minimum(count - 1 - place, count - 2)

            @pl.when(place > 0)
            def _():
                sum_copy(side, hop, chunk, staged.at[side, hop, chunk]).wait_recv()
                sums_ref[...] += arrived[side, hop, chunk].astype(F32)

        finish(chunk, sums_ref[...])

    gathers = [(full_ref, cut(chunk)) for chunk in range(CHUNKS)]
    gathers += [(full, pl.ds(0, full.shape[1])) for _, full in riders]

    def row_copy(side, hop, which, block):
        full, part = gathers[which]
        return pltpu.make_async_remote_copy(
            src_ref=full.at[block, part],
            dst_ref=full.at[block, part],
            send_sem=send_b.at[side, hop, which],
            recv_sem=recv_b.at[side, hop, which],
            device_id={"tp": places[side][1]},
            device_id_type=MESH,
        )

    def offer(which):
        for side, (place, _) in enumerate(places):

            @pl.when(place < count - 1)
            def _():
                row_copy(side, 0, which, me).start()

    def forward(which, hop):
        for side, (place, _) in enumerate(places):
            block = block_at(side, jnp.maximum(place - hop, 0))

            @pl.when(place >= hop)
            def _():
                row_copy(side, hop - 1, which, block).wait_recv()

            if hop < count - 1:

                @pl.when((place >= hop) & (place < count - 1))
                def _():
                    row_copy(side, hop, which, block).start()

    for rows_ref, full in riders:
        full[me] = rows_ref[...]
    steps = []
    for chunk in range(CHUNKS):
        run = [functools.partial(add_hop, chunk, hop) for hop in range(count - 1)]
        run += [lambda chunk=chunk: (close(chunk), offer(chunk))]
        run += [functools.partial(forward, chunk, hop) for hop in range(1, count)]
        steps.append(run)
    for rider in range(CHUNKS, len(gathers)):
        steps.append([functools.partial(offer, rider), *[functools.partial(forward, rider, hop) for hop in range(1, count)]])
    length = max(LAG * at + len(run) for at, run in enumerate(steps))
    for tick in range(length):
        for at, run in enumerate(steps):
            if 0 <= tick - LAG * at < len(run):
                run[tick - LAG * at]()

    def drain():
        for side, (place, _) in enumerate(places):
            for hop in range(count - 1):

                @pl.when(count - 1 - hop > place)
                def _():
                    for chunk in range(CHUNKS):
                        sum_copy(side, hop, chunk, staged.at[side, hop, chunk]).wait_send()

                @pl.when((place >= hop) & (place < count - 1))
                def _():
                    block = block_at(side, jnp.maximum(place - hop, 0))
                    for which in range(len(gathers)):
                        row_copy(side, hop, which, block).wait_send()

    return drain


def plane_peers():
    shards, ctxs = lax.axis_size("shard"), lax.axis_size("ctx")
    devices = shards * ctxs
    me = lax.axis_index("shard") * ctxs + lax.axis_index("ctx")
    peers = [lax.rem(me + k, devices) for k in range(1, devices)]
    places = [{"shard": lax.div(peer, ctxs), "ctx": lax.rem(peer, ctxs)} for peer in peers]
    return me, peers, places


def start_scatter(sources, targets, send_sems, recv_sems):
    me, peers, places = plane_peers()
    copies = []
    for i, (source, target) in enumerate(zip(sources, targets)):
        step = target.shape[2]

        def block(at):
            if len(source.shape) == 3:
                return source.at[at]
            return source.at[:, pl.ds(pl.multiple_of(at * step, step), step)]

        for k, (peer, place) in enumerate(zip(peers, places)):
            copy = pltpu.make_async_remote_copy(
                src_ref=block(peer),
                dst_ref=target.at[me],
                send_sem=send_sems.at[i, k],
                recv_sem=recv_sems.at[i, k],
                device_id=place,
                device_id_type=MESH,
            )
            copy.start()
            copies.append(copy)
    for source, target in zip(sources, targets):
        target[me] = block_of(source, me, target.shape[2])
    return copies


def block_of(source, at, step):
    if len(source.shape) == 3:
        return source[at]
    return source[:, pl.ds(pl.multiple_of(at * step, step), step)]


def start_sums(row_ref, landed, send_sems, recv_sems, peers, places, me):
    copies = []
    landed[me] = row_ref[...]
    for k, place in enumerate(places):
        copy = pltpu.make_async_remote_copy(
            src_ref=row_ref,
            dst_ref=landed.at[me],
            send_sem=send_sems.at[k],
            recv_sem=recv_sems.at[k],
            device_id=place,
            device_id_type=MESH,
        )
        copy.start()
        copies.append(copy)
    return copies


def summed(landed):
    total = landed[0]
    for k in range(1, landed.shape[0]):
        total = total + landed[k]
    return total


def exchange_kernel(epilogue, n_in, n_rows, n_moved, n_riders, n_sums, partial_ref, *refs):
    me, peers = tp_peers()
    inputs, refs = refs[:n_in], refs[n_in:]
    sources, refs = refs[:n_moved], refs[n_moved:]
    riders, refs = refs[:n_riders], refs[n_riders:]
    full_ref, refs = refs[0], refs[1:]
    outputs, refs = refs[:n_rows], refs[n_rows:]
    targets, refs = refs[:n_moved], refs[n_moved:]
    fulls, refs = refs[:n_riders], refs[n_riders:]
    sums, refs = refs[: 2 * n_sums], refs[2 * n_sums :]
    arrived, staged, sums_ref, send_a, recv_a, send_b, recv_b, send_m, recv_m = refs[:9]
    own, plane, places = plane_peers()
    across = [{"tp": peer} for peer in peers]
    greet(across + (places if n_moved or n_sums else []))
    moves = start_scatter(sources, targets, send_m, recv_m)
    rows = full_ref.shape[1] // CHUNKS
    started = []

    def finish(chunk, total):
        part = pl.ds(chunk * rows, rows)
        full_ref[me, part] = epilogue(total, me, part, chunk == 0, inputs, outputs)
        if n_sums and chunk == CHUNKS - 1:
            row_ref, in_plane, _, _, send_p, recv_p = refs[9:15]
            width = outputs[0].shape[1]
            row_ref[:, :width] = outputs[0][...]
            row_ref[:, width:] = inputs[-1][...]
            started.extend(start_sums(row_ref, in_plane, send_p, recv_p, plane, places, own))

    drain = tp_line(
        partial_ref, full_ref, list(zip(riders, fulls)), arrived, staged, sums_ref, finish, send_a, recv_a, send_b, recv_b
    )
    if n_sums:
        row_ref, in_plane, plane_row, in_tp, send_p, recv_p, send_t, recv_t = refs[9:]
        for copy in started:
            copy.wait()
        plane_row[...] = summed(in_plane)
        sums[0][...] = plane_row[...]
        for copy in start_sums(plane_row, in_tp, send_t, recv_t, peers, across, me):
            copy.wait()
        sums[1][...] = summed(in_tp)
    drain()
    for copy in moves:
        copy.wait()


def run_exchange(epilogue, name, collective_id, partial, inputs, row_outputs, moved=(), riders=(), summing=False):
    tp = lax.axis_size("tp")
    devices = lax.axis_size(GROUPED)
    tokens, columns = partial.shape
    share = tokens // tp
    partial = partial.reshape(tp, share, columns)
    step = columns // devices
    if step % 128:
        moved = [m.reshape(tokens, devices, step).transpose(1, 0, 2) for m in moved]
    count = len(moved)
    scratch = [
        *[pltpu.VMEM((2, tp - 1, CHUNKS, share // CHUNKS, columns), BF)] * 2,
        pltpu.VMEM((share // CHUNKS, columns), F32),
        *[pltpu.SemaphoreType.DMA((2, tp - 1, CHUNKS))] * 2,
        *[pltpu.SemaphoreType.DMA((2, tp - 1, CHUNKS + len(riders)))] * 2,
        *[pltpu.SemaphoreType.DMA((max(count, 1), devices - 1))] * 2,
    ]
    extra = ()
    if summing:
        row = row_outputs[0].shape[1] + inputs[-1].shape[1]
        extra = (jax.ShapeDtypeStruct((1, row), F32),) * 2
        scratch += [
            pltpu.VMEM((1, row), F32),
            pltpu.VMEM((devices, 1, row), F32),
            pltpu.VMEM((1, row), F32),
            pltpu.VMEM((tp, 1, row), F32),
            *[pltpu.SemaphoreType.DMA((devices - 1,))] * 2,
            *[pltpu.SemaphoreType.DMA((tp - 1,))] * 2,
        ]
    out_shape = (
        jax.ShapeDtypeStruct((tp, share, columns), BF),
        *row_outputs,
        *[jax.ShapeDtypeStruct((devices, tokens, step), BF)] * count,
        *[jax.ShapeDtypeStruct((tp, *r.shape), BF) for r in riders],
        *extra,
    )
    outs = pl.pallas_call(
        functools.partial(
            exchange_kernel, epilogue, len(inputs), len(row_outputs), count, len(riders), int(summing)
        ),
        out_shape=out_shape,
        in_specs=[pl.BlockSpec(memory_space=pltpu.VMEM)] * (1 + len(inputs) + count + len(riders)),
        out_specs=tuple([pl.BlockSpec(memory_space=pltpu.VMEM)] * len(out_shape)),
        scratch_shapes=scratch,
        compiler_params=pltpu.CompilerParams(collective_id=collective_id, has_side_effects=True),
        name=name,
    )(partial, *inputs, *moved, *riders)
    start = 1 + len(row_outputs)
    return (
        outs[0].reshape(tokens, columns),
        *outs[1:start],
        *[o.reshape(devices * tokens, step) for o in outs[start : start + count]],
        *[o.reshape(tokens, -1) for o in outs[start + count : start + count + len(riders)]],
        *outs[start + count + len(riders) :],
    )


def middle_epilogue(total, me, part, first, inputs, outputs):
    hidden_ref, gain_ref = inputs
    (branch_ref,) = outputs
    branch_ref[part, :] = total
    middle = hidden_ref[me, part].astype(F32) + total
    scale = lax.rsqrt(jnp.mean(middle * middle, axis=1, keepdims=True) + EPSILON)
    return (middle * scale * gain_ref[...]).astype(BF)


def result_epilogue(total, me, part, first, inputs, outputs):
    hidden_ref, branch_ref, teacher_out_ref, teacher_mix_ref, cotangent_ref, mask_ref, scale_ref = inputs
    output_ref, grad_ref, losses_ref = outputs
    branch = branch_ref[part, :]
    result = hidden_ref[me, part].astype(F32) + branch + total
    output_ref[part, :] = result.astype(BF)
    mask = mask_ref[me, part]
    gap = result - teacher_out_ref[me, part].astype(F32)
    gap_mix = branch - teacher_mix_ref[me, part].astype(F32)
    loss_out = jnp.sum(mask * (gap * gap), keepdims=True)
    loss_mix = jnp.sum(mask * (gap_mix * gap_mix), keepdims=True)
    lane = lax.broadcasted_iota(jnp.int32, (1, 128), 1)
    losses = jnp.where(lane == 0, loss_out, 0.0) + jnp.where(lane == 1, loss_mix, 0.0)
    losses_ref[...] = losses if first else losses_ref[...] + losses
    grad = cotangent_ref[me, part].astype(F32) + scale_ref[...] * mask * gap
    grad_ref[part, :] = grad
    return grad.astype(BF)


def norm_back(grad, rows, gain):
    scale = lax.rsqrt(jnp.mean(rows * rows, axis=1, keepdims=True) + EPSILON)
    unit = rows * scale
    gain_grad = jnp.sum(grad * unit, axis=0, keepdims=True)
    inner = grad * gain
    return scale * (inner - unit * jnp.mean(unit * inner, axis=1, keepdims=True)), gain_grad


def branch_epilogue(total, me, part, first, inputs, outputs):
    hidden_ref, branch_ref, teacher_mix_ref, grad_ref, mask_ref, scale_ref, gain_ref = inputs
    grad_middle_ref, gain_grad_ref = outputs
    branch = branch_ref[part, :]
    back, gain_grad = norm_back(total, hidden_ref[me, part].astype(F32) + branch, gain_ref[...])
    gain_grad_ref[...] = gain_grad if first else gain_grad_ref[...] + gain_grad
    grad_middle = back + grad_ref[part, :]
    grad_middle_ref[part, :] = grad_middle
    gap_mix = branch - teacher_mix_ref[me, part].astype(F32)
    return (grad_middle + scale_ref[...] * mask_ref[me, part] * gap_mix).astype(BF)


def input_epilogue(total, me, part, first, inputs, outputs):
    hidden_ref, grad_middle_ref, gain_ref = inputs[:3]
    (gain_grad_ref,) = outputs
    back, gain_grad = norm_back(total, hidden_ref[me, part].astype(F32), gain_ref[...])
    gain_grad_ref[...] = gain_grad if first else gain_grad_ref[...] + gain_grad
    return (back + grad_middle_ref[part, :]).astype(BF)


def passed_along(value, axis, steps):
    count = lax.axis_size(axis)
    leading, last = (max(0, -steps), min(count, count - steps))
    return lax.ppermute(value, axis, [(source, source + steps) for source in range(leading, last)])


def relay(value, decay, axis, steps):
    carried = passed_along(value, axis, steps)
    for _ in range(lax.axis_size(axis) - 2):
        carried = passed_along(value + decay * carried, axis, steps)
    return carried


def gathered(value):
    return lax.all_gather(value, GROUPED, axis=0, tiled=True)


def per_device(
    hidden_in,
    cotangent,
    teacher_out,
    teacher_mix,
    valid_mask,
    doc_start,
    attn_gain,
    w_query,
    w_key,
    w_value,
    w_forget,
    forget_bias,
    head_gain,
    w_outgate,
    w_out,
    mlp_gain,
    w_gate,
    w_up,
    w_down,
):
    tokens, features = hidden_in.shape
    devices = lax.axis_size(GROUPED)
    tp = lax.axis_size("tp")
    share = tokens // tp
    rows = w_query.shape[0]
    width = w_query.shape[1]
    slots = w_forget.shape[1]
    units = w_gate.shape[1]
    tokens_all = tokens * devices
    mask_flat = valid_mask.astype(F32)

    def column(vector):
        flat = vector.reshape(-1, 1).astype(BF)
        return jnp.pad(flat, ((0, rows - flat.shape[0]), (0, 0)))

    count_own = jnp.sum(mask_flat).reshape(1)
    extras = jnp.concatenate(
        [column(attn_gain), column(mlp_gain), column(forget_bias), column(head_gain), column(count_own)], axis=1
    )
    extras = jnp.pad(extras, ((0, 0), (0, 128 - slots - extras.shape[1])))
    first = gathered(jnp.concatenate([w_query, w_key, w_value, w_outgate, w_forget, extras, w_out], axis=1))
    pack = jnp.concatenate([w_gate, w_up, w_down], axis=1)
    pack, first = lax.optimization_barrier((pack, first))
    second = gathered(pack)

    inner = 4 * width + 128
    out_w = first[:, inner:]
    first = first[:, :inner]
    spare = first[:, 4 * width + slots :].astype(F32)
    attn_scale = spare[:, 0].reshape(1, -1)
    mlp_scale = spare[:, 1].reshape(1, -1)
    bias = spare[:, 2].reshape(devices, rows)[:, : slots // devices].reshape(1, slots)
    head_scale = spare[:, 3].reshape(devices, rows)[:, : width // devices].reshape(1, width)
    count_total = jnp.sum(spare[:, 4].reshape(devices, rows)[:, 0])
    loss_scale = (tokens_all / count_total).reshape(1, 1)

    hidden_f = hidden_in.astype(F32)
    scale = lax.rsqrt(jnp.mean(hidden_f * hidden_f, axis=-1, keepdims=True) + EPSILON)
    normed_in = (hidden_f * scale * attn_scale).astype(BF)
    pre_all = dot_nn(normed_in, first)
    query_pre = pre_all[:, :width]
    keys_pre = pre_all[:, width : 2 * width]
    query = jax.nn.silu(query_pre).astype(BF)
    keys = jax.nn.silu(keys_pre).astype(BF)
    values = pre_all[:, 2 * width : 3 * width].astype(BF)
    gate_pre = pre_all[:, 3 * width : 4 * width]
    forget_pre = pre_all[:, 4 * width : 4 * width + slots] + bias
    resets = doc_start.astype(F32)[:, None]

    spans, total, ends = run_ends(forget_pre, resets, keys, values)
    decay = total.reshape(slots, 1)
    state = relay(ends, decay, "ctx", 1)
    probs, pairs, mixing, mix, gated = run_forward(
        query, keys, values, forget_pre, spans, state, gate_pre, head_scale
    )
    gate_w = second[:, :units]
    up_w = second[:, units : 2 * units]
    down_w = second[:, 2 * units :]

    by_share = lambda tensor: tensor.reshape(tp, share, -1)
    hidden_s, teacher_out_s, teacher_mix_s, cotangent_s = map(by_share, (hidden_in, teacher_out, teacher_mix, cotangent))
    mask_s = by_share(mask_flat)
    narrow = lambda *shape: jax.ShapeDtypeStruct(shape, F32)

    normed_mid, branch = run_exchange(
        middle_epilogue, "sum_branch", 1, dot_nt(gated, out_w).astype(BF), (hidden_s, mlp_scale),
        (narrow(share, features),),
    )
    gate_val = dot_nn(normed_mid, gate_w)
    up_val = dot_nn(normed_mid, up_w)
    hidden_units = (jax.nn.silu(gate_val) * up_val).astype(BF)
    forward_all = gathered(jnp.concatenate([gated, hidden_units], axis=1))
    grad_mlp, output_rows, grad_result, losses, normed_in_c, normed_mid_c = run_exchange(
        result_epilogue, "sum_result", 2, dot_nt(hidden_units, down_w).astype(BF),
        (hidden_s, branch, teacher_out_s, teacher_mix_s, cotangent_s, mask_s, loss_scale),
        (jax.ShapeDtypeStruct((share, features), BF), narrow(share, features), narrow(1, 128)),
        moved=(normed_in, normed_mid),
    )
    forward_all, grad_mlp = lax.optimization_barrier((forward_all, grad_mlp))
    grad_units = dot_nn(grad_mlp, down_w)
    gate_sig = jax.nn.sigmoid(gate_val)
    grad_gate_val = (grad_units * up_val * (gate_sig * (1.0 + gate_val * (1.0 - gate_sig)))).astype(BF)
    grad_up_val = (grad_units * (gate_val * gate_sig)).astype(BF)
    grad_both = jnp.concatenate([grad_gate_val, grad_up_val], axis=1)
    mlp_all = gathered(grad_both)
    grad_branch, grad_middle, mlp_gain_part, grad_mlp_c = run_exchange(
        branch_epilogue, "sum_middle", 3, dot_nt(grad_both, second[:, : 2 * units]).astype(BF),
        (hidden_s, branch, teacher_mix_s, grad_result, mask_s, loss_scale, mlp_scale),
        (narrow(share, features), narrow(1, features)),
        moved=(grad_mlp,),
    )
    grad_gated = dot_nn(grad_branch, out_w)
    gquery, gkeys, gvalues, ggate, head_gain_part, gwrite, glog, carry = run_backward(
        grad_gated, query, keys, values, forget_pre, spans, state, gate_pre, head_scale, probs, pairs, mixing, mix
    )
    later = relay(carry, decay, "ctx", -1)
    grad_pre = run_finish(
        gquery, gkeys, gvalues, ggate, gwrite, glog, keys, values, forget_pre, spans, query_pre, keys_pre,
        state, total, later,
    )
    mlp_all, grad_pre = lax.optimization_barrier((mlp_all, grad_pre))
    attn_all = gathered(grad_pre)
    grad_in, _, grad_branch_c, output, plane_sums, all_sums = run_exchange(
        input_epilogue, "sum_input", 4, dot_nt(grad_pre, first).astype(BF),
        (hidden_s, grad_middle, attn_scale, jnp.concatenate([mlp_gain_part, head_gain_part, losses], axis=1)),
        (narrow(1, features),), moved=(grad_branch,), riders=(output_rows,), summing=True,
    )
    gate_grad = dot_tn(normed_mid_c, mlp_all[:, :units])
    up_grad = dot_tn(normed_mid_c, mlp_all[:, units:])
    out_grad = dot_tn(grad_branch_c, forward_all[:, :width])
    down_grad = dot_tn(grad_mlp_c, forward_all[:, width:])
    query_grad = dot_tn(normed_in_c, attn_all[:, :width])
    keys_grad = dot_tn(normed_in_c, attn_all[:, width : 2 * width])
    values_grad = dot_tn(normed_in_c, attn_all[:, 2 * width : 3 * width])
    outgate_grad = dot_tn(normed_in_c, attn_all[:, 3 * width : 4 * width])
    forget_all = attn_all[:, 4 * width : 4 * width + slots]
    forget_grad = dot_tn(normed_in_c, forget_all)
    index = lax.axis_index(GROUPED)
    bias_grad = jnp.sum(forget_all.astype(F32), axis=0, keepdims=True)
    bias_grad = lax.dynamic_slice_in_dim(bias_grad, index * (slots // devices), slots // devices, axis=1)

    cut = lambda row, size: lax.dynamic_slice_in_dim(row, index * size, size, axis=1)
    attn_gain_grad = cut(all_sums[:, :features], features // devices).reshape(-1)
    mlp_gain_grad = cut(all_sums[:, features : 2 * features], features // devices).reshape(-1)
    head_gain_grad = cut(plane_sums[:, 2 * features : 2 * features + width], width // devices)
    sums = all_sums[0, 2 * features + width :]
    loss_out = sums[0] / (2.0 * features * count_total)
    loss_mix = sums[1] / (2.0 * features * count_total)
    return (
        output,
        loss_out,
        loss_mix,
        grad_in.astype(F32),
        attn_gain_grad,
        query_grad,
        keys_grad,
        values_grad,
        forget_grad,
        bias_grad,
        head_gain_grad,
        outgate_grad,
        out_grad,
        mlp_gain_grad,
        gate_grad,
        up_grad,
        down_grad,
    )


def solution(mesh):
    return jax.shard_map(
        per_device,
        mesh=mesh,
        in_specs=(
            P(("shard", "ctx"), None),
            P(("shard", "ctx"), None),
            P(("shard", "ctx"), None),
            P(("shard", "ctx"), None),
            P(("shard", "ctx")),
            P(("shard", "ctx")),
            P(("shard", "ctx")),
            P(("shard", "ctx"), "tp"),
            P(("shard", "ctx"), "tp"),
            P(("shard", "ctx"), "tp"),
            P(("shard", "ctx"), "tp"),
            P("tp", ("shard", "ctx")),
            P("tp", ("shard", "ctx")),
            P(("shard", "ctx"), "tp"),
            P(("shard", "ctx"), "tp"),
            P(("shard", "ctx")),
            P(("shard", "ctx"), "tp"),
            P(("shard", "ctx"), "tp"),
            P(("shard", "ctx"), "tp"),
        ),
        out_specs=(
            P(("shard", "ctx"), None),
            P(),
            P(),
            P(("shard", "ctx"), None),
            P(("shard", "ctx")),
            P(("shard", "ctx"), "tp"),
            P(("shard", "ctx"), "tp"),
            P(("shard", "ctx"), "tp"),
            P(("shard", "ctx"), "tp"),
            P("tp", ("shard", "ctx")),
            P("tp", ("shard", "ctx")),
            P(("shard", "ctx"), "tp"),
            P(("shard", "ctx"), "tp"),
            P(("shard", "ctx")),
            P(("shard", "ctx"), "tp"),
            P(("shard", "ctx"), "tp"),
            P(("shard", "ctx"), "tp"),
        ),
        check_vma=False,
    )
```

```python
import functools

import jax
import jax.numpy as jnp
from jax import lax
from jax.experimental import pallas as pl
from jax.experimental.pallas import tpu as pltpu
from jax.sharding import PartitionSpec as P

F32 = jnp.float32
BF = jnp.bfloat16
EPSILON = 1e-06
GATE_NORM = 8.0


def dot_nn(a, b):
    return lax.dot_general(a, b, (((1,), (0,)), ((), ())), preferred_element_type=F32)


def dot_nt(a, b):
    return lax.dot_general(a, b, (((1,), (1,)), ((), ())), preferred_element_type=F32)


def dot_tn(a, b):
    return lax.dot_general(a, b, (((0,), (0,)), ((), ())), preferred_element_type=F32)


def halves(x):
    hi = x.astype(BF)
    return hi, (x - hi.astype(F32)).astype(BF)


def sigmoid(u):
    return 1.0 / (1.0 + jnp.exp(-u))


def n_levels(tokens):
    return tokens.bit_length() - 1


def span_matrix(level, tokens):
    t = lax.broadcasted_iota(jnp.int32, (tokens, tokens), 0)
    u = lax.broadcasted_iota(jnp.int32, (tokens, tokens), 1)
    depth = n_levels(tokens)
    if level == depth:
        keep = u <= t
    elif level == depth + 1:
        keep = u > t
    else:
        half = 1 << level
        edge = (t & ~(2 * half - 1)) + half
        odd = (t & half) > 0
        keep = (odd & (u >= edge) & (u <= t)) | (~odd & (u > t) & (u < edge))
    return keep.astype(F32).astype(BF)


def odd_rows(level, tokens, columns):
    t = lax.broadcasted_iota(jnp.int32, (tokens, columns), 0)
    return (t & (1 << level)) > 0


def same_pair(level, tokens):
    t = lax.broadcasted_iota(jnp.int32, (tokens, tokens), 0)
    u = lax.broadcasted_iota(jnp.int32, (tokens, tokens), 1)
    return (t >> (level + 1)) == (u >> (level + 1))


def ends_kernel(pre_ref, resets_ref, keys_ref, values_ref, spans_ref, total_ref, ends_ref):
    tokens, slots = pre_ref.shape
    depth = n_levels(tokens)
    width = keys_ref.shape[1]
    pre = pre_ref[...]
    log_decay = (jnp.minimum(pre, 0.0) - jnp.log1p(jnp.exp(-jnp.abs(pre)))) / GATE_NORM
    write = 1.0 - jnp.exp(log_decay)
    hi, lo = halves(log_decay)
    resets = jnp.broadcast_to(resets_ref[...], (tokens, slots)).astype(BF)
    stacked = jnp.concatenate([hi, lo, resets], axis=1)
    for level in range(depth + 2):
        sums = dot_nn(span_matrix(level, tokens), stacked)
        gap = sums[:, :slots] + sums[:, slots : 2 * slots]
        live = sums[:, 2 * slots :] < 0.5
        span = jnp.where(live, jnp.exp(gap), 0.0)
        spans_ref[level] = span
        if level == depth:
            total_ref[...] = span[tokens - 1 :, :]
        if level == depth + 1:
            hi, lo = halves(span * write)
            ends_ref[:, :width] = dot_tn(hi, keys_ref[...]) + dot_tn(lo, keys_ref[...])
            ends_ref[:, width:] = dot_tn(hi, values_ref[...]) + dot_tn(lo, values_ref[...])


def run_ends(pre, resets, keys, values):
    tokens, slots = pre.shape
    depth = n_levels(tokens)
    return pl.pallas_call(
        ends_kernel,
        out_shape=(
            jax.ShapeDtypeStruct((depth + 2, tokens, slots), F32),
            jax.ShapeDtypeStruct((1, slots), F32),
            jax.ShapeDtypeStruct((slots, keys.shape[1] + values.shape[1]), F32),
        ),
        name="slot_ends",
    )(pre, resets, keys, values)


def decay_write(pre):
    log_decay = (jnp.minimum(pre, 0.0) - jnp.log1p(jnp.exp(-jnp.abs(pre)))) / GATE_NORM
    return jnp.exp(log_decay)


def forward_kernel(
    query_ref, keys_ref, values_ref, pre_ref, spans_ref, state_ref, gate_ref, gain_ref,
    probs_ref, pairs_ref, mixing_ref, mix_ref, gated_ref,
):
    tokens, slots = pre_ref.shape
    depth = n_levels(tokens)
    width = keys_ref.shape[1]
    scaling = width ** (-0.5)
    write = 1.0 - decay_write(pre_ref[...])
    query = query_ref[...]
    pairs = dot_nt(query, keys_ref[...])
    pairs_ref[...] = pairs
    t = lax.broadcasted_iota(jnp.int32, (tokens, tokens), 0)
    u = lax.broadcasted_iota(jnp.int32, (tokens, tokens), 1)
    diagonal = jnp.sum(jnp.where(t == u, pairs, 0.0), axis=1, keepdims=True)
    state_hi, state_lo = halves(state_ref[:, :width])
    head = spans_ref[depth]
    raw = head * (dot_nt(query, state_hi) + dot_nt(query, state_lo)) + diagonal * write
    for level in range(depth):
        span = spans_ref[level]
        odd = odd_rows(level, tokens, slots)
        left, left_lo = halves(jnp.where(same_pair(level, tokens), pairs, 0.0))
        right, right_lo = halves(jnp.where(odd, 0.0, span * write))
        pulled = dot_nn(left, right) + dot_nn(left_lo, right) + dot_nn(left, right_lo)
        raw = raw + jnp.where(odd, span, 0.0) * pulled
    scores = scaling * raw
    scores = scores - jnp.max(scores, axis=1, keepdims=True)
    raised = jnp.exp(scores)
    probs = raised / jnp.sum(raised, axis=1, keepdims=True)
    probs_ref[...] = probs
    probs = probs.astype(BF).astype(F32)
    mixing = jnp.zeros((tokens, tokens), F32)
    for level in reversed(range(depth)):
        span = spans_ref[level]
        odd = odd_rows(level, tokens, slots)
        left, left_lo = halves(jnp.where(odd, span * probs, 0.0))
        right, right_lo = halves(jnp.where(odd, 0.0, span * write))
        pushed = dot_nt(left, right) + dot_nt(left_lo, right) + dot_nt(left, right_lo)
        mixing = jnp.where(same_pair(level, tokens), pushed, mixing)
    mixing = jnp.where(t == u, jnp.sum(probs * write, axis=1, keepdims=True), mixing)
    mixing, mixing_lo = halves(mixing)
    mixing_ref[...] = mixing
    state_hi, state_lo = halves(state_ref[:, width:])
    carried, carried_lo = halves(probs * head)
    mix = dot_nn(mixing, values_ref[...]) + dot_nn(mixing_lo, values_ref[...])
    mix = mix + dot_nn(carried, state_hi) + dot_nn(carried, state_lo) + dot_nn(carried_lo, state_hi)
    mix_ref[...] = mix
    scale = lax.rsqrt(jnp.mean(mix * mix, axis=1, keepdims=True) + EPSILON)
    gate = gate_ref[...]
    gated_ref[...] = (mix * scale * gain_ref[...] * (gate * sigmoid(gate))).astype(BF)


def run_forward(query, keys, values, pre, spans, state, gate, gain):
    tokens, slots = pre.shape
    width = keys.shape[1]
    return pl.pallas_call(
        forward_kernel,
        out_shape=(
            jax.ShapeDtypeStruct((tokens, slots), F32),
            jax.ShapeDtypeStruct((tokens, tokens), F32),
            jax.ShapeDtypeStruct((tokens, tokens), BF),
            jax.ShapeDtypeStruct((tokens, width), F32),
            jax.ShapeDtypeStruct((tokens, width), BF),
        ),
        name="slot_forward",
    )(query, keys, values, pre, spans, state, gate, gain)


def backward_kernel(
    grad_ref, query_ref, keys_ref, values_ref, pre_ref, spans_ref, state_ref, gate_ref, gain_ref,
    probs_ref, pairs_ref, mixing_ref, mix_ref,
    gquery_ref, gkeys_ref, gvalues_ref, ggate_ref, ggain_ref, gwrite_ref, glog_ref, carry_ref,
):
    tokens, slots = pre_ref.shape
    depth = n_levels(tokens)
    width = keys_ref.shape[1]
    scaling = width ** (-0.5)
    gate = gate_ref[...]
    sig = sigmoid(gate)
    silu = gate * sig
    gain = gain_ref[...]
    mix = mix_ref[...]
    scale = lax.rsqrt(jnp.mean(mix * mix, axis=1, keepdims=True) + EPSILON)
    normed = mix * scale
    grad = grad_ref[...]
    ggate_ref[...] = (grad * gain * normed * (sig * (1.0 + gate * (1.0 - sig)))).astype(BF)
    ggain_ref[...] = jnp.sum(grad * normed * silu, axis=0, keepdims=True)
    inner = grad * gain * silu
    mix_grad = scale * (inner - normed * jnp.mean(normed * inner, axis=1, keepdims=True))
    mix_low = mix_grad.astype(BF)

    write = 1.0 - decay_write(pre_ref[...])
    query, keys, values = query_ref[...], keys_ref[...], values_ref[...]
    pairs = pairs_ref[...]
    pairs_t = dot_nt(keys, query)
    mix_rest = (mix_grad - mix_low.astype(F32)).astype(BF)
    weigh = dot_nt(mix_low, values) + dot_nt(mix_rest, values)
    weigh_t = dot_nt(values, mix_low) + dot_nt(values, mix_rest)
    t = lax.broadcasted_iota(jnp.int32, (tokens, tokens), 0)
    u = lax.broadcasted_iota(jnp.int32, (tokens, tokens), 1)
    pair_diag = jnp.sum(jnp.where(t == u, pairs, 0.0), axis=1, keepdims=True)
    weigh_diag = jnp.sum(jnp.where(t == u, weigh, 0.0), axis=1, keepdims=True)
    head = spans_ref[depth]
    probs = probs_ref[...]
    probs_low = probs.astype(BF).astype(F32)

    vstate_hi, vstate_lo = halves(state_ref[:, width:])
    head_probs = head * (
        dot_nt(mix_low, vstate_hi) + dot_nt(mix_low, vstate_lo) + dot_nt(mix_rest, vstate_hi)
    )
    probs_grad = head_probs + weigh_diag * write
    row_values, row_keys = [], []
    for level in range(depth):
        span = spans_ref[level]
        odd = odd_rows(level, tokens, slots)
        same = same_pair(level, tokens)
        right, right_lo = halves(jnp.where(odd, 0.0, span * write))
        reach = jnp.where(odd, span, 0.0)
        left, left_lo = halves(jnp.where(same, weigh, 0.0))
        term = reach * (dot_nn(left, right) + dot_nn(left_lo, right) + dot_nn(left, right_lo))
        row_values.append(term)
        left, left_lo = halves(jnp.where(same, pairs, 0.0))
        row_keys.append(reach * (dot_nn(left, right) + dot_nn(left_lo, right) + dot_nn(left, right_lo)))
        probs_grad = probs_grad + term
    scores_grad = probs * (probs_grad - jnp.sum(probs_grad * probs, axis=1, keepdims=True))
    scores_grad = scaling * scores_grad

    kstate_hi, kstate_lo = halves(state_ref[:, :width])
    head_keys = head * (dot_nt(query, kstate_hi) + dot_nt(query, kstate_lo))
    gwrite = pair_diag * scores_grad + weigh_diag * probs_low
    glog = dot_tn(span_matrix(depth, tokens), (head_keys * scores_grad + head_probs * probs_low).astype(BF))
    gpairs = jnp.zeros((tokens, tokens), F32)
    for level in reversed(range(depth)):
        span = spans_ref[level]
        odd = odd_rows(level, tokens, slots)
        same = same_pair(level, tokens)
        reach = jnp.where(odd, span, 0.0)
        source = jnp.where(odd, 0.0, span)
        key_side, key_rest = halves(reach * scores_grad)
        value_side, value_rest = halves(reach * probs_low)
        seen, seen_rest = halves(jnp.where(same, pairs_t, 0.0))
        felt, felt_rest = halves(jnp.where(same, weigh_t, 0.0))
        sent, sent_rest = halves(source * write)
        pushed = dot_nt(key_side, sent) + dot_nt(key_rest, sent) + dot_nt(key_side, sent_rest)
        gpairs = jnp.where(same, pushed, gpairs)
        column = source * (
            dot_nn(seen, key_side) + dot_nn(seen, key_rest) + dot_nn(seen_rest, key_side)
            + dot_nn(felt, value_side) + dot_nn(felt, value_rest) + dot_nn(felt_rest, value_side)
        )
        gwrite = gwrite + column
        moved = column * write + row_values[level] * probs_low + row_keys[level] * scores_grad
        spread = span_matrix(level, tokens)
        moved, moved_rest = halves(moved)
        glog = glog + dot_tn(spread, moved) + dot_tn(spread, moved_rest)
    gpairs = jnp.where(t == u, jnp.sum(scores_grad * write, axis=1, keepdims=True), gpairs)
    gpairs, gpairs_rest = halves(gpairs)
    gwrite_ref[...] = gwrite
    glog_ref[...] = glog
    key_head, key_head_rest = halves(scores_grad * head)
    gquery_ref[...] = (
        dot_nn(gpairs, keys)
        + dot_nn(gpairs_rest, keys)
        + dot_nn(key_head, kstate_hi)
        + dot_nn(key_head, kstate_lo)
        + dot_nn(key_head_rest, kstate_hi)
    )
    gkeys_ref[...] = dot_tn(gpairs, query) + dot_tn(gpairs_rest, query)
    gvalues_ref[...] = dot_tn(mixing_ref[...], mix_low)
    carry_ref[:, :width] = dot_tn(key_head, query) + dot_tn(key_head_rest, query)
    carry_ref[:, width:] = dot_tn((probs_low * head).astype(BF), mix_low)


def run_backward(grad, query, keys, values, pre, spans, state, gate, gain, probs, pairs, mixing, mix):
    tokens, slots = pre.shape
    width = keys.shape[1]
    wide = jax.ShapeDtypeStruct((tokens, width), F32)
    narrow = jax.ShapeDtypeStruct((tokens, slots), F32)
    return pl.pallas_call(
        backward_kernel,
        out_shape=(
            wide, wide, wide,
            jax.ShapeDtypeStruct((tokens, width), BF),
            jax.ShapeDtypeStruct((1, width), F32),
            narrow, narrow,
            jax.ShapeDtypeStruct((slots, 2 * width), F32),
        ),
        name="slot_backward",
    )(grad, query, keys, values, pre, spans, state, gate, gain, probs, pairs, mixing, mix)


def finish_kernel(
    gquery_ref, gkeys_ref, gvalues_ref, ggate_ref, gwrite_ref, glog_ref,
    keys_ref, values_ref, pre_ref, spans_ref, query_pre_ref, keys_pre_ref,
    state_ref, total_ref, ends_ref, out_ref,
):
    tokens, slots = pre_ref.shape
    depth = n_levels(tokens)
    width = keys_ref.shape[1]
    pre = pre_ref[...]
    decay = decay_write(pre)
    write = 1.0 - decay
    keys, values = keys_ref[...], values_ref[...]
    ends = ends_ref[...]
    ends_low = ends.astype(BF)
    tail = spans_ref[depth + 1]
    sent = (tail * write).astype(BF)
    column = tail * (dot_nt(keys, ends_low[:, :width]) + dot_nt(values, ends_low[:, width:]))
    glog = glog_ref[...] + dot_tn(span_matrix(depth + 1, tokens), (column * write).astype(BF))
    carried = lax.dot_general(
        jnp.ones((1, 2 * width), F32), ends * state_ref[...], (((1,), (1,)), ((), ())),
        precision=lax.Precision.HIGHEST, preferred_element_type=F32,
    )
    glog = glog + carried * total_ref[...]
    glog = glog - decay * (gwrite_ref[...] + column)
    u = query_pre_ref[...]
    s = sigmoid(u)
    out_ref[:, :width] = (gquery_ref[...] * (s * (1.0 + u * (1.0 - s)))).astype(BF)
    u = keys_pre_ref[...]
    s = sigmoid(u)
    gkeys = gkeys_ref[...] + dot_nn(sent, ends_low[:, :width])
    out_ref[:, width : 2 * width] = (gkeys * (s * (1.0 + u * (1.0 - s)))).astype(BF)
    out_ref[:, 2 * width : 3 * width] = (gvalues_ref[...] + dot_nn(sent, ends_low[:, width:])).astype(BF)
    out_ref[:, 3 * width : 4 * width] = ggate_ref[...]
    gforget = glog * sigmoid(-pre) / GATE_NORM
    room = out_ref.shape[1] - 4 * width - slots
    out_ref[:, 4 * width :] = jnp.concatenate(
        [gforget.astype(BF), jnp.zeros((tokens, room), BF)], axis=1
    )


def run_finish(gquery, gkeys, gvalues, ggate, gwrite, glog, keys, values, pre, spans, query_pre, keys_pre, state, total, ends):
    tokens, slots = pre.shape
    width = keys.shape[1]
    return pl.pallas_call(
        finish_kernel,
        out_shape=jax.ShapeDtypeStruct((tokens, 4 * width + 128), BF),
        name="slot_finish",
    )(gquery, gkeys, gvalues, ggate, gwrite, glog, keys, values, pre, spans, query_pre, keys_pre, state, total, ends)


MESH = pl.DeviceIdType.MESH
GROUPED = ("shard", "ctx")


def greet(axes_of_peers):
    barrier = pltpu.get_barrier_semaphore()
    for peer in axes_of_peers:
        pl.semaphore_signal(barrier, inc=1, device_id=peer, device_id_type=MESH)
    pl.semaphore_wait(barrier, len(axes_of_peers))


def tp_peers():
    count = lax.axis_size("tp")
    me = lax.axis_index("tp")
    return me, [lax.rem(me + k, count) for k in range(1, count)]


CHUNKS = 4
LATENCY = 1.6


def tp_line(partial_ref, full_ref, arrived, staged, sums_ref, finish, send_a, recv_a, send_b, recv_b):
    count = lax.axis_size("tp")
    me = lax.axis_index("tp")
    rows = partial_ref.shape[1] // CHUNKS
    peers = [lax.rem(me + 1, count), lax.rem(me + count - 1, count)]

    def at_place(side, place):
        return place if side == 0 else count - 1 - place

    def cut(chunk):
        return pl.ds(chunk * rows, rows)

    def sum_copy(side, hop, chunk, source):
        return pltpu.make_async_remote_copy(
            src_ref=source,
            dst_ref=arrived.at[side, hop, chunk],
            send_sem=send_a.at[side, hop, chunk],
            recv_sem=recv_a.at[side, hop, chunk],
            device_id={"tp": peers[side]},
            device_id_type=MESH,
        )

    def row_copy(side, hop, chunk, block):
        return pltpu.make_async_remote_copy(
            src_ref=full_ref.at[block, cut(chunk)],
            dst_ref=full_ref.at[block, cut(chunk)],
            send_sem=send_b.at[side, hop, chunk],
            recv_sem=recv_b.at[side, hop, chunk],
            device_id={"tp": peers[side]},
            device_id_type=MESH,
        )

    def own(side, hop, chunk):
        return partial_ref.at[at_place(side, count - 1 - hop), cut(chunk)]

    def send_own(chunk):
        for side in range(2):

            @pl.when(me == at_place(side, 0))
            def _():
                for hop in range(count - 1):
                    sum_copy(side, hop, chunk, own(side, hop, chunk)).start()

    def add_hop(side, place, hop, chunk):
        @pl.when(me == at_place(side, place))
        def _():
            slot = staged.at[side, hop, chunk]
            copy = sum_copy(side, hop, chunk, slot)
            copy.wait_recv()
            slot[...] = (own(side, hop, chunk)[...].astype(F32) + arrived[side, hop, chunk].astype(F32)).astype(BF)
            copy.start()

    def close(chunk):
        sums_ref[...] = partial_ref[me, cut(chunk)].astype(F32)
        for side in range(2):
            place = me if side == 0 else count - 1 - me
            hop = jnp.minimum(count - 1 - place, count - 2)

            @pl.when(place > 0)
            def _():
                sum_copy(side, hop, chunk, staged.at[side, hop, chunk]).wait_recv()
                sums_ref[...] += arrived[side, hop, chunk].astype(F32)

        finish(chunk, sums_ref[...])
        for side in range(2):

            @pl.when(me != at_place(side, count - 1))
            def _():
                row_copy(side, 0, chunk, me).start()

    def forward(side, place, distance, chunk):
        @pl.when(me == at_place(side, place))
        def _():
            block = at_place(side, place - distance)
            row_copy(side, distance - 1, chunk, block).wait_recv()
            if place < count - 1:
                row_copy(side, distance, chunk, block).start()

    step = 1 + LATENCY
    events = []
    for chunk in range(CHUNKS):
        base = (count - 1) * chunk
        closed = base + (count - 1) + (count - 2) * LATENCY
        events.append((base - 1.5 * (count - 1), functools.partial(send_own, chunk)))
        events.append((closed, functools.partial(close, chunk)))
        for side in range(2):
            for place in range(1, count):
                for hop in range(count - 1 - place):
                    due = base + hop + place * step
                    events.append((due, functools.partial(add_hop, side, place, hop, chunk)))
                for distance in range(1, place + 1):
                    due = closed + 2 + distance * step
                    if place == count - 1:
                        due += 1000
                    events.append((due, functools.partial(forward, side, place, distance, chunk)))
    for _, event in sorted(events, key=lambda event: event[0]):
        event()

    def drain():
        for side in range(2):
            for place in range(count - 1):

                @pl.when(me == at_place(side, place))
                def _():
                    for chunk in range(CHUNKS):
                        for hop in range(count - 1 - place):
                            sum_copy(side, hop, chunk, staged.at[side, hop, chunk]).wait_send()
                        for hop in range(place + 1):
                            row_copy(side, hop, chunk, at_place(side, place - hop)).wait_send()

    return drain


def plane_peers():
    shards, ctxs = lax.axis_size("shard"), lax.axis_size("ctx")
    devices = shards * ctxs
    me = lax.axis_index("shard") * ctxs + lax.axis_index("ctx")
    peers = [lax.rem(me + k, devices) for k in range(1, devices)]
    places = [{"shard": lax.div(peer, ctxs), "ctx": lax.rem(peer, ctxs)} for peer in peers]
    return me, peers, places


def start_scatter(sources, targets, send_sems, recv_sems):
    me, peers, places = plane_peers()
    copies = []
    for i, (source, target) in enumerate(zip(sources, targets)):
        step = target.shape[2]

        def block(at):
            if len(source.shape) == 3:
                return source.at[at]
            return source.at[:, pl.ds(pl.multiple_of(at * step, step), step)]

        for k, (peer, place) in enumerate(zip(peers, places)):
            copy = pltpu.make_async_remote_copy(
                src_ref=block(peer),
                dst_ref=target.at[me],
                send_sem=send_sems.at[i, k],
                recv_sem=recv_sems.at[i, k],
                device_id=place,
                device_id_type=MESH,
            )
            copy.start()
            copies.append(copy)
    for source, target in zip(sources, targets):
        target[me] = block_of(source, me, target.shape[2])
    return copies


def block_of(source, at, step):
    if len(source.shape) == 3:
        return source[at]
    return source[:, pl.ds(pl.multiple_of(at * step, step), step)]


def start_sums(row_ref, landed, send_sems, recv_sems, peers, places, me):
    copies = []
    landed[me] = row_ref[...]
    for k, place in enumerate(places):
        copy = pltpu.make_async_remote_copy(
            src_ref=row_ref,
            dst_ref=landed.at[me],
            send_sem=send_sems.at[k],
            recv_sem=recv_sems.at[k],
            device_id=place,
            device_id_type=MESH,
        )
        copy.start()
        copies.append(copy)
    return copies


def summed(landed):
    total = landed[0]
    for k in range(1, landed.shape[0]):
        total = total + landed[k]
    return total


def exchange_kernel(epilogue, n_in, n_rows, n_moved, n_sums, partial_ref, *refs):
    me, peers = tp_peers()
    inputs, refs = refs[:n_in], refs[n_in:]
    sources, refs = refs[:n_moved], refs[n_moved:]
    full_ref, refs = refs[0], refs[1:]
    outputs, refs = refs[:n_rows], refs[n_rows:]
    targets, refs = refs[:n_moved], refs[n_moved:]
    sums, refs = refs[: 2 * n_sums], refs[2 * n_sums :]
    arrived, staged, sums_ref, send_a, recv_a, send_b, recv_b, send_m, recv_m = refs[:9]
    own, plane, places = plane_peers()
    across = [{"tp": peer} for peer in peers]
    greet(across + (places if n_moved or n_sums else []))
    moves = start_scatter(sources, targets, send_m, recv_m)
    rows = full_ref.shape[1] // CHUNKS
    started = []

    def finish(chunk, total):
        part = pl.ds(chunk * rows, rows)
        full_ref[me, part] = epilogue(total, me, part, chunk == 0, inputs, outputs)
        if n_sums and chunk == CHUNKS - 1:
            row_ref, in_plane, _, _, send_p, recv_p = refs[9:15]
            width = outputs[0].shape[1]
            row_ref[:, :width] = outputs[0][...]
            row_ref[:, width:] = inputs[-1][...]
            started.extend(start_sums(row_ref, in_plane, send_p, recv_p, plane, places, own))

    drain = tp_line(partial_ref, full_ref, arrived, staged, sums_ref, finish, send_a, recv_a, send_b, recv_b)
    if n_sums:
        row_ref, in_plane, plane_row, in_tp, send_p, recv_p, send_t, recv_t = refs[9:]
        for copy in started:
            copy.wait()
        plane_row[...] = summed(in_plane)
        sums[0][...] = plane_row[...]
        for copy in start_sums(plane_row, in_tp, send_t, recv_t, peers, across, me):
            copy.wait()
        sums[1][...] = summed(in_tp)
    drain()
    for copy in moves:
        copy.wait()


def run_exchange(epilogue, name, collective_id, partial, inputs, row_outputs, moved=(), summing=False):
    tp = lax.axis_size("tp")
    devices = lax.axis_size(GROUPED)
    tokens, columns = partial.shape
    share = tokens // tp
    partial = partial.reshape(tp, share, columns)
    step = columns // devices
    if step % 128:
        moved = [m.reshape(tokens, devices, step).transpose(1, 0, 2) for m in moved]
    count = len(moved)
    scratch = [
        *[pltpu.VMEM((2, tp - 1, CHUNKS, share // CHUNKS, columns), BF)] * 2,
        pltpu.VMEM((share // CHUNKS, columns), F32),
        *[pltpu.SemaphoreType.DMA((2, tp - 1, CHUNKS))] * 4,
        *[pltpu.SemaphoreType.DMA((max(count, 1), devices - 1))] * 2,
    ]
    extra = ()
    if summing:
        row = row_outputs[0].shape[1] + inputs[-1].shape[1]
        extra = (jax.ShapeDtypeStruct((1, row), F32),) * 2
        scratch += [
            pltpu.VMEM((1, row), F32),
            pltpu.VMEM((devices, 1, row), F32),
            pltpu.VMEM((1, row), F32),
            pltpu.VMEM((tp, 1, row), F32),
            *[pltpu.SemaphoreType.DMA((devices - 1,))] * 2,
            *[pltpu.SemaphoreType.DMA((tp - 1,))] * 2,
        ]
    out_shape = (
        jax.ShapeDtypeStruct((tp, share, columns), BF),
        *row_outputs,
        *[jax.ShapeDtypeStruct((devices, tokens, step), BF)] * count,
        *extra,
    )
    outs = pl.pallas_call(
        functools.partial(exchange_kernel, epilogue, len(inputs), len(row_outputs), count, int(summing)),
        out_shape=out_shape,
        in_specs=[pl.BlockSpec(memory_space=pltpu.VMEM)] * (1 + len(inputs) + count),
        out_specs=tuple([pl.BlockSpec(memory_space=pltpu.VMEM)] * len(out_shape)),
        scratch_shapes=scratch,
        compiler_params=pltpu.CompilerParams(collective_id=collective_id, has_side_effects=True),
        name=name,
    )(partial, *inputs, *moved)
    start = 1 + len(row_outputs)
    return (
        outs[0].reshape(tokens, columns),
        *outs[1:start],
        *[o.reshape(devices * tokens, step) for o in outs[start : start + count]],
        *outs[start + count :],
    )


def middle_epilogue(total, me, part, first, inputs, outputs):
    hidden_ref, gain_ref = inputs
    (branch_ref,) = outputs
    branch_ref[part, :] = total
    middle = hidden_ref[me, part].astype(F32) + total
    scale = lax.rsqrt(jnp.mean(middle * middle, axis=1, keepdims=True) + EPSILON)
    return (middle * scale * gain_ref[...]).astype(BF)


def result_epilogue(total, me, part, first, inputs, outputs):
    hidden_ref, branch_ref, teacher_out_ref, teacher_mix_ref, cotangent_ref, mask_ref, scale_ref = inputs
    grad_ref, losses_ref = outputs
    branch = branch_ref[part, :]
    result = hidden_ref[me, part].astype(F32) + branch + total
    mask = mask_ref[me, part]
    gap = result - teacher_out_ref[me, part].astype(F32)
    gap_mix = branch - teacher_mix_ref[me, part].astype(F32)
    loss_out = jnp.sum(mask * (gap * gap), keepdims=True)
    loss_mix = jnp.sum(mask * (gap_mix * gap_mix), keepdims=True)
    lane = lax.broadcasted_iota(jnp.int32, (1, 128), 1)
    losses = jnp.where(lane == 0, loss_out, 0.0) + jnp.where(lane == 1, loss_mix, 0.0)
    losses_ref[...] = losses if first else losses_ref[...] + losses
    grad_ref[part, :] = cotangent_ref[me, part].astype(F32) + scale_ref[...] * mask * gap
    return result.astype(BF)


def norm_back(grad, rows, gain):
    scale = lax.rsqrt(jnp.mean(rows * rows, axis=1, keepdims=True) + EPSILON)
    unit = rows * scale
    gain_grad = jnp.sum(grad * unit, axis=0, keepdims=True)
    inner = grad * gain
    return scale * (inner - unit * jnp.mean(unit * inner, axis=1, keepdims=True)), gain_grad


def branch_epilogue(total, me, part, first, inputs, outputs):
    hidden_ref, branch_ref, teacher_mix_ref, grad_ref, mask_ref, scale_ref, gain_ref = inputs
    grad_middle_ref, gain_grad_ref = outputs
    branch = branch_ref[part, :]
    back, gain_grad = norm_back(total, hidden_ref[me, part].astype(F32) + branch, gain_ref[...])
    gain_grad_ref[...] = gain_grad if first else gain_grad_ref[...] + gain_grad
    grad_middle = back + grad_ref[part, :]
    grad_middle_ref[part, :] = grad_middle
    gap_mix = branch - teacher_mix_ref[me, part].astype(F32)
    return (grad_middle + scale_ref[...] * mask_ref[me, part] * gap_mix).astype(BF)


def input_epilogue(total, me, part, first, inputs, outputs):
    hidden_ref, grad_middle_ref, gain_ref = inputs[:3]
    (gain_grad_ref,) = outputs
    back, gain_grad = norm_back(total, hidden_ref[me, part].astype(F32), gain_ref[...])
    gain_grad_ref[...] = gain_grad if first else gain_grad_ref[...] + gain_grad
    return (back + grad_middle_ref[part, :]).astype(BF)


def passed_along(value, axis, steps):
    count = lax.axis_size(axis)
    leading, last = (max(0, -steps), min(count, count - steps))
    return lax.ppermute(value, axis, [(source, source + steps) for source in range(leading, last)])


def relay(value, decay, axis, steps):
    carried = passed_along(value, axis, steps)
    for _ in range(lax.axis_size(axis) - 2):
        carried = passed_along(value + decay * carried, axis, steps)
    return carried


def gathered(value):
    return lax.all_gather(value, GROUPED, axis=0, tiled=True)


def per_device(
    hidden_in,
    cotangent,
    teacher_out,
    teacher_mix,
    valid_mask,
    doc_start,
    attn_gain,
    w_query,
    w_key,
    w_value,
    w_forget,
    forget_bias,
    head_gain,
    w_outgate,
    w_out,
    mlp_gain,
    w_gate,
    w_up,
    w_down,
):
    tokens, features = hidden_in.shape
    devices = lax.axis_size(GROUPED)
    tp = lax.axis_size("tp")
    share = tokens // tp
    rows = w_query.shape[0]
    width = w_query.shape[1]
    slots = w_forget.shape[1]
    units = w_gate.shape[1]
    tokens_all = tokens * devices
    mask_flat = valid_mask.astype(F32)

    def column(vector):
        flat = vector.reshape(-1, 1).astype(BF)
        return jnp.pad(flat, ((0, rows - flat.shape[0]), (0, 0)))

    count_own = jnp.sum(mask_flat).reshape(1)
    extras = jnp.concatenate(
        [column(attn_gain), column(mlp_gain), column(forget_bias), column(head_gain), column(count_own)], axis=1
    )
    extras = jnp.pad(extras, ((0, 0), (0, 128 - slots - extras.shape[1])))
    first = gathered(jnp.concatenate([w_query, w_key, w_value, w_outgate, w_forget, extras, w_out], axis=1))
    pack = jnp.concatenate([w_gate, w_up, w_down], axis=1)
    pack, first = lax.optimization_barrier((pack, first))
    second = gathered(pack)

    inner = 4 * width + 128
    out_w = first[:, inner:]
    first = first[:, :inner]
    spare = first[:, 4 * width + slots :].astype(F32)
    attn_scale = spare[:, 0].reshape(1, -1)
    mlp_scale = spare[:, 1].reshape(1, -1)
    bias = spare[:, 2].reshape(devices, rows)[:, : slots // devices].reshape(1, slots)
    head_scale = spare[:, 3].reshape(devices, rows)[:, : width // devices].reshape(1, width)
    count_total = jnp.sum(spare[:, 4].reshape(devices, rows)[:, 0])
    loss_scale = (tokens_all / count_total).reshape(1, 1)

    hidden_f = hidden_in.astype(F32)
    scale = lax.rsqrt(jnp.mean(hidden_f * hidden_f, axis=-1, keepdims=True) + EPSILON)
    normed_in = (hidden_f * scale * attn_scale).astype(BF)
    pre_all = dot_nn(normed_in, first)
    query_pre = pre_all[:, :width]
    keys_pre = pre_all[:, width : 2 * width]
    query = jax.nn.silu(query_pre).astype(BF)
    keys = jax.nn.silu(keys_pre).astype(BF)
    values = pre_all[:, 2 * width : 3 * width].astype(BF)
    gate_pre = pre_all[:, 3 * width : 4 * width]
    forget_pre = pre_all[:, 4 * width : 4 * width + slots] + bias
    resets = doc_start.astype(F32)[:, None]

    spans, total, ends = run_ends(forget_pre, resets, keys, values)
    decay = total.reshape(slots, 1)
    state = relay(ends, decay, "ctx", 1)
    probs, pairs, mixing, mix, gated = run_forward(
        query, keys, values, forget_pre, spans, state, gate_pre, head_scale
    )
    gate_w = second[:, :units]
    up_w = second[:, units : 2 * units]
    down_w = second[:, 2 * units :]

    by_share = lambda tensor: tensor.reshape(tp, share, -1)
    hidden_s, teacher_out_s, teacher_mix_s, cotangent_s = map(by_share, (hidden_in, teacher_out, teacher_mix, cotangent))
    mask_s = by_share(mask_flat)
    narrow = lambda *shape: jax.ShapeDtypeStruct(shape, F32)

    normed_mid, branch = run_exchange(
        middle_epilogue, "sum_branch", 1, dot_nt(gated, out_w).astype(BF), (hidden_s, mlp_scale),
        (narrow(share, features),),
    )
    gate_val = dot_nn(normed_mid, gate_w)
    up_val = dot_nn(normed_mid, up_w)
    hidden_units = (jax.nn.silu(gate_val) * up_val).astype(BF)
    forward_all = gathered(jnp.concatenate([gated, hidden_units], axis=1))
    output, grad_result, losses, normed_in_c, normed_mid_c = run_exchange(
        result_epilogue, "sum_result", 2, dot_nt(hidden_units, down_w).astype(BF),
        (hidden_s, branch, teacher_out_s, teacher_mix_s, cotangent_s, mask_s, loss_scale),
        (narrow(share, features), narrow(1, 128)),
        moved=(normed_in, normed_mid),
    )
    gap = output.astype(F32) - teacher_out.astype(F32)
    grad_mlp = (cotangent.astype(F32) + loss_scale * mask_flat[:, None] * gap).astype(BF)
    grad_units = dot_nn(grad_mlp, down_w)
    gate_sig = jax.nn.sigmoid(gate_val)
    grad_gate_val = (grad_units * up_val * (gate_sig * (1.0 + gate_val * (1.0 - gate_sig)))).astype(BF)
    grad_up_val = (grad_units * (gate_val * gate_sig)).astype(BF)
    grad_both = jnp.concatenate([grad_gate_val, grad_up_val], axis=1)
    partial = dot_nt(grad_both, second[:, : 2 * units]).astype(BF)
    forward_all, grad_both = lax.optimization_barrier((forward_all, grad_both))
    partial = lax.optimization_barrier((partial, grad_both))[0]
    mlp_all = gathered(grad_both)
    grad_branch, grad_middle, mlp_gain_part, grad_mlp_c = run_exchange(
        branch_epilogue, "sum_middle", 3, partial,
        (hidden_s, branch, teacher_mix_s, grad_result, mask_s, loss_scale, mlp_scale),
        (narrow(share, features), narrow(1, features)),
        moved=(grad_mlp,),
    )
    grad_gated = dot_nn(grad_branch, out_w)
    gquery, gkeys, gvalues, ggate, head_gain_part, gwrite, glog, carry = run_backward(
        grad_gated, query, keys, values, forget_pre, spans, state, gate_pre, head_scale, probs, pairs, mixing, mix
    )
    later = relay(carry, decay, "ctx", -1)
    grad_pre = run_finish(
        gquery, gkeys, gvalues, ggate, gwrite, glog, keys, values, forget_pre, spans, query_pre, keys_pre,
        state, total, later,
    )
    partial = dot_nt(grad_pre, first).astype(BF)
    mlp_all, grad_pre = lax.optimization_barrier((mlp_all, grad_pre))
    partial = lax.optimization_barrier((partial, grad_pre))[0]
    attn_all = gathered(grad_pre)
    grad_in, _, grad_branch_c, plane_sums, all_sums = run_exchange(
        input_epilogue, "sum_input", 4, partial,
        (hidden_s, grad_middle, attn_scale, jnp.concatenate([mlp_gain_part, head_gain_part, losses], axis=1)),
        (narrow(1, features),), moved=(grad_branch,), summing=True,
    )
    gate_grad = dot_tn(normed_mid_c, mlp_all[:, :units])
    up_grad = dot_tn(normed_mid_c, mlp_all[:, units:])
    out_grad = dot_tn(grad_branch_c, forward_all[:, :width])
    down_grad = dot_tn(grad_mlp_c, forward_all[:, width:])
    query_grad = dot_tn(normed_in_c, attn_all[:, :width])
    keys_grad = dot_tn(normed_in_c, attn_all[:, width : 2 * width])
    values_grad = dot_tn(normed_in_c, attn_all[:, 2 * width : 3 * width])
    outgate_grad = dot_tn(normed_in_c, attn_all[:, 3 * width : 4 * width])
    forget_all = attn_all[:, 4 * width : 4 * width + slots]
    forget_grad = dot_tn(normed_in_c, forget_all)
    index = lax.axis_index(GROUPED)
    bias_grad = jnp.sum(forget_all.astype(F32), axis=0, keepdims=True)
    bias_grad = lax.dynamic_slice_in_dim(bias_grad, index * (slots // devices), slots // devices, axis=1)

    cut = lambda row, size: lax.dynamic_slice_in_dim(row, index * size, size, axis=1)
    attn_gain_grad = cut(all_sums[:, :features], features // devices).reshape(-1)
    mlp_gain_grad = cut(all_sums[:, features : 2 * features], features // devices).reshape(-1)
    head_gain_grad = cut(plane_sums[:, 2 * features : 2 * features + width], width // devices)
    sums = all_sums[0, 2 * features + width :]
    loss_out = sums[0] / (2.0 * features * count_total)
    loss_mix = sums[1] / (2.0 * features * count_total)
    return (
        output,
        loss_out,
        loss_mix,
        grad_in.astype(F32),
        attn_gain_grad,
        query_grad,
        keys_grad,
        values_grad,
        forget_grad,
        bias_grad,
        head_gain_grad,
        outgate_grad,
        out_grad,
        mlp_gain_grad,
        gate_grad,
        up_grad,
        down_grad,
    )


def solution(mesh):
    return jax.shard_map(
        per_device,
        mesh=mesh,
        in_specs=(
            P(("shard", "ctx"), None),
            P(("shard", "ctx"), None),
            P(("shard", "ctx"), None),
            P(("shard", "ctx"), None),
            P(("shard", "ctx")),
            P(("shard", "ctx")),
            P(("shard", "ctx")),
            P(("shard", "ctx"), "tp"),
            P(("shard", "ctx"), "tp"),
            P(("shard", "ctx"), "tp"),
            P(("shard", "ctx"), "tp"),
            P("tp", ("shard", "ctx")),
            P("tp", ("shard", "ctx")),
            P(("shard", "ctx"), "tp"),
            P(("shard", "ctx"), "tp"),
            P(("shard", "ctx")),
            P(("shard", "ctx"), "tp"),
            P(("shard", "ctx"), "tp"),
            P(("shard", "ctx"), "tp"),
        ),
        out_specs=(
            P(("shard", "ctx"), None),
            P(),
            P(),
            P(("shard", "ctx"), None),
            P(("shard", "ctx")),
            P(("shard", "ctx"), "tp"),
            P(("shard", "ctx"), "tp"),
            P(("shard", "ctx"), "tp"),
            P(("shard", "ctx"), "tp"),
            P("tp", ("shard", "ctx")),
            P("tp", ("shard", "ctx")),
            P(("shard", "ctx"), "tp"),
            P(("shard", "ctx"), "tp"),
            P(("shard", "ctx")),
            P(("shard", "ctx"), "tp"),
            P(("shard", "ctx"), "tp"),
            P(("shard", "ctx"), "tp"),
        ),
        check_vma=False,
    )
```

```python
import functools

import jax
import jax.numpy as jnp
from jax import lax
from jax.experimental import pallas as pl
from jax.experimental.pallas import tpu as pltpu
from jax.sharding import PartitionSpec as P

F32 = jnp.float32
BF = jnp.bfloat16
EPSILON = 1e-06
GATE_NORM = 8.0


def dot_nn(a, b):
    return lax.dot_general(a, b, (((1,), (0,)), ((), ())), preferred_element_type=F32)


def dot_nt(a, b):
    return lax.dot_general(a, b, (((1,), (1,)), ((), ())), preferred_element_type=F32)


def dot_tn(a, b):
    return lax.dot_general(a, b, (((0,), (0,)), ((), ())), preferred_element_type=F32)


def halves(x):
    hi = x.astype(BF)
    return hi, (x - hi.astype(F32)).astype(BF)


def sigmoid(u):
    return 1.0 / (1.0 + jnp.exp(-u))


def n_levels(tokens):
    return tokens.bit_length() - 1


def span_matrix(level, tokens):
    t = lax.broadcasted_iota(jnp.int32, (tokens, tokens), 0)
    u = lax.broadcasted_iota(jnp.int32, (tokens, tokens), 1)
    depth = n_levels(tokens)
    if level == depth:
        keep = u <= t
    elif level == depth + 1:
        keep = u > t
    else:
        half = 1 << level
        edge = (t & ~(2 * half - 1)) + half
        odd = (t & half) > 0
        keep = (odd & (u >= edge) & (u <= t)) | (~odd & (u > t) & (u < edge))
    return keep.astype(F32).astype(BF)


def odd_rows(level, tokens, columns):
    t = lax.broadcasted_iota(jnp.int32, (tokens, columns), 0)
    return (t & (1 << level)) > 0


def same_pair(level, tokens):
    t = lax.broadcasted_iota(jnp.int32, (tokens, tokens), 0)
    u = lax.broadcasted_iota(jnp.int32, (tokens, tokens), 1)
    return (t >> (level + 1)) == (u >> (level + 1))


def ends_kernel(pre_ref, resets_ref, keys_ref, values_ref, spans_ref, total_ref, ends_ref):
    tokens, slots = pre_ref.shape
    depth = n_levels(tokens)
    width = keys_ref.shape[1]
    pre = pre_ref[...]
    log_decay = (jnp.minimum(pre, 0.0) - jnp.log1p(jnp.exp(-jnp.abs(pre)))) / GATE_NORM
    write = 1.0 - jnp.exp(log_decay)
    hi, lo = halves(log_decay)
    resets = jnp.broadcast_to(resets_ref[...], (tokens, slots)).astype(BF)
    stacked = jnp.concatenate([hi, lo, resets], axis=1)
    for level in range(depth + 2):
        sums = dot_nn(span_matrix(level, tokens), stacked)
        gap = sums[:, :slots] + sums[:, slots : 2 * slots]
        live = sums[:, 2 * slots :] < 0.5
        span = jnp.where(live, jnp.exp(gap), 0.0)
        spans_ref[level] = span
        if level == depth:
            total_ref[...] = span[tokens - 1 :, :]
        if level == depth + 1:
            hi, lo = halves(span * write)
            ends_ref[:, :width] = dot_tn(hi, keys_ref[...]) + dot_tn(lo, keys_ref[...])
            ends_ref[:, width:] = dot_tn(hi, values_ref[...]) + dot_tn(lo, values_ref[...])


def run_ends(pre, resets, keys, values):
    tokens, slots = pre.shape
    depth = n_levels(tokens)
    return pl.pallas_call(
        ends_kernel,
        out_shape=(
            jax.ShapeDtypeStruct((depth + 2, tokens, slots), F32),
            jax.ShapeDtypeStruct((1, slots), F32),
            jax.ShapeDtypeStruct((slots, keys.shape[1] + values.shape[1]), F32),
        ),
        name="slot_ends",
    )(pre, resets, keys, values)


def decay_write(pre):
    log_decay = (jnp.minimum(pre, 0.0) - jnp.log1p(jnp.exp(-jnp.abs(pre)))) / GATE_NORM
    return jnp.exp(log_decay)


def forward_kernel(
    query_ref, keys_ref, values_ref, pre_ref, spans_ref, state_ref, gate_ref, gain_ref,
    probs_ref, pairs_ref, mixing_ref, mix_ref, gated_ref,
):
    tokens, slots = pre_ref.shape
    depth = n_levels(tokens)
    width = keys_ref.shape[1]
    scaling = width ** (-0.5)
    write = 1.0 - decay_write(pre_ref[...])
    query = query_ref[...]
    pairs = dot_nt(query, keys_ref[...])
    pairs_ref[...] = pairs
    t = lax.broadcasted_iota(jnp.int32, (tokens, tokens), 0)
    u = lax.broadcasted_iota(jnp.int32, (tokens, tokens), 1)
    diagonal = jnp.sum(jnp.where(t == u, pairs, 0.0), axis=1, keepdims=True)
    state_hi, state_lo = halves(state_ref[:, :width])
    head = spans_ref[depth]
    raw = head * (dot_nt(query, state_hi) + dot_nt(query, state_lo)) + diagonal * write
    for level in range(depth):
        span = spans_ref[level]
        odd = odd_rows(level, tokens, slots)
        left, left_lo = halves(jnp.where(same_pair(level, tokens), pairs, 0.0))
        right, right_lo = halves(jnp.where(odd, 0.0, span * write))
        pulled = dot_nn(left, right) + dot_nn(left_lo, right) + dot_nn(left, right_lo)
        raw = raw + jnp.where(odd, span, 0.0) * pulled
    scores = scaling * raw
    scores = scores - jnp.max(scores, axis=1, keepdims=True)
    raised = jnp.exp(scores)
    probs = raised / jnp.sum(raised, axis=1, keepdims=True)
    probs_ref[...] = probs
    probs = probs.astype(BF).astype(F32)
    mixing = jnp.zeros((tokens, tokens), F32)
    for level in reversed(range(depth)):
        span = spans_ref[level]
        odd = odd_rows(level, tokens, slots)
        left, left_lo = halves(jnp.where(odd, span * probs, 0.0))
        right, right_lo = halves(jnp.where(odd, 0.0, span * write))
        pushed = dot_nt(left, right) + dot_nt(left_lo, right) + dot_nt(left, right_lo)
        mixing = jnp.where(same_pair(level, tokens), pushed, mixing)
    mixing = jnp.where(t == u, jnp.sum(probs * write, axis=1, keepdims=True), mixing)
    mixing, mixing_lo = halves(mixing)
    mixing_ref[...] = mixing
    state_hi, state_lo = halves(state_ref[:, width:])
    carried, carried_lo = halves(probs * head)
    mix = dot_nn(mixing, values_ref[...]) + dot_nn(mixing_lo, values_ref[...])
    mix = mix + dot_nn(carried, state_hi) + dot_nn(carried, state_lo) + dot_nn(carried_lo, state_hi)
    mix_ref[...] = mix
    scale = lax.rsqrt(jnp.mean(mix * mix, axis=1, keepdims=True) + EPSILON)
    gate = gate_ref[...]
    gated_ref[...] = (mix * scale * gain_ref[...] * (gate * sigmoid(gate))).astype(BF)


def run_forward(query, keys, values, pre, spans, state, gate, gain):
    tokens, slots = pre.shape
    width = keys.shape[1]
    return pl.pallas_call(
        forward_kernel,
        out_shape=(
            jax.ShapeDtypeStruct((tokens, slots), F32),
            jax.ShapeDtypeStruct((tokens, tokens), F32),
            jax.ShapeDtypeStruct((tokens, tokens), BF),
            jax.ShapeDtypeStruct((tokens, width), F32),
            jax.ShapeDtypeStruct((tokens, width), BF),
        ),
        name="slot_forward",
    )(query, keys, values, pre, spans, state, gate, gain)


def backward_kernel(
    grad_ref, query_ref, keys_ref, values_ref, pre_ref, spans_ref, state_ref, gate_ref, gain_ref,
    probs_ref, pairs_ref, mixing_ref, mix_ref,
    gquery_ref, gkeys_ref, gvalues_ref, ggate_ref, ggain_ref, gwrite_ref, glog_ref, carry_ref,
):
    tokens, slots = pre_ref.shape
    depth = n_levels(tokens)
    width = keys_ref.shape[1]
    scaling = width ** (-0.5)
    gate = gate_ref[...]
    sig = sigmoid(gate)
    silu = gate * sig
    gain = gain_ref[...]
    mix = mix_ref[...]
    scale = lax.rsqrt(jnp.mean(mix * mix, axis=1, keepdims=True) + EPSILON)
    normed = mix * scale
    grad = grad_ref[...]
    ggate_ref[...] = (grad * gain * normed * (sig * (1.0 + gate * (1.0 - sig)))).astype(BF)
    ggain_ref[...] = jnp.sum(grad * normed * silu, axis=0, keepdims=True)
    inner = grad * gain * silu
    mix_grad = scale * (inner - normed * jnp.mean(normed * inner, axis=1, keepdims=True))
    mix_low = mix_grad.astype(BF)

    write = 1.0 - decay_write(pre_ref[...])
    query, keys, values = query_ref[...], keys_ref[...], values_ref[...]
    pairs = pairs_ref[...]
    pairs_t = dot_nt(keys, query)
    mix_rest = (mix_grad - mix_low.astype(F32)).astype(BF)
    weigh = dot_nt(mix_low, values) + dot_nt(mix_rest, values)
    weigh_t = dot_nt(values, mix_low) + dot_nt(values, mix_rest)
    t = lax.broadcasted_iota(jnp.int32, (tokens, tokens), 0)
    u = lax.broadcasted_iota(jnp.int32, (tokens, tokens), 1)
    pair_diag = jnp.sum(jnp.where(t == u, pairs, 0.0), axis=1, keepdims=True)
    weigh_diag = jnp.sum(jnp.where(t == u, weigh, 0.0), axis=1, keepdims=True)
    head = spans_ref[depth]
    probs = probs_ref[...]
    probs_low = probs.astype(BF).astype(F32)

    vstate_hi, vstate_lo = halves(state_ref[:, width:])
    head_probs = head * (
        dot_nt(mix_low, vstate_hi) + dot_nt(mix_low, vstate_lo) + dot_nt(mix_rest, vstate_hi)
    )
    probs_grad = head_probs + weigh_diag * write
    row_values, row_keys = [], []
    for level in range(depth):
        span = spans_ref[level]
        odd = odd_rows(level, tokens, slots)
        same = same_pair(level, tokens)
        right, right_lo = halves(jnp.where(odd, 0.0, span * write))
        reach = jnp.where(odd, span, 0.0)
        left, left_lo = halves(jnp.where(same, weigh, 0.0))
        term = reach * (dot_nn(left, right) + dot_nn(left_lo, right) + dot_nn(left, right_lo))
        row_values.append(term)
        left, left_lo = halves(jnp.where(same, pairs, 0.0))
        row_keys.append(reach * (dot_nn(left, right) + dot_nn(left_lo, right) + dot_nn(left, right_lo)))
        probs_grad = probs_grad + term
    scores_grad = probs * (probs_grad - jnp.sum(probs_grad * probs, axis=1, keepdims=True))
    scores_grad = scaling * scores_grad

    kstate_hi, kstate_lo = halves(state_ref[:, :width])
    head_keys = head * (dot_nt(query, kstate_hi) + dot_nt(query, kstate_lo))
    gwrite = pair_diag * scores_grad + weigh_diag * probs_low
    glog = dot_tn(span_matrix(depth, tokens), (head_keys * scores_grad + head_probs * probs_low).astype(BF))
    gpairs = jnp.zeros((tokens, tokens), F32)
    for level in reversed(range(depth)):
        span = spans_ref[level]
        odd = odd_rows(level, tokens, slots)
        same = same_pair(level, tokens)
        reach = jnp.where(odd, span, 0.0)
        source = jnp.where(odd, 0.0, span)
        key_side, key_rest = halves(reach * scores_grad)
        value_side, value_rest = halves(reach * probs_low)
        seen, seen_rest = halves(jnp.where(same, pairs_t, 0.0))
        felt, felt_rest = halves(jnp.where(same, weigh_t, 0.0))
        sent, sent_rest = halves(source * write)
        pushed = dot_nt(key_side, sent) + dot_nt(key_rest, sent) + dot_nt(key_side, sent_rest)
        gpairs = jnp.where(same, pushed, gpairs)
        column = source * (
            dot_nn(seen, key_side) + dot_nn(seen, key_rest) + dot_nn(seen_rest, key_side)
            + dot_nn(felt, value_side) + dot_nn(felt, value_rest) + dot_nn(felt_rest, value_side)
        )
        gwrite = gwrite + column
        moved = column * write + row_values[level] * probs_low + row_keys[level] * scores_grad
        spread = span_matrix(level, tokens)
        moved, moved_rest = halves(moved)
        glog = glog + dot_tn(spread, moved) + dot_tn(spread, moved_rest)
    gpairs = jnp.where(t == u, jnp.sum(scores_grad * write, axis=1, keepdims=True), gpairs)
    gpairs, gpairs_rest = halves(gpairs)
    gwrite_ref[...] = gwrite
    glog_ref[...] = glog
    key_head, key_head_rest = halves(scores_grad * head)
    gquery_ref[...] = (
        dot_nn(gpairs, keys)
        + dot_nn(gpairs_rest, keys)
        + dot_nn(key_head, kstate_hi)
        + dot_nn(key_head, kstate_lo)
        + dot_nn(key_head_rest, kstate_hi)
    )
    gkeys_ref[...] = dot_tn(gpairs, query) + dot_tn(gpairs_rest, query)
    gvalues_ref[...] = dot_tn(mixing_ref[...], mix_low)
    carry_ref[:, :width] = dot_tn(key_head, query) + dot_tn(key_head_rest, query)
    carry_ref[:, width:] = dot_tn((probs_low * head).astype(BF), mix_low)


def run_backward(grad, query, keys, values, pre, spans, state, gate, gain, probs, pairs, mixing, mix):
    tokens, slots = pre.shape
    width = keys.shape[1]
    wide = jax.ShapeDtypeStruct((tokens, width), F32)
    narrow = jax.ShapeDtypeStruct((tokens, slots), F32)
    return pl.pallas_call(
        backward_kernel,
        out_shape=(
            wide, wide, wide,
            jax.ShapeDtypeStruct((tokens, width), BF),
            jax.ShapeDtypeStruct((1, width), F32),
            narrow, narrow,
            jax.ShapeDtypeStruct((slots, 2 * width), F32),
        ),
        name="slot_backward",
    )(grad, query, keys, values, pre, spans, state, gate, gain, probs, pairs, mixing, mix)


def finish_kernel(
    gquery_ref, gkeys_ref, gvalues_ref, ggate_ref, gwrite_ref, glog_ref,
    keys_ref, values_ref, pre_ref, spans_ref, query_pre_ref, keys_pre_ref,
    state_ref, total_ref, ends_ref, out_ref,
):
    tokens, slots = pre_ref.shape
    depth = n_levels(tokens)
    width = keys_ref.shape[1]
    pre = pre_ref[...]
    decay = decay_write(pre)
    write = 1.0 - decay
    keys, values = keys_ref[...], values_ref[...]
    ends = ends_ref[...]
    ends_low = ends.astype(BF)
    tail = spans_ref[depth + 1]
    sent = (tail * write).astype(BF)
    column = tail * (dot_nt(keys, ends_low[:, :width]) + dot_nt(values, ends_low[:, width:]))
    glog = glog_ref[...] + dot_tn(span_matrix(depth + 1, tokens), (column * write).astype(BF))
    carried = lax.dot_general(
        jnp.ones((1, 2 * width), F32), ends * state_ref[...], (((1,), (1,)), ((), ())),
        precision=lax.Precision.HIGHEST, preferred_element_type=F32,
    )
    glog = glog + carried * total_ref[...]
    glog = glog - decay * (gwrite_ref[...] + column)
    u = query_pre_ref[...]
    s = sigmoid(u)
    out_ref[:, :width] = (gquery_ref[...] * (s * (1.0 + u * (1.0 - s)))).astype(BF)
    u = keys_pre_ref[...]
    s = sigmoid(u)
    gkeys = gkeys_ref[...] + dot_nn(sent, ends_low[:, :width])
    out_ref[:, width : 2 * width] = (gkeys * (s * (1.0 + u * (1.0 - s)))).astype(BF)
    out_ref[:, 2 * width : 3 * width] = (gvalues_ref[...] + dot_nn(sent, ends_low[:, width:])).astype(BF)
    out_ref[:, 3 * width : 4 * width] = ggate_ref[...]
    gforget = glog * sigmoid(-pre) / GATE_NORM
    room = out_ref.shape[1] - 4 * width - slots
    out_ref[:, 4 * width :] = jnp.concatenate(
        [gforget.astype(BF), jnp.zeros((tokens, room), BF)], axis=1
    )


def run_finish(gquery, gkeys, gvalues, ggate, gwrite, glog, keys, values, pre, spans, query_pre, keys_pre, state, total, ends):
    tokens, slots = pre.shape
    width = keys.shape[1]
    return pl.pallas_call(
        finish_kernel,
        out_shape=jax.ShapeDtypeStruct((tokens, 4 * width + 128), BF),
        name="slot_finish",
    )(gquery, gkeys, gvalues, ggate, gwrite, glog, keys, values, pre, spans, query_pre, keys_pre, state, total, ends)


MESH = pl.DeviceIdType.MESH
GROUPED = ("shard", "ctx")


def greet(axes_of_peers):
    barrier = pltpu.get_barrier_semaphore()
    for peer in axes_of_peers:
        pl.semaphore_signal(barrier, inc=1, device_id=peer, device_id_type=MESH)
    pl.semaphore_wait(barrier, len(axes_of_peers))


def tp_peers():
    count = lax.axis_size("tp")
    me = lax.axis_index("tp")
    return me, [lax.rem(me + k, count) for k in range(1, count)]


CHUNKS = 4
LATENCY = 1.6


def tp_line(partial_ref, full_ref, arrived, staged, sums_ref, finish, send_a, recv_a, send_b, recv_b):
    count = lax.axis_size("tp")
    me = lax.axis_index("tp")
    rows = partial_ref.shape[1] // CHUNKS
    peers = [lax.rem(me + 1, count), lax.rem(me + count - 1, count)]

    def at_place(side, place):
        return place if side == 0 else count - 1 - place

    def cut(chunk):
        return pl.ds(chunk * rows, rows)

    def sum_copy(side, hop, chunk, source):
        return pltpu.make_async_remote_copy(
            src_ref=source,
            dst_ref=arrived.at[side, hop, chunk],
            send_sem=send_a.at[side, hop, chunk],
            recv_sem=recv_a.at[side, hop, chunk],
            device_id={"tp": peers[side]},
            device_id_type=MESH,
        )

    def row_copy(side, hop, chunk, block):
        return pltpu.make_async_remote_copy(
            src_ref=full_ref.at[block, cut(chunk)],
            dst_ref=full_ref.at[block, cut(chunk)],
            send_sem=send_b.at[side, hop, chunk],
            recv_sem=recv_b.at[side, hop, chunk],
            device_id={"tp": peers[side]},
            device_id_type=MESH,
        )

    def own(side, hop, chunk):
        return partial_ref.at[at_place(side, count - 1 - hop), cut(chunk)]

    def send_own(chunk):
        for side in range(2):

            @pl.when(me == at_place(side, 0))
            def _():
                for hop in range(count - 1):
                    sum_copy(side, hop, chunk, own(side, hop, chunk)).start()

    def add_hop(side, place, hop, chunk):
        @pl.when(me == at_place(side, place))
        def _():
            slot = staged.at[side, hop, chunk]
            copy = sum_copy(side, hop, chunk, slot)
            copy.wait_recv()
            slot[...] = (own(side, hop, chunk)[...].astype(F32) + arrived[side, hop, chunk].astype(F32)).astype(BF)
            copy.start()

    def close(chunk):
        sums_ref[...] = partial_ref[me, cut(chunk)].astype(F32)
        for side in range(2):
            place = me if side == 0 else count - 1 - me
            hop = jnp.minimum(count - 1 - place, count - 2)

            @pl.when(place > 0)
            def _():
                sum_copy(side, hop, chunk, staged.at[side, hop, chunk]).wait_recv()
                sums_ref[...] += arrived[side, hop, chunk].astype(F32)

        finish(chunk, sums_ref[...])
        for side in range(2):

            @pl.when(me != at_place(side, count - 1))
            def _():
                row_copy(side, 0, chunk, me).start()

    def forward(side, place, distance, chunk):
        @pl.when(me == at_place(side, place))
        def _():
            block = at_place(side, place - distance)
            row_copy(side, distance - 1, chunk, block).wait_recv()
            if place < count - 1:
                row_copy(side, distance, chunk, block).start()

    step = 1 + LATENCY
    events = []
    for chunk in range(CHUNKS):
        base = (count - 1) * chunk
        closed = base + (count - 1) + (count - 2) * LATENCY
        events.append((base - 1.5 * (count - 1), functools.partial(send_own, chunk)))
        events.append((closed, functools.partial(close, chunk)))
        for side in range(2):
            for place in range(1, count):
                for hop in range(count - 1 - place):
                    due = base + hop + place * step
                    events.append((due, functools.partial(add_hop, side, place, hop, chunk)))
                for distance in range(1, place + 1):
                    due = closed + 2 + distance * step
                    if place == count - 1:
                        due += 1000
                    events.append((due, functools.partial(forward, side, place, distance, chunk)))
    for _, event in sorted(events, key=lambda event: event[0]):
        event()

    def drain():
        for side in range(2):
            for place in range(count - 1):

                @pl.when(me == at_place(side, place))
                def _():
                    for chunk in range(CHUNKS):
                        for hop in range(count - 1 - place):
                            sum_copy(side, hop, chunk, staged.at[side, hop, chunk]).wait_send()
                        for hop in range(place + 1):
                            row_copy(side, hop, chunk, at_place(side, place - hop)).wait_send()

    return drain


def plane_peers():
    shards, ctxs = lax.axis_size("shard"), lax.axis_size("ctx")
    devices = shards * ctxs
    me = lax.axis_index("shard") * ctxs + lax.axis_index("ctx")
    peers = [lax.rem(me + k, devices) for k in range(1, devices)]
    places = [{"shard": lax.div(peer, ctxs), "ctx": lax.rem(peer, ctxs)} for peer in peers]
    return me, peers, places


def start_scatter(sources, targets, send_sems, recv_sems):
    me, peers, places = plane_peers()
    copies = []
    for i, (source, target) in enumerate(zip(sources, targets)):
        step = target.shape[2]

        def block(at):
            if len(source.shape) == 3:
                return source.at[at]
            return source.at[:, pl.ds(pl.multiple_of(at * step, step), step)]

        for k, (peer, place) in enumerate(zip(peers, places)):
            copy = pltpu.make_async_remote_copy(
                src_ref=block(peer),
                dst_ref=target.at[me],
                send_sem=send_sems.at[i, k],
                recv_sem=recv_sems.at[i, k],
                device_id=place,
                device_id_type=MESH,
            )
            copy.start()
            copies.append(copy)
    for source, target in zip(sources, targets):
        target[me] = block_of(source, me, target.shape[2])
    return copies


def block_of(source, at, step):
    if len(source.shape) == 3:
        return source[at]
    return source[:, pl.ds(pl.multiple_of(at * step, step), step)]


def spread_kernel(n_parts, with_row, *refs):
    parts, refs = refs[:n_parts], refs[n_parts:]
    if with_row:
        row_ref, out_ref, rows_ref, slab, part_sems, own_sem, send_sems, recv_sems, row_send, row_recv = refs
    else:
        out_ref, slab, part_sems, own_sem, send_sems, recv_sems = refs
    shard, core = lax.axis_index("shard"), lax.axis_index("ctx")
    me, _, places = plane_peers()
    across = shard + 1 - 2 * lax.rem(shard, 2)
    along = lax.rem(shard + 2, 4)
    corner = lax.rem(across + 2, 4)
    other = 1 - core
    to_x, to_y, to_core = {"shard": across}, {"shard": along}, {"ctx": other}
    rows = slab.shape[0]
    half = rows // 2

    loads = []
    start = 0
    for i, part in enumerate(parts):
        load = pltpu.make_async_copy(part, slab.at[:, pl.ds(start, part.shape[1])], part_sems.at[i])
        load.start()
        loads.append(load)
        start += part.shape[1]
    greet(places)
    for load in loads:
        load.wait()
    keep = pltpu.make_async_copy(slab, out_ref.at[pl.ds(pl.multiple_of(me * rows, rows), rows)], own_sem)
    keep.start()

    def landing(block, part):
        return out_ref.at[pl.ds(pl.multiple_of(block * rows + part * half, half), half)]

    started = []

    def send(kind, source, block, part, place):
        copy = pltpu.make_async_remote_copy(
            src_ref=source,
            dst_ref=landing(block, part),
            send_sem=send_sems.at[kind],
            recv_sem=recv_sems.at[kind],
            device_id=place,
            device_id_type=MESH,
        )
        copy.start()
        started.append(copy)

    def receive(kind, block, part, place):
        region = landing(block, part)
        pltpu.make_async_remote_copy(
            src_ref=region,
            dst_ref=region,
            send_sem=send_sems.at[kind],
            recv_sem=recv_sems.at[kind],
            device_id=place,
            device_id_type=MESH,
        ).wait_recv()

    def own(part):
        return slab.at[pl.ds(part * half, half)]

    def block(place, at_core):
        return 2 * place + at_core

    send(0, own(0), me, 0, to_x)
    send(1, own(1), me, 1, to_y)
    if with_row:
        copies = start_sums(row_ref, rows_ref, row_send, row_recv, [], places, me)
    send(2, own(1), me, 1, to_x)
    send(3, own(0), me, 0, to_y)
    send(4, own(0), me, 0, to_core)
    send(5, own(1), me, 1, to_core)
    x_block, y_block, far_block = block(across, core), block(along, core), block(corner, core)
    receive(0, x_block, 0, to_x)
    send(6, landing(x_block, 0), x_block, 0, to_y)
    send(8, landing(x_block, 0), x_block, 0, to_core)
    receive(1, y_block, 1, to_y)
    send(7, landing(y_block, 1), y_block, 1, to_x)
    send(9, landing(y_block, 1), y_block, 1, to_core)
    receive(2, x_block, 1, to_x)
    send(10, landing(x_block, 1), x_block, 1, to_core)
    receive(3, y_block, 0, to_y)
    send(11, landing(y_block, 0), y_block, 0, to_core)
    receive(6, far_block, 0, to_y)
    send(12, landing(far_block, 0), far_block, 0, to_core)
    receive(7, far_block, 1, to_x)
    send(13, landing(far_block, 1), far_block, 1, to_core)
    for kind, place, part in (
        (4, shard, 0), (5, shard, 1), (8, across, 0), (9, along, 1), (10, across, 1), (11, along, 0),
        (12, corner, 0), (13, corner, 1),
    ):
        receive(kind, block(place, other), part, to_core)
    for copy in started:
        copy.wait_send()
    keep.wait()
    if with_row:
        for copy in copies:
            copy.wait()


def run_spread(name, collective_id, parts, row=None):
    devices = lax.axis_size(GROUPED)
    rows = parts[0].shape[0]
    columns = sum(part.shape[1] for part in parts)
    anywhere = pl.BlockSpec(memory_space=pl.ANY)
    in_specs, out_specs = [anywhere] * len(parts), [anywhere]
    out_shape = [jax.ShapeDtypeStruct((devices * rows, columns), BF)]
    scratch = [
        pltpu.VMEM((rows, columns), BF),
        pltpu.SemaphoreType.DMA((len(parts),)),
        pltpu.SemaphoreType.DMA,
        *[pltpu.SemaphoreType.DMA((14,))] * 2,
    ]
    args = list(parts)
    if row is not None:
        args.append(row)
        in_specs.append(pl.BlockSpec(memory_space=pltpu.VMEM))
        out_specs.append(pl.BlockSpec(memory_space=pltpu.VMEM))
        out_shape.append(jax.ShapeDtypeStruct((devices, *row.shape), BF))
        scratch += [pltpu.SemaphoreType.DMA((devices - 1,))] * 2
    return pl.pallas_call(
        functools.partial(spread_kernel, len(parts), row is not None),
        out_shape=tuple(out_shape),
        in_specs=in_specs,
        out_specs=tuple(out_specs),
        scratch_shapes=scratch,
        compiler_params=pltpu.CompilerParams(collective_id=collective_id, has_side_effects=True),
        name=name,
    )(*args)


def start_sums(row_ref, landed, send_sems, recv_sems, peers, places, me):
    copies = []
    landed[me] = row_ref[...]
    for k, place in enumerate(places):
        copy = pltpu.make_async_remote_copy(
            src_ref=row_ref,
            dst_ref=landed.at[me],
            send_sem=send_sems.at[k],
            recv_sem=recv_sems.at[k],
            device_id=place,
            device_id_type=MESH,
        )
        copy.start()
        copies.append(copy)
    return copies


def summed(landed):
    total = landed[0]
    for k in range(1, landed.shape[0]):
        total = total + landed[k]
    return total


def exchange_kernel(epilogue, n_in, n_rows, n_moved, n_sums, partial_ref, *refs):
    me, peers = tp_peers()
    inputs, refs = refs[:n_in], refs[n_in:]
    sources, refs = refs[:n_moved], refs[n_moved:]
    full_ref, refs = refs[0], refs[1:]
    outputs, refs = refs[:n_rows], refs[n_rows:]
    targets, refs = refs[:n_moved], refs[n_moved:]
    sums, refs = refs[: 2 * n_sums], refs[2 * n_sums :]
    arrived, staged, sums_ref, send_a, recv_a, send_b, recv_b, send_m, recv_m = refs[:9]
    own, plane, places = plane_peers()
    across = [{"tp": peer} for peer in peers]
    greet(across + (places if n_moved or n_sums else []))
    moves = start_scatter(sources, targets, send_m, recv_m)
    rows = full_ref.shape[1] // CHUNKS
    started = []

    def finish(chunk, total):
        part = pl.ds(chunk * rows, rows)
        full_ref[me, part] = epilogue(total, me, part, chunk == 0, inputs, outputs)
        if n_sums and chunk == CHUNKS - 1:
            row_ref, in_plane, _, _, send_p, recv_p = refs[9:15]
            width = outputs[0].shape[1]
            row_ref[:, :width] = outputs[0][...]
            row_ref[:, width:] = inputs[-1][...]
            started.extend(start_sums(row_ref, in_plane, send_p, recv_p, plane, places, own))

    drain = tp_line(partial_ref, full_ref, arrived, staged, sums_ref, finish, send_a, recv_a, send_b, recv_b)
    if n_sums:
        row_ref, in_plane, plane_row, in_tp, send_p, recv_p, send_t, recv_t = refs[9:]
        for copy in started:
            copy.wait()
        plane_row[...] = summed(in_plane)
        sums[0][...] = plane_row[...]
        for copy in start_sums(plane_row, in_tp, send_t, recv_t, peers, across, me):
            copy.wait()
        sums[1][...] = summed(in_tp)
    drain()
    for copy in moves:
        copy.wait()


def run_exchange(epilogue, name, collective_id, partial, inputs, row_outputs, moved=(), summing=False):
    tp = lax.axis_size("tp")
    devices = lax.axis_size(GROUPED)
    tokens, columns = partial.shape
    share = tokens // tp
    partial = partial.reshape(tp, share, columns)
    step = columns // devices
    if step % 128:
        moved = [m.reshape(tokens, devices, step).transpose(1, 0, 2) for m in moved]
    count = len(moved)
    scratch = [
        *[pltpu.VMEM((2, tp - 1, CHUNKS, share // CHUNKS, columns), BF)] * 2,
        pltpu.VMEM((share // CHUNKS, columns), F32),
        *[pltpu.SemaphoreType.DMA((2, tp - 1, CHUNKS))] * 4,
        *[pltpu.SemaphoreType.DMA((max(count, 1), devices - 1))] * 2,
    ]
    extra = ()
    if summing:
        row = row_outputs[0].shape[1] + inputs[-1].shape[1]
        extra = (jax.ShapeDtypeStruct((1, row), F32),) * 2
        scratch += [
            pltpu.VMEM((1, row), F32),
            pltpu.VMEM((devices, 1, row), F32),
            pltpu.VMEM((1, row), F32),
            pltpu.VMEM((tp, 1, row), F32),
            *[pltpu.SemaphoreType.DMA((devices - 1,))] * 2,
            *[pltpu.SemaphoreType.DMA((tp - 1,))] * 2,
        ]
    out_shape = (
        jax.ShapeDtypeStruct((tp, share, columns), BF),
        *row_outputs,
        *[jax.ShapeDtypeStruct((devices, tokens, step), BF)] * count,
        *extra,
    )
    outs = pl.pallas_call(
        functools.partial(exchange_kernel, epilogue, len(inputs), len(row_outputs), count, int(summing)),
        out_shape=out_shape,
        in_specs=[pl.BlockSpec(memory_space=pltpu.VMEM)] * (1 + len(inputs) + count),
        out_specs=tuple([pl.BlockSpec(memory_space=pltpu.VMEM)] * len(out_shape)),
        scratch_shapes=scratch,
        compiler_params=pltpu.CompilerParams(collective_id=collective_id, has_side_effects=True),
        name=name,
    )(partial, *inputs, *moved)
    start = 1 + len(row_outputs)
    return (
        outs[0].reshape(tokens, columns),
        *outs[1:start],
        *[o.reshape(devices * tokens, step) for o in outs[start : start + count]],
        *outs[start + count :],
    )


def middle_epilogue(total, me, part, first, inputs, outputs):
    hidden_ref, gain_ref = inputs
    (branch_ref,) = outputs
    branch_ref[part, :] = total
    middle = hidden_ref[me, part].astype(F32) + total
    scale = lax.rsqrt(jnp.mean(middle * middle, axis=1, keepdims=True) + EPSILON)
    return (middle * scale * gain_ref[...]).astype(BF)


def result_epilogue(total, me, part, first, inputs, outputs):
    hidden_ref, branch_ref, teacher_out_ref, teacher_mix_ref, cotangent_ref, mask_ref, scale_ref = inputs
    grad_ref, losses_ref = outputs
    branch = branch_ref[part, :]
    result = hidden_ref[me, part].astype(F32) + branch + total
    mask = mask_ref[me, part]
    gap = result - teacher_out_ref[me, part].astype(F32)
    gap_mix = branch - teacher_mix_ref[me, part].astype(F32)
    loss_out = jnp.sum(mask * (gap * gap), keepdims=True)
    loss_mix = jnp.sum(mask * (gap_mix * gap_mix), keepdims=True)
    lane = lax.broadcasted_iota(jnp.int32, (1, 128), 1)
    losses = jnp.where(lane == 0, loss_out, 0.0) + jnp.where(lane == 1, loss_mix, 0.0)
    losses_ref[...] = losses if first else losses_ref[...] + losses
    grad_ref[part, :] = cotangent_ref[me, part].astype(F32) + scale_ref[...] * mask * gap
    return result.astype(BF)


def norm_back(grad, rows, gain):
    scale = lax.rsqrt(jnp.mean(rows * rows, axis=1, keepdims=True) + EPSILON)
    unit = rows * scale
    gain_grad = jnp.sum(grad * unit, axis=0, keepdims=True)
    inner = grad * gain
    return scale * (inner - unit * jnp.mean(unit * inner, axis=1, keepdims=True)), gain_grad


def branch_epilogue(total, me, part, first, inputs, outputs):
    hidden_ref, branch_ref, teacher_mix_ref, grad_ref, mask_ref, scale_ref, gain_ref = inputs
    grad_middle_ref, gain_grad_ref = outputs
    branch = branch_ref[part, :]
    back, gain_grad = norm_back(total, hidden_ref[me, part].astype(F32) + branch, gain_ref[...])
    gain_grad_ref[...] = gain_grad if first else gain_grad_ref[...] + gain_grad
    grad_middle = back + grad_ref[part, :]
    grad_middle_ref[part, :] = grad_middle
    gap_mix = branch - teacher_mix_ref[me, part].astype(F32)
    return (grad_middle + scale_ref[...] * mask_ref[me, part] * gap_mix).astype(BF)


def input_epilogue(total, me, part, first, inputs, outputs):
    hidden_ref, grad_middle_ref, gain_ref = inputs[:3]
    (gain_grad_ref,) = outputs
    back, gain_grad = norm_back(total, hidden_ref[me, part].astype(F32), gain_ref[...])
    gain_grad_ref[...] = gain_grad if first else gain_grad_ref[...] + gain_grad
    return (back + grad_middle_ref[part, :]).astype(BF)


def passed_along(value, axis, steps):
    count = lax.axis_size(axis)
    leading, last = (max(0, -steps), min(count, count - steps))
    return lax.ppermute(value, axis, [(source, source + steps) for source in range(leading, last)])


def relay(value, decay, axis, steps):
    carried = passed_along(value, axis, steps)
    for _ in range(lax.axis_size(axis) - 2):
        carried = passed_along(value + decay * carried, axis, steps)
    return carried


def gathered(value):
    return lax.all_gather(value, GROUPED, axis=0, tiled=True)


def per_device(
    hidden_in,
    cotangent,
    teacher_out,
    teacher_mix,
    valid_mask,
    doc_start,
    attn_gain,
    w_query,
    w_key,
    w_value,
    w_forget,
    forget_bias,
    head_gain,
    w_outgate,
    w_out,
    mlp_gain,
    w_gate,
    w_up,
    w_down,
):
    tokens, features = hidden_in.shape
    devices = lax.axis_size(GROUPED)
    tp = lax.axis_size("tp")
    share = tokens // tp
    rows = w_query.shape[0]
    width = w_query.shape[1]
    slots = w_forget.shape[1]
    units = w_gate.shape[1]
    tokens_all = tokens * devices
    mask_flat = valid_mask.astype(F32)

    count_own = jnp.sum(mask_flat).astype(BF).reshape(1)
    small = [attn_gain, mlp_gain, forget_bias.reshape(-1), head_gain.reshape(-1), count_own]
    row = jnp.concatenate(small)
    row = jnp.pad(row, (0, -row.shape[0] % 2048)).reshape(-1, 128)
    forget_w = jnp.pad(w_forget, ((0, 0), (0, 128 - slots)))
    attn_parts = [w_query, w_key, w_value, w_outgate, forget_w]
    pack = jnp.concatenate([w_gate, w_up, w_down], axis=1)
    if (lax.axis_size("shard"), lax.axis_size("ctx")) == (4, 2):
        first, row_all = run_spread("gather_attention", 5, attn_parts, row)
        pack, first = lax.optimization_barrier((pack, first))
        second = gathered(pack)
        out_own, first = lax.optimization_barrier((w_out, first))
        (out_w,) = run_spread("gather_out", 6, [out_own])
        first, row_all, out_w = lax.optimization_barrier((first, row_all, out_w))
    else:
        row_all = gathered(row)
        first = gathered(jnp.concatenate([*attn_parts, w_out], axis=1))
        pack, first = lax.optimization_barrier((pack, first))
        second = gathered(pack)
        out_w = first[:, 4 * width + 128 :]
        first = first[:, : 4 * width + 128]

    spare = row_all.reshape(devices, -1).astype(F32)
    attn_scale = spare[:, :rows].reshape(1, -1)
    mlp_scale = spare[:, rows : 2 * rows].reshape(1, -1)
    place = 2 * rows
    bias = spare[:, place : place + slots // devices].reshape(1, slots)
    place += slots // devices
    head_scale = spare[:, place : place + width // devices].reshape(1, width)
    place += width // devices
    count_total = jnp.sum(spare[:, place])
    loss_scale = (tokens_all / count_total).reshape(1, 1)

    hidden_f = hidden_in.astype(F32)
    scale = lax.rsqrt(jnp.mean(hidden_f * hidden_f, axis=-1, keepdims=True) + EPSILON)
    normed_in = (hidden_f * scale * attn_scale).astype(BF)
    pre_all = dot_nn(normed_in, first)
    query_pre = pre_all[:, :width]
    keys_pre = pre_all[:, width : 2 * width]
    query = jax.nn.silu(query_pre).astype(BF)
    keys = jax.nn.silu(keys_pre).astype(BF)
    values = pre_all[:, 2 * width : 3 * width].astype(BF)
    gate_pre = pre_all[:, 3 * width : 4 * width]
    forget_pre = pre_all[:, 4 * width : 4 * width + slots] + bias
    resets = doc_start.astype(F32)[:, None]

    spans, total, ends = run_ends(forget_pre, resets, keys, values)
    decay = total.reshape(slots, 1)
    state = relay(ends, decay, "ctx", 1)
    probs, pairs, mixing, mix, gated = run_forward(
        query, keys, values, forget_pre, spans, state, gate_pre, head_scale
    )
    gate_w = second[:, :units]
    up_w = second[:, units : 2 * units]
    down_w = second[:, 2 * units :]

    by_share = lambda tensor: tensor.reshape(tp, share, -1)
    hidden_s, teacher_out_s, teacher_mix_s, cotangent_s = map(by_share, (hidden_in, teacher_out, teacher_mix, cotangent))
    mask_s = by_share(mask_flat)
    narrow = lambda *shape: jax.ShapeDtypeStruct(shape, F32)

    normed_mid, branch = run_exchange(
        middle_epilogue, "sum_branch", 1, dot_nt(gated, out_w).astype(BF), (hidden_s, mlp_scale),
        (narrow(share, features),),
    )
    gate_val = dot_nn(normed_mid, gate_w)
    up_val = dot_nn(normed_mid, up_w)
    hidden_units = (jax.nn.silu(gate_val) * up_val).astype(BF)
    forward_all = gathered(jnp.concatenate([gated, hidden_units], axis=1))
    output, grad_result, losses, normed_in_c, normed_mid_c = run_exchange(
        result_epilogue, "sum_result", 2, dot_nt(hidden_units, down_w).astype(BF),
        (hidden_s, branch, teacher_out_s, teacher_mix_s, cotangent_s, mask_s, loss_scale),
        (narrow(share, features), narrow(1, 128)),
        moved=(normed_in, normed_mid),
    )
    gap = output.astype(F32) - teacher_out.astype(F32)
    grad_mlp = (cotangent.astype(F32) + loss_scale * mask_flat[:, None] * gap).astype(BF)
    grad_units = dot_nn(grad_mlp, down_w)
    gate_sig = jax.nn.sigmoid(gate_val)
    grad_gate_val = (grad_units * up_val * (gate_sig * (1.0 + gate_val * (1.0 - gate_sig)))).astype(BF)
    grad_up_val = (grad_units * (gate_val * gate_sig)).astype(BF)
    grad_both = jnp.concatenate([grad_gate_val, grad_up_val], axis=1)
    partial = dot_nt(grad_both, second[:, : 2 * units]).astype(BF)
    forward_all, grad_both = lax.optimization_barrier((forward_all, grad_both))
    partial = lax.optimization_barrier((partial, grad_both))[0]
    mlp_all = gathered(grad_both)
    grad_branch, grad_middle, mlp_gain_part, grad_mlp_c = run_exchange(
        branch_epilogue, "sum_middle", 3, partial,
        (hidden_s, branch, teacher_mix_s, grad_result, mask_s, loss_scale, mlp_scale),
        (narrow(share, features), narrow(1, features)),
        moved=(grad_mlp,),
    )
    grad_gated = dot_nn(grad_branch, out_w)
    gquery, gkeys, gvalues, ggate, head_gain_part, gwrite, glog, carry = run_backward(
        grad_gated, query, keys, values, forget_pre, spans, state, gate_pre, head_scale, probs, pairs, mixing, mix
    )
    later = relay(carry, decay, "ctx", -1)
    grad_pre = run_finish(
        gquery, gkeys, gvalues, ggate, gwrite, glog, keys, values, forget_pre, spans, query_pre, keys_pre,
        state, total, later,
    )
    partial = dot_nt(grad_pre, first).astype(BF)
    mlp_all, grad_pre = lax.optimization_barrier((mlp_all, grad_pre))
    partial = lax.optimization_barrier((partial, grad_pre))[0]
    attn_all = gathered(grad_pre)
    grad_in, _, grad_branch_c, plane_sums, all_sums = run_exchange(
        input_epilogue, "sum_input", 4, partial,
        (hidden_s, grad_middle, attn_scale, jnp.concatenate([mlp_gain_part, head_gain_part, losses], axis=1)),
        (narrow(1, features),), moved=(grad_branch,), summing=True,
    )
    gate_grad = dot_tn(normed_mid_c, mlp_all[:, :units])
    up_grad = dot_tn(normed_mid_c, mlp_all[:, units:])
    out_grad = dot_tn(grad_branch_c, forward_all[:, :width])
    down_grad = dot_tn(grad_mlp_c, forward_all[:, width:])
    query_grad = dot_tn(normed_in_c, attn_all[:, :width])
    keys_grad = dot_tn(normed_in_c, attn_all[:, width : 2 * width])
    values_grad = dot_tn(normed_in_c, attn_all[:, 2 * width : 3 * width])
    outgate_grad = dot_tn(normed_in_c, attn_all[:, 3 * width : 4 * width])
    forget_all = attn_all[:, 4 * width : 4 * width + slots]
    forget_grad = dot_tn(normed_in_c, forget_all)
    index = lax.axis_index(GROUPED)
    bias_grad = jnp.sum(forget_all.astype(F32), axis=0, keepdims=True)
    bias_grad = lax.dynamic_slice_in_dim(bias_grad, index * (slots // devices), slots // devices, axis=1)

    cut = lambda row, size: lax.dynamic_slice_in_dim(row, index * size, size, axis=1)
    attn_gain_grad = cut(all_sums[:, :features], features // devices).reshape(-1)
    mlp_gain_grad = cut(all_sums[:, features : 2 * features], features // devices).reshape(-1)
    head_gain_grad = cut(plane_sums[:, 2 * features : 2 * features + width], width // devices)
    sums = all_sums[0, 2 * features + width :]
    loss_out = sums[0] / (2.0 * features * count_total)
    loss_mix = sums[1] / (2.0 * features * count_total)
    return (
        output,
        loss_out,
        loss_mix,
        grad_in.astype(F32),
        attn_gain_grad,
        query_grad,
        keys_grad,
        values_grad,
        forget_grad,
        bias_grad,
        head_gain_grad,
        outgate_grad,
        out_grad,
        mlp_gain_grad,
        gate_grad,
        up_grad,
        down_grad,
    )


def solution(mesh):
    return jax.shard_map(
        per_device,
        mesh=mesh,
        in_specs=(
            P(("shard", "ctx"), None),
            P(("shard", "ctx"), None),
            P(("shard", "ctx"), None),
            P(("shard", "ctx"), None),
            P(("shard", "ctx")),
            P(("shard", "ctx")),
            P(("shard", "ctx")),
            P(("shard", "ctx"), "tp"),
            P(("shard", "ctx"), "tp"),
            P(("shard", "ctx"), "tp"),
            P(("shard", "ctx"), "tp"),
            P("tp", ("shard", "ctx")),
            P("tp", ("shard", "ctx")),
            P(("shard", "ctx"), "tp"),
            P(("shard", "ctx"), "tp"),
            P(("shard", "ctx")),
            P(("shard", "ctx"), "tp"),
            P(("shard", "ctx"), "tp"),
            P(("shard", "ctx"), "tp"),
        ),
        out_specs=(
            P(("shard", "ctx"), None),
            P(),
            P(),
            P(("shard", "ctx"), None),
            P(("shard", "ctx")),
            P(("shard", "ctx"), "tp"),
            P(("shard", "ctx"), "tp"),
            P(("shard", "ctx"), "tp"),
            P(("shard", "ctx"), "tp"),
            P("tp", ("shard", "ctx")),
            P("tp", ("shard", "ctx")),
            P(("shard", "ctx"), "tp"),
            P(("shard", "ctx"), "tp"),
            P(("shard", "ctx")),
            P(("shard", "ctx"), "tp"),
            P(("shard", "ctx"), "tp"),
            P(("shard", "ctx"), "tp"),
        ),
        check_vma=False,
    )
```

```python
import functools

import jax
import jax.numpy as jnp
from jax import lax
from jax.experimental import pallas as pl
from jax.experimental.pallas import tpu as pltpu
from jax.sharding import PartitionSpec as P

F32 = jnp.float32
BF = jnp.bfloat16
EPSILON = 1e-06
GATE_NORM = 8.0


def dot_nn(a, b):
    return lax.dot_general(a, b, (((1,), (0,)), ((), ())), preferred_element_type=F32)


def dot_nt(a, b):
    return lax.dot_general(a, b, (((1,), (1,)), ((), ())), preferred_element_type=F32)


def dot_tn(a, b):
    return lax.dot_general(a, b, (((0,), (0,)), ((), ())), preferred_element_type=F32)


def halves(x):
    hi = x.astype(BF)
    return hi, (x - hi.astype(F32)).astype(BF)


def sigmoid(u):
    return 1.0 / (1.0 + jnp.exp(-u))


def n_levels(tokens):
    return tokens.bit_length() - 1


def span_matrix(level, tokens):
    t = lax.broadcasted_iota(jnp.int32, (tokens, tokens), 0)
    u = lax.broadcasted_iota(jnp.int32, (tokens, tokens), 1)
    depth = n_levels(tokens)
    if level == depth:
        keep = u <= t
    elif level == depth + 1:
        keep = u > t
    else:
        half = 1 << level
        edge = (t & ~(2 * half - 1)) + half
        odd = (t & half) > 0
        keep = (odd & (u >= edge) & (u <= t)) | (~odd & (u > t) & (u < edge))
    return keep.astype(F32).astype(BF)


def odd_rows(level, tokens, columns):
    t = lax.broadcasted_iota(jnp.int32, (tokens, columns), 0)
    return (t & (1 << level)) > 0


def same_pair(level, tokens):
    t = lax.broadcasted_iota(jnp.int32, (tokens, tokens), 0)
    u = lax.broadcasted_iota(jnp.int32, (tokens, tokens), 1)
    return (t >> (level + 1)) == (u >> (level + 1))


def ends_kernel(pre_ref, resets_ref, keys_ref, values_ref, spans_ref, total_ref, ends_ref):
    tokens, slots = pre_ref.shape
    depth = n_levels(tokens)
    width = keys_ref.shape[1]
    pre = pre_ref[...]
    log_decay = (jnp.minimum(pre, 0.0) - jnp.log1p(jnp.exp(-jnp.abs(pre)))) / GATE_NORM
    write = 1.0 - jnp.exp(log_decay)
    hi, lo = halves(log_decay)
    resets = jnp.broadcast_to(resets_ref[...], (tokens, slots)).astype(BF)
    stacked = jnp.concatenate([hi, lo, resets], axis=1)
    for level in range(depth + 2):
        sums = dot_nn(span_matrix(level, tokens), stacked)
        gap = sums[:, :slots] + sums[:, slots : 2 * slots]
        live = sums[:, 2 * slots :] < 0.5
        span = jnp.where(live, jnp.exp(gap), 0.0)
        spans_ref[level] = span
        if level == depth:
            total_ref[...] = span[tokens - 1 :, :]
        if level == depth + 1:
            hi, lo = halves(span * write)
            ends_ref[:, :width] = dot_tn(hi, keys_ref[...]) + dot_tn(lo, keys_ref[...])
            ends_ref[:, width:] = dot_tn(hi, values_ref[...]) + dot_tn(lo, values_ref[...])


def run_ends(pre, resets, keys, values):
    tokens, slots = pre.shape
    depth = n_levels(tokens)
    return pl.pallas_call(
        ends_kernel,
        out_shape=(
            jax.ShapeDtypeStruct((depth + 2, tokens, slots), F32),
            jax.ShapeDtypeStruct((1, slots), F32),
            jax.ShapeDtypeStruct((slots, keys.shape[1] + values.shape[1]), F32),
        ),
        name="slot_ends",
    )(pre, resets, keys, values)


def decay_write(pre):
    log_decay = (jnp.minimum(pre, 0.0) - jnp.log1p(jnp.exp(-jnp.abs(pre)))) / GATE_NORM
    return jnp.exp(log_decay)


def forward_kernel(
    query_ref, keys_ref, values_ref, pre_ref, spans_ref, state_ref, gate_ref, gain_ref,
    probs_ref, pairs_ref, mixing_ref, mix_ref, gated_ref,
):
    tokens, slots = pre_ref.shape
    depth = n_levels(tokens)
    width = keys_ref.shape[1]
    scaling = width ** (-0.5)
    write = 1.0 - decay_write(pre_ref[...])
    query = query_ref[...]
    pairs = dot_nt(query, keys_ref[...])
    pairs_ref[...] = pairs
    t = lax.broadcasted_iota(jnp.int32, (tokens, tokens), 0)
    u = lax.broadcasted_iota(jnp.int32, (tokens, tokens), 1)
    diagonal = jnp.sum(jnp.where(t == u, pairs, 0.0), axis=1, keepdims=True)
    state_hi, state_lo = halves(state_ref[:, :width])
    head = spans_ref[depth]
    raw = head * (dot_nt(query, state_hi) + dot_nt(query, state_lo)) + diagonal * write
    for level in range(depth):
        span = spans_ref[level]
        odd = odd_rows(level, tokens, slots)
        left, left_lo = halves(jnp.where(same_pair(level, tokens), pairs, 0.0))
        right, right_lo = halves(jnp.where(odd, 0.0, span * write))
        pulled = dot_nn(left, right) + dot_nn(left_lo, right) + dot_nn(left, right_lo)
        raw = raw + jnp.where(odd, span, 0.0) * pulled
    scores = scaling * raw
    scores = scores - jnp.max(scores, axis=1, keepdims=True)
    raised = jnp.exp(scores)
    probs = raised / jnp.sum(raised, axis=1, keepdims=True)
    probs_ref[...] = probs
    probs = probs.astype(BF).astype(F32)
    mixing = jnp.zeros((tokens, tokens), F32)
    for level in reversed(range(depth)):
        span = spans_ref[level]
        odd = odd_rows(level, tokens, slots)
        left, left_lo = halves(jnp.where(odd, span * probs, 0.0))
        right, right_lo = halves(jnp.where(odd, 0.0, span * write))
        pushed = dot_nt(left, right) + dot_nt(left_lo, right) + dot_nt(left, right_lo)
        mixing = jnp.where(same_pair(level, tokens), pushed, mixing)
    mixing = jnp.where(t == u, jnp.sum(probs * write, axis=1, keepdims=True), mixing)
    mixing, mixing_lo = halves(mixing)
    mixing_ref[...] = mixing
    state_hi, state_lo = halves(state_ref[:, width:])
    carried, carried_lo = halves(probs * head)
    mix = dot_nn(mixing, values_ref[...]) + dot_nn(mixing_lo, values_ref[...])
    mix = mix + dot_nn(carried, state_hi) + dot_nn(carried, state_lo) + dot_nn(carried_lo, state_hi)
    mix_ref[...] = mix
    scale = lax.rsqrt(jnp.mean(mix * mix, axis=1, keepdims=True) + EPSILON)
    gate = gate_ref[...]
    gated_ref[...] = (mix * scale * gain_ref[...] * (gate * sigmoid(gate))).astype(BF)


def run_forward(query, keys, values, pre, spans, state, gate, gain):
    tokens, slots = pre.shape
    width = keys.shape[1]
    return pl.pallas_call(
        forward_kernel,
        out_shape=(
            jax.ShapeDtypeStruct((tokens, slots), F32),
            jax.ShapeDtypeStruct((tokens, tokens), F32),
            jax.ShapeDtypeStruct((tokens, tokens), BF),
            jax.ShapeDtypeStruct((tokens, width), F32),
            jax.ShapeDtypeStruct((tokens, width), BF),
        ),
        name="slot_forward",
    )(query, keys, values, pre, spans, state, gate, gain)


def backward_kernel(
    grad_ref, query_ref, keys_ref, values_ref, pre_ref, spans_ref, state_ref, gate_ref, gain_ref,
    probs_ref, pairs_ref, mixing_ref, mix_ref,
    gquery_ref, gkeys_ref, gvalues_ref, ggate_ref, ggain_ref, gwrite_ref, glog_ref, carry_ref,
):
    tokens, slots = pre_ref.shape
    depth = n_levels(tokens)
    width = keys_ref.shape[1]
    scaling = width ** (-0.5)
    gate = gate_ref[...]
    sig = sigmoid(gate)
    silu = gate * sig
    gain = gain_ref[...]
    mix = mix_ref[...]
    scale = lax.rsqrt(jnp.mean(mix * mix, axis=1, keepdims=True) + EPSILON)
    normed = mix * scale
    grad = grad_ref[...]
    ggate_ref[...] = (grad * gain * normed * (sig * (1.0 + gate * (1.0 - sig)))).astype(BF)
    ggain_ref[...] = jnp.sum(grad * normed * silu, axis=0, keepdims=True)
    inner = grad * gain * silu
    mix_grad = scale * (inner - normed * jnp.mean(normed * inner, axis=1, keepdims=True))
    mix_low = mix_grad.astype(BF)

    write = 1.0 - decay_write(pre_ref[...])
    query, keys, values = query_ref[...], keys_ref[...], values_ref[...]
    pairs = pairs_ref[...]
    pairs_t = dot_nt(keys, query)
    mix_rest = (mix_grad - mix_low.astype(F32)).astype(BF)
    weigh = dot_nt(mix_low, values) + dot_nt(mix_rest, values)
    weigh_t = dot_nt(values, mix_low) + dot_nt(values, mix_rest)
    t = lax.broadcasted_iota(jnp.int32, (tokens, tokens), 0)
    u = lax.broadcasted_iota(jnp.int32, (tokens, tokens), 1)
    pair_diag = jnp.sum(jnp.where(t == u, pairs, 0.0), axis=1, keepdims=True)
    weigh_diag = jnp.sum(jnp.where(t == u, weigh, 0.0), axis=1, keepdims=True)
    head = spans_ref[depth]
    probs = probs_ref[...]
    probs_low = probs.astype(BF).astype(F32)

    vstate_hi, vstate_lo = halves(state_ref[:, width:])
    head_probs = head * (
        dot_nt(mix_low, vstate_hi) + dot_nt(mix_low, vstate_lo) + dot_nt(mix_rest, vstate_hi)
    )
    probs_grad = head_probs + weigh_diag * write
    row_values, row_keys = [], []
    for level in range(depth):
        span = spans_ref[level]
        odd = odd_rows(level, tokens, slots)
        same = same_pair(level, tokens)
        right, right_lo = halves(jnp.where(odd, 0.0, span * write))
        reach = jnp.where(odd, span, 0.0)
        left, left_lo = halves(jnp.where(same, weigh, 0.0))
        term = reach * (dot_nn(left, right) + dot_nn(left_lo, right) + dot_nn(left, right_lo))
        row_values.append(term)
        left, left_lo = halves(jnp.where(same, pairs, 0.0))
        row_keys.append(reach * (dot_nn(left, right) + dot_nn(left_lo, right) + dot_nn(left, right_lo)))
        probs_grad = probs_grad + term
    scores_grad = probs * (probs_grad - jnp.sum(probs_grad * probs, axis=1, keepdims=True))
    scores_grad = scaling * scores_grad

    kstate_hi, kstate_lo = halves(state_ref[:, :width])
    head_keys = head * (dot_nt(query, kstate_hi) + dot_nt(query, kstate_lo))
    gwrite = pair_diag * scores_grad + weigh_diag * probs_low
    glog = dot_tn(span_matrix(depth, tokens), (head_keys * scores_grad + head_probs * probs_low).astype(BF))
    gpairs = jnp.zeros((tokens, tokens), F32)
    for level in reversed(range(depth)):
        span = spans_ref[level]
        odd = odd_rows(level, tokens, slots)
        same = same_pair(level, tokens)
        reach = jnp.where(odd, span, 0.0)
        source = jnp.where(odd, 0.0, span)
        key_side, key_rest = halves(reach * scores_grad)
        value_side, value_rest = halves(reach * probs_low)
        seen, seen_rest = halves(jnp.where(same, pairs_t, 0.0))
        felt, felt_rest = halves(jnp.where(same, weigh_t, 0.0))
        sent, sent_rest = halves(source * write)
        pushed = dot_nt(key_side, sent) + dot_nt(key_rest, sent) + dot_nt(key_side, sent_rest)
        gpairs = jnp.where(same, pushed, gpairs)
        column = source * (
            dot_nn(seen, key_side) + dot_nn(seen, key_rest) + dot_nn(seen_rest, key_side)
            + dot_nn(felt, value_side) + dot_nn(felt, value_rest) + dot_nn(felt_rest, value_side)
        )
        gwrite = gwrite + column
        moved = column * write + row_values[level] * probs_low + row_keys[level] * scores_grad
        spread = span_matrix(level, tokens)
        moved, moved_rest = halves(moved)
        glog = glog + dot_tn(spread, moved) + dot_tn(spread, moved_rest)
    gpairs = jnp.where(t == u, jnp.sum(scores_grad * write, axis=1, keepdims=True), gpairs)
    gpairs, gpairs_rest = halves(gpairs)
    gwrite_ref[...] = gwrite
    glog_ref[...] = glog
    key_head, key_head_rest = halves(scores_grad * head)
    gquery_ref[...] = (
        dot_nn(gpairs, keys)
        + dot_nn(gpairs_rest, keys)
        + dot_nn(key_head, kstate_hi)
        + dot_nn(key_head, kstate_lo)
        + dot_nn(key_head_rest, kstate_hi)
    )
    gkeys_ref[...] = dot_tn(gpairs, query) + dot_tn(gpairs_rest, query)
    gvalues_ref[...] = dot_tn(mixing_ref[...], mix_low)
    carry_ref[:, :width] = dot_tn(key_head, query) + dot_tn(key_head_rest, query)
    carry_ref[:, width:] = dot_tn((probs_low * head).astype(BF), mix_low)


def run_backward(grad, query, keys, values, pre, spans, state, gate, gain, probs, pairs, mixing, mix):
    tokens, slots = pre.shape
    width = keys.shape[1]
    wide = jax.ShapeDtypeStruct((tokens, width), F32)
    narrow = jax.ShapeDtypeStruct((tokens, slots), F32)
    return pl.pallas_call(
        backward_kernel,
        out_shape=(
            wide, wide, wide,
            jax.ShapeDtypeStruct((tokens, width), BF),
            jax.ShapeDtypeStruct((1, width), F32),
            narrow, narrow,
            jax.ShapeDtypeStruct((slots, 2 * width), F32),
        ),
        name="slot_backward",
    )(grad, query, keys, values, pre, spans, state, gate, gain, probs, pairs, mixing, mix)


def finish_kernel(
    gquery_ref, gkeys_ref, gvalues_ref, ggate_ref, gwrite_ref, glog_ref,
    keys_ref, values_ref, pre_ref, spans_ref, query_pre_ref, keys_pre_ref,
    state_ref, total_ref, ends_ref, gated_ref, out_ref,
):
    tokens, slots = pre_ref.shape
    depth = n_levels(tokens)
    width = keys_ref.shape[1]
    pre = pre_ref[...]
    decay = decay_write(pre)
    write = 1.0 - decay
    keys, values = keys_ref[...], values_ref[...]
    ends = ends_ref[...]
    ends_low = ends.astype(BF)
    tail = spans_ref[depth + 1]
    sent = (tail * write).astype(BF)
    column = tail * (dot_nt(keys, ends_low[:, :width]) + dot_nt(values, ends_low[:, width:]))
    glog = glog_ref[...] + dot_tn(span_matrix(depth + 1, tokens), (column * write).astype(BF))
    carried = lax.dot_general(
        jnp.ones((1, 2 * width), F32), ends * state_ref[...], (((1,), (1,)), ((), ())),
        precision=lax.Precision.HIGHEST, preferred_element_type=F32,
    )
    glog = glog + carried * total_ref[...]
    glog = glog - decay * (gwrite_ref[...] + column)
    u = query_pre_ref[...]
    s = sigmoid(u)
    out_ref[:, :width] = (gquery_ref[...] * (s * (1.0 + u * (1.0 - s)))).astype(BF)
    u = keys_pre_ref[...]
    s = sigmoid(u)
    gkeys = gkeys_ref[...] + dot_nn(sent, ends_low[:, :width])
    out_ref[:, width : 2 * width] = (gkeys * (s * (1.0 + u * (1.0 - s)))).astype(BF)
    out_ref[:, 2 * width : 3 * width] = (gvalues_ref[...] + dot_nn(sent, ends_low[:, width:])).astype(BF)
    out_ref[:, 3 * width : 4 * width] = ggate_ref[...]
    gforget = glog * sigmoid(-pre) / GATE_NORM
    room = 128 - slots
    out_ref[:, 4 * width + 128 :] = gated_ref[...]
    out_ref[:, 4 * width : 4 * width + 128] = jnp.concatenate(
        [gforget.astype(BF), jnp.zeros((tokens, room), BF)], axis=1
    )


def run_finish(gquery, gkeys, gvalues, ggate, gwrite, glog, keys, values, pre, spans, query_pre, keys_pre, state, total, ends, gated):
    tokens, slots = pre.shape
    width = keys.shape[1]
    return pl.pallas_call(
        finish_kernel,
        out_shape=jax.ShapeDtypeStruct((tokens, 5 * width + 128), BF),
        name="slot_finish",
    )(gquery, gkeys, gvalues, ggate, gwrite, glog, keys, values, pre, spans, query_pre, keys_pre, state, total, ends, gated)


MESH = pl.DeviceIdType.MESH
GROUPED = ("shard", "ctx")


def greet(axes_of_peers):
    barrier = pltpu.get_barrier_semaphore()
    for peer in axes_of_peers:
        pl.semaphore_signal(barrier, inc=1, device_id=peer, device_id_type=MESH)
    pl.semaphore_wait(barrier, len(axes_of_peers))


def tp_peers():
    count = lax.axis_size("tp")
    me = lax.axis_index("tp")
    return me, [lax.rem(me + k, count) for k in range(1, count)]


CHUNKS = 4
LATENCY = 2.2
LEAD = 10
CLOSING = 3


def tp_line(partial_ref, full_ref, arrived, staged, sums_ref, finish, send_a, recv_a, send_b, recv_b):
    count = lax.axis_size("tp")
    me = lax.axis_index("tp")
    rows = partial_ref.shape[1] // CHUNKS
    peers = [lax.rem(me + 1, count), lax.rem(me + count - 1, count)]

    def at_place(side, place):
        return place if side == 0 else count - 1 - place

    def cut(chunk):
        return pl.ds(chunk * rows, rows)

    def sum_copy(side, hop, chunk, source):
        return pltpu.make_async_remote_copy(
            src_ref=source,
            dst_ref=arrived.at[side, hop, chunk],
            send_sem=send_a.at[side, hop, chunk],
            recv_sem=recv_a.at[side, hop, chunk],
            device_id={"tp": peers[side]},
            device_id_type=MESH,
        )

    def row_copy(side, hop, chunk, block):
        return pltpu.make_async_remote_copy(
            src_ref=full_ref.at[block, cut(chunk)],
            dst_ref=full_ref.at[block, cut(chunk)],
            send_sem=send_b.at[side, hop, chunk],
            recv_sem=recv_b.at[side, hop, chunk],
            device_id={"tp": peers[side]},
            device_id_type=MESH,
        )

    def own(side, hop, chunk):
        return partial_ref.at[at_place(side, count - 1 - hop), cut(chunk)]

    def send_own(chunk):
        for side in range(2):

            @pl.when(me == at_place(side, 0))
            def _():
                for hop in range(count - 1):
                    sum_copy(side, hop, chunk, own(side, hop, chunk)).start()

    def add_hop(side, place, hop, chunk):
        @pl.when(me == at_place(side, place))
        def _():
            slot = staged.at[side, hop, chunk]
            copy = sum_copy(side, hop, chunk, slot)
            copy.wait_recv()
            slot[...] = (own(side, hop, chunk)[...].astype(F32) + arrived[side, hop, chunk].astype(F32)).astype(BF)
            copy.start()

    def close(chunk):
        sums_ref[...] = partial_ref[me, cut(chunk)].astype(F32)
        for side in range(2):
            place = me if side == 0 else count - 1 - me
            hop = jnp.minimum(count - 1 - place, count - 2)

            @pl.when(place > 0)
            def _():
                sum_copy(side, hop, chunk, staged.at[side, hop, chunk]).wait_recv()
                sums_ref[...] += arrived[side, hop, chunk].astype(F32)

        finish(chunk, sums_ref[...])
        for side in range(2):

            @pl.when(me != at_place(side, count - 1))
            def _():
                row_copy(side, 0, chunk, me).start()

    def forward(side, place, distance, chunk):
        @pl.when(me == at_place(side, place))
        def _():
            block = at_place(side, place - distance)
            row_copy(side, distance - 1, chunk, block).wait_recv()
            if place < count - 1:
                row_copy(side, distance, chunk, block).start()

    step = 1 + LATENCY
    events = []
    for chunk in range(CHUNKS):
        base = (count - 1) * chunk
        closed = base + (count - 1) + (count - 2) * LATENCY
        events.append((base - LEAD * (count - 1), functools.partial(send_own, chunk)))
        events.append((closed, functools.partial(close, chunk)))
        for side in range(2):
            for place in range(1, count):
                for hop in range(count - 1 - place):
                    due = base + hop + place * step
                    events.append((due, functools.partial(add_hop, side, place, hop, chunk)))
                for distance in range(1, place + 1):
                    due = closed + CLOSING + distance * step
                    if place == count - 1:
                        due += 1000
                    events.append((due, functools.partial(forward, side, place, distance, chunk)))
    for _, event in sorted(events, key=lambda event: event[0]):
        event()

    def drain():
        for side in range(2):
            for place in range(count - 1):

                @pl.when(me == at_place(side, place))
                def _():
                    for chunk in range(CHUNKS):
                        for hop in range(count - 1 - place):
                            sum_copy(side, hop, chunk, staged.at[side, hop, chunk]).wait_send()
                        for hop in range(place + 1):
                            row_copy(side, hop, chunk, at_place(side, place - hop)).wait_send()

    return drain


def plane_peers():
    shards, ctxs = lax.axis_size("shard"), lax.axis_size("ctx")
    devices = shards * ctxs
    me = lax.axis_index("shard") * ctxs + lax.axis_index("ctx")
    peers = [lax.rem(me + k, devices) for k in range(1, devices)]
    places = [{"shard": lax.div(peer, ctxs), "ctx": lax.rem(peer, ctxs)} for peer in peers]
    return me, peers, places


def start_scatter(sources, targets, send_sems, recv_sems):
    me, peers, places = plane_peers()
    copies = []
    for i, (source, target) in enumerate(zip(sources, targets)):
        step = target.shape[2]

        def block(at):
            if len(source.shape) == 3:
                return source.at[at]
            return source.at[:, pl.ds(pl.multiple_of(at * step, step), step)]

        for k, (peer, place) in enumerate(zip(peers, places)):
            copy = pltpu.make_async_remote_copy(
                src_ref=block(peer),
                dst_ref=target.at[me],
                send_sem=send_sems.at[i, k],
                recv_sem=recv_sems.at[i, k],
                device_id=place,
                device_id_type=MESH,
            )
            copy.start()
            copies.append(copy)
    for source, target in zip(sources, targets):
        target[me] = block_of(source, me, target.shape[2])
    return copies


def block_of(source, at, step):
    if len(source.shape) == 3:
        return source[at]
    return source[:, pl.ds(pl.multiple_of(at * step, step), step)]


def spread_kernel(n_parts, n_packed, *refs):
    parts, refs = refs[:n_parts], refs[n_parts:]
    packed, refs = refs[:n_packed], refs[n_packed:]
    if n_packed:
        row_ref, out_ref, rows_ref, pack_ref, slab, part_sems, own_sem, send_sems, recv_sems = refs[:9]
        row_send, row_recv, pack_slab, pack_sems, pack_sem = refs[9:]
    else:
        out_ref, slab, part_sems, own_sem, send_sems, recv_sems = refs
    shard, core = lax.axis_index("shard"), lax.axis_index("ctx")
    me, _, places = plane_peers()
    across = shard + 1 - 2 * lax.rem(shard, 2)
    along = lax.rem(shard + 2, 4)
    corner = lax.rem(across + 2, 4)
    other = 1 - core
    to_x, to_y, to_core = {"shard": across}, {"shard": along}, {"ctx": other}
    rows = slab.shape[0]
    half = rows // 2

    def load_all(sources, target, sems):
        loads = []
        start = 0
        for i, part in enumerate(sources):
            load = pltpu.make_async_copy(part, target.at[:, pl.ds(start, part.shape[1])], sems.at[i])
            load.start()
            loads.append(load)
            start += part.shape[1]
        return loads

    loads = load_all(parts, slab, part_sems)
    greet(places)
    for load in loads:
        load.wait()
    keep = pltpu.make_async_copy(slab, out_ref.at[pl.ds(pl.multiple_of(me * rows, rows), rows)], own_sem)
    keep.start()

    def landing(block, part):
        return out_ref.at[pl.ds(pl.multiple_of(block * rows + part * half, half), half)]

    started = []

    def send(kind, source, block, part, place):
        copy = pltpu.make_async_remote_copy(
            src_ref=source,
            dst_ref=landing(block, part),
            send_sem=send_sems.at[kind],
            recv_sem=recv_sems.at[kind],
            device_id=place,
            device_id_type=MESH,
        )
        copy.start()
        started.append(copy)

    def receive(kind, block, part, place):
        region = landing(block, part)
        pltpu.make_async_remote_copy(
            src_ref=region,
            dst_ref=region,
            send_sem=send_sems.at[kind],
            recv_sem=recv_sems.at[kind],
            device_id=place,
            device_id_type=MESH,
        ).wait_recv()

    def own(part):
        return slab.at[pl.ds(part * half, half)]

    def block(place, at_core):
        return 2 * place + at_core

    send(0, own(0), me, 0, to_x)
    send(1, own(1), me, 1, to_y)
    if n_packed:
        copies = start_sums(row_ref, rows_ref, row_send, row_recv, [], places, me)
    send(2, own(1), me, 1, to_x)
    send(3, own(0), me, 0, to_y)
    send(4, own(0), me, 0, to_core)
    send(5, own(1), me, 1, to_core)
    if n_packed:
        for load in load_all(packed, pack_slab, pack_sems):
            load.wait()
        store = pltpu.make_async_copy(pack_slab, pack_ref, pack_sem)
        store.start()
    x_block, y_block, far_block = block(across, core), block(along, core), block(corner, core)
    receive(0, x_block, 0, to_x)
    send(6, landing(x_block, 0), x_block, 0, to_y)
    send(8, landing(x_block, 0), x_block, 0, to_core)
    receive(1, y_block, 1, to_y)
    send(7, landing(y_block, 1), y_block, 1, to_x)
    send(9, landing(y_block, 1), y_block, 1, to_core)
    receive(2, x_block, 1, to_x)
    send(10, landing(x_block, 1), x_block, 1, to_core)
    receive(3, y_block, 0, to_y)
    send(11, landing(y_block, 0), y_block, 0, to_core)
    receive(6, far_block, 0, to_y)
    send(12, landing(far_block, 0), far_block, 0, to_core)
    receive(7, far_block, 1, to_x)
    send(13, landing(far_block, 1), far_block, 1, to_core)
    for kind, place, part in (
        (4, shard, 0), (5, shard, 1), (8, across, 0), (9, along, 1), (10, across, 1), (11, along, 0),
        (12, corner, 0), (13, corner, 1),
    ):
        receive(kind, block(place, other), part, to_core)
    for copy in started:
        copy.wait_send()
    keep.wait()
    if n_packed:
        store.wait()
        for copy in copies:
            copy.wait()


def run_spread(name, collective_id, parts, packed=(), row=None):
    devices = lax.axis_size(GROUPED)
    rows = parts[0].shape[0]
    columns = sum(part.shape[1] for part in parts)
    anywhere = pl.BlockSpec(memory_space=pl.ANY)
    in_specs, out_specs = [anywhere] * len(parts), [anywhere]
    out_shape = [jax.ShapeDtypeStruct((devices * rows, columns), BF)]
    scratch = [
        pltpu.VMEM((rows, columns), BF),
        pltpu.SemaphoreType.DMA((len(parts),)),
        pltpu.SemaphoreType.DMA,
        *[pltpu.SemaphoreType.DMA((14,))] * 2,
    ]
    args = list(parts)
    if packed:
        packed_shape = (rows, sum(part.shape[1] for part in packed))
        args += [*packed, row]
        in_specs += [*[anywhere] * len(packed), pl.BlockSpec(memory_space=pltpu.VMEM)]
        out_specs += [pl.BlockSpec(memory_space=pltpu.VMEM), anywhere]
        out_shape += [jax.ShapeDtypeStruct((devices, *row.shape), BF), jax.ShapeDtypeStruct(packed_shape, BF)]
        scratch += [
            *[pltpu.SemaphoreType.DMA((devices - 1,))] * 2,
            pltpu.VMEM(packed_shape, BF),
            pltpu.SemaphoreType.DMA((len(packed),)),
            pltpu.SemaphoreType.DMA,
        ]
    return pl.pallas_call(
        functools.partial(spread_kernel, len(parts), len(packed)),
        out_shape=tuple(out_shape),
        in_specs=in_specs,
        out_specs=tuple(out_specs),
        scratch_shapes=scratch,
        compiler_params=pltpu.CompilerParams(collective_id=collective_id, has_side_effects=True),
        name=name,
    )(*args)


def start_sums(row_ref, landed, send_sems, recv_sems, peers, places, me):
    copies = []
    landed[me] = row_ref[...]
    for k, place in enumerate(places):
        copy = pltpu.make_async_remote_copy(
            src_ref=row_ref,
            dst_ref=landed.at[me],
            send_sem=send_sems.at[k],
            recv_sem=recv_sems.at[k],
            device_id=place,
            device_id_type=MESH,
        )
        copy.start()
        copies.append(copy)
    return copies


def summed(landed):
    total = landed[0]
    for k in range(1, landed.shape[0]):
        total = total + landed[k]
    return total


def exchange_kernel(epilogue, n_in, n_rows, n_moved, n_sums, partial_ref, *refs):
    me, peers = tp_peers()
    inputs, refs = refs[:n_in], refs[n_in:]
    sources, refs = refs[:n_moved], refs[n_moved:]
    full_ref, refs = refs[0], refs[1:]
    outputs, refs = refs[:n_rows], refs[n_rows:]
    targets, refs = refs[:n_moved], refs[n_moved:]
    sums, refs = refs[: 2 * n_sums], refs[2 * n_sums :]
    arrived, staged, sums_ref, send_a, recv_a, send_b, recv_b, send_m, recv_m = refs[:9]
    own, plane, places = plane_peers()
    across = [{"tp": peer} for peer in peers]
    greet(across + (places if n_moved or n_sums else []))
    moves = start_scatter(sources, targets, send_m, recv_m)
    rows = full_ref.shape[1] // CHUNKS
    started = []

    def finish(chunk, total):
        part = pl.ds(chunk * rows, rows)
        full_ref[me, part] = epilogue(total, me, part, chunk == 0, inputs, outputs)
        if n_sums and chunk == CHUNKS - 1:
            row_ref, in_plane, _, _, send_p, recv_p = refs[9:15]
            width = outputs[0].shape[1]
            row_ref[:, :width] = outputs[0][...]
            row_ref[:, width:] = inputs[-1][...]
            started.extend(start_sums(row_ref, in_plane, send_p, recv_p, plane, places, own))

    drain = tp_line(partial_ref, full_ref, arrived, staged, sums_ref, finish, send_a, recv_a, send_b, recv_b)
    if n_sums:
        row_ref, in_plane, plane_row, in_tp, send_p, recv_p, send_t, recv_t = refs[9:]
        for copy in started:
            copy.wait()
        plane_row[...] = summed(in_plane)
        sums[0][...] = plane_row[...]
        for copy in start_sums(plane_row, in_tp, send_t, recv_t, peers, across, me):
            copy.wait()
        sums[1][...] = summed(in_tp)
    drain()
    for copy in moves:
        copy.wait()


def run_exchange(epilogue, name, collective_id, partial, inputs, row_outputs, moved=(), summing=False):
    tp = lax.axis_size("tp")
    devices = lax.axis_size(GROUPED)
    tokens, columns = partial.shape
    share = tokens // tp
    partial = partial.reshape(tp, share, columns)
    step = columns // devices
    if step % 128:
        moved = [m.reshape(tokens, devices, step).transpose(1, 0, 2) for m in moved]
    count = len(moved)
    scratch = [
        *[pltpu.VMEM((2, tp - 1, CHUNKS, share // CHUNKS, columns), BF)] * 2,
        pltpu.VMEM((share // CHUNKS, columns), F32),
        *[pltpu.SemaphoreType.DMA((2, tp - 1, CHUNKS))] * 4,
        *[pltpu.SemaphoreType.DMA((max(count, 1), devices - 1))] * 2,
    ]
    extra = ()
    if summing:
        row = row_outputs[0].shape[1] + inputs[-1].shape[1]
        extra = (jax.ShapeDtypeStruct((1, row), F32),) * 2
        scratch += [
            pltpu.VMEM((1, row), F32),
            pltpu.VMEM((devices, 1, row), F32),
            pltpu.VMEM((1, row), F32),
            pltpu.VMEM((tp, 1, row), F32),
            *[pltpu.SemaphoreType.DMA((devices - 1,))] * 2,
            *[pltpu.SemaphoreType.DMA((tp - 1,))] * 2,
        ]
    out_shape = (
        jax.ShapeDtypeStruct((tp, share, columns), BF),
        *row_outputs,
        *[jax.ShapeDtypeStruct((devices, tokens, step), BF)] * count,
        *extra,
    )
    outs = pl.pallas_call(
        functools.partial(exchange_kernel, epilogue, len(inputs), len(row_outputs), count, int(summing)),
        out_shape=out_shape,
        in_specs=[pl.BlockSpec(memory_space=pltpu.VMEM)] * (1 + len(inputs) + count),
        out_specs=tuple([pl.BlockSpec(memory_space=pltpu.VMEM)] * len(out_shape)),
        scratch_shapes=scratch,
        compiler_params=pltpu.CompilerParams(collective_id=collective_id, has_side_effects=True),
        name=name,
    )(partial, *inputs, *moved)
    start = 1 + len(row_outputs)
    return (
        outs[0].reshape(tokens, columns),
        *outs[1:start],
        *[o.reshape(devices * tokens, step) for o in outs[start : start + count]],
        *outs[start + count :],
    )


def middle_epilogue(total, me, part, first, inputs, outputs):
    hidden_ref, gain_ref = inputs
    (branch_ref,) = outputs
    branch_ref[part, :] = total
    middle = hidden_ref[me, part].astype(F32) + total
    scale = lax.rsqrt(jnp.mean(middle * middle, axis=1, keepdims=True) + EPSILON)
    return (middle * scale * gain_ref[...]).astype(BF)


def result_epilogue(total, me, part, first, inputs, outputs):
    hidden_ref, branch_ref, teacher_out_ref, teacher_mix_ref, cotangent_ref, mask_ref, scale_ref = inputs
    grad_ref, losses_ref = outputs
    branch = branch_ref[part, :]
    result = hidden_ref[me, part].astype(F32) + branch + total
    mask = mask_ref[me, part]
    gap = result - teacher_out_ref[me, part].astype(F32)
    gap_mix = branch - teacher_mix_ref[me, part].astype(F32)
    loss_out = jnp.sum(mask * (gap * gap), keepdims=True)
    loss_mix = jnp.sum(mask * (gap_mix * gap_mix), keepdims=True)
    lane = lax.broadcasted_iota(jnp.int32, (1, 128), 1)
    losses = jnp.where(lane == 0, loss_out, 0.0) + jnp.where(lane == 1, loss_mix, 0.0)
    losses_ref[...] = losses if first else losses_ref[...] + losses
    grad_ref[part, :] = cotangent_ref[me, part].astype(F32) + scale_ref[...] * mask * gap
    return result.astype(BF)


def norm_back(grad, rows, gain):
    scale = lax.rsqrt(jnp.mean(rows * rows, axis=1, keepdims=True) + EPSILON)
    unit = rows * scale
    gain_grad = jnp.sum(grad * unit, axis=0, keepdims=True)
    inner = grad * gain
    return scale * (inner - unit * jnp.mean(unit * inner, axis=1, keepdims=True)), gain_grad


def branch_epilogue(total, me, part, first, inputs, outputs):
    hidden_ref, branch_ref, teacher_mix_ref, grad_ref, mask_ref, scale_ref, gain_ref = inputs
    grad_middle_ref, gain_grad_ref = outputs
    branch = branch_ref[part, :]
    back, gain_grad = norm_back(total, hidden_ref[me, part].astype(F32) + branch, gain_ref[...])
    gain_grad_ref[...] = gain_grad if first else gain_grad_ref[...] + gain_grad
    grad_middle = back + grad_ref[part, :]
    grad_middle_ref[part, :] = grad_middle
    gap_mix = branch - teacher_mix_ref[me, part].astype(F32)
    return (grad_middle + scale_ref[...] * mask_ref[me, part] * gap_mix).astype(BF)


def input_epilogue(total, me, part, first, inputs, outputs):
    hidden_ref, grad_middle_ref, gain_ref = inputs[:3]
    (gain_grad_ref,) = outputs
    back, gain_grad = norm_back(total, hidden_ref[me, part].astype(F32), gain_ref[...])
    gain_grad_ref[...] = gain_grad if first else gain_grad_ref[...] + gain_grad
    return (back + grad_middle_ref[part, :]).astype(BF)


def passed_along(value, axis, steps):
    count = lax.axis_size(axis)
    leading, last = (max(0, -steps), min(count, count - steps))
    return lax.ppermute(value, axis, [(source, source + steps) for source in range(leading, last)])


def relay(value, decay, axis, steps):
    carried = passed_along(value, axis, steps)
    for _ in range(lax.axis_size(axis) - 2):
        carried = passed_along(value + decay * carried, axis, steps)
    return carried


def gathered(value):
    return lax.all_gather(value, GROUPED, axis=0, tiled=True)


def per_device(
    hidden_in,
    cotangent,
    teacher_out,
    teacher_mix,
    valid_mask,
    doc_start,
    attn_gain,
    w_query,
    w_key,
    w_value,
    w_forget,
    forget_bias,
    head_gain,
    w_outgate,
    w_out,
    mlp_gain,
    w_gate,
    w_up,
    w_down,
):
    tokens, features = hidden_in.shape
    devices = lax.axis_size(GROUPED)
    tp = lax.axis_size("tp")
    share = tokens // tp
    rows = w_query.shape[0]
    width = w_query.shape[1]
    slots = w_forget.shape[1]
    units = w_gate.shape[1]
    tokens_all = tokens * devices
    mask_flat = valid_mask.astype(F32)

    count_own = jnp.sum(mask_flat).astype(BF).reshape(1)
    small = [attn_gain, mlp_gain, forget_bias.reshape(-1), head_gain.reshape(-1), count_own]
    row = jnp.concatenate(small)
    row = jnp.pad(row, (0, -row.shape[0] % 2048)).reshape(-1, 128)
    forget_w = jnp.pad(w_forget, ((0, 0), (0, 128 - slots)))
    attn_parts = [w_query, w_key, w_value, w_outgate, forget_w]
    mlp_parts = [w_gate, w_up, w_down]
    if (lax.axis_size("shard"), lax.axis_size("ctx")) == (4, 2):
        first, row_all, pack = run_spread("gather_attention", 5, attn_parts, mlp_parts, row)
        second = gathered(pack)
        out_own, first = lax.optimization_barrier((w_out, first))
        (out_w,) = run_spread("gather_out", 6, [out_own])
        first, row_all, out_w = lax.optimization_barrier((first, row_all, out_w))
    else:
        row_all = gathered(row)
        first = gathered(jnp.concatenate([*attn_parts, w_out], axis=1))
        pack, first = lax.optimization_barrier((jnp.concatenate(mlp_parts, axis=1), first))
        second = gathered(pack)
        out_w = first[:, 4 * width + 128 :]
        first = first[:, : 4 * width + 128]

    spare = row_all.reshape(devices, -1).astype(F32)
    attn_scale = spare[:, :rows].reshape(1, -1)
    mlp_scale = spare[:, rows : 2 * rows].reshape(1, -1)
    place = 2 * rows
    bias = spare[:, place : place + slots // devices].reshape(1, slots)
    place += slots // devices
    head_scale = spare[:, place : place + width // devices].reshape(1, width)
    place += width // devices
    count_total = jnp.sum(spare[:, place])
    loss_scale = (tokens_all / count_total).reshape(1, 1)

    hidden_f = hidden_in.astype(F32)
    scale = lax.rsqrt(jnp.mean(hidden_f * hidden_f, axis=-1, keepdims=True) + EPSILON)
    normed_in = (hidden_f * scale * attn_scale).astype(BF)
    pre_all = dot_nn(normed_in, first)
    query_pre = pre_all[:, :width]
    keys_pre = pre_all[:, width : 2 * width]
    query = jax.nn.silu(query_pre).astype(BF)
    keys = jax.nn.silu(keys_pre).astype(BF)
    values = pre_all[:, 2 * width : 3 * width].astype(BF)
    gate_pre = pre_all[:, 3 * width : 4 * width]
    forget_pre = pre_all[:, 4 * width : 4 * width + slots] + bias
    resets = doc_start.astype(F32)[:, None]

    spans, total, ends = run_ends(forget_pre, resets, keys, values)
    decay = total.reshape(slots, 1)
    state = relay(ends, decay, "ctx", 1)
    probs, pairs, mixing, mix, gated = run_forward(
        query, keys, values, forget_pre, spans, state, gate_pre, head_scale
    )
    gate_w = second[:, :units]
    up_w = second[:, units : 2 * units]
    down_w = second[:, 2 * units :]

    by_share = lambda tensor: tensor.reshape(tp, share, -1)
    hidden_s, teacher_out_s, teacher_mix_s, cotangent_s = map(by_share, (hidden_in, teacher_out, teacher_mix, cotangent))
    mask_s = by_share(mask_flat)
    narrow = lambda *shape: jax.ShapeDtypeStruct(shape, F32)

    normed_mid, branch = run_exchange(
        middle_epilogue, "sum_branch", 1, dot_nt(gated, out_w).astype(BF), (hidden_s, mlp_scale),
        (narrow(share, features),),
    )
    gate_val = dot_nn(normed_mid, gate_w)
    up_val = dot_nn(normed_mid, up_w)
    hidden_units = (jax.nn.silu(gate_val) * up_val).astype(BF)
    units_all = gathered(hidden_units)
    output, grad_result, losses, normed_in_c, normed_mid_c = run_exchange(
        result_epilogue, "sum_result", 2, dot_nt(hidden_units, down_w).astype(BF),
        (hidden_s, branch, teacher_out_s, teacher_mix_s, cotangent_s, mask_s, loss_scale),
        (narrow(share, features), narrow(1, 128)),
        moved=(normed_in, normed_mid),
    )
    gap = output.astype(F32) - teacher_out.astype(F32)
    grad_mlp = (cotangent.astype(F32) + loss_scale * mask_flat[:, None] * gap).astype(BF)
    grad_units = dot_nn(grad_mlp, down_w)
    gate_sig = jax.nn.sigmoid(gate_val)
    grad_gate_val = (grad_units * up_val * (gate_sig * (1.0 + gate_val * (1.0 - gate_sig)))).astype(BF)
    grad_up_val = (grad_units * (gate_val * gate_sig)).astype(BF)
    grad_both = jnp.concatenate([grad_gate_val, grad_up_val], axis=1)
    partial = dot_nt(grad_both, second[:, : 2 * units]).astype(BF)
    units_all, grad_both = lax.optimization_barrier((units_all, grad_both))
    partial = lax.optimization_barrier((partial, grad_both))[0]
    mlp_all = gathered(grad_both)
    grad_branch, grad_middle, mlp_gain_part, grad_mlp_c = run_exchange(
        branch_epilogue, "sum_middle", 3, partial,
        (hidden_s, branch, teacher_mix_s, grad_result, mask_s, loss_scale, mlp_scale),
        (narrow(share, features), narrow(1, features)),
        moved=(grad_mlp,),
    )
    grad_gated = dot_nn(grad_branch, out_w)
    gquery, gkeys, gvalues, ggate, head_gain_part, gwrite, glog, carry = run_backward(
        grad_gated, query, keys, values, forget_pre, spans, state, gate_pre, head_scale, probs, pairs, mixing, mix
    )
    later = relay(carry, decay, "ctx", -1)
    grad_pre = run_finish(
        gquery, gkeys, gvalues, ggate, gwrite, glog, keys, values, forget_pre, spans, query_pre, keys_pre,
        state, total, later, gated,
    )
    partial = dot_nt(grad_pre[:, : 4 * width + 128], first).astype(BF)
    mlp_all, grad_pre = lax.optimization_barrier((mlp_all, grad_pre))
    partial = lax.optimization_barrier((partial, grad_pre))[0]
    attn_all = gathered(grad_pre)
    grad_in, _, grad_branch_c, plane_sums, all_sums = run_exchange(
        input_epilogue, "sum_input", 4, partial,
        (hidden_s, grad_middle, attn_scale, jnp.concatenate([mlp_gain_part, head_gain_part, losses], axis=1)),
        (narrow(1, features),), moved=(grad_branch,), summing=True,
    )
    gate_grad = dot_tn(normed_mid_c, mlp_all[:, :units])
    up_grad = dot_tn(normed_mid_c, mlp_all[:, units:])
    out_grad = dot_tn(grad_branch_c, attn_all[:, 4 * width + 128 :])
    down_grad = dot_tn(grad_mlp_c, units_all)
    query_grad = dot_tn(normed_in_c, attn_all[:, :width])
    keys_grad = dot_tn(normed_in_c, attn_all[:, width : 2 * width])
    values_grad = dot_tn(normed_in_c, attn_all[:, 2 * width : 3 * width])
    outgate_grad = dot_tn(normed_in_c, attn_all[:, 3 * width : 4 * width])
    forget_all = attn_all[:, 4 * width : 4 * width + slots]
    forget_grad = dot_tn(normed_in_c, forget_all)
    index = lax.axis_index(GROUPED)
    bias_grad = jnp.sum(forget_all.astype(F32), axis=0, keepdims=True)
    bias_grad = lax.dynamic_slice_in_dim(bias_grad, index * (slots // devices), slots // devices, axis=1)

    cut = lambda row, size: lax.dynamic_slice_in_dim(row, index * size, size, axis=1)
    attn_gain_grad = cut(all_sums[:, :features], features // devices).reshape(-1)
    mlp_gain_grad = cut(all_sums[:, features : 2 * features], features // devices).reshape(-1)
    head_gain_grad = cut(plane_sums[:, 2 * features : 2 * features + width], width // devices)
    sums = all_sums[0, 2 * features + width :]
    loss_out = sums[0] / (2.0 * features * count_total)
    loss_mix = sums[1] / (2.0 * features * count_total)
    return (
        output,
        loss_out,
        loss_mix,
        grad_in.astype(F32),
        attn_gain_grad,
        query_grad,
        keys_grad,
        values_grad,
        forget_grad,
        bias_grad,
        head_gain_grad,
        outgate_grad,
        out_grad,
        mlp_gain_grad,
        gate_grad,
        up_grad,
        down_grad,
    )


def solution(mesh):
    return jax.shard_map(
        per_device,
        mesh=mesh,
        in_specs=(
            P(("shard", "ctx"), None),
            P(("shard", "ctx"), None),
            P(("shard", "ctx"), None),
            P(("shard", "ctx"), None),
            P(("shard", "ctx")),
            P(("shard", "ctx")),
            P(("shard", "ctx")),
            P(("shard", "ctx"), "tp"),
            P(("shard", "ctx"), "tp"),
            P(("shard", "ctx"), "tp"),
            P(("shard", "ctx"), "tp"),
            P("tp", ("shard", "ctx")),
            P("tp", ("shard", "ctx")),
            P(("shard", "ctx"), "tp"),
            P(("shard", "ctx"), "tp"),
            P(("shard", "ctx")),
            P(("shard", "ctx"), "tp"),
            P(("shard", "ctx"), "tp"),
            P(("shard", "ctx"), "tp"),
        ),
        out_specs=(
            P(("shard", "ctx"), None),
            P(),
            P(),
            P(("shard", "ctx"), None),
            P(("shard", "ctx")),
            P(("shard", "ctx"), "tp"),
            P(("shard", "ctx"), "tp"),
            P(("shard", "ctx"), "tp"),
            P(("shard", "ctx"), "tp"),
            P("tp", ("shard", "ctx")),
            P("tp", ("shard", "ctx")),
            P(("shard", "ctx"), "tp"),
            P(("shard", "ctx"), "tp"),
            P(("shard", "ctx")),
            P(("shard", "ctx"), "tp"),
            P(("shard", "ctx"), "tp"),
            P(("shard", "ctx"), "tp"),
        ),
        check_vma=False,
    )
```

```python
import functools

import jax
import jax.numpy as jnp
from jax import lax
from jax.experimental import pallas as pl
from jax.experimental.pallas import tpu as pltpu
from jax.sharding import PartitionSpec as P

F32 = jnp.float32
BF = jnp.bfloat16
EPSILON = 1e-06
GATE_NORM = 8.0


def dot_nn(a, b):
    return lax.dot_general(a, b, (((1,), (0,)), ((), ())), preferred_element_type=F32)


def dot_nt(a, b):
    return lax.dot_general(a, b, (((1,), (1,)), ((), ())), preferred_element_type=F32)


def dot_tn(a, b):
    return lax.dot_general(a, b, (((0,), (0,)), ((), ())), preferred_element_type=F32)


def halves(x):
    hi = x.astype(BF)
    return hi, (x - hi.astype(F32)).astype(BF)


def sigmoid(u):
    return 1.0 / (1.0 + jnp.exp(-u))


def n_levels(tokens):
    return tokens.bit_length() - 1


def span_matrix(level, tokens):
    t = lax.broadcasted_iota(jnp.int32, (tokens, tokens), 0)
    u = lax.broadcasted_iota(jnp.int32, (tokens, tokens), 1)
    depth = n_levels(tokens)
    if level == depth:
        keep = u <= t
    elif level == depth + 1:
        keep = u > t
    else:
        half = 1 << level
        edge = (t & ~(2 * half - 1)) + half
        odd = (t & half) > 0
        keep = (odd & (u >= edge) & (u <= t)) | (~odd & (u > t) & (u < edge))
    return keep.astype(F32).astype(BF)


def odd_rows(level, tokens, columns):
    t = lax.broadcasted_iota(jnp.int32, (tokens, columns), 0)
    return (t & (1 << level)) > 0


def same_pair(level, tokens):
    t = lax.broadcasted_iota(jnp.int32, (tokens, tokens), 0)
    u = lax.broadcasted_iota(jnp.int32, (tokens, tokens), 1)
    return (t >> (level + 1)) == (u >> (level + 1))


def ends_kernel(pre_ref, resets_ref, keys_ref, values_ref, spans_ref, total_ref, ends_ref):
    tokens, slots = pre_ref.shape
    depth = n_levels(tokens)
    width = keys_ref.shape[1]
    pre = pre_ref[...]
    log_decay = (jnp.minimum(pre, 0.0) - jnp.log1p(jnp.exp(-jnp.abs(pre)))) / GATE_NORM
    write = 1.0 - jnp.exp(log_decay)
    hi, lo = halves(log_decay)
    resets = jnp.broadcast_to(resets_ref[...], (tokens, slots)).astype(BF)
    stacked = jnp.concatenate([hi, lo, resets], axis=1)
    for level in range(depth + 2):
        sums = dot_nn(span_matrix(level, tokens), stacked)
        gap = sums[:, :slots] + sums[:, slots : 2 * slots]
        live = sums[:, 2 * slots :] < 0.5
        span = jnp.where(live, jnp.exp(gap), 0.0)
        spans_ref[level] = span
        if level == depth:
            total_ref[...] = span[tokens - 1 :, :]
        if level == depth + 1:
            hi, lo = halves(span * write)
            ends_ref[:, :width] = dot_tn(hi, keys_ref[...]) + dot_tn(lo, keys_ref[...])
            ends_ref[:, width:] = dot_tn(hi, values_ref[...]) + dot_tn(lo, values_ref[...])


def run_ends(pre, resets, keys, values):
    tokens, slots = pre.shape
    depth = n_levels(tokens)
    return pl.pallas_call(
        ends_kernel,
        out_shape=(
            jax.ShapeDtypeStruct((depth + 2, tokens, slots), F32),
            jax.ShapeDtypeStruct((1, slots), F32),
            jax.ShapeDtypeStruct((slots, keys.shape[1] + values.shape[1]), F32),
        ),
        name="slot_ends",
    )(pre, resets, keys, values)


def decay_write(pre):
    log_decay = (jnp.minimum(pre, 0.0) - jnp.log1p(jnp.exp(-jnp.abs(pre)))) / GATE_NORM
    return jnp.exp(log_decay)


def forward_kernel(
    query_ref, keys_ref, values_ref, pre_ref, spans_ref, state_ref, gate_ref, gain_ref,
    probs_ref, pairs_ref, mixing_ref, mix_ref, gated_ref,
):
    tokens, slots = pre_ref.shape
    depth = n_levels(tokens)
    width = keys_ref.shape[1]
    scaling = width ** (-0.5)
    write = 1.0 - decay_write(pre_ref[...])
    query = query_ref[...]
    pairs = dot_nt(query, keys_ref[...])
    pairs_ref[...] = pairs
    t = lax.broadcasted_iota(jnp.int32, (tokens, tokens), 0)
    u = lax.broadcasted_iota(jnp.int32, (tokens, tokens), 1)
    diagonal = jnp.sum(jnp.where(t == u, pairs, 0.0), axis=1, keepdims=True)
    state_hi, state_lo = halves(state_ref[:, :width])
    head = spans_ref[depth]
    raw = head * (dot_nt(query, state_hi) + dot_nt(query, state_lo)) + diagonal * write
    for level in range(depth):
        span = spans_ref[level]
        odd = odd_rows(level, tokens, slots)
        left, left_lo = halves(jnp.where(same_pair(level, tokens), pairs, 0.0))
        right, right_lo = halves(jnp.where(odd, 0.0, span * write))
        pulled = dot_nn(left, right) + dot_nn(left_lo, right) + dot_nn(left, right_lo)
        raw = raw + jnp.where(odd, span, 0.0) * pulled
    scores = scaling * raw
    scores = scores - jnp.max(scores, axis=1, keepdims=True)
    raised = jnp.exp(scores)
    probs = raised / jnp.sum(raised, axis=1, keepdims=True)
    probs_ref[...] = probs
    probs = probs.astype(BF).astype(F32)
    mixing = jnp.zeros((tokens, tokens), F32)
    for level in reversed(range(depth)):
        span = spans_ref[level]
        odd = odd_rows(level, tokens, slots)
        left, left_lo = halves(jnp.where(odd, span * probs, 0.0))
        right, right_lo = halves(jnp.where(odd, 0.0, span * write))
        pushed = dot_nt(left, right) + dot_nt(left_lo, right) + dot_nt(left, right_lo)
        mixing = jnp.where(same_pair(level, tokens), pushed, mixing)
    mixing = jnp.where(t == u, jnp.sum(probs * write, axis=1, keepdims=True), mixing)
    mixing, mixing_lo = halves(mixing)
    mixing_ref[...] = mixing
    state_hi, state_lo = halves(state_ref[:, width:])
    carried, carried_lo = halves(probs * head)
    mix = dot_nn(mixing, values_ref[...]) + dot_nn(mixing_lo, values_ref[...])
    mix = mix + dot_nn(carried, state_hi) + dot_nn(carried, state_lo) + dot_nn(carried_lo, state_hi)
    mix_ref[...] = mix
    scale = lax.rsqrt(jnp.mean(mix * mix, axis=1, keepdims=True) + EPSILON)
    gate = gate_ref[...]
    gated_ref[...] = (mix * scale * gain_ref[...] * (gate * sigmoid(gate))).astype(BF)


def run_forward(query, keys, values, pre, spans, state, gate, gain):
    tokens, slots = pre.shape
    width = keys.shape[1]
    return pl.pallas_call(
        forward_kernel,
        out_shape=(
            jax.ShapeDtypeStruct((tokens, slots), F32),
            jax.ShapeDtypeStruct((tokens, tokens), F32),
            jax.ShapeDtypeStruct((tokens, tokens), BF),
            jax.ShapeDtypeStruct((tokens, width), F32),
            jax.ShapeDtypeStruct((tokens, width), BF),
        ),
        name="slot_forward",
    )(query, keys, values, pre, spans, state, gate, gain)


def backward_kernel(
    grad_ref, query_ref, keys_ref, values_ref, pre_ref, spans_ref, state_ref, gate_ref, gain_ref,
    probs_ref, pairs_ref, mixing_ref, mix_ref,
    gquery_ref, gkeys_ref, gvalues_ref, ggate_ref, ggain_ref, gwrite_ref, glog_ref, carry_ref,
):
    tokens, slots = pre_ref.shape
    depth = n_levels(tokens)
    width = keys_ref.shape[1]
    scaling = width ** (-0.5)
    gate = gate_ref[...]
    sig = sigmoid(gate)
    silu = gate * sig
    gain = gain_ref[...]
    mix = mix_ref[...]
    scale = lax.rsqrt(jnp.mean(mix * mix, axis=1, keepdims=True) + EPSILON)
    normed = mix * scale
    grad = grad_ref[...]
    ggate_ref[...] = (grad * gain * normed * (sig * (1.0 + gate * (1.0 - sig)))).astype(BF)
    ggain_ref[...] = jnp.sum(grad * normed * silu, axis=0, keepdims=True)
    inner = grad * gain * silu
    mix_grad = scale * (inner - normed * jnp.mean(normed * inner, axis=1, keepdims=True))
    mix_low = mix_grad.astype(BF)

    write = 1.0 - decay_write(pre_ref[...])
    query, keys, values = query_ref[...], keys_ref[...], values_ref[...]
    pairs = pairs_ref[...]
    pairs_t = dot_nt(keys, query)
    mix_rest = (mix_grad - mix_low.astype(F32)).astype(BF)
    weigh = dot_nt(mix_low, values) + dot_nt(mix_rest, values)
    weigh_t = dot_nt(values, mix_low) + dot_nt(values, mix_rest)
    t = lax.broadcasted_iota(jnp.int32, (tokens, tokens), 0)
    u = lax.broadcasted_iota(jnp.int32, (tokens, tokens), 1)
    pair_diag = jnp.sum(jnp.where(t == u, pairs, 0.0), axis=1, keepdims=True)
    weigh_diag = jnp.sum(jnp.where(t == u, weigh, 0.0), axis=1, keepdims=True)
    head = spans_ref[depth]
    probs = probs_ref[...]
    probs_low = probs.astype(BF).astype(F32)

    vstate_hi, vstate_lo = halves(state_ref[:, width:])
    head_probs = head * (
        dot_nt(mix_low, vstate_hi) + dot_nt(mix_low, vstate_lo) + dot_nt(mix_rest, vstate_hi)
    )
    probs_grad = head_probs + weigh_diag * write
    row_values, row_keys = [], []
    for level in range(depth):
        span = spans_ref[level]
        odd = odd_rows(level, tokens, slots)
        same = same_pair(level, tokens)
        right, right_lo = halves(jnp.where(odd, 0.0, span * write))
        reach = jnp.where(odd, span, 0.0)
        left, left_lo = halves(jnp.where(same, weigh, 0.0))
        term = reach * (dot_nn(left, right) + dot_nn(left_lo, right) + dot_nn(left, right_lo))
        row_values.append(term)
        left, left_lo = halves(jnp.where(same, pairs, 0.0))
        row_keys.append(reach * (dot_nn(left, right) + dot_nn(left_lo, right) + dot_nn(left, right_lo)))
        probs_grad = probs_grad + term
    scores_grad = probs * (probs_grad - jnp.sum(probs_grad * probs, axis=1, keepdims=True))
    scores_grad = scaling * scores_grad

    kstate_hi, kstate_lo = halves(state_ref[:, :width])
    head_keys = head * (dot_nt(query, kstate_hi) + dot_nt(query, kstate_lo))
    gwrite = pair_diag * scores_grad + weigh_diag * probs_low
    glog = dot_tn(span_matrix(depth, tokens), (head_keys * scores_grad + head_probs * probs_low).astype(BF))
    gpairs = jnp.zeros((tokens, tokens), F32)
    for level in reversed(range(depth)):
        span = spans_ref[level]
        odd = odd_rows(level, tokens, slots)
        same = same_pair(level, tokens)
        reach = jnp.where(odd, span, 0.0)
        source = jnp.where(odd, 0.0, span)
        key_side, key_rest = halves(reach * scores_grad)
        value_side, value_rest = halves(reach * probs_low)
        seen, seen_rest = halves(jnp.where(same, pairs_t, 0.0))
        felt, felt_rest = halves(jnp.where(same, weigh_t, 0.0))
        sent, sent_rest = halves(source * write)
        pushed = dot_nt(key_side, sent) + dot_nt(key_rest, sent) + dot_nt(key_side, sent_rest)
        gpairs = jnp.where(same, pushed, gpairs)
        column = source * (
            dot_nn(seen, key_side) + dot_nn(seen, key_rest) + dot_nn(seen_rest, key_side)
            + dot_nn(felt, value_side) + dot_nn(felt, value_rest) + dot_nn(felt_rest, value_side)
        )
        gwrite = gwrite + column
        moved = column * write + row_values[level] * probs_low + row_keys[level] * scores_grad
        spread = span_matrix(level, tokens)
        moved, moved_rest = halves(moved)
        glog = glog + dot_tn(spread, moved) + dot_tn(spread, moved_rest)
    gpairs = jnp.where(t == u, jnp.sum(scores_grad * write, axis=1, keepdims=True), gpairs)
    gpairs, gpairs_rest = halves(gpairs)
    gwrite_ref[...] = gwrite
    glog_ref[...] = glog
    key_head, key_head_rest = halves(scores_grad * head)
    gquery_ref[...] = (
        dot_nn(gpairs, keys)
        + dot_nn(gpairs_rest, keys)
        + dot_nn(key_head, kstate_hi)
        + dot_nn(key_head, kstate_lo)
        + dot_nn(key_head_rest, kstate_hi)
    )
    gkeys_ref[...] = dot_tn(gpairs, query) + dot_tn(gpairs_rest, query)
    gvalues_ref[...] = dot_tn(mixing_ref[...], mix_low)
    carry_ref[:, :width] = dot_tn(key_head, query) + dot_tn(key_head_rest, query)
    carry_ref[:, width:] = dot_tn((probs_low * head).astype(BF), mix_low)


def run_backward(grad, query, keys, values, pre, spans, state, gate, gain, probs, pairs, mixing, mix):
    tokens, slots = pre.shape
    width = keys.shape[1]
    wide = jax.ShapeDtypeStruct((tokens, width), F32)
    narrow = jax.ShapeDtypeStruct((tokens, slots), F32)
    return pl.pallas_call(
        backward_kernel,
        out_shape=(
            wide, wide, wide,
            jax.ShapeDtypeStruct((tokens, width), BF),
            jax.ShapeDtypeStruct((1, width), F32),
            narrow, narrow,
            jax.ShapeDtypeStruct((slots, 2 * width), F32),
        ),
        name="slot_backward",
    )(grad, query, keys, values, pre, spans, state, gate, gain, probs, pairs, mixing, mix)


def finish_kernel(
    gquery_ref, gkeys_ref, gvalues_ref, ggate_ref, gwrite_ref, glog_ref,
    keys_ref, values_ref, pre_ref, spans_ref, query_pre_ref, keys_pre_ref,
    state_ref, total_ref, ends_ref, gated_ref, out_ref, bias_ref,
):
    tokens, slots = pre_ref.shape
    depth = n_levels(tokens)
    width = keys_ref.shape[1]
    pre = pre_ref[...]
    decay = decay_write(pre)
    write = 1.0 - decay
    keys, values = keys_ref[...], values_ref[...]
    ends = ends_ref[...]
    ends_low = ends.astype(BF)
    tail = spans_ref[depth + 1]
    sent = (tail * write).astype(BF)
    column = tail * (dot_nt(keys, ends_low[:, :width]) + dot_nt(values, ends_low[:, width:]))
    glog = glog_ref[...] + dot_tn(span_matrix(depth + 1, tokens), (column * write).astype(BF))
    carried = lax.dot_general(
        jnp.ones((1, 2 * width), F32), ends * state_ref[...], (((1,), (1,)), ((), ())),
        precision=lax.Precision.HIGHEST, preferred_element_type=F32,
    )
    glog = glog + carried * total_ref[...]
    glog = glog - decay * (gwrite_ref[...] + column)
    def put(part, value):
        out_ref[:, part * width : (part + 1) * width] = value.astype(BF)

    put(0, gated_ref[...])
    u = query_pre_ref[...]
    s = sigmoid(u)
    put(1, gquery_ref[...] * (s * (1.0 + u * (1.0 - s))))
    u = keys_pre_ref[...]
    s = sigmoid(u)
    gkeys = gkeys_ref[...] + dot_nn(sent, ends_low[:, :width])
    put(2, gkeys * (s * (1.0 + u * (1.0 - s))))
    put(3, gvalues_ref[...] + dot_nn(sent, ends_low[:, width:]))
    put(4, ggate_ref[...])
    gforget = (glog * sigmoid(-pre) / GATE_NORM).astype(BF)
    gforget = jnp.concatenate([gforget, jnp.zeros((tokens, 128 - slots), BF)], axis=1)
    out_ref[:, 5 * width :] = gforget
    bias_ref[...] = jnp.sum(gforget.astype(F32), axis=0, keepdims=True)


def run_finish(gquery, gkeys, gvalues, ggate, gwrite, glog, keys, values, pre, spans, query_pre, keys_pre, state, total, ends, gated):
    tokens, slots = pre.shape
    width = keys.shape[1]
    return pl.pallas_call(
        finish_kernel,
        out_shape=(jax.ShapeDtypeStruct((tokens, 5 * width + 128), BF), jax.ShapeDtypeStruct((1, 128), F32)),
        name="slot_finish",
    )(gquery, gkeys, gvalues, ggate, gwrite, glog, keys, values, pre, spans, query_pre, keys_pre, state, total, ends, gated)


MESH = pl.DeviceIdType.MESH
GROUPED = ("shard", "ctx")


def greet(axes_of_peers):
    barrier = pltpu.get_barrier_semaphore()
    for peer in axes_of_peers:
        pl.semaphore_signal(barrier, inc=1, device_id=peer, device_id_type=MESH)
    pl.semaphore_wait(barrier, len(axes_of_peers))


def tp_peers():
    count = lax.axis_size("tp")
    me = lax.axis_index("tp")
    return me, [lax.rem(me + k, count) for k in range(1, count)]


CHUNKS = 4
LATENCY = 2.2
LEAD = 10
CLOSING = 3


def tp_line(partial_ref, full_ref, arrived, staged, sums_ref, finish, send_a, recv_a, send_b, recv_b):
    count = lax.axis_size("tp")
    me = lax.axis_index("tp")
    rows = partial_ref.shape[1] // CHUNKS
    peers = [lax.rem(me + 1, count), lax.rem(me + count - 1, count)]

    def at_place(side, place):
        return place if side == 0 else count - 1 - place

    def cut(chunk):
        return pl.ds(chunk * rows, rows)

    def sum_copy(side, hop, chunk, source):
        return pltpu.make_async_remote_copy(
            src_ref=source,
            dst_ref=arrived.at[side, hop, chunk],
            send_sem=send_a.at[side, hop, chunk],
            recv_sem=recv_a.at[side, hop, chunk],
            device_id={"tp": peers[side]},
            device_id_type=MESH,
        )

    def row_copy(side, hop, chunk, block):
        return pltpu.make_async_remote_copy(
            src_ref=full_ref.at[block, cut(chunk)],
            dst_ref=full_ref.at[block, cut(chunk)],
            send_sem=send_b.at[side, hop, chunk],
            recv_sem=recv_b.at[side, hop, chunk],
            device_id={"tp": peers[side]},
            device_id_type=MESH,
        )

    def own(side, hop, chunk):
        return partial_ref.at[at_place(side, count - 1 - hop), cut(chunk)]

    def send_own(chunk):
        for side in range(2):

            @pl.when(me == at_place(side, 0))
            def _():
                for hop in range(count - 1):
                    sum_copy(side, hop, chunk, own(side, hop, chunk)).start()

    def add_hop(side, place, hop, chunk):
        @pl.when(me == at_place(side, place))
        def _():
            slot = staged.at[side, hop, chunk]
            copy = sum_copy(side, hop, chunk, slot)
            copy.wait_recv()
            slot[...] = (own(side, hop, chunk)[...].astype(F32) + arrived[side, hop, chunk].astype(F32)).astype(BF)
            copy.start()

    def close(chunk):
        sums_ref[...] = partial_ref[me, cut(chunk)].astype(F32)
        for side in range(2):
            place = me if side == 0 else count - 1 - me
            hop = jnp.minimum(count - 1 - place, count - 2)

            @pl.when(place > 0)
            def _():
                sum_copy(side, hop, chunk, staged.at[side, hop, chunk]).wait_recv()
                sums_ref[...] += arrived[side, hop, chunk].astype(F32)

        finish(chunk, sums_ref[...])
        for side in range(2):

            @pl.when(me != at_place(side, count - 1))
            def _():
                row_copy(side, 0, chunk, me).start()

    def forward(side, place, distance, chunk):
        @pl.when(me == at_place(side, place))
        def _():
            block = at_place(side, place - distance)
            row_copy(side, distance - 1, chunk, block).wait_recv()
            if place < count - 1:
                row_copy(side, distance, chunk, block).start()

    step = 1 + LATENCY
    events = []
    for chunk in range(CHUNKS):
        base = (count - 1) * chunk
        closed = base + (count - 1) + (count - 2) * LATENCY
        events.append((base - LEAD * (count - 1), functools.partial(send_own, chunk)))
        events.append((closed, functools.partial(close, chunk)))
        for side in range(2):
            for place in range(1, count):
                for hop in range(count - 1 - place):
                    due = base + hop + place * step
                    events.append((due, functools.partial(add_hop, side, place, hop, chunk)))
                for distance in range(1, place + 1):
                    due = closed + CLOSING + distance * step
                    if place == count - 1:
                        due += 1000
                    events.append((due, functools.partial(forward, side, place, distance, chunk)))
    for _, event in sorted(events, key=lambda event: event[0]):
        event()

    def drain():
        for side in range(2):
            for place in range(count - 1):

                @pl.when(me == at_place(side, place))
                def _():
                    for chunk in range(CHUNKS):
                        for hop in range(count - 1 - place):
                            sum_copy(side, hop, chunk, staged.at[side, hop, chunk]).wait_send()
                        for hop in range(place + 1):
                            row_copy(side, hop, chunk, at_place(side, place - hop)).wait_send()

    return drain


def plane_peers():
    shards, ctxs = lax.axis_size("shard"), lax.axis_size("ctx")
    devices = shards * ctxs
    me = lax.axis_index("shard") * ctxs + lax.axis_index("ctx")
    peers = [lax.rem(me + k, devices) for k in range(1, devices)]
    places = [{"shard": lax.div(peer, ctxs), "ctx": lax.rem(peer, ctxs)} for peer in peers]
    return me, peers, places


def start_scatter(sources, targets, send_sems, recv_sems):
    me, peers, places = plane_peers()
    copies = []
    for i, (source, target) in enumerate(zip(sources, targets)):
        step = target.shape[2]

        def block(at):
            if len(source.shape) == 3:
                return source.at[at]
            return source.at[:, pl.ds(pl.multiple_of(at * step, step), step)]

        for k, (peer, place) in enumerate(zip(peers, places)):
            copy = pltpu.make_async_remote_copy(
                src_ref=block(peer),
                dst_ref=target.at[me],
                send_sem=send_sems.at[i, k],
                recv_sem=recv_sems.at[i, k],
                device_id=place,
                device_id_type=MESH,
            )
            copy.start()
            copies.append(copy)
    for source, target in zip(sources, targets):
        target[me] = block_of(source, me, target.shape[2])
    return copies


def block_of(source, at, step):
    if len(source.shape) == 3:
        return source[at]
    return source[:, pl.ds(pl.multiple_of(at * step, step), step)]


def spread_kernel(n_parts, n_packed, *refs):
    parts, refs = refs[:n_parts], refs[n_parts:]
    packed, refs = refs[:n_packed], refs[n_packed:]
    if n_packed:
        forget_ref, mask_ref, vectors, refs = refs[0], refs[1], refs[2:6], refs[6:]
        out_ref, rows_ref, pack_ref, slab, part_sems, own_sem, send_sems, recv_sems = refs[:8]
        row_ref, row_send, row_recv, pack_slab, pack_sems, pack_sem = refs[8:]
    else:
        out_ref, slab, part_sems, own_sem, send_sems, recv_sems = refs
    shard, core = lax.axis_index("shard"), lax.axis_index("ctx")
    me, _, places = plane_peers()
    across = shard + 1 - 2 * lax.rem(shard, 2)
    along = lax.rem(shard + 2, 4)
    corner = lax.rem(across + 2, 4)
    other = 1 - core
    to_x, to_y, to_core = {"shard": across}, {"shard": along}, {"ctx": other}
    rows = slab.shape[0]
    half = rows // 2

    def load_all(sources, target, sems):
        loads = []
        start = 0
        for i, part in enumerate(sources):
            load = pltpu.make_async_copy(part, target.at[:, pl.ds(start, part.shape[1])], sems.at[i])
            load.start()
            loads.append(load)
            start += part.shape[1]
        return loads

    loads = load_all(parts, slab, part_sems)
    if n_packed:
        room = jnp.zeros((rows, 128 - forget_ref.shape[1]), BF)
        slab[:, slab.shape[1] - 128 :] = jnp.concatenate([forget_ref[...], room], axis=1)
        row_ref[...] = jnp.zeros_like(row_ref)
        for i, vector in enumerate(vectors):
            row_ref[i : i + 1, : vector.shape[1]] = vector[...].astype(F32)
        count = jnp.sum(mask_ref[...].astype(F32), axis=1, keepdims=True)
        row_ref[4:5, :] = jnp.broadcast_to(count, (1, row_ref.shape[1]))
    greet(places)
    for load in loads:
        load.wait()
    keep = pltpu.make_async_copy(slab, out_ref.at[pl.ds(pl.multiple_of(me * rows, rows), rows)], own_sem)
    keep.start()

    def landing(block, part):
        return out_ref.at[pl.ds(pl.multiple_of(block * rows + part * half, half), half)]

    started = []

    def send(kind, source, block, part, place):
        copy = pltpu.make_async_remote_copy(
            src_ref=source,
            dst_ref=landing(block, part),
            send_sem=send_sems.at[kind],
            recv_sem=recv_sems.at[kind],
            device_id=place,
            device_id_type=MESH,
        )
        copy.start()
        started.append(copy)

    def receive(kind, block, part, place):
        region = landing(block, part)
        pltpu.make_async_remote_copy(
            src_ref=region,
            dst_ref=region,
            send_sem=send_sems.at[kind],
            recv_sem=recv_sems.at[kind],
            device_id=place,
            device_id_type=MESH,
        ).wait_recv()

    def own(part):
        return slab.at[pl.ds(part * half, half)]

    def block(place, at_core):
        return 2 * place + at_core

    send(0, own(0), me, 0, to_x)
    send(1, own(1), me, 1, to_y)
    if n_packed:
        copies = start_sums(row_ref, rows_ref, row_send, row_recv, [], places, me)
    send(2, own(1), me, 1, to_x)
    send(3, own(0), me, 0, to_y)
    send(4, own(0), me, 0, to_core)
    send(5, own(1), me, 1, to_core)
    if n_packed:
        for load in load_all(packed, pack_slab, pack_sems):
            load.wait()
        store = pltpu.make_async_copy(pack_slab, pack_ref, pack_sem)
        store.start()
    x_block, y_block, far_block = block(across, core), block(along, core), block(corner, core)
    receive(0, x_block, 0, to_x)
    send(6, landing(x_block, 0), x_block, 0, to_y)
    send(8, landing(x_block, 0), x_block, 0, to_core)
    receive(1, y_block, 1, to_y)
    send(7, landing(y_block, 1), y_block, 1, to_x)
    send(9, landing(y_block, 1), y_block, 1, to_core)
    receive(2, x_block, 1, to_x)
    send(10, landing(x_block, 1), x_block, 1, to_core)
    receive(3, y_block, 0, to_y)
    send(11, landing(y_block, 0), y_block, 0, to_core)
    receive(6, far_block, 0, to_y)
    send(12, landing(far_block, 0), far_block, 0, to_core)
    receive(7, far_block, 1, to_x)
    send(13, landing(far_block, 1), far_block, 1, to_core)
    for kind, place, part in (
        (4, shard, 0), (5, shard, 1), (8, across, 0), (9, along, 1), (10, across, 1), (11, along, 0),
        (12, corner, 0), (13, corner, 1),
    ):
        receive(kind, block(place, other), part, to_core)
    for copy in started:
        copy.wait_send()
    keep.wait()
    if n_packed:
        store.wait()
        for copy in copies:
            copy.wait()


def run_spread(name, collective_id, parts, packed=(), forget=None, mask=None, vectors=()):
    devices = lax.axis_size(GROUPED)
    rows = parts[0].shape[0]
    columns = sum(part.shape[1] for part in parts) + (128 if packed else 0)
    anywhere = pl.BlockSpec(memory_space=pl.ANY)
    in_specs, out_specs = [anywhere] * len(parts), [anywhere]
    out_shape = [jax.ShapeDtypeStruct((devices * rows, columns), BF)]
    scratch = [
        pltpu.VMEM((rows, columns), BF),
        pltpu.SemaphoreType.DMA((len(parts),)),
        pltpu.SemaphoreType.DMA,
        *[pltpu.SemaphoreType.DMA((14,))] * 2,
    ]
    args = list(parts)
    if packed:
        packed_shape = (rows, sum(part.shape[1] for part in packed))
        args += [*packed, forget, mask, *vectors]
        in_specs += [*[anywhere] * len(packed), *[pl.BlockSpec(memory_space=pltpu.VMEM)] * (2 + len(vectors))]
        out_specs += [pl.BlockSpec(memory_space=pltpu.VMEM), anywhere]
        out_shape += [jax.ShapeDtypeStruct((devices, 8, rows), F32), jax.ShapeDtypeStruct(packed_shape, BF)]
        scratch += [
            pltpu.VMEM((8, rows), F32),
            *[pltpu.SemaphoreType.DMA((devices - 1,))] * 2,
            pltpu.VMEM(packed_shape, BF),
            pltpu.SemaphoreType.DMA((len(packed),)),
            pltpu.SemaphoreType.DMA,
        ]
    return pl.pallas_call(
        functools.partial(spread_kernel, len(parts), len(packed)),
        out_shape=tuple(out_shape),
        in_specs=in_specs,
        out_specs=tuple(out_specs),
        scratch_shapes=scratch,
        compiler_params=pltpu.CompilerParams(collective_id=collective_id, has_side_effects=True),
        name=name,
    )(*args)


def start_sums(row_ref, landed, send_sems, recv_sems, peers, places, me):
    copies = []
    landed[me] = row_ref[...]
    for k, place in enumerate(places):
        copy = pltpu.make_async_remote_copy(
            src_ref=row_ref,
            dst_ref=landed.at[me],
            send_sem=send_sems.at[k],
            recv_sem=recv_sems.at[k],
            device_id=place,
            device_id_type=MESH,
        )
        copy.start()
        copies.append(copy)
    return copies


def summed(landed):
    total = landed[0]
    for k in range(1, landed.shape[0]):
        total = total + landed[k]
    return total


def exchange_kernel(epilogue, n_in, n_rows, n_moved, n_sums, partial_ref, *refs):
    me, peers = tp_peers()
    inputs, refs = refs[:n_in], refs[n_in:]
    sources, refs = refs[:n_moved], refs[n_moved:]
    full_ref, refs = refs[0], refs[1:]
    outputs, refs = refs[:n_rows], refs[n_rows:]
    targets, refs = refs[:n_moved], refs[n_moved:]
    sums, refs = refs[: 2 * n_sums], refs[2 * n_sums :]
    arrived, staged, sums_ref, send_a, recv_a, send_b, recv_b, send_m, recv_m = refs[:9]
    own, plane, places = plane_peers()
    across = [{"tp": peer} for peer in peers]
    greet(across + (places if n_moved or n_sums else []))
    moves = start_scatter(sources, targets, send_m, recv_m)
    rows = full_ref.shape[1] // CHUNKS
    started = []

    def finish(chunk, total):
        part = pl.ds(chunk * rows, rows)
        full_ref[me, part] = epilogue(total, me, part, chunk == 0, inputs, outputs)
        if n_sums and chunk == CHUNKS - 1:
            row_ref, in_plane, _, _, send_p, recv_p = refs[9:15]
            width = outputs[0].shape[1]
            row_ref[:, :width] = outputs[0][...]
            row_ref[:, width:] = inputs[-1][...]
            started.extend(start_sums(row_ref, in_plane, send_p, recv_p, plane, places, own))

    drain = tp_line(partial_ref, full_ref, arrived, staged, sums_ref, finish, send_a, recv_a, send_b, recv_b)
    if n_sums:
        row_ref, in_plane, plane_row, in_tp, send_p, recv_p, send_t, recv_t = refs[9:]
        for copy in started:
            copy.wait()
        plane_row[...] = summed(in_plane)
        sums[0][...] = plane_row[...]
        for copy in start_sums(plane_row, in_tp, send_t, recv_t, peers, across, me):
            copy.wait()
        sums[1][...] = summed(in_tp)
    drain()
    for copy in moves:
        copy.wait()


def run_exchange(epilogue, name, collective_id, partial, inputs, row_outputs, moved=(), summing=False):
    tp = lax.axis_size("tp")
    devices = lax.axis_size(GROUPED)
    tokens, columns = partial.shape
    share = tokens // tp
    partial = partial.reshape(tp, share, columns)
    step = columns // devices
    if step % 128:
        moved = [m.reshape(tokens, devices, step).transpose(1, 0, 2) for m in moved]
    count = len(moved)
    scratch = [
        *[pltpu.VMEM((2, tp - 1, CHUNKS, share // CHUNKS, columns), BF)] * 2,
        pltpu.VMEM((share // CHUNKS, columns), F32),
        *[pltpu.SemaphoreType.DMA((2, tp - 1, CHUNKS))] * 4,
        *[pltpu.SemaphoreType.DMA((max(count, 1), devices - 1))] * 2,
    ]
    extra = ()
    if summing:
        row = row_outputs[0].shape[1] + inputs[-1].shape[1]
        extra = (jax.ShapeDtypeStruct((1, row), F32),) * 2
        scratch += [
            pltpu.VMEM((1, row), F32),
            pltpu.VMEM((devices, 1, row), F32),
            pltpu.VMEM((1, row), F32),
            pltpu.VMEM((tp, 1, row), F32),
            *[pltpu.SemaphoreType.DMA((devices - 1,))] * 2,
            *[pltpu.SemaphoreType.DMA((tp - 1,))] * 2,
        ]
    out_shape = (
        jax.ShapeDtypeStruct((tp, share, columns), BF),
        *row_outputs,
        *[jax.ShapeDtypeStruct((devices, tokens, step), BF)] * count,
        *extra,
    )
    outs = pl.pallas_call(
        functools.partial(exchange_kernel, epilogue, len(inputs), len(row_outputs), count, int(summing)),
        out_shape=out_shape,
        in_specs=[pl.BlockSpec(memory_space=pltpu.VMEM)] * (1 + len(inputs) + count),
        out_specs=tuple([pl.BlockSpec(memory_space=pltpu.VMEM)] * len(out_shape)),
        scratch_shapes=scratch,
        compiler_params=pltpu.CompilerParams(collective_id=collective_id, has_side_effects=True),
        name=name,
    )(partial, *inputs, *moved)
    start = 1 + len(row_outputs)
    return (
        outs[0].reshape(tokens, columns),
        *outs[1:start],
        *[o.reshape(devices * tokens, step) for o in outs[start : start + count]],
        *outs[start + count :],
    )


def middle_epilogue(total, me, part, first, inputs, outputs):
    hidden_ref, gain_ref = inputs
    (branch_ref,) = outputs
    branch_ref[part, :] = total
    middle = hidden_ref[me, part].astype(F32) + total
    scale = lax.rsqrt(jnp.mean(middle * middle, axis=1, keepdims=True) + EPSILON)
    return (middle * scale * gain_ref[...]).astype(BF)


def result_epilogue(total, me, part, first, inputs, outputs):
    hidden_ref, branch_ref, teacher_out_ref, teacher_mix_ref, cotangent_ref, mask_ref, scale_ref = inputs
    grad_ref, losses_ref = outputs
    branch = branch_ref[part, :]
    result = hidden_ref[me, part].astype(F32) + branch + total
    mask = mask_ref[me, part]
    gap = result - teacher_out_ref[me, part].astype(F32)
    gap_mix = branch - teacher_mix_ref[me, part].astype(F32)
    loss_out = jnp.sum(mask * (gap * gap), keepdims=True)
    loss_mix = jnp.sum(mask * (gap_mix * gap_mix), keepdims=True)
    lane = lax.broadcasted_iota(jnp.int32, (1, 128), 1)
    losses = jnp.where(lane == 0, loss_out, 0.0) + jnp.where(lane == 1, loss_mix, 0.0)
    losses_ref[...] = losses if first else losses_ref[...] + losses
    grad_ref[part, :] = cotangent_ref[me, part].astype(F32) + scale_ref[...] * mask * gap
    return result.astype(BF)


def norm_back(grad, rows, gain):
    scale = lax.rsqrt(jnp.mean(rows * rows, axis=1, keepdims=True) + EPSILON)
    unit = rows * scale
    gain_grad = jnp.sum(grad * unit, axis=0, keepdims=True)
    inner = grad * gain
    return scale * (inner - unit * jnp.mean(unit * inner, axis=1, keepdims=True)), gain_grad


def branch_epilogue(total, me, part, first, inputs, outputs):
    hidden_ref, branch_ref, teacher_mix_ref, grad_ref, mask_ref, scale_ref, gain_ref = inputs
    grad_middle_ref, gain_grad_ref = outputs
    branch = branch_ref[part, :]
    back, gain_grad = norm_back(total, hidden_ref[me, part].astype(F32) + branch, gain_ref[...])
    gain_grad_ref[...] = gain_grad if first else gain_grad_ref[...] + gain_grad
    grad_middle = back + grad_ref[part, :]
    grad_middle_ref[part, :] = grad_middle
    gap_mix = branch - teacher_mix_ref[me, part].astype(F32)
    return (grad_middle + scale_ref[...] * mask_ref[me, part] * gap_mix).astype(BF)


def input_epilogue(total, me, part, first, inputs, outputs):
    hidden_ref, grad_middle_ref, gain_ref = inputs[:3]
    (gain_grad_ref,) = outputs
    back, gain_grad = norm_back(total, hidden_ref[me, part].astype(F32), gain_ref[...])
    gain_grad_ref[...] = gain_grad if first else gain_grad_ref[...] + gain_grad
    return (back + grad_middle_ref[part, :]).astype(BF)


def weights_kernel(segments, n_rows, n_columns, *refs):
    rows, refs = refs[:n_rows], refs[n_rows:]
    columns, outs = refs[:n_columns], refs[n_columns:]
    at = pl.program_id(0)
    turned = [ref[...].T for ref in rows]
    for (row, column, start, width), out in zip(segments, outs):
        term = dot_nn(turned[row], columns[column][:, pl.ds(start, width)])

        @pl.when(at == 0)
        def _():
            out[...] = term

        @pl.when(at > 0)
        def _():
            out[...] += term


def run_weights(name, rows, columns, segments):
    tokens, features = rows[0].shape
    block = 512
    whole = lambda width: pl.BlockSpec((block, width), lambda i: (i, 0))
    shapes = [(features, segment[3]) for segment in segments]
    return pl.pallas_call(
        functools.partial(weights_kernel, segments, len(rows), len(columns)),
        grid=(tokens // block,),
        in_specs=[*[whole(features)] * len(rows), *[whole(c.shape[1]) for c in columns]],
        out_specs=tuple(pl.BlockSpec(shape, lambda i: (0, 0)) for shape in shapes),
        out_shape=tuple(jax.ShapeDtypeStruct(shape, F32) for shape in shapes),
        compiler_params=pltpu.CompilerParams(dimension_semantics=("arbitrary",)),
        name=name,
    )(*rows, *columns)


def attention_weights_kernel(out_rows_ref, rows_ref, block_ref, forget_ref, *refs):
    outs, forget_out, turned = refs[:5], refs[5], refs[6]
    at = pl.program_id(0)

    @pl.when(at == 0)
    def _():
        turned[0] = out_rows_ref[...].T
        turned[1] = rows_ref[...].T
        forget_out[...] = dot_tn(forget_ref[...], rows_ref[...])[: forget_out.shape[0]]

    term = dot_nn(turned[jnp.minimum(at, 1)], block_ref[...])
    for i, out in enumerate(outs):

        @pl.when(at == i)
        def _():
            out[...] = term


def run_attention_weights(out_rows, rows, gathered_all, width, slots):
    tokens, features = rows.shape
    fixed = lambda shape: pl.BlockSpec(shape, lambda i: (0, 0))
    last = 5 * width // 128
    shapes = [(features, width)] * 5 + [(slots, features)]
    return pl.pallas_call(
        attention_weights_kernel,
        grid=(5,),
        in_specs=[
            fixed((tokens, features)), fixed((tokens, features)),
            pl.BlockSpec((tokens, width), lambda i: (0, i)),
            pl.BlockSpec((tokens, 128), lambda i: (0, last)),
        ],
        out_specs=tuple(fixed(shape) for shape in shapes),
        out_shape=tuple(jax.ShapeDtypeStruct(shape, F32) for shape in shapes),
        scratch_shapes=[pltpu.VMEM((2, features, tokens), BF)],
        compiler_params=pltpu.CompilerParams(dimension_semantics=("arbitrary",)),
        name="attention_weights",
    )(out_rows, rows, gathered_all, gathered_all)


def passed_along(value, axis, steps):
    count = lax.axis_size(axis)
    leading, last = (max(0, -steps), min(count, count - steps))
    return lax.ppermute(value, axis, [(source, source + steps) for source in range(leading, last)])


def relay(value, decay, axis, steps):
    carried = passed_along(value, axis, steps)
    for _ in range(lax.axis_size(axis) - 2):
        carried = passed_along(value + decay * carried, axis, steps)
    return carried


def gathered(value):
    return lax.all_gather(value, GROUPED, axis=0, tiled=True)


def per_device(
    hidden_in,
    cotangent,
    teacher_out,
    teacher_mix,
    valid_mask,
    doc_start,
    attn_gain,
    w_query,
    w_key,
    w_value,
    w_forget,
    forget_bias,
    head_gain,
    w_outgate,
    w_out,
    mlp_gain,
    w_gate,
    w_up,
    w_down,
):
    tokens, features = hidden_in.shape
    devices = lax.axis_size(GROUPED)
    tp = lax.axis_size("tp")
    share = tokens // tp
    rows = w_query.shape[0]
    width = w_query.shape[1]
    slots = w_forget.shape[1]
    units = w_gate.shape[1]
    tokens_all = tokens * devices
    mask_flat = valid_mask.astype(F32)

    vectors = [attn_gain.reshape(1, -1), mlp_gain.reshape(1, -1), head_gain, forget_bias]
    attn_parts = [w_query, w_key, w_value, w_outgate]
    mlp_parts = [w_gate, w_up, w_down]
    if (lax.axis_size("shard"), lax.axis_size("ctx")) == (4, 2):
        first, row_all, pack = run_spread(
            "gather_attention", 5, attn_parts, mlp_parts, w_forget, valid_mask.reshape(1, -1), vectors
        )
        second = gathered(pack)
        out_own, first = lax.optimization_barrier((w_out, first))
        (out_w,) = run_spread("gather_out", 6, [out_own])
        first, row_all, out_w = lax.optimization_barrier((first, row_all, out_w))
    else:
        vectors.append(jnp.sum(mask_flat).reshape(1, 1))
        row = [jnp.pad(v.astype(F32), ((0, 0), (0, rows - v.shape[1]))) for v in vectors]
        row_all = gathered(jnp.concatenate(row, axis=0)[None])
        forget_w = jnp.pad(w_forget, ((0, 0), (0, 128 - slots)))
        first = gathered(jnp.concatenate([*attn_parts, forget_w, w_out], axis=1))
        pack, first = lax.optimization_barrier((jnp.concatenate(mlp_parts, axis=1), first))
        second = gathered(pack)
        out_w = first[:, 4 * width + 128 :]
        first = first[:, : 4 * width + 128]

    attn_scale = row_all[:, 0].reshape(1, -1)
    mlp_scale = row_all[:, 1].reshape(1, -1)
    head_scale = row_all[:, 2, : width // devices].reshape(1, width)
    bias = row_all[:, 3, : slots // devices].reshape(1, slots)
    count_total = jnp.sum(row_all[:, 4, 0])
    loss_scale = (tokens_all / count_total).reshape(1, 1)

    hidden_f = hidden_in.astype(F32)
    scale = lax.rsqrt(jnp.mean(hidden_f * hidden_f, axis=-1, keepdims=True) + EPSILON)
    normed_in = (hidden_f * scale * attn_scale).astype(BF)
    pre_all = dot_nn(normed_in, first)
    query_pre = pre_all[:, :width]
    keys_pre = pre_all[:, width : 2 * width]
    query = jax.nn.silu(query_pre).astype(BF)
    keys = jax.nn.silu(keys_pre).astype(BF)
    values = pre_all[:, 2 * width : 3 * width].astype(BF)
    gate_pre = pre_all[:, 3 * width : 4 * width]
    forget_pre = pre_all[:, 4 * width : 4 * width + slots] + bias
    resets = doc_start.astype(F32)[:, None]

    spans, total, ends = run_ends(forget_pre, resets, keys, values)
    decay = total.reshape(slots, 1)
    state = relay(ends, decay, "ctx", 1)
    probs, pairs, mixing, mix, gated = run_forward(
        query, keys, values, forget_pre, spans, state, gate_pre, head_scale
    )
    gate_w = second[:, :units]
    up_w = second[:, units : 2 * units]
    down_w = second[:, 2 * units :]

    by_share = lambda tensor: tensor.reshape(tp, share, -1)
    hidden_s, teacher_out_s, teacher_mix_s, cotangent_s = map(by_share, (hidden_in, teacher_out, teacher_mix, cotangent))
    mask_s = by_share(mask_flat)
    narrow = lambda *shape: jax.ShapeDtypeStruct(shape, F32)

    normed_mid, branch = run_exchange(
        middle_epilogue, "sum_branch", 1, dot_nt(gated, out_w).astype(BF), (hidden_s, mlp_scale),
        (narrow(share, features),),
    )
    gate_val = dot_nn(normed_mid, gate_w)
    up_val = dot_nn(normed_mid, up_w)
    hidden_units = (jax.nn.silu(gate_val) * up_val).astype(BF)
    units_all = gathered(hidden_units)
    output, grad_result, losses, normed_in_c, normed_mid_c = run_exchange(
        result_epilogue, "sum_result", 2, dot_nt(hidden_units, down_w).astype(BF),
        (hidden_s, branch, teacher_out_s, teacher_mix_s, cotangent_s, mask_s, loss_scale),
        (narrow(share, features), narrow(1, 128)),
        moved=(normed_in, normed_mid),
    )
    gap = output.astype(F32) - teacher_out.astype(F32)
    grad_mlp = (cotangent.astype(F32) + loss_scale * mask_flat[:, None] * gap).astype(BF)
    grad_units = dot_nn(grad_mlp, down_w)
    gate_sig = jax.nn.sigmoid(gate_val)
    grad_gate_val = (grad_units * up_val * (gate_sig * (1.0 + gate_val * (1.0 - gate_sig)))).astype(BF)
    grad_up_val = (grad_units * (gate_val * gate_sig)).astype(BF)
    grad_both = jnp.concatenate([grad_gate_val, grad_up_val], axis=1)
    partial = dot_nt(grad_both, second[:, : 2 * units]).astype(BF)
    units_all, grad_both = lax.optimization_barrier((units_all, grad_both))
    partial = lax.optimization_barrier((partial, grad_both))[0]
    mlp_all = gathered(grad_both)
    grad_branch, grad_middle, mlp_gain_part, grad_mlp_c = run_exchange(
        branch_epilogue, "sum_middle", 3, partial,
        (hidden_s, branch, teacher_mix_s, grad_result, mask_s, loss_scale, mlp_scale),
        (narrow(share, features), narrow(1, features)),
        moved=(grad_mlp,),
    )
    grad_gated = dot_nn(grad_branch, out_w)
    gquery, gkeys, gvalues, ggate, head_gain_part, gwrite, glog, carry = run_backward(
        grad_gated, query, keys, values, forget_pre, spans, state, gate_pre, head_scale, probs, pairs, mixing, mix
    )
    later = relay(carry, decay, "ctx", -1)
    grad_pre, bias_part = run_finish(
        gquery, gkeys, gvalues, ggate, gwrite, glog, keys, values, forget_pre, spans, query_pre, keys_pre,
        state, total, later, gated,
    )
    partial = dot_nt(grad_pre[:, width:], first).astype(BF)
    mlp_all, grad_pre = lax.optimization_barrier((mlp_all, grad_pre))
    partial = lax.optimization_barrier((partial, grad_pre))[0]
    attn_all = gathered(grad_pre)
    grad_in, _, grad_branch_c, plane_sums, all_sums = run_exchange(
        input_epilogue, "sum_input", 4, partial,
        (hidden_s, grad_middle, attn_scale, jnp.concatenate([mlp_gain_part, head_gain_part, bias_part, losses], axis=1)),
        (narrow(1, features),), moved=(grad_branch,), summing=True,
    )
    gate_grad, up_grad, down_grad = run_weights(
        "mlp_weights", (normed_mid_c, grad_mlp_c), (mlp_all, units_all),
        ((0, 0, 0, units), (0, 0, units, units), (1, 1, 0, units)),
    )
    out_grad, query_grad, keys_grad, values_grad, outgate_grad, forget_grad = run_attention_weights(
        grad_branch_c, normed_in_c, attn_all, width, slots
    )
    index = lax.axis_index(GROUPED)

    cut = lambda row, size: lax.dynamic_slice_in_dim(row, index * size, size, axis=1)
    attn_gain_grad = cut(all_sums[:, :features], features // devices).reshape(-1)
    mlp_gain_grad = cut(all_sums[:, features : 2 * features], features // devices).reshape(-1)
    head_gain_grad = cut(plane_sums[:, 2 * features : 2 * features + width], width // devices)
    bias_grad = cut(plane_sums[:, 2 * features + width : 2 * features + width + slots], slots // devices)
    sums = all_sums[0, 2 * features + width + 128 :]
    loss_out = sums[0] / (2.0 * features * count_total)
    loss_mix = sums[1] / (2.0 * features * count_total)
    return (
        output,
        loss_out,
        loss_mix,
        grad_in.astype(F32),
        attn_gain_grad,
        query_grad,
        keys_grad,
        values_grad,
        forget_grad.T,
        bias_grad,
        head_gain_grad,
        outgate_grad,
        out_grad,
        mlp_gain_grad,
        gate_grad,
        up_grad,
        down_grad,
    )


def solution(mesh):
    return jax.shard_map(
        per_device,
        mesh=mesh,
        in_specs=(
            P(("shard", "ctx"), None),
            P(("shard", "ctx"), None),
            P(("shard", "ctx"), None),
            P(("shard", "ctx"), None),
            P(("shard", "ctx")),
            P(("shard", "ctx")),
            P(("shard", "ctx")),
            P(("shard", "ctx"), "tp"),
            P(("shard", "ctx"), "tp"),
            P(("shard", "ctx"), "tp"),
            P(("shard", "ctx"), "tp"),
            P("tp", ("shard", "ctx")),
            P("tp", ("shard", "ctx")),
            P(("shard", "ctx"), "tp"),
            P(("shard", "ctx"), "tp"),
            P(("shard", "ctx")),
            P(("shard", "ctx"), "tp"),
            P(("shard", "ctx"), "tp"),
            P(("shard", "ctx"), "tp"),
        ),
        out_specs=(
            P(("shard", "ctx"), None),
            P(),
            P(),
            P(("shard", "ctx"), None),
            P(("shard", "ctx")),
            P(("shard", "ctx"), "tp"),
            P(("shard", "ctx"), "tp"),
            P(("shard", "ctx"), "tp"),
            P(("shard", "ctx"), "tp"),
            P("tp", ("shard", "ctx")),
            P("tp", ("shard", "ctx")),
            P(("shard", "ctx"), "tp"),
            P(("shard", "ctx"), "tp"),
            P(("shard", "ctx")),
            P(("shard", "ctx"), "tp"),
            P(("shard", "ctx"), "tp"),
            P(("shard", "ctx"), "tp"),
        ),
        check_vma=False,
    )
```

```python
import functools

import jax
import jax.numpy as jnp
from jax import lax
from jax.experimental import pallas as pl
from jax.experimental.pallas import tpu as pltpu
from jax.sharding import PartitionSpec as P

F32 = jnp.float32
BF = jnp.bfloat16
EPSILON = 1e-06
GATE_NORM = 8.0


def dot_nn(a, b):
    return lax.dot_general(a, b, (((1,), (0,)), ((), ())), preferred_element_type=F32)


def dot_nt(a, b):
    return lax.dot_general(a, b, (((1,), (1,)), ((), ())), preferred_element_type=F32)


def dot_tn(a, b):
    return lax.dot_general(a, b, (((0,), (0,)), ((), ())), preferred_element_type=F32)


def halves(x):
    hi = x.astype(BF)
    return hi, (x - hi.astype(F32)).astype(BF)


def sigmoid(u):
    return 1.0 / (1.0 + jnp.exp(-u))


def n_levels(tokens):
    return tokens.bit_length() - 1


def span_matrix(level, tokens):
    t = lax.broadcasted_iota(jnp.int32, (tokens, tokens), 0)
    u = lax.broadcasted_iota(jnp.int32, (tokens, tokens), 1)
    depth = n_levels(tokens)
    if level == depth:
        keep = u <= t
    elif level == depth + 1:
        keep = u > t
    else:
        half = 1 << level
        edge = (t & ~(2 * half - 1)) + half
        odd = (t & half) > 0
        keep = (odd & (u >= edge) & (u <= t)) | (~odd & (u > t) & (u < edge))
    return keep.astype(F32).astype(BF)


def odd_rows(level, tokens, columns):
    t = lax.broadcasted_iota(jnp.int32, (tokens, columns), 0)
    return (t & (1 << level)) > 0


def same_pair(level, tokens):
    t = lax.broadcasted_iota(jnp.int32, (tokens, tokens), 0)
    u = lax.broadcasted_iota(jnp.int32, (tokens, tokens), 1)
    return (t >> (level + 1)) == (u >> (level + 1))


def ends_kernel(pre_ref, resets_ref, keys_ref, values_ref, spans_ref, total_ref, ends_ref):
    tokens, slots = pre_ref.shape
    depth = n_levels(tokens)
    width = keys_ref.shape[1]
    pre = pre_ref[...]
    log_decay = (jnp.minimum(pre, 0.0) - jnp.log1p(jnp.exp(-jnp.abs(pre)))) / GATE_NORM
    write = 1.0 - jnp.exp(log_decay)
    hi, lo = halves(log_decay)
    resets = jnp.broadcast_to(resets_ref[...], (tokens, slots)).astype(BF)
    stacked = jnp.concatenate([hi, lo, resets], axis=1)
    for level in range(depth + 2):
        sums = dot_nn(span_matrix(level, tokens), stacked)
        gap = sums[:, :slots] + sums[:, slots : 2 * slots]
        live = sums[:, 2 * slots :] < 0.5
        span = jnp.where(live, jnp.exp(gap), 0.0)
        spans_ref[level] = span
        if level == depth:
            total_ref[...] = span[tokens - 1 :, :]
        if level == depth + 1:
            hi, lo = halves(span * write)
            ends_ref[:, :width] = dot_tn(hi, keys_ref[...]) + dot_tn(lo, keys_ref[...])
            ends_ref[:, width:] = dot_tn(hi, values_ref[...]) + dot_tn(lo, values_ref[...])


def run_ends(pre, resets, keys, values):
    tokens, slots = pre.shape
    depth = n_levels(tokens)
    return pl.pallas_call(
        ends_kernel,
        out_shape=(
            jax.ShapeDtypeStruct((depth + 2, tokens, slots), F32),
            jax.ShapeDtypeStruct((1, slots), F32),
            jax.ShapeDtypeStruct((slots, keys.shape[1] + values.shape[1]), F32),
        ),
        name="slot_ends",
    )(pre, resets, keys, values)


def decay_write(pre):
    log_decay = (jnp.minimum(pre, 0.0) - jnp.log1p(jnp.exp(-jnp.abs(pre)))) / GATE_NORM
    return jnp.exp(log_decay)


def forward_kernel(
    query_ref, keys_ref, values_ref, pre_ref, spans_ref, state_ref, gate_ref, gain_ref,
    probs_ref, pairs_ref, mixing_ref, mix_ref, gated_ref,
):
    tokens, slots = pre_ref.shape
    depth = n_levels(tokens)
    width = keys_ref.shape[1]
    scaling = width ** (-0.5)
    write = 1.0 - decay_write(pre_ref[...])
    query = query_ref[...]
    pairs = dot_nt(query, keys_ref[...])
    pairs_ref[...] = pairs
    t = lax.broadcasted_iota(jnp.int32, (tokens, tokens), 0)
    u = lax.broadcasted_iota(jnp.int32, (tokens, tokens), 1)
    diagonal = jnp.sum(jnp.where(t == u, pairs, 0.0), axis=1, keepdims=True)
    state_hi, state_lo = halves(state_ref[:, :width])
    head = spans_ref[depth]
    raw = head * (dot_nt(query, state_hi) + dot_nt(query, state_lo)) + diagonal * write
    for level in range(depth):
        span = spans_ref[level]
        odd = odd_rows(level, tokens, slots)
        left, left_lo = halves(jnp.where(same_pair(level, tokens), pairs, 0.0))
        right, right_lo = halves(jnp.where(odd, 0.0, span * write))
        pulled = dot_nn(left, right) + dot_nn(left_lo, right) + dot_nn(left, right_lo)
        raw = raw + jnp.where(odd, span, 0.0) * pulled
    scores = scaling * raw
    scores = scores - jnp.max(scores, axis=1, keepdims=True)
    raised = jnp.exp(scores)
    probs = raised / jnp.sum(raised, axis=1, keepdims=True)
    probs_ref[...] = probs
    probs = probs.astype(BF).astype(F32)
    mixing = jnp.zeros((tokens, tokens), F32)
    for level in reversed(range(depth)):
        span = spans_ref[level]
        odd = odd_rows(level, tokens, slots)
        left, left_lo = halves(jnp.where(odd, span * probs, 0.0))
        right, right_lo = halves(jnp.where(odd, 0.0, span * write))
        pushed = dot_nt(left, right) + dot_nt(left_lo, right) + dot_nt(left, right_lo)
        mixing = jnp.where(same_pair(level, tokens), pushed, mixing)
    mixing = jnp.where(t == u, jnp.sum(probs * write, axis=1, keepdims=True), mixing)
    mixing, mixing_lo = halves(mixing)
    mixing_ref[...] = mixing
    state_hi, state_lo = halves(state_ref[:, width:])
    carried, carried_lo = halves(probs * head)
    mix = dot_nn(mixing, values_ref[...]) + dot_nn(mixing_lo, values_ref[...])
    mix = mix + dot_nn(carried, state_hi) + dot_nn(carried, state_lo) + dot_nn(carried_lo, state_hi)
    mix_ref[...] = mix
    scale = lax.rsqrt(jnp.mean(mix * mix, axis=1, keepdims=True) + EPSILON)
    gate = gate_ref[...]
    gated_ref[...] = (mix * scale * gain_ref[...] * (gate * sigmoid(gate))).astype(BF)


def run_forward(query, keys, values, pre, spans, state, gate, gain):
    tokens, slots = pre.shape
    width = keys.shape[1]
    return pl.pallas_call(
        forward_kernel,
        out_shape=(
            jax.ShapeDtypeStruct((tokens, slots), F32),
            jax.ShapeDtypeStruct((tokens, tokens), F32),
            jax.ShapeDtypeStruct((tokens, tokens), BF),
            jax.ShapeDtypeStruct((tokens, width), F32),
            jax.ShapeDtypeStruct((tokens, width), BF),
        ),
        name="slot_forward",
    )(query, keys, values, pre, spans, state, gate, gain)


def backward_kernel(
    grad_ref, query_ref, keys_ref, values_ref, pre_ref, spans_ref, state_ref, gate_ref, gain_ref,
    probs_ref, pairs_ref, mixing_ref, mix_ref,
    gquery_ref, gkeys_ref, gvalues_ref, ggate_ref, ggain_ref, gwrite_ref, glog_ref, carry_ref,
):
    tokens, slots = pre_ref.shape
    depth = n_levels(tokens)
    width = keys_ref.shape[1]
    scaling = width ** (-0.5)
    gate = gate_ref[...]
    sig = sigmoid(gate)
    silu = gate * sig
    gain = gain_ref[...]
    mix = mix_ref[...]
    scale = lax.rsqrt(jnp.mean(mix * mix, axis=1, keepdims=True) + EPSILON)
    normed = mix * scale
    grad = grad_ref[...]
    ggate_ref[...] = (grad * gain * normed * (sig * (1.0 + gate * (1.0 - sig)))).astype(BF)
    ggain_ref[...] = jnp.sum(grad * normed * silu, axis=0, keepdims=True)
    inner = grad * gain * silu
    mix_grad = scale * (inner - normed * jnp.mean(normed * inner, axis=1, keepdims=True))
    mix_low = mix_grad.astype(BF)

    write = 1.0 - decay_write(pre_ref[...])
    query, keys, values = query_ref[...], keys_ref[...], values_ref[...]
    pairs = pairs_ref[...]
    pairs_t = dot_nt(keys, query)
    mix_rest = (mix_grad - mix_low.astype(F32)).astype(BF)
    weigh = dot_nt(mix_low, values) + dot_nt(mix_rest, values)
    weigh_t = dot_nt(values, mix_low) + dot_nt(values, mix_rest)
    t = lax.broadcasted_iota(jnp.int32, (tokens, tokens), 0)
    u = lax.broadcasted_iota(jnp.int32, (tokens, tokens), 1)
    pair_diag = jnp.sum(jnp.where(t == u, pairs, 0.0), axis=1, keepdims=True)
    weigh_diag = jnp.sum(jnp.where(t == u, weigh, 0.0), axis=1, keepdims=True)
    head = spans_ref[depth]
    probs = probs_ref[...]
    probs_low = probs.astype(BF).astype(F32)

    vstate_hi, vstate_lo = halves(state_ref[:, width:])
    head_probs = head * (
        dot_nt(mix_low, vstate_hi) + dot_nt(mix_low, vstate_lo) + dot_nt(mix_rest, vstate_hi)
    )
    probs_grad = head_probs + weigh_diag * write
    row_values, row_keys = [], []
    for level in range(depth):
        span = spans_ref[level]
        odd = odd_rows(level, tokens, slots)
        same = same_pair(level, tokens)
        right, right_lo = halves(jnp.where(odd, 0.0, span * write))
        reach = jnp.where(odd, span, 0.0)
        left, left_lo = halves(jnp.where(same, weigh, 0.0))
        term = reach * (dot_nn(left, right) + dot_nn(left_lo, right) + dot_nn(left, right_lo))
        row_values.append(term)
        left, left_lo = halves(jnp.where(same, pairs, 0.0))
        row_keys.append(reach * (dot_nn(left, right) + dot_nn(left_lo, right) + dot_nn(left, right_lo)))
        probs_grad = probs_grad + term
    scores_grad = probs * (probs_grad - jnp.sum(probs_grad * probs, axis=1, keepdims=True))
    scores_grad = scaling * scores_grad

    kstate_hi, kstate_lo = halves(state_ref[:, :width])
    head_keys = head * (dot_nt(query, kstate_hi) + dot_nt(query, kstate_lo))
    gwrite = pair_diag * scores_grad + weigh_diag * probs_low
    glog = dot_tn(span_matrix(depth, tokens), (head_keys * scores_grad + head_probs * probs_low).astype(BF))
    gpairs = jnp.zeros((tokens, tokens), F32)
    for level in reversed(range(depth)):
        span = spans_ref[level]
        odd = odd_rows(level, tokens, slots)
        same = same_pair(level, tokens)
        reach = jnp.where(odd, span, 0.0)
        source = jnp.where(odd, 0.0, span)
        key_side, key_rest = halves(reach * scores_grad)
        value_side, value_rest = halves(reach * probs_low)
        seen, seen_rest = halves(jnp.where(same, pairs_t, 0.0))
        felt, felt_rest = halves(jnp.where(same, weigh_t, 0.0))
        sent, sent_rest = halves(source * write)
        pushed = dot_nt(key_side, sent) + dot_nt(key_rest, sent) + dot_nt(key_side, sent_rest)
        gpairs = jnp.where(same, pushed, gpairs)
        column = source * (
            dot_nn(seen, key_side) + dot_nn(seen, key_rest) + dot_nn(seen_rest, key_side)
            + dot_nn(felt, value_side) + dot_nn(felt, value_rest) + dot_nn(felt_rest, value_side)
        )
        gwrite = gwrite + column
        moved = column * write + row_values[level] * probs_low + row_keys[level] * scores_grad
        spread = span_matrix(level, tokens)
        moved, moved_rest = halves(moved)
        glog = glog + dot_tn(spread, moved) + dot_tn(spread, moved_rest)
    gpairs = jnp.where(t == u, jnp.sum(scores_grad * write, axis=1, keepdims=True), gpairs)
    gpairs, gpairs_rest = halves(gpairs)
    gwrite_ref[...] = gwrite
    glog_ref[...] = glog
    key_head, key_head_rest = halves(scores_grad * head)
    gquery_ref[...] = (
        dot_nn(gpairs, keys)
        + dot_nn(gpairs_rest, keys)
        + dot_nn(key_head, kstate_hi)
        + dot_nn(key_head, kstate_lo)
        + dot_nn(key_head_rest, kstate_hi)
    )
    gkeys_ref[...] = dot_tn(gpairs, query) + dot_tn(gpairs_rest, query)
    gvalues_ref[...] = dot_tn(mixing_ref[...], mix_low)
    carry_ref[:, :width] = dot_tn(key_head, query) + dot_tn(key_head_rest, query)
    carry_ref[:, width:] = dot_tn((probs_low * head).astype(BF), mix_low)


def run_backward(grad, query, keys, values, pre, spans, state, gate, gain, probs, pairs, mixing, mix):
    tokens, slots = pre.shape
    width = keys.shape[1]
    wide = jax.ShapeDtypeStruct((tokens, width), F32)
    narrow = jax.ShapeDtypeStruct((tokens, slots), F32)
    return pl.pallas_call(
        backward_kernel,
        out_shape=(
            wide, wide, wide,
            jax.ShapeDtypeStruct((tokens, width), BF),
            jax.ShapeDtypeStruct((1, width), F32),
            narrow, narrow,
            jax.ShapeDtypeStruct((slots, 2 * width), F32),
        ),
        name="slot_backward",
    )(grad, query, keys, values, pre, spans, state, gate, gain, probs, pairs, mixing, mix)


def finish_kernel(
    gquery_ref, gkeys_ref, gvalues_ref, ggate_ref, gwrite_ref, glog_ref,
    keys_ref, values_ref, pre_ref, spans_ref, query_pre_ref, keys_pre_ref,
    state_ref, total_ref, ends_ref, gated_ref, out_ref, bias_ref,
):
    tokens, slots = pre_ref.shape
    depth = n_levels(tokens)
    width = keys_ref.shape[1]
    pre = pre_ref[...]
    decay = decay_write(pre)
    write = 1.0 - decay
    keys, values = keys_ref[...], values_ref[...]
    ends = ends_ref[...]
    ends_low = ends.astype(BF)
    tail = spans_ref[depth + 1]
    sent = (tail * write).astype(BF)
    column = tail * (dot_nt(keys, ends_low[:, :width]) + dot_nt(values, ends_low[:, width:]))
    glog = glog_ref[...] + dot_tn(span_matrix(depth + 1, tokens), (column * write).astype(BF))
    carried = lax.dot_general(
        jnp.ones((1, 2 * width), F32), ends * state_ref[...], (((1,), (1,)), ((), ())),
        precision=lax.Precision.HIGHEST, preferred_element_type=F32,
    )
    glog = glog + carried * total_ref[...]
    glog = glog - decay * (gwrite_ref[...] + column)
    def put(part, value):
        out_ref[:, part * width : (part + 1) * width] = value.astype(BF)

    put(0, gated_ref[...])
    u = query_pre_ref[...]
    s = sigmoid(u)
    put(1, gquery_ref[...] * (s * (1.0 + u * (1.0 - s))))
    u = keys_pre_ref[...]
    s = sigmoid(u)
    gkeys = gkeys_ref[...] + dot_nn(sent, ends_low[:, :width])
    put(2, gkeys * (s * (1.0 + u * (1.0 - s))))
    put(3, gvalues_ref[...] + dot_nn(sent, ends_low[:, width:]))
    put(4, ggate_ref[...])
    gforget = (glog * sigmoid(-pre) / GATE_NORM).astype(BF)
    gforget = jnp.concatenate([gforget, jnp.zeros((tokens, 128 - slots), BF)], axis=1)
    out_ref[:, 5 * width :] = gforget
    bias_ref[...] = jnp.sum(gforget.astype(F32), axis=0, keepdims=True)


def run_finish(gquery, gkeys, gvalues, ggate, gwrite, glog, keys, values, pre, spans, query_pre, keys_pre, state, total, ends, gated):
    tokens, slots = pre.shape
    width = keys.shape[1]
    return pl.pallas_call(
        finish_kernel,
        out_shape=(jax.ShapeDtypeStruct((tokens, 5 * width + 128), BF), jax.ShapeDtypeStruct((1, 128), F32)),
        name="slot_finish",
    )(gquery, gkeys, gvalues, ggate, gwrite, glog, keys, values, pre, spans, query_pre, keys_pre, state, total, ends, gated)


MESH = pl.DeviceIdType.MESH
GROUPED = ("shard", "ctx")


def greet(axes_of_peers):
    barrier = pltpu.get_barrier_semaphore()
    for peer in axes_of_peers:
        pl.semaphore_signal(barrier, inc=1, device_id=peer, device_id_type=MESH)
    pl.semaphore_wait(barrier, len(axes_of_peers))


def tp_peers():
    count = lax.axis_size("tp")
    me = lax.axis_index("tp")
    return me, [lax.rem(me + k, count) for k in range(1, count)]


CHUNKS = 4
LATENCY = 2.2
LEAD = 10
CLOSING = 3


def tp_line(partial_ref, full_ref, arrived, staged, sums_ref, finish, settle, send_a, recv_a, send_b, recv_b):
    count = lax.axis_size("tp")
    me = lax.axis_index("tp")
    rows = partial_ref.shape[1] // CHUNKS
    peers = [lax.rem(me + 1, count), lax.rem(me + count - 1, count)]

    def at_place(side, place):
        return place if side == 0 else count - 1 - place

    def cut(chunk):
        return pl.ds(chunk * rows, rows)

    def sum_copy(side, hop, chunk, source):
        return pltpu.make_async_remote_copy(
            src_ref=source,
            dst_ref=arrived.at[side, hop, chunk],
            send_sem=send_a.at[side, hop, chunk],
            recv_sem=recv_a.at[side, hop, chunk],
            device_id={"tp": peers[side]},
            device_id_type=MESH,
        )

    def row_copy(side, hop, chunk, block):
        return pltpu.make_async_remote_copy(
            src_ref=full_ref.at[block, cut(chunk)],
            dst_ref=full_ref.at[block, cut(chunk)],
            send_sem=send_b.at[side, hop, chunk],
            recv_sem=recv_b.at[side, hop, chunk],
            device_id={"tp": peers[side]},
            device_id_type=MESH,
        )

    def own(side, hop, chunk):
        return partial_ref.at[at_place(side, count - 1 - hop), cut(chunk)]

    def send_own(chunk):
        for side in range(2):

            @pl.when(me == at_place(side, 0))
            def _():
                for hop in range(count - 1):
                    sum_copy(side, hop, chunk, own(side, hop, chunk)).start()

    def add_hop(side, place, hop, chunk):
        @pl.when(me == at_place(side, place))
        def _():
            slot = staged.at[side, hop, chunk]
            copy = sum_copy(side, hop, chunk, slot)
            copy.wait_recv()
            slot[...] = (own(side, hop, chunk)[...].astype(F32) + arrived[side, hop, chunk].astype(F32)).astype(BF)
            copy.start()

    def close(chunk):
        sums_ref[...] = partial_ref[me, cut(chunk)].astype(F32)
        for side in range(2):
            place = me if side == 0 else count - 1 - me
            hop = jnp.minimum(count - 1 - place, count - 2)

            @pl.when(place > 0)
            def _():
                sum_copy(side, hop, chunk, staged.at[side, hop, chunk]).wait_recv()
                sums_ref[...] += arrived[side, hop, chunk].astype(F32)

        finish(chunk, sums_ref[...])
        for side in range(2):

            @pl.when(me != at_place(side, count - 1))
            def _():
                row_copy(side, 0, chunk, me).start()

    def forward(side, place, distance, chunk):
        @pl.when(me == at_place(side, place))
        def _():
            block = at_place(side, place - distance)
            row_copy(side, distance - 1, chunk, block).wait_recv()
            if place < count - 1:
                row_copy(side, distance, chunk, block).start()

    step = 1 + LATENCY
    events = [(900, settle)]
    for chunk in range(CHUNKS):
        base = (count - 1) * chunk
        closed = base + (count - 1) + (count - 2) * LATENCY
        events.append((base - LEAD * (count - 1), functools.partial(send_own, chunk)))
        events.append((closed, functools.partial(close, chunk)))
        for side in range(2):
            for place in range(1, count):
                for hop in range(count - 1 - place):
                    due = base + hop + place * step
                    events.append((due, functools.partial(add_hop, side, place, hop, chunk)))
                for distance in range(1, place + 1):
                    due = closed + CLOSING + distance * step
                    if place == count - 1:
                        due += 1000
                    events.append((due, functools.partial(forward, side, place, distance, chunk)))
    for _, event in sorted(events, key=lambda event: event[0]):
        event()

    def drain():
        for side in range(2):
            for place in range(count - 1):

                @pl.when(me == at_place(side, place))
                def _():
                    for chunk in range(CHUNKS):
                        for hop in range(count - 1 - place):
                            sum_copy(side, hop, chunk, staged.at[side, hop, chunk]).wait_send()
                        for hop in range(place + 1):
                            row_copy(side, hop, chunk, at_place(side, place - hop)).wait_send()

    return drain


def plane_peers():
    shards, ctxs = lax.axis_size("shard"), lax.axis_size("ctx")
    devices = shards * ctxs
    me = lax.axis_index("shard") * ctxs + lax.axis_index("ctx")
    peers = [lax.rem(me + k, devices) for k in range(1, devices)]
    places = [{"shard": lax.div(peer, ctxs), "ctx": lax.rem(peer, ctxs)} for peer in peers]
    return me, peers, places


def start_scatter(sources, targets, send_sems, recv_sems):
    me, peers, places = plane_peers()
    copies = []
    for i, (source, target) in enumerate(zip(sources, targets)):
        step = target.shape[2]

        def block(at):
            if len(source.shape) == 3:
                return source.at[at]
            return source.at[:, pl.ds(pl.multiple_of(at * step, step), step)]

        for k, (peer, place) in enumerate(zip(peers, places)):
            copy = pltpu.make_async_remote_copy(
                src_ref=block(peer),
                dst_ref=target.at[me],
                send_sem=send_sems.at[i, k],
                recv_sem=recv_sems.at[i, k],
                device_id=place,
                device_id_type=MESH,
            )
            copy.start()
            copies.append(copy)
    for source, target in zip(sources, targets):
        target[me] = block_of(source, me, target.shape[2])
    return copies


def block_of(source, at, step):
    if len(source.shape) == 3:
        return source[at]
    return source[:, pl.ds(pl.multiple_of(at * step, step), step)]


def spread_kernel(n_parts, n_packed, *refs):
    parts, refs = refs[:n_parts], refs[n_parts:]
    packed, refs = refs[:n_packed], refs[n_packed:]
    if n_packed:
        forget_ref, mask_ref, vectors, refs = refs[0], refs[1], refs[2:6], refs[6:]
        out_ref, rows_ref, pack_ref, slab, part_sems, own_sem, send_sems, recv_sems = refs[:8]
        row_ref, row_send, row_recv, pack_slab, pack_sems, pack_sem = refs[8:]
    else:
        out_ref, slab, part_sems, own_sem, send_sems, recv_sems = refs
    shard, core = lax.axis_index("shard"), lax.axis_index("ctx")
    me, _, places = plane_peers()
    across = shard + 1 - 2 * lax.rem(shard, 2)
    along = lax.rem(shard + 2, 4)
    corner = lax.rem(across + 2, 4)
    other = 1 - core
    to_x, to_y, to_core = {"shard": across}, {"shard": along}, {"ctx": other}
    rows = slab.shape[0]
    half = rows // 2

    def load_all(sources, target, sems):
        loads = []
        start = 0
        for i, part in enumerate(sources):
            load = pltpu.make_async_copy(part, target.at[:, pl.ds(start, part.shape[1])], sems.at[i])
            load.start()
            loads.append(load)
            start += part.shape[1]
        return loads

    loads = load_all(parts, slab, part_sems)
    if n_packed:
        room = jnp.zeros((rows, 128 - forget_ref.shape[1]), BF)
        slab[:, slab.shape[1] - 128 :] = jnp.concatenate([forget_ref[...], room], axis=1)
        row_ref[...] = jnp.zeros_like(row_ref)
        for i, vector in enumerate(vectors):
            row_ref[i : i + 1, : vector.shape[1]] = vector[...].astype(F32)
        count = jnp.sum(mask_ref[...].astype(F32), axis=1, keepdims=True)
        row_ref[4:5, :] = jnp.broadcast_to(count, (1, row_ref.shape[1]))
    greet(places)
    for load in loads:
        load.wait()
    keep = pltpu.make_async_copy(slab, out_ref.at[pl.ds(pl.multiple_of(me * rows, rows), rows)], own_sem)
    keep.start()

    def landing(block, part):
        return out_ref.at[pl.ds(pl.multiple_of(block * rows + part * half, half), half)]

    started = []

    def send(kind, source, block, part, place):
        copy = pltpu.make_async_remote_copy(
            src_ref=source,
            dst_ref=landing(block, part),
            send_sem=send_sems.at[kind],
            recv_sem=recv_sems.at[kind],
            device_id=place,
            device_id_type=MESH,
        )
        copy.start()
        started.append(copy)

    def receive(kind, block, part, place):
        region = landing(block, part)
        pltpu.make_async_remote_copy(
            src_ref=region,
            dst_ref=region,
            send_sem=send_sems.at[kind],
            recv_sem=recv_sems.at[kind],
            device_id=place,
            device_id_type=MESH,
        ).wait_recv()

    def own(part):
        return slab.at[pl.ds(part * half, half)]

    def block(place, at_core):
        return 2 * place + at_core

    send(0, own(0), me, 0, to_x)
    send(1, own(1), me, 1, to_y)
    if n_packed:
        copies = start_sums(row_ref, rows_ref, row_send, row_recv, [], places, me)
    send(2, own(1), me, 1, to_x)
    send(3, own(0), me, 0, to_y)
    send(4, own(0), me, 0, to_core)
    send(5, own(1), me, 1, to_core)
    if n_packed:
        for load in load_all(packed, pack_slab, pack_sems):
            load.wait()
        store = pltpu.make_async_copy(pack_slab, pack_ref, pack_sem)
        store.start()
    x_block, y_block, far_block = block(across, core), block(along, core), block(corner, core)
    receive(0, x_block, 0, to_x)
    send(6, landing(x_block, 0), x_block, 0, to_y)
    send(8, landing(x_block, 0), x_block, 0, to_core)
    receive(1, y_block, 1, to_y)
    send(7, landing(y_block, 1), y_block, 1, to_x)
    send(9, landing(y_block, 1), y_block, 1, to_core)
    receive(2, x_block, 1, to_x)
    send(10, landing(x_block, 1), x_block, 1, to_core)
    receive(3, y_block, 0, to_y)
    send(11, landing(y_block, 0), y_block, 0, to_core)
    receive(6, far_block, 0, to_y)
    send(12, landing(far_block, 0), far_block, 0, to_core)
    receive(7, far_block, 1, to_x)
    send(13, landing(far_block, 1), far_block, 1, to_core)
    for kind, place, part in (
        (4, shard, 0), (5, shard, 1), (8, across, 0), (9, along, 1), (10, across, 1), (11, along, 0),
        (12, corner, 0), (13, corner, 1),
    ):
        receive(kind, block(place, other), part, to_core)
    for copy in started:
        copy.wait_send()
    keep.wait()
    if n_packed:
        store.wait()
        for copy in copies:
            copy.wait()


def run_spread(name, collective_id, parts, packed=(), forget=None, mask=None, vectors=()):
    devices = lax.axis_size(GROUPED)
    rows = parts[0].shape[0]
    columns = sum(part.shape[1] for part in parts) + (128 if packed else 0)
    anywhere = pl.BlockSpec(memory_space=pl.ANY)
    in_specs, out_specs = [anywhere] * len(parts), [anywhere]
    out_shape = [jax.ShapeDtypeStruct((devices * rows, columns), BF)]
    scratch = [
        pltpu.VMEM((rows, columns), BF),
        pltpu.SemaphoreType.DMA((len(parts),)),
        pltpu.SemaphoreType.DMA,
        *[pltpu.SemaphoreType.DMA((14,))] * 2,
    ]
    args = list(parts)
    if packed:
        packed_shape = (rows, sum(part.shape[1] for part in packed))
        args += [*packed, forget, mask, *vectors]
        in_specs += [*[anywhere] * len(packed), *[pl.BlockSpec(memory_space=pltpu.VMEM)] * (2 + len(vectors))]
        out_specs += [pl.BlockSpec(memory_space=pltpu.VMEM), anywhere]
        out_shape += [jax.ShapeDtypeStruct((devices, 8, rows), F32), jax.ShapeDtypeStruct(packed_shape, BF)]
        scratch += [
            pltpu.VMEM((8, rows), F32),
            *[pltpu.SemaphoreType.DMA((devices - 1,))] * 2,
            pltpu.VMEM(packed_shape, BF),
            pltpu.SemaphoreType.DMA((len(packed),)),
            pltpu.SemaphoreType.DMA,
        ]
    return pl.pallas_call(
        functools.partial(spread_kernel, len(parts), len(packed)),
        out_shape=tuple(out_shape),
        in_specs=in_specs,
        out_specs=tuple(out_specs),
        scratch_shapes=scratch,
        compiler_params=pltpu.CompilerParams(collective_id=collective_id, has_side_effects=True),
        name=name,
    )(*args)


def start_sums(row_ref, landed, send_sems, recv_sems, peers, places, me):
    copies = []
    landed[me] = row_ref[...]
    for k, place in enumerate(places):
        copy = pltpu.make_async_remote_copy(
            src_ref=row_ref,
            dst_ref=landed.at[me],
            send_sem=send_sems.at[k],
            recv_sem=recv_sems.at[k],
            device_id=place,
            device_id_type=MESH,
        )
        copy.start()
        copies.append(copy)
    return copies


def summed(landed):
    total = landed[0]
    for k in range(1, landed.shape[0]):
        total = total + landed[k]
    return total


def exchange_kernel(epilogue, n_in, n_rows, n_moved, n_sums, partial_ref, *refs):
    me, peers = tp_peers()
    inputs, refs = refs[:n_in], refs[n_in:]
    sources, refs = refs[:n_moved], refs[n_moved:]
    full_ref, refs = refs[0], refs[1:]
    outputs, refs = refs[:n_rows], refs[n_rows:]
    targets, refs = refs[:n_moved], refs[n_moved:]
    sums, refs = refs[: 2 * n_sums], refs[2 * n_sums :]
    arrived, staged, sums_ref, send_a, recv_a, send_b, recv_b, send_m, recv_m = refs[:9]
    own, plane, places = plane_peers()
    across = [{"tp": peer} for peer in peers]
    greet(across + (places if n_moved or n_sums else []))
    moves = start_scatter(sources, targets, send_m, recv_m)
    rows = full_ref.shape[1] // CHUNKS
    started = []

    def finish(chunk, total):
        part = pl.ds(chunk * rows, rows)
        full_ref[me, part] = epilogue(total, me, part, chunk == 0, inputs, outputs)
        if n_sums and chunk == CHUNKS - 1:
            row_ref, in_plane, _, _, send_p, recv_p = refs[9:15]
            width = outputs[0].shape[1]
            row_ref[:, :width] = outputs[0][...]
            row_ref[:, width:] = inputs[-1][...]
            started.extend(start_sums(row_ref, in_plane, send_p, recv_p, plane, places, own))

    def settle():
        if not n_sums:
            return
        row_ref, in_plane, plane_row, in_tp, send_p, recv_p, send_t, recv_t = refs[9:]
        for copy in started:
            copy.wait()
        plane_row[...] = summed(in_plane)
        sums[0][...] = plane_row[...]
        for copy in start_sums(plane_row, in_tp, send_t, recv_t, peers, across, me):
            copy.wait()
        sums[1][...] = summed(in_tp)

    drain = tp_line(
        partial_ref, full_ref, arrived, staged, sums_ref, finish, settle, send_a, recv_a, send_b, recv_b
    )
    drain()
    for copy in moves:
        copy.wait()


def run_exchange(epilogue, name, collective_id, partial, inputs, row_outputs, moved=(), summing=False):
    tp = lax.axis_size("tp")
    devices = lax.axis_size(GROUPED)
    tokens, columns = partial.shape
    share = tokens // tp
    partial = partial.reshape(tp, share, columns)
    step = columns // devices
    if step % 128:
        moved = [m.reshape(tokens, devices, step).transpose(1, 0, 2) for m in moved]
    count = len(moved)
    scratch = [
        *[pltpu.VMEM((2, tp - 1, CHUNKS, share // CHUNKS, columns), BF)] * 2,
        pltpu.VMEM((share // CHUNKS, columns), F32),
        *[pltpu.SemaphoreType.DMA((2, tp - 1, CHUNKS))] * 4,
        *[pltpu.SemaphoreType.DMA((max(count, 1), devices - 1))] * 2,
    ]
    extra = ()
    if summing:
        row = row_outputs[0].shape[1] + inputs[-1].shape[1]
        extra = (jax.ShapeDtypeStruct((1, row), F32),) * 2
        scratch += [
            pltpu.VMEM((1, row), F32),
            pltpu.VMEM((devices, 1, row), F32),
            pltpu.VMEM((1, row), F32),
            pltpu.VMEM((tp, 1, row), F32),
            *[pltpu.SemaphoreType.DMA((devices - 1,))] * 2,
            *[pltpu.SemaphoreType.DMA((tp - 1,))] * 2,
        ]
    out_shape = (
        jax.ShapeDtypeStruct((tp, share, columns), BF),
        *row_outputs,
        *[jax.ShapeDtypeStruct((devices, tokens, step), BF)] * count,
        *extra,
    )
    outs = pl.pallas_call(
        functools.partial(exchange_kernel, epilogue, len(inputs), len(row_outputs), count, int(summing)),
        out_shape=out_shape,
        in_specs=[pl.BlockSpec(memory_space=pltpu.VMEM)] * (1 + len(inputs) + count),
        out_specs=tuple([pl.BlockSpec(memory_space=pltpu.VMEM)] * len(out_shape)),
        scratch_shapes=scratch,
        compiler_params=pltpu.CompilerParams(collective_id=collective_id, has_side_effects=True),
        name=name,
    )(partial, *inputs, *moved)
    start = 1 + len(row_outputs)
    return (
        outs[0].reshape(tokens, columns),
        *outs[1:start],
        *[o.reshape(devices * tokens, step) for o in outs[start : start + count]],
        *outs[start + count :],
    )


def middle_epilogue(total, me, part, first, inputs, outputs):
    hidden_ref, gain_ref = inputs
    (branch_ref,) = outputs
    branch_ref[part, :] = total
    middle = hidden_ref[me, part].astype(F32) + total
    scale = lax.rsqrt(jnp.mean(middle * middle, axis=1, keepdims=True) + EPSILON)
    return (middle * scale * gain_ref[...]).astype(BF)


def result_epilogue(total, me, part, first, inputs, outputs):
    hidden_ref, branch_ref, teacher_out_ref, teacher_mix_ref, cotangent_ref, mask_ref, scale_ref = inputs
    grad_ref, losses_ref = outputs
    branch = branch_ref[part, :]
    result = hidden_ref[me, part].astype(F32) + branch + total
    mask = mask_ref[me, part]
    gap = result - teacher_out_ref[me, part].astype(F32)
    gap_mix = branch - teacher_mix_ref[me, part].astype(F32)
    loss_out = jnp.sum(mask * (gap * gap), keepdims=True)
    loss_mix = jnp.sum(mask * (gap_mix * gap_mix), keepdims=True)
    lane = lax.broadcasted_iota(jnp.int32, (1, 128), 1)
    losses = jnp.where(lane == 0, loss_out, 0.0) + jnp.where(lane == 1, loss_mix, 0.0)
    losses_ref[...] = losses if first else losses_ref[...] + losses
    grad_ref[part, :] = cotangent_ref[me, part].astype(F32) + scale_ref[...] * mask * gap
    return result.astype(BF)


def norm_back(grad, rows, gain):
    scale = lax.rsqrt(jnp.mean(rows * rows, axis=1, keepdims=True) + EPSILON)
    unit = rows * scale
    gain_grad = jnp.sum(grad * unit, axis=0, keepdims=True)
    inner = grad * gain
    return scale * (inner - unit * jnp.mean(unit * inner, axis=1, keepdims=True)), gain_grad


def branch_epilogue(total, me, part, first, inputs, outputs):
    hidden_ref, branch_ref, teacher_mix_ref, grad_ref, mask_ref, scale_ref, gain_ref = inputs
    grad_middle_ref, gain_grad_ref = outputs
    branch = branch_ref[part, :]
    back, gain_grad = norm_back(total, hidden_ref[me, part].astype(F32) + branch, gain_ref[...])
    gain_grad_ref[...] = gain_grad if first else gain_grad_ref[...] + gain_grad
    grad_middle = back + grad_ref[part, :]
    grad_middle_ref[part, :] = grad_middle
    gap_mix = branch - teacher_mix_ref[me, part].astype(F32)
    return (grad_middle + scale_ref[...] * mask_ref[me, part] * gap_mix).astype(BF)


def input_epilogue(total, me, part, first, inputs, outputs):
    hidden_ref, grad_middle_ref, gain_ref = inputs[:3]
    (gain_grad_ref,) = outputs
    back, gain_grad = norm_back(total, hidden_ref[me, part].astype(F32), gain_ref[...])
    gain_grad_ref[...] = gain_grad if first else gain_grad_ref[...] + gain_grad
    return (back + grad_middle_ref[part, :]).astype(BF)


def weights_kernel(segments, n_rows, n_columns, n_turned, *refs):
    rows, refs = refs[:n_rows], refs[n_rows:]
    columns, refs = refs[:n_columns], refs[n_columns:]
    straight, outs = refs[:n_turned], refs[n_turned:]
    at = pl.program_id(0)
    for ref, out in zip(straight, outs[len(segments) :]):
        out[...] = ref[...].T
    turned = [ref[...].T for ref in rows]
    for (row, column, start, width), out in zip(segments, outs):
        term = dot_nn(turned[row], columns[column][:, pl.ds(start, width)])

        @pl.when(at == 0)
        def _():
            out[...] = term

        @pl.when(at > 0)
        def _():
            out[...] += term


def run_weights(name, rows, columns, segments, turned):
    tokens, features = rows[0].shape
    block = 512
    whole = lambda width: pl.BlockSpec((block, width), lambda i: (i, 0))
    shapes = [(features, segment[3]) for segment in segments]
    return pl.pallas_call(
        functools.partial(weights_kernel, segments, len(rows), len(columns), len(turned)),
        grid=(tokens // block,),
        in_specs=[*[whole(features)] * len(rows), *[whole(c.shape[1]) for c in (*columns, *turned)]],
        out_specs=(
            *[pl.BlockSpec(shape, lambda i: (0, 0)) for shape in shapes],
            *[pl.BlockSpec((t.shape[1], block), lambda i: (0, i)) for t in turned],
        ),
        out_shape=(
            *[jax.ShapeDtypeStruct(shape, F32) for shape in shapes],
            *[jax.ShapeDtypeStruct((t.shape[1], tokens), BF) for t in turned],
        ),
        compiler_params=pltpu.CompilerParams(dimension_semantics=("arbitrary",)),
        name=name,
    )(*rows, *columns, *turned)


def attention_weights_kernel(out_rows_ref, rows_ref, block_ref, forget_ref, *refs):
    outs, forget_out = refs[:5], refs[5]
    at = pl.program_id(0)

    @pl.when(at == 0)
    def _():
        forget_out[...] = dot_nn(rows_ref[...], forget_ref[...]).T[: forget_out.shape[0]]
        outs[0][...] = dot_nn(out_rows_ref[...], block_ref[...])

    @pl.when(at > 0)
    def _():
        term = dot_nn(rows_ref[...], block_ref[...])
        for i, out in enumerate(outs[1:]):

            @pl.when(at == i + 1)
            def _():
                out[...] = term


def run_attention_weights(out_rows, rows, gathered_all, width, slots):
    features, tokens = rows.shape
    fixed = lambda shape: pl.BlockSpec(shape, lambda i: (0, 0))
    last = 5 * width // 128
    shapes = [(features, width)] * 5 + [(slots, features)]
    return pl.pallas_call(
        attention_weights_kernel,
        grid=(5,),
        in_specs=[
            fixed((features, tokens)), fixed((features, tokens)),
            pl.BlockSpec((tokens, width), lambda i: (0, i)),
            pl.BlockSpec((tokens, 128), lambda i: (0, last)),
        ],
        out_specs=tuple(fixed(shape) for shape in shapes),
        out_shape=tuple(jax.ShapeDtypeStruct(shape, F32) for shape in shapes),
        compiler_params=pltpu.CompilerParams(dimension_semantics=("arbitrary",)),
        name="attention_weights",
    )(out_rows, rows, gathered_all, gathered_all)


def passed_along(value, axis, steps):
    count = lax.axis_size(axis)
    leading, last = (max(0, -steps), min(count, count - steps))
    return lax.ppermute(value, axis, [(source, source + steps) for source in range(leading, last)])


def relay(value, decay, axis, steps):
    carried = passed_along(value, axis, steps)
    for _ in range(lax.axis_size(axis) - 2):
        carried = passed_along(value + decay * carried, axis, steps)
    return carried


def gathered(value):
    return lax.all_gather(value, GROUPED, axis=0, tiled=True)


def per_device(
    hidden_in,
    cotangent,
    teacher_out,
    teacher_mix,
    valid_mask,
    doc_start,
    attn_gain,
    w_query,
    w_key,
    w_value,
    w_forget,
    forget_bias,
    head_gain,
    w_outgate,
    w_out,
    mlp_gain,
    w_gate,
    w_up,
    w_down,
):
    tokens, features = hidden_in.shape
    devices = lax.axis_size(GROUPED)
    tp = lax.axis_size("tp")
    share = tokens // tp
    rows = w_query.shape[0]
    width = w_query.shape[1]
    slots = w_forget.shape[1]
    units = w_gate.shape[1]
    tokens_all = tokens * devices
    mask_flat = valid_mask.astype(F32)

    vectors = [attn_gain.reshape(1, -1), mlp_gain.reshape(1, -1), head_gain, forget_bias]
    attn_parts = [w_query, w_key, w_value, w_outgate]
    mlp_parts = [w_gate, w_up, w_down]
    if (lax.axis_size("shard"), lax.axis_size("ctx")) == (4, 2):
        first, row_all, pack = run_spread(
            "gather_attention", 5, attn_parts, mlp_parts, w_forget, valid_mask.reshape(1, -1), vectors
        )
        second = gathered(pack)
        out_own, first = lax.optimization_barrier((w_out, first))
        (out_w,) = run_spread("gather_out", 6, [out_own])
        first, row_all, out_w = lax.optimization_barrier((first, row_all, out_w))
    else:
        vectors.append(jnp.sum(mask_flat).reshape(1, 1))
        row = [jnp.pad(v.astype(F32), ((0, 0), (0, rows - v.shape[1]))) for v in vectors]
        row_all = gathered(jnp.concatenate(row, axis=0)[None])
        forget_w = jnp.pad(w_forget, ((0, 0), (0, 128 - slots)))
        first = gathered(jnp.concatenate([*attn_parts, forget_w, w_out], axis=1))
        pack, first = lax.optimization_barrier((jnp.concatenate(mlp_parts, axis=1), first))
        second = gathered(pack)
        out_w = first[:, 4 * width + 128 :]
        first = first[:, : 4 * width + 128]

    attn_scale = row_all[:, 0].reshape(1, -1)
    mlp_scale = row_all[:, 1].reshape(1, -1)
    head_scale = row_all[:, 2, : width // devices].reshape(1, width)
    bias = row_all[:, 3, : slots // devices].reshape(1, slots)
    count_total = jnp.sum(row_all[:, 4, 0])
    loss_scale = (tokens_all / count_total).reshape(1, 1)

    hidden_f = hidden_in.astype(F32)
    scale = lax.rsqrt(jnp.mean(hidden_f * hidden_f, axis=-1, keepdims=True) + EPSILON)
    normed_in = (hidden_f * scale * attn_scale).astype(BF)
    pre_all = dot_nn(normed_in, first)
    query_pre = pre_all[:, :width]
    keys_pre = pre_all[:, width : 2 * width]
    query = jax.nn.silu(query_pre).astype(BF)
    keys = jax.nn.silu(keys_pre).astype(BF)
    values = pre_all[:, 2 * width : 3 * width].astype(BF)
    gate_pre = pre_all[:, 3 * width : 4 * width]
    forget_pre = pre_all[:, 4 * width : 4 * width + slots] + bias
    resets = doc_start.astype(F32)[:, None]

    spans, total, ends = run_ends(forget_pre, resets, keys, values)
    decay = total.reshape(slots, 1)
    state = relay(ends, decay, "ctx", 1)
    probs, pairs, mixing, mix, gated = run_forward(
        query, keys, values, forget_pre, spans, state, gate_pre, head_scale
    )
    gate_w = second[:, :units]
    up_w = second[:, units : 2 * units]
    down_w = second[:, 2 * units :]

    by_share = lambda tensor: tensor.reshape(tp, share, -1)
    hidden_s, teacher_out_s, teacher_mix_s, cotangent_s = map(by_share, (hidden_in, teacher_out, teacher_mix, cotangent))
    mask_s = by_share(mask_flat)
    narrow = lambda *shape: jax.ShapeDtypeStruct(shape, F32)

    partial = dot_nt(gated, out_w).astype(BF)
    partial, mask_s, loss_scale = lax.optimization_barrier((partial, mask_s, loss_scale))
    normed_mid, branch = run_exchange(
        middle_epilogue, "sum_branch", 1, partial, (hidden_s, mlp_scale),
        (narrow(share, features),),
    )
    gate_val = dot_nn(normed_mid, gate_w)
    up_val = dot_nn(normed_mid, up_w)
    hidden_units = (jax.nn.silu(gate_val) * up_val).astype(BF)
    units_all = gathered(hidden_units)
    output, grad_result, losses, normed_in_c, normed_mid_c = run_exchange(
        result_epilogue, "sum_result", 2, dot_nt(hidden_units, down_w).astype(BF),
        (hidden_s, branch, teacher_out_s, teacher_mix_s, cotangent_s, mask_s, loss_scale),
        (narrow(share, features), narrow(1, 128)),
        moved=(normed_in, normed_mid),
    )
    gap = output.astype(F32) - teacher_out.astype(F32)
    grad_mlp = (cotangent.astype(F32) + loss_scale * mask_flat[:, None] * gap).astype(BF)
    grad_units = dot_nn(grad_mlp, down_w)
    gate_sig = jax.nn.sigmoid(gate_val)
    grad_gate_val = (grad_units * up_val * (gate_sig * (1.0 + gate_val * (1.0 - gate_sig)))).astype(BF)
    grad_up_val = (grad_units * (gate_val * gate_sig)).astype(BF)
    grad_both = jnp.concatenate([grad_gate_val, grad_up_val], axis=1)
    partial = dot_nt(grad_both, second[:, : 2 * units]).astype(BF)
    units_all, grad_both = lax.optimization_barrier((units_all, grad_both))
    partial = lax.optimization_barrier((partial, grad_both))[0]
    mlp_all = gathered(grad_both)
    grad_branch, grad_middle, mlp_gain_part, grad_mlp_c = run_exchange(
        branch_epilogue, "sum_middle", 3, partial,
        (hidden_s, branch, teacher_mix_s, grad_result, mask_s, loss_scale, mlp_scale),
        (narrow(share, features), narrow(1, features)),
        moved=(grad_mlp,),
    )
    grad_gated = dot_nn(grad_branch, out_w)
    gquery, gkeys, gvalues, ggate, head_gain_part, gwrite, glog, carry = run_backward(
        grad_gated, query, keys, values, forget_pre, spans, state, gate_pre, head_scale, probs, pairs, mixing, mix
    )
    later = relay(carry, decay, "ctx", -1)
    grad_pre, bias_part = run_finish(
        gquery, gkeys, gvalues, ggate, gwrite, glog, keys, values, forget_pre, spans, query_pre, keys_pre,
        state, total, later, gated,
    )
    partial = dot_nt(grad_pre[:, width:], first).astype(BF)
    mlp_all, grad_pre = lax.optimization_barrier((mlp_all, grad_pre))
    partial = lax.optimization_barrier((partial, grad_pre))[0]
    attn_all = gathered(grad_pre)
    grad_in, _, grad_branch_c, plane_sums, all_sums = run_exchange(
        input_epilogue, "sum_input", 4, partial,
        (hidden_s, grad_middle, attn_scale, jnp.concatenate([mlp_gain_part, head_gain_part, bias_part, losses], axis=1)),
        (narrow(1, features),), moved=(grad_branch,), summing=True,
    )
    gate_grad, up_grad, down_grad, turned_branch, turned_in = run_weights(
        "mlp_weights", (normed_mid_c, grad_mlp_c), (mlp_all, units_all),
        ((0, 0, 0, units), (0, 0, units, units), (1, 1, 0, units)), (grad_branch_c, normed_in_c),
    )
    out_grad, query_grad, keys_grad, values_grad, outgate_grad, forget_grad = run_attention_weights(
        turned_branch, turned_in, attn_all, width, slots
    )
    index = lax.axis_index(GROUPED)

    cut = lambda row, size: lax.dynamic_slice_in_dim(row, index * size, size, axis=1)
    attn_gain_grad = cut(all_sums[:, :features], features // devices).reshape(-1)
    mlp_gain_grad = cut(all_sums[:, features : 2 * features], features // devices).reshape(-1)
    head_gain_grad = cut(plane_sums[:, 2 * features : 2 * features + width], width // devices)
    bias_grad = cut(plane_sums[:, 2 * features + width : 2 * features + width + slots], slots // devices)
    sums = all_sums[0, 2 * features + width + 128 :]
    loss_out = sums[0] / (2.0 * features * count_total)
    loss_mix = sums[1] / (2.0 * features * count_total)
    return (
        output,
        loss_out,
        loss_mix,
        grad_in.astype(F32),
        attn_gain_grad,
        query_grad,
        keys_grad,
        values_grad,
        forget_grad.T,
        bias_grad,
        head_gain_grad,
        outgate_grad,
        out_grad,
        mlp_gain_grad,
        gate_grad,
        up_grad,
        down_grad,
    )


def solution(mesh):
    return jax.shard_map(
        per_device,
        mesh=mesh,
        in_specs=(
            P(("shard", "ctx"), None),
            P(("shard", "ctx"), None),
            P(("shard", "ctx"), None),
            P(("shard", "ctx"), None),
            P(("shard", "ctx")),
            P(("shard", "ctx")),
            P(("shard", "ctx")),
            P(("shard", "ctx"), "tp"),
            P(("shard", "ctx"), "tp"),
            P(("shard", "ctx"), "tp"),
            P(("shard", "ctx"), "tp"),
            P("tp", ("shard", "ctx")),
            P("tp", ("shard", "ctx")),
            P(("shard", "ctx"), "tp"),
            P(("shard", "ctx"), "tp"),
            P(("shard", "ctx")),
            P(("shard", "ctx"), "tp"),
            P(("shard", "ctx"), "tp"),
            P(("shard", "ctx"), "tp"),
        ),
        out_specs=(
            P(("shard", "ctx"), None),
            P(),
            P(),
            P(("shard", "ctx"), None),
            P(("shard", "ctx")),
            P(("shard", "ctx"), "tp"),
            P(("shard", "ctx"), "tp"),
            P(("shard", "ctx"), "tp"),
            P(("shard", "ctx"), "tp"),
            P("tp", ("shard", "ctx")),
            P("tp", ("shard", "ctx")),
            P(("shard", "ctx"), "tp"),
            P(("shard", "ctx"), "tp"),
            P(("shard", "ctx")),
            P(("shard", "ctx"), "tp"),
            P(("shard", "ctx"), "tp"),
            P(("shard", "ctx"), "tp"),
        ),
        check_vma=False,
    )
```

```python
import functools

import jax
import jax.numpy as jnp
from jax import lax
from jax.experimental import pallas as pl
from jax.experimental.pallas import tpu as pltpu
from jax.sharding import PartitionSpec as P

F32 = jnp.float32
BF = jnp.bfloat16
EPSILON = 1e-06
GATE_NORM = 8.0


def dot_nn(a, b):
    return lax.dot_general(a, b, (((1,), (0,)), ((), ())), preferred_element_type=F32)


def dot_nt(a, b):
    return lax.dot_general(a, b, (((1,), (1,)), ((), ())), preferred_element_type=F32)


def dot_tn(a, b):
    return lax.dot_general(a, b, (((0,), (0,)), ((), ())), preferred_element_type=F32)


def halves(x):
    hi = x.astype(BF)
    return hi, (x - hi.astype(F32)).astype(BF)


def sigmoid(u):
    return 1.0 / (1.0 + jnp.exp(-u))


def n_levels(tokens):
    return tokens.bit_length() - 1


def span_matrix(level, tokens):
    t = lax.broadcasted_iota(jnp.int32, (tokens, tokens), 0)
    u = lax.broadcasted_iota(jnp.int32, (tokens, tokens), 1)
    depth = n_levels(tokens)
    if level == depth:
        keep = u <= t
    elif level == depth + 1:
        keep = u > t
    else:
        half = 1 << level
        edge = (t & ~(2 * half - 1)) + half
        odd = (t & half) > 0
        keep = (odd & (u >= edge) & (u <= t)) | (~odd & (u > t) & (u < edge))
    return keep.astype(F32).astype(BF)


def odd_rows(level, tokens, columns):
    t = lax.broadcasted_iota(jnp.int32, (tokens, columns), 0)
    return (t & (1 << level)) > 0


def same_pair(level, tokens):
    t = lax.broadcasted_iota(jnp.int32, (tokens, tokens), 0)
    u = lax.broadcasted_iota(jnp.int32, (tokens, tokens), 1)
    return (t >> (level + 1)) == (u >> (level + 1))


def ends_kernel(pre_ref, resets_ref, keys_ref, values_ref, spans_ref, total_ref, ends_ref):
    tokens, slots = pre_ref.shape
    depth = n_levels(tokens)
    width = keys_ref.shape[1]
    pre = pre_ref[...]
    log_decay = (jnp.minimum(pre, 0.0) - jnp.log1p(jnp.exp(-jnp.abs(pre)))) / GATE_NORM
    write = 1.0 - jnp.exp(log_decay)
    hi, lo = halves(log_decay)
    resets = jnp.broadcast_to(resets_ref[...], (tokens, slots)).astype(BF)
    stacked = jnp.concatenate([hi, lo, resets], axis=1)
    for level in range(depth + 2):
        sums = dot_nn(span_matrix(level, tokens), stacked)
        gap = sums[:, :slots] + sums[:, slots : 2 * slots]
        live = sums[:, 2 * slots :] < 0.5
        span = jnp.where(live, jnp.exp(gap), 0.0)
        spans_ref[level] = span
        if level == depth:
            total_ref[...] = span[tokens - 1 :, :]
        if level == depth + 1:
            hi, lo = halves(span * write)
            ends_ref[:, :width] = dot_tn(hi, keys_ref[...]) + dot_tn(lo, keys_ref[...])
            ends_ref[:, width:] = dot_tn(hi, values_ref[...]) + dot_tn(lo, values_ref[...])


def run_ends(pre, resets, keys, values):
    tokens, slots = pre.shape
    depth = n_levels(tokens)
    return pl.pallas_call(
        ends_kernel,
        out_shape=(
            jax.ShapeDtypeStruct((depth + 2, tokens, slots), F32),
            jax.ShapeDtypeStruct((1, slots), F32),
            jax.ShapeDtypeStruct((slots, keys.shape[1] + values.shape[1]), F32),
        ),
        name="slot_ends",
    )(pre, resets, keys, values)


def decay_write(pre):
    log_decay = (jnp.minimum(pre, 0.0) - jnp.log1p(jnp.exp(-jnp.abs(pre)))) / GATE_NORM
    return jnp.exp(log_decay)


def forward_kernel(
    query_ref, keys_ref, values_ref, pre_ref, spans_ref, state_ref, gate_ref, gain_ref,
    probs_ref, pairs_ref, mixing_ref, mix_ref, gated_ref,
):
    tokens, slots = pre_ref.shape
    depth = n_levels(tokens)
    width = keys_ref.shape[1]
    scaling = width ** (-0.5)
    write = 1.0 - decay_write(pre_ref[...])
    query = query_ref[...]
    pairs = dot_nt(query, keys_ref[...])
    pairs_ref[...] = pairs
    t = lax.broadcasted_iota(jnp.int32, (tokens, tokens), 0)
    u = lax.broadcasted_iota(jnp.int32, (tokens, tokens), 1)
    diagonal = jnp.sum(jnp.where(t == u, pairs, 0.0), axis=1, keepdims=True)
    state_hi, state_lo = halves(state_ref[:, :width])
    head = spans_ref[depth]
    raw = head * (dot_nt(query, state_hi) + dot_nt(query, state_lo)) + diagonal * write
    for level in range(depth):
        span = spans_ref[level]
        odd = odd_rows(level, tokens, slots)
        left, left_lo = halves(jnp.where(same_pair(level, tokens), pairs, 0.0))
        right, right_lo = halves(jnp.where(odd, 0.0, span * write))
        pulled = dot_nn(left, right) + dot_nn(left_lo, right) + dot_nn(left, right_lo)
        raw = raw + jnp.where(odd, span, 0.0) * pulled
    scores = scaling * raw
    scores = scores - jnp.max(scores, axis=1, keepdims=True)
    raised = jnp.exp(scores)
    probs = raised / jnp.sum(raised, axis=1, keepdims=True)
    probs_ref[...] = probs
    probs = probs.astype(BF).astype(F32)
    mixing = jnp.zeros((tokens, tokens), F32)
    for level in reversed(range(depth)):
        span = spans_ref[level]
        odd = odd_rows(level, tokens, slots)
        left, left_lo = halves(jnp.where(odd, span * probs, 0.0))
        right, right_lo = halves(jnp.where(odd, 0.0, span * write))
        pushed = dot_nt(left, right) + dot_nt(left_lo, right) + dot_nt(left, right_lo)
        mixing = jnp.where(same_pair(level, tokens), pushed, mixing)
    mixing = jnp.where(t == u, jnp.sum(probs * write, axis=1, keepdims=True), mixing)
    mixing, mixing_lo = halves(mixing)
    mixing_ref[...] = mixing
    state_hi, state_lo = halves(state_ref[:, width:])
    carried, carried_lo = halves(probs * head)
    mix = dot_nn(mixing, values_ref[...]) + dot_nn(mixing_lo, values_ref[...])
    mix = mix + dot_nn(carried, state_hi) + dot_nn(carried, state_lo) + dot_nn(carried_lo, state_hi)
    mix_ref[...] = mix
    scale = lax.rsqrt(jnp.mean(mix * mix, axis=1, keepdims=True) + EPSILON)
    gate = gate_ref[...]
    gated_ref[...] = (mix * scale * gain_ref[...] * (gate * sigmoid(gate))).astype(BF)


def run_forward(query, keys, values, pre, spans, state, gate, gain):
    tokens, slots = pre.shape
    width = keys.shape[1]
    return pl.pallas_call(
        forward_kernel,
        out_shape=(
            jax.ShapeDtypeStruct((tokens, slots), F32),
            jax.ShapeDtypeStruct((tokens, tokens), F32),
            jax.ShapeDtypeStruct((tokens, tokens), BF),
            jax.ShapeDtypeStruct((tokens, width), F32),
            jax.ShapeDtypeStruct((tokens, width), BF),
        ),
        name="slot_forward",
    )(query, keys, values, pre, spans, state, gate, gain)


def backward_kernel(
    grad_ref, query_ref, keys_ref, values_ref, pre_ref, spans_ref, state_ref, gate_ref, gain_ref,
    probs_ref, pairs_ref, mixing_ref, mix_ref,
    gquery_ref, gkeys_ref, gvalues_ref, ggate_ref, ggain_ref, gwrite_ref, glog_ref, carry_ref,
):
    tokens, slots = pre_ref.shape
    depth = n_levels(tokens)
    width = keys_ref.shape[1]
    scaling = width ** (-0.5)
    gate = gate_ref[...]
    sig = sigmoid(gate)
    silu = gate * sig
    gain = gain_ref[...]
    mix = mix_ref[...]
    scale = lax.rsqrt(jnp.mean(mix * mix, axis=1, keepdims=True) + EPSILON)
    normed = mix * scale
    grad = grad_ref[...]
    ggate_ref[...] = (grad * gain * normed * (sig * (1.0 + gate * (1.0 - sig)))).astype(BF)
    ggain_ref[...] = jnp.sum(grad * normed * silu, axis=0, keepdims=True)
    inner = grad * gain * silu
    mix_grad = scale * (inner - normed * jnp.mean(normed * inner, axis=1, keepdims=True))
    mix_low = mix_grad.astype(BF)

    write = 1.0 - decay_write(pre_ref[...])
    query, keys, values = query_ref[...], keys_ref[...], values_ref[...]
    pairs = pairs_ref[...]
    pairs_t = dot_nt(keys, query)
    mix_rest = (mix_grad - mix_low.astype(F32)).astype(BF)
    weigh = dot_nt(mix_low, values) + dot_nt(mix_rest, values)
    weigh_t = dot_nt(values, mix_low) + dot_nt(values, mix_rest)
    t = lax.broadcasted_iota(jnp.int32, (tokens, tokens), 0)
    u = lax.broadcasted_iota(jnp.int32, (tokens, tokens), 1)
    pair_diag = jnp.sum(jnp.where(t == u, pairs, 0.0), axis=1, keepdims=True)
    weigh_diag = jnp.sum(jnp.where(t == u, weigh, 0.0), axis=1, keepdims=True)
    head = spans_ref[depth]
    probs = probs_ref[...]
    probs_low = probs.astype(BF).astype(F32)

    vstate_hi, vstate_lo = halves(state_ref[:, width:])
    head_probs = head * (
        dot_nt(mix_low, vstate_hi) + dot_nt(mix_low, vstate_lo) + dot_nt(mix_rest, vstate_hi)
    )
    probs_grad = head_probs + weigh_diag * write
    row_values, row_keys = [], []
    for level in range(depth):
        span = spans_ref[level]
        odd = odd_rows(level, tokens, slots)
        same = same_pair(level, tokens)
        right, right_lo = halves(jnp.where(odd, 0.0, span * write))
        reach = jnp.where(odd, span, 0.0)
        left, left_lo = halves(jnp.where(same, weigh, 0.0))
        term = reach * (dot_nn(left, right) + dot_nn(left_lo, right) + dot_nn(left, right_lo))
        row_values.append(term)
        left, left_lo = halves(jnp.where(same, pairs, 0.0))
        row_keys.append(reach * (dot_nn(left, right) + dot_nn(left_lo, right) + dot_nn(left, right_lo)))
        probs_grad = probs_grad + term
    scores_grad = probs * (probs_grad - jnp.sum(probs_grad * probs, axis=1, keepdims=True))
    scores_grad = scaling * scores_grad

    kstate_hi, kstate_lo = halves(state_ref[:, :width])
    head_keys = head * (dot_nt(query, kstate_hi) + dot_nt(query, kstate_lo))
    gwrite = pair_diag * scores_grad + weigh_diag * probs_low
    glog = dot_tn(span_matrix(depth, tokens), (head_keys * scores_grad + head_probs * probs_low).astype(BF))
    gpairs = jnp.zeros((tokens, tokens), F32)
    for level in reversed(range(depth)):
        span = spans_ref[level]
        odd = odd_rows(level, tokens, slots)
        same = same_pair(level, tokens)
        reach = jnp.where(odd, span, 0.0)
        source = jnp.where(odd, 0.0, span)
        key_side, key_rest = halves(reach * scores_grad)
        value_side, value_rest = halves(reach * probs_low)
        seen, seen_rest = halves(jnp.where(same, pairs_t, 0.0))
        felt, felt_rest = halves(jnp.where(same, weigh_t, 0.0))
        sent, sent_rest = halves(source * write)
        pushed = dot_nt(key_side, sent) + dot_nt(key_rest, sent) + dot_nt(key_side, sent_rest)
        gpairs = jnp.where(same, pushed, gpairs)
        column = source * (
            dot_nn(seen, key_side) + dot_nn(seen, key_rest) + dot_nn(seen_rest, key_side)
            + dot_nn(felt, value_side) + dot_nn(felt, value_rest) + dot_nn(felt_rest, value_side)
        )
        gwrite = gwrite + column
        moved = column * write + row_values[level] * probs_low + row_keys[level] * scores_grad
        spread = span_matrix(level, tokens)
        moved, moved_rest = halves(moved)
        glog = glog + dot_tn(spread, moved) + dot_tn(spread, moved_rest)
    gpairs = jnp.where(t == u, jnp.sum(scores_grad * write, axis=1, keepdims=True), gpairs)
    gpairs, gpairs_rest = halves(gpairs)
    gwrite_ref[...] = gwrite
    glog_ref[...] = glog
    key_head, key_head_rest = halves(scores_grad * head)
    gquery_ref[...] = (
        dot_nn(gpairs, keys)
        + dot_nn(gpairs_rest, keys)
        + dot_nn(key_head, kstate_hi)
        + dot_nn(key_head, kstate_lo)
        + dot_nn(key_head_rest, kstate_hi)
    )
    gkeys_ref[...] = dot_tn(gpairs, query) + dot_tn(gpairs_rest, query)
    gvalues_ref[...] = dot_tn(mixing_ref[...], mix_low)
    carry_ref[:, :width] = dot_tn(key_head, query) + dot_tn(key_head_rest, query)
    carry_ref[:, width:] = dot_tn((probs_low * head).astype(BF), mix_low)


def run_backward(grad, query, keys, values, pre, spans, state, gate, gain, probs, pairs, mixing, mix):
    tokens, slots = pre.shape
    width = keys.shape[1]
    wide = jax.ShapeDtypeStruct((tokens, width), F32)
    narrow = jax.ShapeDtypeStruct((tokens, slots), F32)
    return pl.pallas_call(
        backward_kernel,
        out_shape=(
            wide, wide, wide,
            jax.ShapeDtypeStruct((tokens, width), BF),
            jax.ShapeDtypeStruct((1, width), F32),
            narrow, narrow,
            jax.ShapeDtypeStruct((slots, 2 * width), F32),
        ),
        name="slot_backward",
    )(grad, query, keys, values, pre, spans, state, gate, gain, probs, pairs, mixing, mix)


def finish_kernel(
    gquery_ref, gkeys_ref, gvalues_ref, ggate_ref, gwrite_ref, glog_ref,
    keys_ref, values_ref, pre_ref, spans_ref, query_pre_ref, keys_pre_ref,
    state_ref, total_ref, ends_ref, gated_ref, out_ref, bias_ref,
):
    tokens, slots = pre_ref.shape
    depth = n_levels(tokens)
    width = keys_ref.shape[1]
    pre = pre_ref[...]
    decay = decay_write(pre)
    write = 1.0 - decay
    keys, values = keys_ref[...], values_ref[...]
    ends = ends_ref[...]
    ends_low = ends.astype(BF)
    tail = spans_ref[depth + 1]
    sent = (tail * write).astype(BF)
    column = tail * (dot_nt(keys, ends_low[:, :width]) + dot_nt(values, ends_low[:, width:]))
    glog = glog_ref[...] + dot_tn(span_matrix(depth + 1, tokens), (column * write).astype(BF))
    carried = lax.dot_general(
        jnp.ones((1, 2 * width), F32), ends * state_ref[...], (((1,), (1,)), ((), ())),
        precision=lax.Precision.HIGHEST, preferred_element_type=F32,
    )
    glog = glog + carried * total_ref[...]
    glog = glog - decay * (gwrite_ref[...] + column)
    def put(part, value):
        out_ref[:, part * width : (part + 1) * width] = value.astype(BF)

    put(0, gated_ref[...])
    u = query_pre_ref[...]
    s = sigmoid(u)
    put(1, gquery_ref[...] * (s * (1.0 + u * (1.0 - s))))
    u = keys_pre_ref[...]
    s = sigmoid(u)
    gkeys = gkeys_ref[...] + dot_nn(sent, ends_low[:, :width])
    put(2, gkeys * (s * (1.0 + u * (1.0 - s))))
    put(3, gvalues_ref[...] + dot_nn(sent, ends_low[:, width:]))
    put(4, ggate_ref[...])
    gforget = (glog * sigmoid(-pre) / GATE_NORM).astype(BF)
    gforget = jnp.concatenate([gforget, jnp.zeros((tokens, 128 - slots), BF)], axis=1)
    out_ref[:, 5 * width :] = gforget
    bias_ref[...] = jnp.sum(gforget.astype(F32), axis=0, keepdims=True)


def run_finish(gquery, gkeys, gvalues, ggate, gwrite, glog, keys, values, pre, spans, query_pre, keys_pre, state, total, ends, gated):
    tokens, slots = pre.shape
    width = keys.shape[1]
    return pl.pallas_call(
        finish_kernel,
        out_shape=(jax.ShapeDtypeStruct((tokens, 5 * width + 128), BF), jax.ShapeDtypeStruct((1, 128), F32)),
        name="slot_finish",
    )(gquery, gkeys, gvalues, ggate, gwrite, glog, keys, values, pre, spans, query_pre, keys_pre, state, total, ends, gated)


MESH = pl.DeviceIdType.MESH
GROUPED = ("shard", "ctx")


def greet(axes_of_peers):
    barrier = pltpu.get_barrier_semaphore()
    for peer in axes_of_peers:
        pl.semaphore_signal(barrier, inc=1, device_id=peer, device_id_type=MESH)
    pl.semaphore_wait(barrier, len(axes_of_peers))


def tp_peers():
    count = lax.axis_size("tp")
    me = lax.axis_index("tp")
    return me, [lax.rem(me + k, count) for k in range(1, count)]


CHUNKS = 4
LATENCY = 2.2
LEAD = 10
CLOSING = 3


def tp_line(partial_ref, full_ref, arrived, staged, sums_ref, finish, settle, send_a, recv_a, send_b, recv_b):
    count = lax.axis_size("tp")
    me = lax.axis_index("tp")
    rows = partial_ref.shape[1] // CHUNKS
    peers = [lax.rem(me + 1, count), lax.rem(me + count - 1, count)]

    def at_place(side, place):
        return place if side == 0 else count - 1 - place

    def cut(chunk):
        return pl.ds(chunk * rows, rows)

    def sum_copy(side, hop, chunk, source):
        return pltpu.make_async_remote_copy(
            src_ref=source,
            dst_ref=arrived.at[side, hop, chunk],
            send_sem=send_a.at[side, hop, chunk],
            recv_sem=recv_a.at[side, hop, chunk],
            device_id={"tp": peers[side]},
            device_id_type=MESH,
        )

    def row_copy(side, hop, chunk, block):
        return pltpu.make_async_remote_copy(
            src_ref=full_ref.at[block, cut(chunk)],
            dst_ref=full_ref.at[block, cut(chunk)],
            send_sem=send_b.at[side, hop, chunk],
            recv_sem=recv_b.at[side, hop, chunk],
            device_id={"tp": peers[side]},
            device_id_type=MESH,
        )

    def own(side, hop, chunk):
        return partial_ref.at[at_place(side, count - 1 - hop), cut(chunk)]

    def send_own(chunk):
        for side in range(2):

            @pl.when(me == at_place(side, 0))
            def _():
                for hop in range(count - 1):
                    sum_copy(side, hop, chunk, own(side, hop, chunk)).start()

    def add_hop(side, place, hop, chunk):
        @pl.when(me == at_place(side, place))
        def _():
            slot = staged.at[side, hop, chunk]
            copy = sum_copy(side, hop, chunk, slot)
            copy.wait_recv()
            slot[...] = (own(side, hop, chunk)[...].astype(F32) + arrived[side, hop, chunk].astype(F32)).astype(BF)
            copy.start()

    def close(chunk):
        sums_ref[...] = partial_ref[me, cut(chunk)].astype(F32)
        for side in range(2):
            place = me if side == 0 else count - 1 - me
            hop = jnp.minimum(count - 1 - place, count - 2)

            @pl.when(place > 0)
            def _():
                sum_copy(side, hop, chunk, staged.at[side, hop, chunk]).wait_recv()
                sums_ref[...] += arrived[side, hop, chunk].astype(F32)

        finish(chunk, sums_ref[...])
        for side in range(2):

            @pl.when(me != at_place(side, count - 1))
            def _():
                row_copy(side, 0, chunk, me).start()

    def forward(side, place, distance, chunk):
        @pl.when(me == at_place(side, place))
        def _():
            block = at_place(side, place - distance)
            row_copy(side, distance - 1, chunk, block).wait_recv()
            if place < count - 1:
                row_copy(side, distance, chunk, block).start()

    step = 1 + LATENCY
    events = [(900, settle)]
    for chunk in range(CHUNKS):
        base = (count - 1) * chunk
        closed = base + (count - 1) + (count - 2) * LATENCY
        events.append((base - LEAD * (count - 1), functools.partial(send_own, chunk)))
        events.append((closed, functools.partial(close, chunk)))
        for side in range(2):
            for place in range(1, count):
                for hop in range(count - 1 - place):
                    due = base + hop + place * step
                    events.append((due, functools.partial(add_hop, side, place, hop, chunk)))
                for distance in range(1, place + 1):
                    due = closed + CLOSING + distance * step
                    if place == count - 1:
                        due += 1000
                    events.append((due, functools.partial(forward, side, place, distance, chunk)))
    for _, event in sorted(events, key=lambda event: event[0]):
        event()

    def drain():
        for side in range(2):
            for place in range(count - 1):

                @pl.when(me == at_place(side, place))
                def _():
                    for chunk in range(CHUNKS):
                        for hop in range(count - 1 - place):
                            sum_copy(side, hop, chunk, staged.at[side, hop, chunk]).wait_send()
                        for hop in range(place + 1):
                            row_copy(side, hop, chunk, at_place(side, place - hop)).wait_send()

    return drain


def plane_peers():
    shards, ctxs = lax.axis_size("shard"), lax.axis_size("ctx")
    devices = shards * ctxs
    me = lax.axis_index("shard") * ctxs + lax.axis_index("ctx")
    peers = [lax.rem(me + k, devices) for k in range(1, devices)]
    places = [{"shard": lax.div(peer, ctxs), "ctx": lax.rem(peer, ctxs)} for peer in peers]
    return me, peers, places


def start_scatter(sources, targets, send_sems, recv_sems):
    me, peers, places = plane_peers()
    copies = []
    for i, (source, target) in enumerate(zip(sources, targets)):
        step = target.shape[2]

        def block(at):
            if len(source.shape) == 3:
                return source.at[at]
            return source.at[:, pl.ds(pl.multiple_of(at * step, step), step)]

        for k, (peer, place) in enumerate(zip(peers, places)):
            copy = pltpu.make_async_remote_copy(
                src_ref=block(peer),
                dst_ref=target.at[me],
                send_sem=send_sems.at[i, k],
                recv_sem=recv_sems.at[i, k],
                device_id=place,
                device_id_type=MESH,
            )
            copy.start()
            copies.append(copy)
    for source, target in zip(sources, targets):
        target[me] = block_of(source, me, target.shape[2])
    return copies


def block_of(source, at, step):
    if len(source.shape) == 3:
        return source[at]
    return source[:, pl.ds(pl.multiple_of(at * step, step), step)]


def spread_kernel(n_parts, n_packed, *refs):
    parts, refs = refs[:n_parts], refs[n_parts:]
    packed, refs = refs[:n_packed], refs[n_packed:]
    if n_packed:
        forget_ref, mask_ref, vectors, refs = refs[0], refs[1], refs[2:5], refs[5:]
        out_ref, rows_ref, pack_ref, slab, part_sems, own_sem, send_sems, recv_sems = refs[:8]
        row_ref, row_send, row_recv, pack_slab, pack_sems, pack_sem = refs[8:]
    else:
        out_ref, slab, part_sems, own_sem, send_sems, recv_sems = refs
    shard, core = lax.axis_index("shard"), lax.axis_index("ctx")
    me, _, places = plane_peers()
    across = shard + 1 - 2 * lax.rem(shard, 2)
    along = lax.rem(shard + 2, 4)
    corner = lax.rem(across + 2, 4)
    other = 1 - core
    to_x, to_y, to_core = {"shard": across}, {"shard": along}, {"ctx": other}
    rows = slab.shape[0]
    piece = rows // 4

    def load_all(sources, target, sems):
        loads = []
        start = 0
        for i, part in enumerate(sources):
            load = pltpu.make_async_copy(part, target.at[:, pl.ds(start, part.shape[1])], sems.at[i])
            load.start()
            loads.append(load)
            start += part.shape[1]
        return loads

    loads = load_all(parts, slab, part_sems)
    if n_packed:
        room = jnp.zeros((128 - forget_ref.shape[0], rows), BF)
        slab[:, slab.shape[1] - 128 :] = jnp.concatenate([forget_ref[...], room], axis=0).T
        row_ref[...] = jnp.zeros_like(row_ref)
        for i, vector in zip((0, 2, 3), vectors):
            row_ref[i : i + vector.shape[0], : vector.shape[1]] = vector[...].astype(F32)
        count = jnp.sum(mask_ref[...].astype(F32), axis=1, keepdims=True)
        row_ref[4:5, :] = jnp.broadcast_to(count, (1, row_ref.shape[1]))
    greet(places)
    for load in loads:
        load.wait()
    keep = pltpu.make_async_copy(slab, out_ref.at[pl.ds(pl.multiple_of(me * rows, rows), rows)], own_sem)
    keep.start()

    def landing(block, part):
        return out_ref.at[pl.ds(pl.multiple_of(block * rows + part * piece, piece), piece)]

    started = []

    def send(kind, source, block, part, place):
        copy = pltpu.make_async_remote_copy(
            src_ref=source,
            dst_ref=landing(block, part),
            send_sem=send_sems.at[kind],
            recv_sem=recv_sems.at[kind],
            device_id=place,
            device_id_type=MESH,
        )
        copy.start()
        started.append(copy)

    def receive(kind, block, part, place):
        region = landing(block, part)
        pltpu.make_async_remote_copy(
            src_ref=region,
            dst_ref=region,
            send_sem=send_sems.at[kind],
            recv_sem=recv_sems.at[kind],
            device_id=place,
            device_id_type=MESH,
        ).wait_recv()

    def own(part):
        return slab.at[pl.ds(part * piece, piece)]

    def block(place, at_core):
        return 2 * place + at_core

    for part in range(4):
        turn = (part + 2) % 4
        send(part, own(part), me, part, to_x)
        send(4 + turn, own(turn), me, turn, to_y)
    if n_packed:
        copies = start_sums(row_ref, rows_ref, row_send, row_recv, [], places, me)
    for part in range(4):
        send(8 + part, own(part), me, part, to_core)
    if n_packed:
        for load in load_all(packed, pack_slab, pack_sems):
            load.wait()
        store = pltpu.make_async_copy(pack_slab, pack_ref, pack_sem)
        store.start()
    x_block, y_block, far_block = block(across, core), block(along, core), block(corner, core)
    for part in range(4):
        turn = (part + 2) % 4
        receive(part, x_block, part, to_x)
        if part < 2:
            send(12 + part, landing(x_block, part), x_block, part, to_y)
        send(16 + part, landing(x_block, part), x_block, part, to_core)
        receive(4 + turn, y_block, turn, to_y)
        if turn >= 2:
            send(12 + turn, landing(y_block, turn), y_block, turn, to_x)
        send(20 + turn, landing(y_block, turn), y_block, turn, to_core)
    for part in (0, 2, 1, 3):
        receive(12 + part, far_block, part, to_y if part < 2 else to_x)
        send(24 + part, landing(far_block, part), far_block, part, to_core)
    for kind, place in ((8, shard), (16, across), (20, along), (24, corner)):
        for part in range(4):
            receive(kind + part, block(place, other), part, to_core)
    for copy in started:
        copy.wait_send()
    keep.wait()
    if n_packed:
        store.wait()
        for copy in copies:
            copy.wait()


def run_spread(name, collective_id, parts, packed=(), forget=None, mask=None, vectors=()):
    devices = lax.axis_size(GROUPED)
    rows = parts[0].shape[0]
    columns = sum(part.shape[1] for part in parts) + (128 if packed else 0)
    anywhere = pl.BlockSpec(memory_space=pl.ANY)
    in_specs, out_specs = [anywhere] * len(parts), [anywhere]
    out_shape = [jax.ShapeDtypeStruct((devices * rows, columns), BF)]
    scratch = [
        pltpu.VMEM((rows, columns), BF),
        pltpu.SemaphoreType.DMA((len(parts),)),
        pltpu.SemaphoreType.DMA,
        *[pltpu.SemaphoreType.DMA((28,))] * 2,
    ]
    args = list(parts)
    if packed:
        packed_shape = (rows, sum(part.shape[1] for part in packed))
        args += [*packed, forget, mask, *vectors]
        in_specs += [*[anywhere] * len(packed), *[pl.BlockSpec(memory_space=pltpu.VMEM)] * (2 + len(vectors))]
        out_specs += [pl.BlockSpec(memory_space=pltpu.VMEM), anywhere]
        out_shape += [jax.ShapeDtypeStruct((devices, 8, rows), F32), jax.ShapeDtypeStruct(packed_shape, BF)]
        scratch += [
            pltpu.VMEM((8, rows), F32),
            *[pltpu.SemaphoreType.DMA((devices - 1,))] * 2,
            pltpu.VMEM(packed_shape, BF),
            pltpu.SemaphoreType.DMA((len(packed),)),
            pltpu.SemaphoreType.DMA,
        ]
    return pl.pallas_call(
        functools.partial(spread_kernel, len(parts), len(packed)),
        out_shape=tuple(out_shape),
        in_specs=in_specs,
        out_specs=tuple(out_specs),
        scratch_shapes=scratch,
        compiler_params=pltpu.CompilerParams(collective_id=collective_id, has_side_effects=True),
        name=name,
    )(*args)


def start_sums(row_ref, landed, send_sems, recv_sems, peers, places, me):
    copies = []
    landed[me] = row_ref[...]
    for k, place in enumerate(places):
        copy = pltpu.make_async_remote_copy(
            src_ref=row_ref,
            dst_ref=landed.at[me],
            send_sem=send_sems.at[k],
            recv_sem=recv_sems.at[k],
            device_id=place,
            device_id_type=MESH,
        )
        copy.start()
        copies.append(copy)
    return copies


def summed(landed):
    total = landed[0]
    for k in range(1, landed.shape[0]):
        total = total + landed[k]
    return total


def exchange_kernel(epilogue, n_in, n_rows, n_moved, n_sums, partial_ref, *refs):
    me, peers = tp_peers()
    inputs, refs = refs[:n_in], refs[n_in:]
    sources, refs = refs[:n_moved], refs[n_moved:]
    full_ref, refs = refs[0], refs[1:]
    outputs, refs = refs[:n_rows], refs[n_rows:]
    targets, refs = refs[:n_moved], refs[n_moved:]
    sums, refs = refs[: 2 * n_sums], refs[2 * n_sums :]
    arrived, staged, sums_ref, send_a, recv_a, send_b, recv_b, send_m, recv_m = refs[:9]
    own, plane, places = plane_peers()
    across = [{"tp": peer} for peer in peers]
    greet(across + (places if n_moved or n_sums else []))
    moves = start_scatter(sources, targets, send_m, recv_m)
    rows = full_ref.shape[1] // CHUNKS
    started = []

    def finish(chunk, total):
        part = pl.ds(chunk * rows, rows)
        full_ref[me, part] = epilogue(total, me, part, chunk == 0, inputs, outputs)
        if n_sums and chunk == CHUNKS - 1:
            row_ref, in_plane, _, _, send_p, recv_p = refs[9:15]
            width = outputs[0].shape[1]
            row_ref[:, :width] = outputs[0][...]
            row_ref[:, width:] = inputs[-1][...]
            started.extend(start_sums(row_ref, in_plane, send_p, recv_p, plane, places, own))

    def settle():
        if not n_sums:
            return
        row_ref, in_plane, plane_row, in_tp, send_p, recv_p, send_t, recv_t = refs[9:]
        for copy in started:
            copy.wait()
        plane_row[...] = summed(in_plane)
        sums[0][...] = plane_row[...]
        for copy in start_sums(plane_row, in_tp, send_t, recv_t, peers, across, me):
            copy.wait()
        sums[1][...] = summed(in_tp)

    drain = tp_line(
        partial_ref, full_ref, arrived, staged, sums_ref, finish, settle, send_a, recv_a, send_b, recv_b
    )
    drain()
    for copy in moves:
        copy.wait()


def run_exchange(epilogue, name, collective_id, partial, inputs, row_outputs, moved=(), summing=False):
    tp = lax.axis_size("tp")
    devices = lax.axis_size(GROUPED)
    tokens, columns = partial.shape
    share = tokens // tp
    partial = partial.reshape(tp, share, columns)
    step = columns // devices
    if step % 128:
        moved = [m.reshape(tokens, devices, step).transpose(1, 0, 2) for m in moved]
    count = len(moved)
    scratch = [
        *[pltpu.VMEM((2, tp - 1, CHUNKS, share // CHUNKS, columns), BF)] * 2,
        pltpu.VMEM((share // CHUNKS, columns), F32),
        *[pltpu.SemaphoreType.DMA((2, tp - 1, CHUNKS))] * 4,
        *[pltpu.SemaphoreType.DMA((max(count, 1), devices - 1))] * 2,
    ]
    extra = ()
    if summing:
        row = row_outputs[0].shape[1] + inputs[-1].shape[1]
        extra = (jax.ShapeDtypeStruct((1, row), F32),) * 2
        scratch += [
            pltpu.VMEM((1, row), F32),
            pltpu.VMEM((devices, 1, row), F32),
            pltpu.VMEM((1, row), F32),
            pltpu.VMEM((tp, 1, row), F32),
            *[pltpu.SemaphoreType.DMA((devices - 1,))] * 2,
            *[pltpu.SemaphoreType.DMA((tp - 1,))] * 2,
        ]
    out_shape = (
        jax.ShapeDtypeStruct((tp, share, columns), BF),
        *row_outputs,
        *[jax.ShapeDtypeStruct((devices, tokens, step), BF)] * count,
        *extra,
    )
    outs = pl.pallas_call(
        functools.partial(exchange_kernel, epilogue, len(inputs), len(row_outputs), count, int(summing)),
        out_shape=out_shape,
        in_specs=[pl.BlockSpec(memory_space=pltpu.VMEM)] * (1 + len(inputs) + count),
        out_specs=tuple([pl.BlockSpec(memory_space=pltpu.VMEM)] * len(out_shape)),
        scratch_shapes=scratch,
        compiler_params=pltpu.CompilerParams(collective_id=collective_id, has_side_effects=True),
        name=name,
    )(partial, *inputs, *moved)
    start = 1 + len(row_outputs)
    return (
        outs[0].reshape(tokens, columns),
        *outs[1:start],
        *[o.reshape(devices * tokens, step) for o in outs[start : start + count]],
        *outs[start + count :],
    )


def middle_epilogue(total, me, part, first, inputs, outputs):
    hidden_ref, gain_ref = inputs
    (branch_ref,) = outputs
    branch_ref[part, :] = total
    middle = hidden_ref[me, part].astype(F32) + total
    scale = lax.rsqrt(jnp.mean(middle * middle, axis=1, keepdims=True) + EPSILON)
    return (middle * scale * gain_ref[...]).astype(BF)


def result_epilogue(total, me, part, first, inputs, outputs):
    hidden_ref, branch_ref, teacher_out_ref, teacher_mix_ref, cotangent_ref, mask_ref, scale_ref = inputs
    grad_ref, losses_ref = outputs
    branch = branch_ref[part, :]
    result = hidden_ref[me, part].astype(F32) + branch + total
    mask = mask_ref[me, part]
    gap = result - teacher_out_ref[me, part].astype(F32)
    gap_mix = branch - teacher_mix_ref[me, part].astype(F32)
    loss_out = jnp.sum(mask * (gap * gap), keepdims=True)
    loss_mix = jnp.sum(mask * (gap_mix * gap_mix), keepdims=True)
    lane = lax.broadcasted_iota(jnp.int32, (1, 128), 1)
    losses = jnp.where(lane == 0, loss_out, 0.0) + jnp.where(lane == 1, loss_mix, 0.0)
    losses_ref[...] = losses if first else losses_ref[...] + losses
    grad_ref[part, :] = cotangent_ref[me, part].astype(F32) + scale_ref[...] * mask * gap
    return result.astype(BF)


def norm_back(grad, rows, gain):
    scale = lax.rsqrt(jnp.mean(rows * rows, axis=1, keepdims=True) + EPSILON)
    unit = rows * scale
    gain_grad = jnp.sum(grad * unit, axis=0, keepdims=True)
    inner = grad * gain
    return scale * (inner - unit * jnp.mean(unit * inner, axis=1, keepdims=True)), gain_grad


def branch_epilogue(total, me, part, first, inputs, outputs):
    hidden_ref, branch_ref, teacher_mix_ref, grad_ref, mask_ref, scale_ref, gain_ref = inputs
    grad_middle_ref, gain_grad_ref = outputs
    branch = branch_ref[part, :]
    back, gain_grad = norm_back(total, hidden_ref[me, part].astype(F32) + branch, gain_ref[...])
    gain_grad_ref[...] = gain_grad if first else gain_grad_ref[...] + gain_grad
    grad_middle = back + grad_ref[part, :]
    grad_middle_ref[part, :] = grad_middle
    gap_mix = branch - teacher_mix_ref[me, part].astype(F32)
    return (grad_middle + scale_ref[...] * mask_ref[me, part] * gap_mix).astype(BF)


def input_epilogue(total, me, part, first, inputs, outputs):
    hidden_ref, grad_middle_ref, gain_ref = inputs[:3]
    (gain_grad_ref,) = outputs
    back, gain_grad = norm_back(total, hidden_ref[me, part].astype(F32), gain_ref[...])
    gain_grad_ref[...] = gain_grad if first else gain_grad_ref[...] + gain_grad
    return (back + grad_middle_ref[part, :]).astype(BF)


def weights_kernel(segments, n_rows, n_columns, n_turned, *refs):
    rows, refs = refs[:n_rows], refs[n_rows:]
    columns, refs = refs[:n_columns], refs[n_columns:]
    straight, outs = refs[:n_turned], refs[n_turned:]
    at = pl.program_id(0)
    for ref, out in zip(straight, outs[len(segments) :]):
        out[...] = ref[...].T
    turned = [ref[...].T for ref in rows]
    for (row, column, start, width), out in zip(segments, outs):
        term = dot_nn(turned[row], columns[column][:, pl.ds(start, width)])

        @pl.when(at == 0)
        def _():
            out[...] = term

        @pl.when(at > 0)
        def _():
            out[...] += term


def run_weights(name, rows, columns, segments, turned):
    tokens, features = rows[0].shape
    block = 512
    whole = lambda width: pl.BlockSpec((block, width), lambda i: (i, 0))
    shapes = [(features, segment[3]) for segment in segments]
    return pl.pallas_call(
        functools.partial(weights_kernel, segments, len(rows), len(columns), len(turned)),
        grid=(tokens // block,),
        in_specs=[*[whole(features)] * len(rows), *[whole(c.shape[1]) for c in (*columns, *turned)]],
        out_specs=(
            *[pl.BlockSpec(shape, lambda i: (0, 0)) for shape in shapes],
            *[pl.BlockSpec((t.shape[1], block), lambda i: (0, i)) for t in turned],
        ),
        out_shape=(
            *[jax.ShapeDtypeStruct(shape, F32) for shape in shapes],
            *[jax.ShapeDtypeStruct((t.shape[1], tokens), BF) for t in turned],
        ),
        compiler_params=pltpu.CompilerParams(dimension_semantics=("arbitrary",)),
        name=name,
    )(*rows, *columns, *turned)


def attention_weights_kernel(out_rows_ref, rows_ref, block_ref, forget_ref, *refs):
    outs, forget_out = refs[:5], refs[5]
    at = pl.program_id(0)

    @pl.when(at == 0)
    def _():
        forget_out[...] = dot_nn(rows_ref[...], forget_ref[...]).T[: forget_out.shape[0]]
        outs[0][...] = dot_nn(out_rows_ref[...], block_ref[...])

    @pl.when(at > 0)
    def _():
        term = dot_nn(rows_ref[...], block_ref[...])
        for i, out in enumerate(outs[1:]):

            @pl.when(at == i + 1)
            def _():
                out[...] = term


def run_attention_weights(out_rows, rows, gathered_all, width, slots):
    features, tokens = rows.shape
    fixed = lambda shape: pl.BlockSpec(shape, lambda i: (0, 0))
    last = 5 * width // 128
    shapes = [(features, width)] * 5 + [(slots, features)]
    return pl.pallas_call(
        attention_weights_kernel,
        grid=(5,),
        in_specs=[
            fixed((features, tokens)), fixed((features, tokens)),
            pl.BlockSpec((tokens, width), lambda i: (0, i)),
            pl.BlockSpec((tokens, 128), lambda i: (0, last)),
        ],
        out_specs=tuple(fixed(shape) for shape in shapes),
        out_shape=tuple(jax.ShapeDtypeStruct(shape, F32) for shape in shapes),
        compiler_params=pltpu.CompilerParams(dimension_semantics=("arbitrary",)),
        name="attention_weights",
    )(out_rows, rows, gathered_all, gathered_all)


def passed_along(value, axis, steps):
    count = lax.axis_size(axis)
    leading, last = (max(0, -steps), min(count, count - steps))
    return lax.ppermute(value, axis, [(source, source + steps) for source in range(leading, last)])


def relay(value, decay, axis, steps):
    carried = passed_along(value, axis, steps)
    for _ in range(lax.axis_size(axis) - 2):
        carried = passed_along(value + decay * carried, axis, steps)
    return carried


def gathered(value):
    return lax.all_gather(value, GROUPED, axis=0, tiled=True)


def per_device(
    hidden_in,
    cotangent,
    teacher_out,
    teacher_mix,
    valid_mask,
    doc_start,
    attn_gain,
    w_query,
    w_key,
    w_value,
    w_forget,
    forget_bias,
    head_gain,
    w_outgate,
    w_out,
    mlp_gain,
    w_gate,
    w_up,
    w_down,
):
    tokens, features = hidden_in.shape
    devices = lax.axis_size(GROUPED)
    tp = lax.axis_size("tp")
    share = tokens // tp
    rows = w_query.shape[0]
    width = w_query.shape[1]
    slots = w_forget.shape[1]
    units = w_gate.shape[1]
    tokens_all = tokens * devices
    mask_flat = valid_mask.astype(F32)

    vectors = [jnp.stack([attn_gain, mlp_gain]), head_gain, forget_bias]
    attn_parts = [w_query, w_key, w_value, w_outgate]
    mlp_parts = [w_gate, w_up, w_down]
    if (lax.axis_size("shard"), lax.axis_size("ctx")) == (4, 2):
        first, row_all, pack = run_spread(
            "gather_attention", 5, attn_parts, mlp_parts, w_forget.T, valid_mask.reshape(1, -1), vectors
        )
        second = gathered(pack)
        out_own, first = lax.optimization_barrier((w_out, first))
        (out_w,) = run_spread("gather_out", 6, [out_own])
        first, row_all, out_w = lax.optimization_barrier((first, row_all, out_w))
    else:
        vectors.append(jnp.sum(mask_flat).reshape(1, 1))
        row = [jnp.pad(v.astype(F32), ((0, 0), (0, rows - v.shape[1]))) for v in vectors]
        row_all = gathered(jnp.concatenate(row, axis=0)[None])
        forget_w = jnp.pad(w_forget, ((0, 0), (0, 128 - slots)))
        first = gathered(jnp.concatenate([*attn_parts, forget_w, w_out], axis=1))
        pack, first = lax.optimization_barrier((jnp.concatenate(mlp_parts, axis=1), first))
        second = gathered(pack)
        out_w = first[:, 4 * width + 128 :]
        first = first[:, : 4 * width + 128]

    attn_scale = row_all[:, 0].reshape(1, -1)
    mlp_scale = row_all[:, 1].reshape(1, -1)
    head_scale = row_all[:, 2, : width // devices].reshape(1, width)
    bias = row_all[:, 3, : slots // devices].reshape(1, slots)
    count_total = jnp.sum(row_all[:, 4, 0])
    loss_scale = (tokens_all / count_total).reshape(1, 1)

    hidden_f = hidden_in.astype(F32)
    scale = lax.rsqrt(jnp.mean(hidden_f * hidden_f, axis=-1, keepdims=True) + EPSILON)
    normed_in = (hidden_f * scale * attn_scale).astype(BF)
    pre_all = dot_nn(normed_in, first)
    query_pre = pre_all[:, :width]
    keys_pre = pre_all[:, width : 2 * width]
    query = jax.nn.silu(query_pre).astype(BF)
    keys = jax.nn.silu(keys_pre).astype(BF)
    values = pre_all[:, 2 * width : 3 * width].astype(BF)
    gate_pre = pre_all[:, 3 * width : 4 * width]
    forget_pre = pre_all[:, 4 * width : 4 * width + slots] + bias
    resets = doc_start.astype(F32)[:, None]

    spans, total, ends = run_ends(forget_pre, resets, keys, values)
    decay = total.reshape(slots, 1)
    state = relay(ends, decay, "ctx", 1)
    probs, pairs, mixing, mix, gated = run_forward(
        query, keys, values, forget_pre, spans, state, gate_pre, head_scale
    )
    gate_w = second[:, :units]
    up_w = second[:, units : 2 * units]
    down_w = second[:, 2 * units :]

    by_share = lambda tensor: tensor.reshape(tp, share, -1)
    hidden_s, teacher_out_s, teacher_mix_s, cotangent_s = map(by_share, (hidden_in, teacher_out, teacher_mix, cotangent))
    mask_s = by_share(mask_flat)
    narrow = lambda *shape: jax.ShapeDtypeStruct(shape, F32)

    partial = dot_nt(gated, out_w).astype(BF)
    partial, mask_s, loss_scale = lax.optimization_barrier((partial, mask_s, loss_scale))
    normed_mid, branch = run_exchange(
        middle_epilogue, "sum_branch", 1, partial, (hidden_s, mlp_scale),
        (narrow(share, features),),
    )
    gate_val = dot_nn(normed_mid, gate_w)
    up_val = dot_nn(normed_mid, up_w)
    hidden_units = (jax.nn.silu(gate_val) * up_val).astype(BF)
    units_all = gathered(hidden_units)
    output, grad_result, losses, normed_in_c, normed_mid_c = run_exchange(
        result_epilogue, "sum_result", 2, dot_nt(hidden_units, down_w).astype(BF),
        (hidden_s, branch, teacher_out_s, teacher_mix_s, cotangent_s, mask_s, loss_scale),
        (narrow(share, features), narrow(1, 128)),
        moved=(normed_in, normed_mid),
    )
    gap = output.astype(F32) - teacher_out.astype(F32)
    grad_mlp = (cotangent.astype(F32) + loss_scale * mask_flat[:, None] * gap).astype(BF)
    grad_units = dot_nn(grad_mlp, down_w)
    gate_sig = jax.nn.sigmoid(gate_val)
    grad_gate_val = (grad_units * up_val * (gate_sig * (1.0 + gate_val * (1.0 - gate_sig)))).astype(BF)
    grad_up_val = (grad_units * (gate_val * gate_sig)).astype(BF)
    grad_both = jnp.concatenate([grad_gate_val, grad_up_val], axis=1)
    partial = dot_nt(grad_both, second[:, : 2 * units]).astype(BF)
    units_all, grad_both = lax.optimization_barrier((units_all, grad_both))
    partial = lax.optimization_barrier((partial, grad_both))[0]
    mlp_all = gathered(grad_both)
    grad_branch, grad_middle, mlp_gain_part, grad_mlp_c = run_exchange(
        branch_epilogue, "sum_middle", 3, partial,
        (hidden_s, branch, teacher_mix_s, grad_result, mask_s, loss_scale, mlp_scale),
        (narrow(share, features), narrow(1, features)),
        moved=(grad_mlp,),
    )
    grad_gated = dot_nn(grad_branch, out_w)
    gquery, gkeys, gvalues, ggate, head_gain_part, gwrite, glog, carry = run_backward(
        grad_gated, query, keys, values, forget_pre, spans, state, gate_pre, head_scale, probs, pairs, mixing, mix
    )
    later = relay(carry, decay, "ctx", -1)
    grad_pre, bias_part = run_finish(
        gquery, gkeys, gvalues, ggate, gwrite, glog, keys, values, forget_pre, spans, query_pre, keys_pre,
        state, total, later, gated,
    )
    partial = dot_nt(grad_pre[:, width:], first).astype(BF)
    mlp_all, grad_pre = lax.optimization_barrier((mlp_all, grad_pre))
    partial = lax.optimization_barrier((partial, grad_pre))[0]
    attn_all = gathered(grad_pre)
    grad_in, _, grad_branch_c, plane_sums, all_sums = run_exchange(
        input_epilogue, "sum_input", 4, partial,
        (hidden_s, grad_middle, attn_scale, jnp.concatenate([mlp_gain_part, head_gain_part, bias_part, losses], axis=1)),
        (narrow(1, features),), moved=(grad_branch,), summing=True,
    )
    gate_grad, up_grad, down_grad, turned_branch, turned_in = run_weights(
        "mlp_weights", (normed_mid_c, grad_mlp_c), (mlp_all, units_all),
        ((0, 0, 0, units), (0, 0, units, units), (1, 1, 0, units)), (grad_branch_c, normed_in_c),
    )
    out_grad, query_grad, keys_grad, values_grad, outgate_grad, forget_grad = run_attention_weights(
        turned_branch, turned_in, attn_all, width, slots
    )
    index = lax.axis_index(GROUPED)

    cut = lambda row, size: lax.dynamic_slice_in_dim(row, index * size, size, axis=1)
    attn_gain_grad = cut(all_sums[:, :features], features // devices).reshape(-1)
    mlp_gain_grad = cut(all_sums[:, features : 2 * features], features // devices).reshape(-1)
    head_gain_grad = cut(plane_sums[:, 2 * features : 2 * features + width], width // devices)
    bias_grad = cut(plane_sums[:, 2 * features + width : 2 * features + width + slots], slots // devices)
    sums = all_sums[0, 2 * features + width + 128 :]
    loss_out = sums[0] / (2.0 * features * count_total)
    loss_mix = sums[1] / (2.0 * features * count_total)
    return (
        output,
        loss_out,
        loss_mix,
        grad_in.astype(F32),
        attn_gain_grad,
        query_grad,
        keys_grad,
        values_grad,
        forget_grad.T,
        bias_grad,
        head_gain_grad,
        outgate_grad,
        out_grad,
        mlp_gain_grad,
        gate_grad,
        up_grad,
        down_grad,
    )


def solution(mesh):
    return jax.shard_map(
        per_device,
        mesh=mesh,
        in_specs=(
            P(("shard", "ctx"), None),
            P(("shard", "ctx"), None),
            P(("shard", "ctx"), None),
            P(("shard", "ctx"), None),
            P(("shard", "ctx")),
            P(("shard", "ctx")),
            P(("shard", "ctx")),
            P(("shard", "ctx"), "tp"),
            P(("shard", "ctx"), "tp"),
            P(("shard", "ctx"), "tp"),
            P(("shard", "ctx"), "tp"),
            P("tp", ("shard", "ctx")),
            P("tp", ("shard", "ctx")),
            P(("shard", "ctx"), "tp"),
            P(("shard", "ctx"), "tp"),
            P(("shard", "ctx")),
            P(("shard", "ctx"), "tp"),
            P(("shard", "ctx"), "tp"),
            P(("shard", "ctx"), "tp"),
        ),
        out_specs=(
            P(("shard", "ctx"), None),
            P(),
            P(),
            P(("shard", "ctx"), None),
            P(("shard", "ctx")),
            P(("shard", "ctx"), "tp"),
            P(("shard", "ctx"), "tp"),
            P(("shard", "ctx"), "tp"),
            P(("shard", "ctx"), "tp"),
            P("tp", ("shard", "ctx")),
            P("tp", ("shard", "ctx")),
            P(("shard", "ctx"), "tp"),
            P(("shard", "ctx"), "tp"),
            P(("shard", "ctx")),
            P(("shard", "ctx"), "tp"),
            P(("shard", "ctx"), "tp"),
            P(("shard", "ctx"), "tp"),
        ),
        check_vma=False,
    )
```

```python
import functools

import jax
import jax.numpy as jnp
from jax import lax
from jax.experimental import pallas as pl
from jax.experimental.pallas import tpu as pltpu
from jax.sharding import PartitionSpec as P

F32 = jnp.float32
BF = jnp.bfloat16
EPSILON = 1e-06
GATE_NORM = 8.0


def dot_nn(a, b):
    return lax.dot_general(a, b, (((1,), (0,)), ((), ())), preferred_element_type=F32)


def dot_nt(a, b):
    return lax.dot_general(a, b, (((1,), (1,)), ((), ())), preferred_element_type=F32)


def dot_tn(a, b):
    return lax.dot_general(a, b, (((0,), (0,)), ((), ())), preferred_element_type=F32)


def halves(x):
    hi = x.astype(BF)
    return hi, (x - hi.astype(F32)).astype(BF)


def sigmoid(u):
    return 1.0 / (1.0 + jnp.exp(-u))


def n_levels(tokens):
    return tokens.bit_length() - 1


def span_matrix(level, tokens):
    t = lax.broadcasted_iota(jnp.int32, (tokens, tokens), 0)
    u = lax.broadcasted_iota(jnp.int32, (tokens, tokens), 1)
    depth = n_levels(tokens)
    if level == depth:
        keep = u <= t
    elif level == depth + 1:
        keep = u > t
    else:
        half = 1 << level
        edge = (t & ~(2 * half - 1)) + half
        odd = (t & half) > 0
        keep = (odd & (u >= edge) & (u <= t)) | (~odd & (u > t) & (u < edge))
    return keep.astype(F32).astype(BF)


def odd_rows(level, tokens, columns):
    t = lax.broadcasted_iota(jnp.int32, (tokens, columns), 0)
    return (t & (1 << level)) > 0


def same_pair(level, tokens):
    t = lax.broadcasted_iota(jnp.int32, (tokens, tokens), 0)
    u = lax.broadcasted_iota(jnp.int32, (tokens, tokens), 1)
    return (t >> (level + 1)) == (u >> (level + 1))


def ends_kernel(pre_ref, resets_ref, keys_ref, values_ref, spans_ref, total_ref, ends_ref):
    tokens, slots = pre_ref.shape
    depth = n_levels(tokens)
    width = keys_ref.shape[1]
    pre = pre_ref[...]
    log_decay = (jnp.minimum(pre, 0.0) - jnp.log1p(jnp.exp(-jnp.abs(pre)))) / GATE_NORM
    write = 1.0 - jnp.exp(log_decay)
    hi, lo = halves(log_decay)
    resets = jnp.broadcast_to(resets_ref[...], (tokens, slots)).astype(BF)
    stacked = jnp.concatenate([hi, lo, resets], axis=1)
    for level in range(depth + 2):
        sums = dot_nn(span_matrix(level, tokens), stacked)
        gap = sums[:, :slots] + sums[:, slots : 2 * slots]
        live = sums[:, 2 * slots :] < 0.5
        span = jnp.where(live, jnp.exp(gap), 0.0)
        spans_ref[level] = span
        if level == depth:
            total_ref[...] = span[tokens - 1 :, :]
        if level == depth + 1:
            hi, lo = halves(span * write)
            ends_ref[:, :width] = dot_tn(hi, keys_ref[...]) + dot_tn(lo, keys_ref[...])
            ends_ref[:, width:] = dot_tn(hi, values_ref[...]) + dot_tn(lo, values_ref[...])


def run_ends(pre, resets, keys, values):
    tokens, slots = pre.shape
    depth = n_levels(tokens)
    return pl.pallas_call(
        ends_kernel,
        out_shape=(
            jax.ShapeDtypeStruct((depth + 2, tokens, slots), F32),
            jax.ShapeDtypeStruct((1, slots), F32),
            jax.ShapeDtypeStruct((slots, keys.shape[1] + values.shape[1]), F32),
        ),
        name="slot_ends",
    )(pre, resets, keys, values)


def decay_write(pre):
    log_decay = (jnp.minimum(pre, 0.0) - jnp.log1p(jnp.exp(-jnp.abs(pre)))) / GATE_NORM
    return jnp.exp(log_decay)


def forward_kernel(
    query_ref, keys_ref, values_ref, pre_ref, spans_ref, state_ref, gate_ref, gain_ref,
    probs_ref, pairs_ref, mixing_ref, mix_ref, gated_ref,
):
    tokens, slots = pre_ref.shape
    depth = n_levels(tokens)
    width = keys_ref.shape[1]
    scaling = width ** (-0.5)
    write = 1.0 - decay_write(pre_ref[...])
    query = query_ref[...]
    pairs = dot_nt(query, keys_ref[...])
    pairs_ref[...] = pairs
    t = lax.broadcasted_iota(jnp.int32, (tokens, tokens), 0)
    u = lax.broadcasted_iota(jnp.int32, (tokens, tokens), 1)
    diagonal = jnp.sum(jnp.where(t == u, pairs, 0.0), axis=1, keepdims=True)
    state_hi, state_lo = halves(state_ref[:, :width])
    head = spans_ref[depth]
    raw = head * (dot_nt(query, state_hi) + dot_nt(query, state_lo)) + diagonal * write
    for level in range(depth):
        span = spans_ref[level]
        odd = odd_rows(level, tokens, slots)
        left, left_lo = halves(jnp.where(same_pair(level, tokens), pairs, 0.0))
        right, right_lo = halves(jnp.where(odd, 0.0, span * write))
        pulled = dot_nn(left, right) + dot_nn(left_lo, right) + dot_nn(left, right_lo)
        raw = raw + jnp.where(odd, span, 0.0) * pulled
    scores = scaling * raw
    scores = scores - jnp.max(scores, axis=1, keepdims=True)
    raised = jnp.exp(scores)
    probs = raised / jnp.sum(raised, axis=1, keepdims=True)
    probs_ref[...] = probs
    probs = probs.astype(BF).astype(F32)
    mixing = jnp.zeros((tokens, tokens), F32)
    for level in reversed(range(depth)):
        span = spans_ref[level]
        odd = odd_rows(level, tokens, slots)
        left, left_lo = halves(jnp.where(odd, span * probs, 0.0))
        right, right_lo = halves(jnp.where(odd, 0.0, span * write))
        pushed = dot_nt(left, right) + dot_nt(left_lo, right) + dot_nt(left, right_lo)
        mixing = jnp.where(same_pair(level, tokens), pushed, mixing)
    mixing = jnp.where(t == u, jnp.sum(probs * write, axis=1, keepdims=True), mixing)
    mixing, mixing_lo = halves(mixing)
    mixing_ref[...] = mixing
    state_hi, state_lo = halves(state_ref[:, width:])
    carried, carried_lo = halves(probs * head)
    mix = dot_nn(mixing, values_ref[...]) + dot_nn(mixing_lo, values_ref[...])
    mix = mix + dot_nn(carried, state_hi) + dot_nn(carried, state_lo) + dot_nn(carried_lo, state_hi)
    mix_ref[...] = mix
    scale = lax.rsqrt(jnp.mean(mix * mix, axis=1, keepdims=True) + EPSILON)
    gate = gate_ref[...]
    gated_ref[...] = (mix * scale * gain_ref[...] * (gate * sigmoid(gate))).astype(BF)


def run_forward(query, keys, values, pre, spans, state, gate, gain):
    tokens, slots = pre.shape
    width = keys.shape[1]
    return pl.pallas_call(
        forward_kernel,
        out_shape=(
            jax.ShapeDtypeStruct((tokens, slots), F32),
            jax.ShapeDtypeStruct((tokens, tokens), F32),
            jax.ShapeDtypeStruct((tokens, tokens), BF),
            jax.ShapeDtypeStruct((tokens, width), F32),
            jax.ShapeDtypeStruct((tokens, width), BF),
        ),
        name="slot_forward",
    )(query, keys, values, pre, spans, state, gate, gain)


def backward_kernel(
    grad_ref, query_ref, keys_ref, values_ref, pre_ref, spans_ref, state_ref, gate_ref, gain_ref,
    probs_ref, pairs_ref, mixing_ref, mix_ref,
    gquery_ref, gkeys_ref, gvalues_ref, ggate_ref, ggain_ref, gwrite_ref, glog_ref, carry_ref,
):
    tokens, slots = pre_ref.shape
    depth = n_levels(tokens)
    width = keys_ref.shape[1]
    scaling = width ** (-0.5)
    gate = gate_ref[...]
    sig = sigmoid(gate)
    silu = gate * sig
    gain = gain_ref[...]
    mix = mix_ref[...]
    scale = lax.rsqrt(jnp.mean(mix * mix, axis=1, keepdims=True) + EPSILON)
    normed = mix * scale
    grad = grad_ref[...]
    ggate_ref[...] = (grad * gain * normed * (sig * (1.0 + gate * (1.0 - sig)))).astype(BF)
    ggain_ref[...] = jnp.sum(grad * normed * silu, axis=0, keepdims=True)
    inner = grad * gain * silu
    mix_grad = scale * (inner - normed * jnp.mean(normed * inner, axis=1, keepdims=True))
    mix_low = mix_grad.astype(BF)

    write = 1.0 - decay_write(pre_ref[...])
    query, keys, values = query_ref[...], keys_ref[...], values_ref[...]
    pairs = pairs_ref[...]
    pairs_t = dot_nt(keys, query)
    mix_rest = (mix_grad - mix_low.astype(F32)).astype(BF)
    weigh = dot_nt(mix_low, values) + dot_nt(mix_rest, values)
    weigh_t = dot_nt(values, mix_low) + dot_nt(values, mix_rest)
    t = lax.broadcasted_iota(jnp.int32, (tokens, tokens), 0)
    u = lax.broadcasted_iota(jnp.int32, (tokens, tokens), 1)
    pair_diag = jnp.sum(jnp.where(t == u, pairs, 0.0), axis=1, keepdims=True)
    weigh_diag = jnp.sum(jnp.where(t == u, weigh, 0.0), axis=1, keepdims=True)
    head = spans_ref[depth]
    probs = probs_ref[...]
    probs_low = probs.astype(BF).astype(F32)

    vstate_hi, vstate_lo = halves(state_ref[:, width:])
    head_probs = head * (
        dot_nt(mix_low, vstate_hi) + dot_nt(mix_low, vstate_lo) + dot_nt(mix_rest, vstate_hi)
    )
    probs_grad = head_probs + weigh_diag * write
    row_values, row_keys = [], []
    for level in range(depth):
        span = spans_ref[level]
        odd = odd_rows(level, tokens, slots)
        same = same_pair(level, tokens)
        right, right_lo = halves(jnp.where(odd, 0.0, span * write))
        reach = jnp.where(odd, span, 0.0)
        left, left_lo = halves(jnp.where(same, weigh, 0.0))
        term = reach * (dot_nn(left, right) + dot_nn(left_lo, right) + dot_nn(left, right_lo))
        row_values.append(term)
        left, left_lo = halves(jnp.where(same, pairs, 0.0))
        row_keys.append(reach * (dot_nn(left, right) + dot_nn(left_lo, right) + dot_nn(left, right_lo)))
        probs_grad = probs_grad + term
    scores_grad = probs * (probs_grad - jnp.sum(probs_grad * probs, axis=1, keepdims=True))
    scores_grad = scaling * scores_grad

    kstate_hi, kstate_lo = halves(state_ref[:, :width])
    head_keys = head * (dot_nt(query, kstate_hi) + dot_nt(query, kstate_lo))
    gwrite = pair_diag * scores_grad + weigh_diag * probs_low
    glog = dot_tn(span_matrix(depth, tokens), (head_keys * scores_grad + head_probs * probs_low).astype(BF))
    gpairs = jnp.zeros((tokens, tokens), F32)
    for level in reversed(range(depth)):
        span = spans_ref[level]
        odd = odd_rows(level, tokens, slots)
        same = same_pair(level, tokens)
        reach = jnp.where(odd, span, 0.0)
        source = jnp.where(odd, 0.0, span)
        key_side, key_rest = halves(reach * scores_grad)
        value_side, value_rest = halves(reach * probs_low)
        seen, seen_rest = halves(jnp.where(same, pairs_t, 0.0))
        felt, felt_rest = halves(jnp.where(same, weigh_t, 0.0))
        sent, sent_rest = halves(source * write)
        pushed = dot_nt(key_side, sent) + dot_nt(key_rest, sent) + dot_nt(key_side, sent_rest)
        gpairs = jnp.where(same, pushed, gpairs)
        column = source * (
            dot_nn(seen, key_side) + dot_nn(seen, key_rest) + dot_nn(seen_rest, key_side)
            + dot_nn(felt, value_side) + dot_nn(felt, value_rest) + dot_nn(felt_rest, value_side)
        )
        gwrite = gwrite + column
        moved = column * write + row_values[level] * probs_low + row_keys[level] * scores_grad
        spread = span_matrix(level, tokens)
        moved, moved_rest = halves(moved)
        glog = glog + dot_tn(spread, moved) + dot_tn(spread, moved_rest)
    gpairs = jnp.where(t == u, jnp.sum(scores_grad * write, axis=1, keepdims=True), gpairs)
    gpairs, gpairs_rest = halves(gpairs)
    gwrite_ref[...] = gwrite
    glog_ref[...] = glog
    key_head, key_head_rest = halves(scores_grad * head)
    gquery_ref[...] = (
        dot_nn(gpairs, keys)
        + dot_nn(gpairs_rest, keys)
        + dot_nn(key_head, kstate_hi)
        + dot_nn(key_head, kstate_lo)
        + dot_nn(key_head_rest, kstate_hi)
    )
    gkeys_ref[...] = dot_tn(gpairs, query) + dot_tn(gpairs_rest, query)
    gvalues_ref[...] = dot_tn(mixing_ref[...], mix_low)
    carry_ref[:, :width] = dot_tn(key_head, query) + dot_tn(key_head_rest, query)
    carry_ref[:, width:] = dot_tn((probs_low * head).astype(BF), mix_low)


def run_backward(grad, query, keys, values, pre, spans, state, gate, gain, probs, pairs, mixing, mix):
    tokens, slots = pre.shape
    width = keys.shape[1]
    wide = jax.ShapeDtypeStruct((tokens, width), F32)
    narrow = jax.ShapeDtypeStruct((tokens, slots), F32)
    return pl.pallas_call(
        backward_kernel,
        out_shape=(
            wide, wide, wide,
            jax.ShapeDtypeStruct((tokens, width), BF),
            jax.ShapeDtypeStruct((1, width), F32),
            narrow, narrow,
            jax.ShapeDtypeStruct((slots, 2 * width), F32),
        ),
        name="slot_backward",
    )(grad, query, keys, values, pre, spans, state, gate, gain, probs, pairs, mixing, mix)


def finish_kernel(
    gquery_ref, gkeys_ref, gvalues_ref, ggate_ref, gwrite_ref, glog_ref,
    keys_ref, values_ref, pre_ref, spans_ref, query_pre_ref, keys_pre_ref,
    state_ref, total_ref, ends_ref, gated_ref, out_ref, bias_ref,
):
    tokens, slots = pre_ref.shape
    depth = n_levels(tokens)
    width = keys_ref.shape[1]
    pre = pre_ref[...]
    decay = decay_write(pre)
    write = 1.0 - decay
    keys, values = keys_ref[...], values_ref[...]
    ends = ends_ref[...]
    ends_low = ends.astype(BF)
    tail = spans_ref[depth + 1]
    sent = (tail * write).astype(BF)
    column = tail * (dot_nt(keys, ends_low[:, :width]) + dot_nt(values, ends_low[:, width:]))
    glog = glog_ref[...] + dot_tn(span_matrix(depth + 1, tokens), (column * write).astype(BF))
    carried = lax.dot_general(
        jnp.ones((1, 2 * width), F32), ends * state_ref[...], (((1,), (1,)), ((), ())),
        precision=lax.Precision.HIGHEST, preferred_element_type=F32,
    )
    glog = glog + carried * total_ref[...]
    glog = glog - decay * (gwrite_ref[...] + column)
    def put(part, value):
        out_ref[:, part * width : (part + 1) * width] = value.astype(BF)

    put(0, gated_ref[...])
    u = query_pre_ref[...]
    s = sigmoid(u)
    put(1, gquery_ref[...] * (s * (1.0 + u * (1.0 - s))))
    u = keys_pre_ref[...]
    s = sigmoid(u)
    gkeys = gkeys_ref[...] + dot_nn(sent, ends_low[:, :width])
    put(2, gkeys * (s * (1.0 + u * (1.0 - s))))
    put(3, gvalues_ref[...] + dot_nn(sent, ends_low[:, width:]))
    put(4, ggate_ref[...])
    gforget = (glog * sigmoid(-pre) / GATE_NORM).astype(BF)
    gforget = jnp.concatenate([gforget, jnp.zeros((tokens, 128 - slots), BF)], axis=1)
    out_ref[:, 5 * width :] = gforget
    bias_ref[...] = jnp.sum(gforget.astype(F32), axis=0, keepdims=True)


def run_finish(gquery, gkeys, gvalues, ggate, gwrite, glog, keys, values, pre, spans, query_pre, keys_pre, state, total, ends, gated):
    tokens, slots = pre.shape
    width = keys.shape[1]
    return pl.pallas_call(
        finish_kernel,
        out_shape=(jax.ShapeDtypeStruct((tokens, 5 * width + 128), BF), jax.ShapeDtypeStruct((1, 128), F32)),
        name="slot_finish",
    )(gquery, gkeys, gvalues, ggate, gwrite, glog, keys, values, pre, spans, query_pre, keys_pre, state, total, ends, gated)


MESH = pl.DeviceIdType.MESH
GROUPED = ("shard", "ctx")


def greet(axes_of_peers):
    barrier = pltpu.get_barrier_semaphore()
    for peer in axes_of_peers:
        pl.semaphore_signal(barrier, inc=1, device_id=peer, device_id_type=MESH)
    pl.semaphore_wait(barrier, len(axes_of_peers))


def tp_peers():
    count = lax.axis_size("tp")
    me = lax.axis_index("tp")
    return me, [lax.rem(me + k, count) for k in range(1, count)]


CHUNKS = 4
LATENCY = 2.2
LEAD = 10
CLOSING = 3


def tp_line(partial_ref, full_ref, arrived, staged, sums_ref, begin, finish, settle, send_a, recv_a, send_b, recv_b):
    count = lax.axis_size("tp")
    me = lax.axis_index("tp")
    rows = partial_ref.shape[1] // CHUNKS
    peers = [lax.rem(me + 1, count), lax.rem(me + count - 1, count)]

    def at_place(side, place):
        return place if side == 0 else count - 1 - place

    def cut(chunk):
        return pl.ds(chunk * rows, rows)

    def sum_copy(side, hop, chunk, source):
        return pltpu.make_async_remote_copy(
            src_ref=source,
            dst_ref=arrived.at[side, hop, chunk],
            send_sem=send_a.at[side, hop, chunk],
            recv_sem=recv_a.at[side, hop, chunk],
            device_id={"tp": peers[side]},
            device_id_type=MESH,
        )

    def row_copy(side, hop, chunk, block):
        return pltpu.make_async_remote_copy(
            src_ref=full_ref.at[block, cut(chunk)],
            dst_ref=full_ref.at[block, cut(chunk)],
            send_sem=send_b.at[side, hop, chunk],
            recv_sem=recv_b.at[side, hop, chunk],
            device_id={"tp": peers[side]},
            device_id_type=MESH,
        )

    def own(side, hop, chunk):
        return partial_ref.at[at_place(side, count - 1 - hop), cut(chunk)]

    def send_own(chunk):
        for side in range(2):

            @pl.when(me == at_place(side, 0))
            def _():
                for hop in range(count - 1):
                    sum_copy(side, hop, chunk, own(side, hop, chunk)).start()

    def add_hop(side, place, hop, chunk):
        @pl.when(me == at_place(side, place))
        def _():
            slot = staged.at[side, hop, chunk]
            copy = sum_copy(side, hop, chunk, slot)
            copy.wait_recv()
            slot[...] = (own(side, hop, chunk)[...].astype(F32) + arrived[side, hop, chunk].astype(F32)).astype(BF)
            copy.start()

    def close(chunk):
        sums_ref[...] = partial_ref[me, cut(chunk)].astype(F32)
        for side in range(2):
            place = me if side == 0 else count - 1 - me
            hop = jnp.minimum(count - 1 - place, count - 2)

            @pl.when(place > 0)
            def _():
                sum_copy(side, hop, chunk, staged.at[side, hop, chunk]).wait_recv()
                sums_ref[...] += arrived[side, hop, chunk].astype(F32)

        finish(chunk, sums_ref[...])
        for side in range(2):

            @pl.when(me != at_place(side, count - 1))
            def _():
                row_copy(side, 0, chunk, me).start()

    def forward(side, place, distance, chunk):
        @pl.when(me == at_place(side, place))
        def _():
            block = at_place(side, place - distance)
            row_copy(side, distance - 1, chunk, block).wait_recv()
            if place < count - 1:
                row_copy(side, distance, chunk, block).start()

    step = 1 + LATENCY
    events = [(-1, begin), (900, settle)]
    for chunk in range(CHUNKS):
        base = (count - 1) * chunk
        closed = base + (count - 1) + (count - 2) * LATENCY
        events.append((base - LEAD * (count - 1), functools.partial(send_own, chunk)))
        events.append((closed, functools.partial(close, chunk)))
        for side in range(2):
            for place in range(1, count):
                for hop in range(count - 1 - place):
                    due = base + hop + place * step
                    events.append((due, functools.partial(add_hop, side, place, hop, chunk)))
                for distance in range(1, place + 1):
                    due = closed + CLOSING + distance * step
                    if place == count - 1:
                        due += 1000
                    events.append((due, functools.partial(forward, side, place, distance, chunk)))
    for _, event in sorted(events, key=lambda event: event[0]):
        event()

    def drain():
        for side in range(2):
            for place in range(count - 1):

                @pl.when(me == at_place(side, place))
                def _():
                    for chunk in range(CHUNKS):
                        for hop in range(count - 1 - place):
                            sum_copy(side, hop, chunk, staged.at[side, hop, chunk]).wait_send()
                        for hop in range(place + 1):
                            row_copy(side, hop, chunk, at_place(side, place - hop)).wait_send()

    return drain


def plane_peers():
    shards, ctxs = lax.axis_size("shard"), lax.axis_size("ctx")
    devices = shards * ctxs
    me = lax.axis_index("shard") * ctxs + lax.axis_index("ctx")
    peers = [lax.rem(me + k, devices) for k in range(1, devices)]
    places = [{"shard": lax.div(peer, ctxs), "ctx": lax.rem(peer, ctxs)} for peer in peers]
    return me, peers, places


def start_scatter(sources, targets, send_sems, recv_sems):
    me, peers, places = plane_peers()
    copies = []
    for i, (source, target) in enumerate(zip(sources, targets)):
        step = target.shape[2]

        def block(at):
            if len(source.shape) == 3:
                return source.at[at]
            return source.at[:, pl.ds(pl.multiple_of(at * step, step), step)]

        for k, (peer, place) in enumerate(zip(peers, places)):
            copy = pltpu.make_async_remote_copy(
                src_ref=block(peer),
                dst_ref=target.at[me],
                send_sem=send_sems.at[i, k],
                recv_sem=recv_sems.at[i, k],
                device_id=place,
                device_id_type=MESH,
            )
            copy.start()
            copies.append(copy)
    for source, target in zip(sources, targets):
        target[me] = block_of(source, me, target.shape[2])
    return copies


def block_of(source, at, step):
    if len(source.shape) == 3:
        return source[at]
    return source[:, pl.ds(pl.multiple_of(at * step, step), step)]


def spread_kernel(n_parts, n_packed, *refs):
    parts, refs = refs[:n_parts], refs[n_parts:]
    packed, refs = refs[:n_packed], refs[n_packed:]
    if n_packed:
        forget_ref, mask_ref, vectors, refs = refs[0], refs[1], refs[2:5], refs[5:]
        out_ref, rows_ref, pack_ref, slab, part_sems, own_sem, send_sems, recv_sems = refs[:8]
        row_ref, row_send, row_recv, pack_slab, pack_sems, pack_sem = refs[8:]
    else:
        out_ref, slab, part_sems, own_sem, send_sems, recv_sems = refs
    shard, core = lax.axis_index("shard"), lax.axis_index("ctx")
    me, _, places = plane_peers()
    across = shard + 1 - 2 * lax.rem(shard, 2)
    along = lax.rem(shard + 2, 4)
    corner = lax.rem(across + 2, 4)
    other = 1 - core
    to_x, to_y, to_core = {"shard": across}, {"shard": along}, {"ctx": other}
    rows = slab.shape[0]
    piece = rows // 4

    def load_all(sources, target, sems):
        loads = []
        start = 0
        for i, part in enumerate(sources):
            load = pltpu.make_async_copy(part, target.at[:, pl.ds(start, part.shape[1])], sems.at[i])
            load.start()
            loads.append(load)
            start += part.shape[1]
        return loads

    loads = load_all(parts, slab, part_sems)
    if n_packed:
        room = jnp.zeros((128 - forget_ref.shape[0], rows), BF)
        slab[:, slab.shape[1] - 128 :] = jnp.concatenate([forget_ref[...], room], axis=0).T
        row_ref[...] = jnp.zeros_like(row_ref)
        for i, vector in zip((0, 2, 3), vectors):
            row_ref[i : i + vector.shape[0], : vector.shape[1]] = vector[...].astype(F32)
        count = jnp.sum(mask_ref[...].astype(F32), axis=1, keepdims=True)
        row_ref[4:5, :] = jnp.broadcast_to(count, (1, row_ref.shape[1]))
    greet(places)
    for load in loads:
        load.wait()
    keep = pltpu.make_async_copy(slab, out_ref.at[pl.ds(pl.multiple_of(me * rows, rows), rows)], own_sem)
    keep.start()

    def landing(block, part):
        return out_ref.at[pl.ds(pl.multiple_of(block * rows + part * piece, piece), piece)]

    started = []

    def send(kind, source, block, part, place):
        copy = pltpu.make_async_remote_copy(
            src_ref=source,
            dst_ref=landing(block, part),
            send_sem=send_sems.at[kind],
            recv_sem=recv_sems.at[kind],
            device_id=place,
            device_id_type=MESH,
        )
        copy.start()
        started.append(copy)

    def receive(kind, block, part, place):
        region = landing(block, part)
        pltpu.make_async_remote_copy(
            src_ref=region,
            dst_ref=region,
            send_sem=send_sems.at[kind],
            recv_sem=recv_sems.at[kind],
            device_id=place,
            device_id_type=MESH,
        ).wait_recv()

    def own(part):
        return slab.at[pl.ds(part * piece, piece)]

    def block(place, at_core):
        return 2 * place + at_core

    for part in range(4):
        turn = (part + 2) % 4
        send(part, own(part), me, part, to_x)
        send(4 + turn, own(turn), me, turn, to_y)
    if n_packed:
        copies = start_sums(row_ref, rows_ref, row_send, row_recv, [], places, me)
    for part in range(4):
        send(8 + part, own(part), me, part, to_core)
    if n_packed:
        for load in load_all(packed, pack_slab, pack_sems):
            load.wait()
        store = pltpu.make_async_copy(pack_slab, pack_ref, pack_sem)
        store.start()
    x_block, y_block, far_block = block(across, core), block(along, core), block(corner, core)
    for part in range(4):
        turn = (part + 2) % 4
        receive(part, x_block, part, to_x)
        if part < 2:
            send(12 + part, landing(x_block, part), x_block, part, to_y)
        send(16 + part, landing(x_block, part), x_block, part, to_core)
        receive(4 + turn, y_block, turn, to_y)
        if turn >= 2:
            send(12 + turn, landing(y_block, turn), y_block, turn, to_x)
        send(20 + turn, landing(y_block, turn), y_block, turn, to_core)
    for part in (0, 2, 1, 3):
        receive(12 + part, far_block, part, to_y if part < 2 else to_x)
        send(24 + part, landing(far_block, part), far_block, part, to_core)
    for kind, place in ((8, shard), (16, across), (20, along), (24, corner)):
        for part in range(4):
            receive(kind + part, block(place, other), part, to_core)
    for copy in started:
        copy.wait_send()
    keep.wait()
    if n_packed:
        store.wait()
        for copy in copies:
            copy.wait()


def run_spread(name, collective_id, parts, packed=(), forget=None, mask=None, vectors=()):
    devices = lax.axis_size(GROUPED)
    rows = parts[0].shape[0]
    columns = sum(part.shape[1] for part in parts) + (128 if packed else 0)
    anywhere = pl.BlockSpec(memory_space=pl.ANY)
    in_specs, out_specs = [anywhere] * len(parts), [anywhere]
    out_shape = [jax.ShapeDtypeStruct((devices * rows, columns), BF)]
    scratch = [
        pltpu.VMEM((rows, columns), BF),
        pltpu.SemaphoreType.DMA((len(parts),)),
        pltpu.SemaphoreType.DMA,
        *[pltpu.SemaphoreType.DMA((28,))] * 2,
    ]
    args = list(parts)
    if packed:
        packed_shape = (rows, sum(part.shape[1] for part in packed))
        args += [*packed, forget, mask, *vectors]
        in_specs += [*[anywhere] * len(packed), *[pl.BlockSpec(memory_space=pltpu.VMEM)] * (2 + len(vectors))]
        out_specs += [pl.BlockSpec(memory_space=pltpu.VMEM), anywhere]
        out_shape += [jax.ShapeDtypeStruct((devices, 8, rows), F32), jax.ShapeDtypeStruct(packed_shape, BF)]
        scratch += [
            pltpu.VMEM((8, rows), F32),
            *[pltpu.SemaphoreType.DMA((devices - 1,))] * 2,
            pltpu.VMEM(packed_shape, BF),
            pltpu.SemaphoreType.DMA((len(packed),)),
            pltpu.SemaphoreType.DMA,
        ]
    return pl.pallas_call(
        functools.partial(spread_kernel, len(parts), len(packed)),
        out_shape=tuple(out_shape),
        in_specs=in_specs,
        out_specs=tuple(out_specs),
        scratch_shapes=scratch,
        compiler_params=pltpu.CompilerParams(collective_id=collective_id, has_side_effects=True),
        name=name,
    )(*args)


def start_sums(row_ref, landed, send_sems, recv_sems, peers, places, me):
    copies = []
    landed[me] = row_ref[...]
    for k, place in enumerate(places):
        copy = pltpu.make_async_remote_copy(
            src_ref=row_ref,
            dst_ref=landed.at[me],
            send_sem=send_sems.at[k],
            recv_sem=recv_sems.at[k],
            device_id=place,
            device_id_type=MESH,
        )
        copy.start()
        copies.append(copy)
    return copies


def summed(landed):
    total = landed[0]
    for k in range(1, landed.shape[0]):
        total = total + landed[k]
    return total


def exchange_kernel(epilogue, n_in, n_rows, n_moved, n_sums, partial_ref, *refs):
    me, peers = tp_peers()
    inputs, refs = refs[:n_in], refs[n_in:]
    sources, refs = refs[:n_moved], refs[n_moved:]
    full_ref, refs = refs[0], refs[1:]
    outputs, refs = refs[:n_rows], refs[n_rows:]
    targets, refs = refs[:n_moved], refs[n_moved:]
    sums, refs = refs[: 2 * n_sums], refs[2 * n_sums :]
    arrived, staged, sums_ref, send_a, recv_a, send_b, recv_b, send_m, recv_m = refs[:9]
    own, plane, places = plane_peers()
    across = [{"tp": peer} for peer in peers]
    greet(across + (places if n_moved or n_sums else []))
    moves = []
    rows = full_ref.shape[1] // CHUNKS
    started = []

    def finish(chunk, total):
        part = pl.ds(chunk * rows, rows)
        full_ref[me, part] = epilogue(total, me, part, chunk == 0, inputs, outputs)
        if n_sums and chunk == CHUNKS - 1:
            row_ref, in_plane, _, _, send_p, recv_p = refs[9:15]
            width = outputs[0].shape[1]
            row_ref[:, :width] = outputs[0][...]
            row_ref[:, width:] = inputs[-1][...]
            started.extend(start_sums(row_ref, in_plane, send_p, recv_p, plane, places, own))

    def begin():
        moves.extend(start_scatter(sources, targets, send_m, recv_m))

    def settle():
        if not n_sums:
            return
        row_ref, in_plane, plane_row, in_tp, send_p, recv_p, send_t, recv_t = refs[9:]
        for copy in started:
            copy.wait()
        plane_row[...] = summed(in_plane)
        sums[0][...] = plane_row[...]
        for copy in start_sums(plane_row, in_tp, send_t, recv_t, peers, across, me):
            copy.wait()
        sums[1][...] = summed(in_tp)

    drain = tp_line(
        partial_ref, full_ref, arrived, staged, sums_ref, begin, finish, settle, send_a, recv_a, send_b, recv_b
    )
    drain()
    for copy in moves:
        copy.wait()


def run_exchange(epilogue, name, collective_id, partial, inputs, row_outputs, moved=(), summing=False):
    tp = lax.axis_size("tp")
    devices = lax.axis_size(GROUPED)
    tokens, columns = partial.shape
    share = tokens // tp
    partial = partial.reshape(tp, share, columns)
    step = columns // devices
    if step % 128:
        moved = [m.reshape(tokens, devices, step).transpose(1, 0, 2) for m in moved]
    count = len(moved)
    scratch = [
        *[pltpu.VMEM((2, tp - 1, CHUNKS, share // CHUNKS, columns), BF)] * 2,
        pltpu.VMEM((share // CHUNKS, columns), F32),
        *[pltpu.SemaphoreType.DMA((2, tp - 1, CHUNKS))] * 4,
        *[pltpu.SemaphoreType.DMA((max(count, 1), devices - 1))] * 2,
    ]
    extra = ()
    if summing:
        row = row_outputs[0].shape[1] + inputs[-1].shape[1]
        extra = (jax.ShapeDtypeStruct((1, row), F32),) * 2
        scratch += [
            pltpu.VMEM((1, row), F32),
            pltpu.VMEM((devices, 1, row), F32),
            pltpu.VMEM((1, row), F32),
            pltpu.VMEM((tp, 1, row), F32),
            *[pltpu.SemaphoreType.DMA((devices - 1,))] * 2,
            *[pltpu.SemaphoreType.DMA((tp - 1,))] * 2,
        ]
    out_shape = (
        jax.ShapeDtypeStruct((tp, share, columns), BF),
        *row_outputs,
        *[jax.ShapeDtypeStruct((devices, tokens, step), BF)] * count,
        *extra,
    )
    outs = pl.pallas_call(
        functools.partial(exchange_kernel, epilogue, len(inputs), len(row_outputs), count, int(summing)),
        out_shape=out_shape,
        in_specs=[pl.BlockSpec(memory_space=pltpu.VMEM)] * (1 + len(inputs) + count),
        out_specs=tuple([pl.BlockSpec(memory_space=pltpu.VMEM)] * len(out_shape)),
        scratch_shapes=scratch,
        compiler_params=pltpu.CompilerParams(collective_id=collective_id, has_side_effects=True),
        name=name,
    )(partial, *inputs, *moved)
    start = 1 + len(row_outputs)
    return (
        outs[0].reshape(tokens, columns),
        *outs[1:start],
        *[o.reshape(devices * tokens, step) for o in outs[start : start + count]],
        *outs[start + count :],
    )


def middle_epilogue(total, me, part, first, inputs, outputs):
    hidden_ref, gain_ref = inputs
    (branch_ref,) = outputs
    branch_ref[part, :] = total
    middle = hidden_ref[me, part].astype(F32) + total
    scale = lax.rsqrt(jnp.mean(middle * middle, axis=1, keepdims=True) + EPSILON)
    return (middle * scale * gain_ref[...]).astype(BF)


def result_epilogue(total, me, part, first, inputs, outputs):
    hidden_ref, branch_ref, teacher_out_ref, teacher_mix_ref, cotangent_ref, mask_ref, scale_ref = inputs
    grad_ref, losses_ref = outputs
    branch = branch_ref[part, :]
    result = hidden_ref[me, part].astype(F32) + branch + total
    mask = mask_ref[me, part]
    gap = result - teacher_out_ref[me, part].astype(F32)
    gap_mix = branch - teacher_mix_ref[me, part].astype(F32)
    loss_out = jnp.sum(mask * (gap * gap), keepdims=True)
    loss_mix = jnp.sum(mask * (gap_mix * gap_mix), keepdims=True)
    lane = lax.broadcasted_iota(jnp.int32, (1, 128), 1)
    losses = jnp.where(lane == 0, loss_out, 0.0) + jnp.where(lane == 1, loss_mix, 0.0)
    losses_ref[...] = losses if first else losses_ref[...] + losses
    grad_ref[part, :] = cotangent_ref[me, part].astype(F32) + scale_ref[...] * mask * gap
    return result.astype(BF)


def norm_back(grad, rows, gain):
    scale = lax.rsqrt(jnp.mean(rows * rows, axis=1, keepdims=True) + EPSILON)
    unit = rows * scale
    gain_grad = jnp.sum(grad * unit, axis=0, keepdims=True)
    inner = grad * gain
    return scale * (inner - unit * jnp.mean(unit * inner, axis=1, keepdims=True)), gain_grad


def branch_epilogue(total, me, part, first, inputs, outputs):
    hidden_ref, branch_ref, teacher_mix_ref, grad_ref, mask_ref, scale_ref, gain_ref = inputs
    grad_middle_ref, gain_grad_ref = outputs
    branch = branch_ref[part, :]
    back, gain_grad = norm_back(total, hidden_ref[me, part].astype(F32) + branch, gain_ref[...])
    gain_grad_ref[...] = gain_grad if first else gain_grad_ref[...] + gain_grad
    grad_middle = back + grad_ref[part, :]
    grad_middle_ref[part, :] = grad_middle
    gap_mix = branch - teacher_mix_ref[me, part].astype(F32)
    return (grad_middle + scale_ref[...] * mask_ref[me, part] * gap_mix).astype(BF)


def input_epilogue(total, me, part, first, inputs, outputs):
    hidden_ref, grad_middle_ref, gain_ref = inputs[:3]
    (gain_grad_ref,) = outputs
    back, gain_grad = norm_back(total, hidden_ref[me, part].astype(F32), gain_ref[...])
    gain_grad_ref[...] = gain_grad if first else gain_grad_ref[...] + gain_grad
    return (back + grad_middle_ref[part, :]).astype(BF)


def weights_kernel(segments, n_rows, n_columns, n_turned, *refs):
    rows, refs = refs[:n_rows], refs[n_rows:]
    columns, refs = refs[:n_columns], refs[n_columns:]
    straight, outs = refs[:n_turned], refs[n_turned:]
    at = pl.program_id(0)
    for ref, out in zip(straight, outs[len(segments) :]):
        out[...] = ref[...].T
    turned = [ref[...].T for ref in rows]
    for (row, column, start, width), out in zip(segments, outs):
        term = dot_nn(turned[row], columns[column][:, pl.ds(start, width)])

        @pl.when(at == 0)
        def _():
            out[...] = term

        @pl.when(at > 0)
        def _():
            out[...] += term


def run_weights(name, rows, columns, segments, turned):
    tokens, features = rows[0].shape
    block = 512
    whole = lambda width: pl.BlockSpec((block, width), lambda i: (i, 0))
    shapes = [(features, segment[3]) for segment in segments]
    return pl.pallas_call(
        functools.partial(weights_kernel, segments, len(rows), len(columns), len(turned)),
        grid=(tokens // block,),
        in_specs=[*[whole(features)] * len(rows), *[whole(c.shape[1]) for c in (*columns, *turned)]],
        out_specs=(
            *[pl.BlockSpec(shape, lambda i: (0, 0)) for shape in shapes],
            *[pl.BlockSpec((t.shape[1], block), lambda i: (0, i)) for t in turned],
        ),
        out_shape=(
            *[jax.ShapeDtypeStruct(shape, F32) for shape in shapes],
            *[jax.ShapeDtypeStruct((t.shape[1], tokens), BF) for t in turned],
        ),
        compiler_params=pltpu.CompilerParams(dimension_semantics=("arbitrary",)),
        name=name,
    )(*rows, *columns, *turned)


def attention_weights_kernel(out_rows_ref, rows_ref, block_ref, forget_ref, *refs):
    outs, forget_out = refs[:5], refs[5]
    at = pl.program_id(0)

    @pl.when(at == 0)
    def _():
        forget_out[...] = dot_nn(rows_ref[...], forget_ref[...]).T[: forget_out.shape[0]]
        outs[0][...] = dot_nn(out_rows_ref[...], block_ref[...])

    @pl.when(at > 0)
    def _():
        term = dot_nn(rows_ref[...], block_ref[...])
        for i, out in enumerate(outs[1:]):

            @pl.when(at == i + 1)
            def _():
                out[...] = term


def run_attention_weights(out_rows, rows, gathered_all, width, slots):
    features, tokens = rows.shape
    fixed = lambda shape: pl.BlockSpec(shape, lambda i: (0, 0))
    last = 5 * width // 128
    shapes = [(features, width)] * 5 + [(slots, features)]
    return pl.pallas_call(
        attention_weights_kernel,
        grid=(5,),
        in_specs=[
            fixed((features, tokens)), fixed((features, tokens)),
            pl.BlockSpec((tokens, width), lambda i: (0, i)),
            pl.BlockSpec((tokens, 128), lambda i: (0, last)),
        ],
        out_specs=tuple(fixed(shape) for shape in shapes),
        out_shape=tuple(jax.ShapeDtypeStruct(shape, F32) for shape in shapes),
        compiler_params=pltpu.CompilerParams(dimension_semantics=("arbitrary",)),
        name="attention_weights",
    )(out_rows, rows, gathered_all, gathered_all)


def passed_along(value, axis, steps):
    count = lax.axis_size(axis)
    leading, last = (max(0, -steps), min(count, count - steps))
    return lax.ppermute(value, axis, [(source, source + steps) for source in range(leading, last)])


def relay(value, decay, axis, steps):
    carried = passed_along(value, axis, steps)
    for _ in range(lax.axis_size(axis) - 2):
        carried = passed_along(value + decay * carried, axis, steps)
    return carried


def gathered(value):
    return lax.all_gather(value, GROUPED, axis=0, tiled=True)


def per_device(
    hidden_in,
    cotangent,
    teacher_out,
    teacher_mix,
    valid_mask,
    doc_start,
    attn_gain,
    w_query,
    w_key,
    w_value,
    w_forget,
    forget_bias,
    head_gain,
    w_outgate,
    w_out,
    mlp_gain,
    w_gate,
    w_up,
    w_down,
):
    tokens, features = hidden_in.shape
    devices = lax.axis_size(GROUPED)
    tp = lax.axis_size("tp")
    share = tokens // tp
    rows = w_query.shape[0]
    width = w_query.shape[1]
    slots = w_forget.shape[1]
    units = w_gate.shape[1]
    tokens_all = tokens * devices
    mask_flat = valid_mask.astype(F32)

    vectors = [jnp.stack([attn_gain, mlp_gain]), head_gain, forget_bias]
    attn_parts = [w_query, w_key, w_value, w_outgate]
    mlp_parts = [w_gate, w_up, w_down]
    if (lax.axis_size("shard"), lax.axis_size("ctx")) == (4, 2):
        first, row_all, pack = run_spread(
            "gather_attention", 5, attn_parts, mlp_parts, w_forget.T, valid_mask.reshape(1, -1), vectors
        )
        second = gathered(pack)
        out_own, first = lax.optimization_barrier((w_out, first))
        (out_w,) = run_spread("gather_out", 6, [out_own])
        first, row_all, out_w = lax.optimization_barrier((first, row_all, out_w))
    else:
        vectors.append(jnp.sum(mask_flat).reshape(1, 1))
        row = [jnp.pad(v.astype(F32), ((0, 0), (0, rows - v.shape[1]))) for v in vectors]
        row_all = gathered(jnp.concatenate(row, axis=0)[None])
        forget_w = jnp.pad(w_forget, ((0, 0), (0, 128 - slots)))
        first = gathered(jnp.concatenate([*attn_parts, forget_w, w_out], axis=1))
        pack, first = lax.optimization_barrier((jnp.concatenate(mlp_parts, axis=1), first))
        second = gathered(pack)
        out_w = first[:, 4 * width + 128 :]
        first = first[:, : 4 * width + 128]

    attn_scale = row_all[:, 0].reshape(1, -1)
    mlp_scale = row_all[:, 1].reshape(1, -1)
    head_scale = row_all[:, 2, : width // devices].reshape(1, width)
    bias = row_all[:, 3, : slots // devices].reshape(1, slots)
    count_total = jnp.sum(row_all[:, 4, 0])
    loss_scale = (tokens_all / count_total).reshape(1, 1)

    hidden_f = hidden_in.astype(F32)
    scale = lax.rsqrt(jnp.mean(hidden_f * hidden_f, axis=-1, keepdims=True) + EPSILON)
    normed_in = (hidden_f * scale * attn_scale).astype(BF)
    pre_all = dot_nn(normed_in, first)
    query_pre = pre_all[:, :width]
    keys_pre = pre_all[:, width : 2 * width]
    query = jax.nn.silu(query_pre).astype(BF)
    keys = jax.nn.silu(keys_pre).astype(BF)
    values = pre_all[:, 2 * width : 3 * width].astype(BF)
    gate_pre = pre_all[:, 3 * width : 4 * width]
    forget_pre = pre_all[:, 4 * width : 4 * width + slots] + bias
    resets = doc_start.astype(F32)[:, None]

    spans, total, ends = run_ends(forget_pre, resets, keys, values)
    decay = total.reshape(slots, 1)
    state = relay(ends, decay, "ctx", 1)
    probs, pairs, mixing, mix, gated = run_forward(
        query, keys, values, forget_pre, spans, state, gate_pre, head_scale
    )
    gate_w = second[:, :units]
    up_w = second[:, units : 2 * units]
    down_w = second[:, 2 * units :]

    by_share = lambda tensor: tensor.reshape(tp, share, -1)
    hidden_s, teacher_out_s, teacher_mix_s, cotangent_s = map(by_share, (hidden_in, teacher_out, teacher_mix, cotangent))
    mask_s = by_share(mask_flat)
    narrow = lambda *shape: jax.ShapeDtypeStruct(shape, F32)

    partial = dot_nt(gated, out_w).astype(BF)
    partial, mask_s, loss_scale = lax.optimization_barrier((partial, mask_s, loss_scale))
    normed_mid, branch = run_exchange(
        middle_epilogue, "sum_branch", 1, partial, (hidden_s, mlp_scale),
        (narrow(share, features),),
    )
    gate_val = dot_nn(normed_mid, gate_w)
    up_val = dot_nn(normed_mid, up_w)
    hidden_units = (jax.nn.silu(gate_val) * up_val).astype(BF)
    units_all = gathered(hidden_units)
    output, grad_result, losses, normed_in_c, normed_mid_c = run_exchange(
        result_epilogue, "sum_result", 2, dot_nt(hidden_units, down_w).astype(BF),
        (hidden_s, branch, teacher_out_s, teacher_mix_s, cotangent_s, mask_s, loss_scale),
        (narrow(share, features), narrow(1, 128)),
        moved=(normed_in, normed_mid),
    )
    gap = output.astype(F32) - teacher_out.astype(F32)
    grad_mlp = (cotangent.astype(F32) + loss_scale * mask_flat[:, None] * gap).astype(BF)
    grad_units = dot_nn(grad_mlp, down_w)
    gate_sig = jax.nn.sigmoid(gate_val)
    grad_gate_val = (grad_units * up_val * (gate_sig * (1.0 + gate_val * (1.0 - gate_sig)))).astype(BF)
    grad_up_val = (grad_units * (gate_val * gate_sig)).astype(BF)
    grad_both = jnp.concatenate([grad_gate_val, grad_up_val], axis=1)
    partial = dot_nt(grad_both, second[:, : 2 * units]).astype(BF)
    units_all, grad_both = lax.optimization_barrier((units_all, grad_both))
    partial = lax.optimization_barrier((partial, grad_both))[0]
    mlp_all = gathered(grad_both)
    grad_branch, grad_middle, mlp_gain_part, grad_mlp_c = run_exchange(
        branch_epilogue, "sum_middle", 3, partial,
        (hidden_s, branch, teacher_mix_s, grad_result, mask_s, loss_scale, mlp_scale),
        (narrow(share, features), narrow(1, features)),
        moved=(grad_mlp,),
    )
    grad_gated = dot_nn(grad_branch, out_w)
    gquery, gkeys, gvalues, ggate, head_gain_part, gwrite, glog, carry = run_backward(
        grad_gated, query, keys, values, forget_pre, spans, state, gate_pre, head_scale, probs, pairs, mixing, mix
    )
    later = relay(carry, decay, "ctx", -1)
    grad_pre, bias_part = run_finish(
        gquery, gkeys, gvalues, ggate, gwrite, glog, keys, values, forget_pre, spans, query_pre, keys_pre,
        state, total, later, gated,
    )
    partial = dot_nt(grad_pre[:, width:], first).astype(BF)
    mlp_all, grad_pre = lax.optimization_barrier((mlp_all, grad_pre))
    partial = lax.optimization_barrier((partial, grad_pre))[0]
    attn_all = gathered(grad_pre)
    grad_in, _, grad_branch_c, plane_sums, all_sums = run_exchange(
        input_epilogue, "sum_input", 4, partial,
        (hidden_s, grad_middle, attn_scale, jnp.concatenate([mlp_gain_part, head_gain_part, bias_part, losses], axis=1)),
        (narrow(1, features),), moved=(grad_branch,), summing=True,
    )
    gate_grad, up_grad, down_grad, turned_branch, turned_in = run_weights(
        "mlp_weights", (normed_mid_c, grad_mlp_c), (mlp_all, units_all),
        ((0, 0, 0, units), (0, 0, units, units), (1, 1, 0, units)), (grad_branch_c, normed_in_c),
    )
    out_grad, query_grad, keys_grad, values_grad, outgate_grad, forget_grad = run_attention_weights(
        turned_branch, turned_in, attn_all, width, slots
    )
    index = lax.axis_index(GROUPED)

    cut = lambda row, size: lax.dynamic_slice_in_dim(row, index * size, size, axis=1)
    attn_gain_grad = cut(all_sums[:, :features], features // devices).reshape(-1)
    mlp_gain_grad = cut(all_sums[:, features : 2 * features], features // devices).reshape(-1)
    head_gain_grad = cut(plane_sums[:, 2 * features : 2 * features + width], width // devices)
    bias_grad = cut(plane_sums[:, 2 * features + width : 2 * features + width + slots], slots // devices)
    sums = all_sums[0, 2 * features + width + 128 :]
    loss_out = sums[0] / (2.0 * features * count_total)
    loss_mix = sums[1] / (2.0 * features * count_total)
    return (
        output,
        loss_out,
        loss_mix,
        grad_in.astype(F32),
        attn_gain_grad,
        query_grad,
        keys_grad,
        values_grad,
        forget_grad.T,
        bias_grad,
        head_gain_grad,
        outgate_grad,
        out_grad,
        mlp_gain_grad,
        gate_grad,
        up_grad,
        down_grad,
    )


def solution(mesh):
    return jax.shard_map(
        per_device,
        mesh=mesh,
        in_specs=(
            P(("shard", "ctx"), None),
            P(("shard", "ctx"), None),
            P(("shard", "ctx"), None),
            P(("shard", "ctx"), None),
            P(("shard", "ctx")),
            P(("shard", "ctx")),
            P(("shard", "ctx")),
            P(("shard", "ctx"), "tp"),
            P(("shard", "ctx"), "tp"),
            P(("shard", "ctx"), "tp"),
            P(("shard", "ctx"), "tp"),
            P("tp", ("shard", "ctx")),
            P("tp", ("shard", "ctx")),
            P(("shard", "ctx"), "tp"),
            P(("shard", "ctx"), "tp"),
            P(("shard", "ctx")),
            P(("shard", "ctx"), "tp"),
            P(("shard", "ctx"), "tp"),
            P(("shard", "ctx"), "tp"),
        ),
        out_specs=(
            P(("shard", "ctx"), None),
            P(),
            P(),
            P(("shard", "ctx"), None),
            P(("shard", "ctx")),
            P(("shard", "ctx"), "tp"),
            P(("shard", "ctx"), "tp"),
            P(("shard", "ctx"), "tp"),
            P(("shard", "ctx"), "tp"),
            P("tp", ("shard", "ctx")),
            P("tp", ("shard", "ctx")),
            P(("shard", "ctx"), "tp"),
            P(("shard", "ctx"), "tp"),
            P(("shard", "ctx")),
            P(("shard", "ctx"), "tp"),
            P(("shard", "ctx"), "tp"),
            P(("shard", "ctx"), "tp"),
        ),
        check_vma=False,
    )
```
